32 devices in a mesh: grp: 4 (over y, x), ctx: 8 (over z, core).
Axes of the slice: x: 2, y: 2, z: 4, core: 2. Of those that a mesh axis runs over, the one named last changes fastest.
Arguments:
- layer_input: bfloat16 [8192, 768], P(('grp', 'ctx')), may hold values from -6 to 6
- block_table: int32 [4, 16], P('grp'), may hold values from 0 to 15, each once within a row
- ln1_gain: bfloat16 [768], replicated, may hold values from 0.5 to 1.5
- ln1_bias: bfloat16 [768], replicated, may hold values from -2 to 2
- ln2_gain: bfloat16 [768], replicated, may hold values from 0.5 to 1.5
- ln2_bias: bfloat16 [768], replicated, may hold values from -2 to 2
- w_query: bfloat16 [768, 768], replicated, may hold values from -0.21875 to 0.21875
- w_keyval: bfloat16 [768, 128], replicated, may hold values from -0.21875 to 0.21875
- w_out: bfloat16 [768, 768], replicated, may hold values from -3.5 to 3.5
- w_up: bfloat16 [768, 3072], replicated, may hold values from -0.21875 to 0.21875
- w_down: bfloat16 [3072, 768], replicated, may hold values from -0.109375 to 0.109375
- cotangent: bfloat16 [8192, 768], P(('grp', 'ctx')), may hold values from -6 to 6
Outputs:
- layer_output: bfloat16 [8192, 768], P(('grp', 'ctx'))
- in_grad: float32 [8192, 768], P(('grp', 'ctx'))
- grad_ln1_gain: float32 [768], P('ctx')
- grad_ln1_bias: float32 [768], P('ctx')
- grad_ln2_gain: float32 [768], P('ctx')
- grad_ln2_bias: float32 [768], P('ctx')
- grad_w_query: float32 [768, 768], P('ctx')
- grad_w_keyval: float32 [768, 128], P('ctx')
- grad_w_out: float32 [768, 768], P('ctx')
- grad_w_up: float32 [768, 3072], P('ctx')
- grad_w_down: float32 [3072, 768], P('ctx')
The draws below stay inside these ranges and needn't reach their ends.
Inputs may be any that keep to these rules, and one draw needn't show every extreme that they name: Each row of block_table names every block of 0 to 15 once.
All inputs are finite; a program needn't handle non-finite values.
Results may differ from the reference program's by a relative error of at most 0.012.
Values may be sent and summed in bfloat16 or wider, within the bound.
No kernel may reach another device: no remote copies, remote signals or barrier semaphores. Data moves between devices by JAX's collectives and lax.ppermute only.
A program may use at most 192 MiB of HBM per device.

```python
import jax
import jax.numpy as jnp
from jax import lax

D = 768
HEADS = 12
HEAD_DIM = 64
ROT = 16
FF = 3072
BLK = 128
CONT = 1024
GROUP = 2048
TOKENS = 8192
NBLK = 16
N_GRP = 4


def steps_of(rng, shape, shards, smallest, high):
    level = 1.0
    for axis_at, shards_of in shards:
        steps = jax.random.uniform(jax.random.fold_in(jax.random.fold_in(rng, 6), axis_at), (shards_of,), jnp.float32, smallest / len(shards), high / len(shards))
        level = level * jnp.repeat(jnp.exp(steps), shape[axis_at] // shards_of).reshape((-1,) + (1,) * (len(shape) - 1 - axis_at))
    return level


def bell_draw(rng, shape, deviation, most, cuts=(), kind=jnp.bfloat16):
    values = deviation * jax.random.normal(rng, shape, jnp.float32)
    if cuts:
        values = values * steps_of(rng, shape, cuts, -0.22, 0.18)
    return jnp.clip(values, -most, most).astype(kind)


def setup_inputs(seed: int = 0) -> dict:
    splits = jax.random.split(jax.random.key(seed), 13)
    layer_input = bell_draw(splits[0], (TOKENS, D), 1.0, 6.0, ((0, 32),))
    block_table = jax.vmap(lambda own: jax.random.permutation(own, NBLK))(jax.random.split(splits[1], N_GRP)).reshape((N_GRP, NBLK)).astype(jnp.int32)
    ln1_gain = jnp.clip(1.0 + 0.1 * jax.random.normal(splits[2], (D,), jnp.float32), 0.5, 1.5).astype(jnp.bfloat16)
    ln1_bias = bell_draw(splits[3], (D,), 0.3, 2.0)
    ln2_gain = jnp.clip(1.0 + 0.1 * jax.random.normal(splits[4], (D,), jnp.float32), 0.5, 1.5).astype(jnp.bfloat16)
    ln2_bias = bell_draw(splits[5], (D,), 0.3, 2.0)
    w_query = bell_draw(splits[6], (D, D), D ** -0.5, 0.21875)
    w_keyval = bell_draw(splits[7], (D, 2 * HEAD_DIM), D ** -0.5, 0.21875)
    w_out = bell_draw(splits[8], (D, D), (max(1, D // 256)) ** -0.5, 3.5)
    w_up = bell_draw(splits[9], (D, FF), D ** -0.5, 0.21875)
    w_down = bell_draw(splits[10], (FF, D), FF ** -0.5, 0.109375)
    cotangent = bell_draw(splits[11], (TOKENS, D), 1.0, 6.0, ((0, 32),))
    return {"layer_input": layer_input, "block_table": block_table, "ln1_gain": ln1_gain, "ln1_bias": ln1_bias, "ln2_gain": ln2_gain, "ln2_bias": ln2_bias, "w_query": w_query, "w_keyval": w_keyval, "w_out": w_out, "w_up": w_up, "w_down": w_down, "cotangent": cotangent}


EPS = 1e-05
highest = lax.Precision.HIGHEST

@jax.custom_vjp
def low(v):
    return lax.optimization_barrier(v.astype(jnp.bfloat16)).astype(jnp.float32)

@jax.custom_vjp
def low_back(v):
    return v

def low_keep(v):
    return (low(v), None)

def low_pass(kept, grad):
    return (grad,)

def back_keep(v):
    return (v, None)

def back_low(kept, grad):
    return (low(grad),)
low.defvjp(low_keep, low_pass)
low_back.defvjp(back_keep, back_low)

def matmul(left, right):
    return jnp.dot(left, right, precision=highest)

def layer_norm(values, gain, bias):
    center = lax.optimization_barrier(jnp.mean(values, -1, keepdims=True))
    shifted = values - center
    spread = lax.optimization_barrier(jnp.mean(shifted * shifted, -1, keepdims=True))
    return shifted * lax.rsqrt(spread + EPS) * gain + bias

def token_meta(canon, group_len):
    prompt_len = group_len // 2
    cont_span = min(CONT, prompt_len)
    after = canon - prompt_len
    segment = jnp.where(canon < prompt_len, 0, 1 + after // cont_span).astype(jnp.int32)
    position = jnp.where(canon < prompt_len, canon, prompt_len + after % cont_span).astype(jnp.int32)
    return (segment, position)

def rope_tables(position):
    half = ROT // 2
    inverse = 10000.0 ** (-(2.0 * jnp.arange(half, dtype=jnp.float32)) / ROT)
    angles = position.astype(jnp.float32)[:, None] * inverse[None, :]
    return (jnp.cos(angles), jnp.sin(angles))

def rotate(values, cosine, sine):
    half = ROT // 2
    first = values[..., :half]
    second = values[..., half:ROT]
    cos_b = cosine[:, None, :]
    sin_b = sine[:, None, :]
    return jnp.concatenate([first * cos_b - second * sin_b, second * cos_b + first * sin_b, values[..., ROT:]], -1)

def reference(layer_input, block_table, ln1_gain, ln1_bias, ln2_gain, ln2_bias, w_query, w_keyval, w_out, w_up, w_down, cotangent):
    offsets = jnp.arange(BLK, dtype=jnp.int32)
    canon = (block_table[:, :, None] * BLK + offsets[None, None, :]).reshape(N_GRP, GROUP)
    segment, position = token_meta(canon, GROUP)
    cosine, sine = rope_tables(position.reshape(TOKENS))
    query_rows = min(512, GROUP)
    count = GROUP // query_rows

    def attend_group(member):
        q_group, k_group, v_group, seg_group, pos_group = member

        def block(inner):
            q_block, seg_block, pos_block = inner
            scores = jnp.einsum('rhd,kd->hrk', q_block, k_group, precision=highest) * 0.125
            scores = low_back(scores)
            visible = ((seg_group[None, :] == 0) | (seg_group[None, :] == seg_block[:, None])) & (pos_group[None, :] <= pos_block[:, None])
            scores = jnp.where(visible[None], scores, -1e+30)
            chance = low(jax.nn.softmax(scores, axis=-1))
            return jnp.einsum('hrk,kd->rhd', chance, v_group, precision=highest)
        mixed_blocks = lax.map(jax.checkpoint(block), (q_group.reshape(count, query_rows, HEADS, HEAD_DIM), seg_group.reshape(count, query_rows), pos_group.reshape(count, query_rows)))
        return mixed_blocks.reshape(GROUP, HEADS, HEAD_DIM)

    def forward(x_full, gain_one, bias_one, gain_two, bias_two, query_w, keyval_w, out_w, up_w, down_w):
        h_one = low(layer_norm(x_full, gain_one, bias_one))
        h_two = low(layer_norm(x_full, gain_two, bias_two))
        q_raw = low_back(matmul(h_one, query_w)).reshape(TOKENS, HEADS, HEAD_DIM)
        kv_raw = low_back(matmul(h_one, keyval_w))
        queries = low(rotate(q_raw, cosine, sine))
        keys = low(rotate(kv_raw[:, None, :HEAD_DIM], cosine, sine)[:, 0, :])
        values = low(kv_raw[:, HEAD_DIM:])
        mixed = lax.map(attend_group, (queries.reshape(N_GRP, GROUP, HEADS, HEAD_DIM), keys.reshape(N_GRP, GROUP, HEAD_DIM), values.reshape(N_GRP, GROUP, HEAD_DIM), segment, position))
        mixed = low(low_back(mixed.reshape(TOKENS, D)))
        up_val = low_back(matmul(h_two, up_w))
        act = low(jax.nn.gelu(up_val, approximate=False))
        return x_full + matmul(mixed, out_w) + matmul(act, down_w)
    params = (layer_input, ln1_gain, ln1_bias, ln2_gain, ln2_bias, w_query, w_keyval, w_out, w_up, w_down)
    params = tuple((member.astype(jnp.float32) for member in params))
    result, pullback = jax.vjp(forward, *params)
    grads = pullback(cotangent.astype(jnp.float32))
    return (result.astype(jnp.bfloat16), grads[0], grads[1], grads[2], grads[3], grads[4], grads[5], grads[6], grads[7], grads[8], grads[9])
```

```python
import functools

import jax
import jax.numpy as jnp
from jax import lax
from jax.experimental import pallas as pl
from jax.experimental.pallas import tpu as pltpu
from jax.sharding import PartitionSpec as P

ROT = 16
BLK = 128
CONT = 1024
TILE = 256
EPS = 1e-05
LOG2E = 1.4426950408889634
LN2 = 0.6931471805599453
BF = jnp.bfloat16
F32 = jnp.float32


def dot(left, right, dims=((1,), (0,))):
    return lax.dot_general(left, right, (dims, ((), ())), preferred_element_type=F32)


def rope_tables(position):
    half = ROT // 2
    inverse = 10000.0 ** (-(2.0 * jnp.arange(half, dtype=F32)) / ROT)
    angles = inverse[:, None] * position.astype(F32)[None, :]
    return (jnp.cos(angles), jnp.sin(angles))


def rotate_rows(values, cosine, sine):
    half = ROT // 2
    first, second = values[:, :half], values[:, half:ROT]
    cos_t, sin_t = cosine.T, sine.T
    return jnp.concatenate(
        [first * cos_t - second * sin_t, second * cos_t + first * sin_t, values[:, ROT:]], -1
    )


def attn_kernel(
    table,
    place,
    q_ref,
    do_ref,
    cos_ref,
    sin_ref,
    kv_ref,
    mix_ref,
    dq_ref,
    dkv_ref,
    kv_c,
    kv_t,
    s_scr,
    p_scr,
    rq,
    rd,
    rqt,
    rdt,
    o_acc,
    dq_acc,
    dkv_acc,
    *,
    blocks,
    heads,
    size,
):
    step, group = pl.program_id(0), pl.program_id(1)
    lanes = heads * BLK
    prompt_blocks = blocks // 2
    prompt_tiles = prompt_blocks * BLK // TILE
    cont_blocks = min(CONT, prompt_blocks * BLK) // BLK

    @pl.when((step == 0) & (group == 0))
    def _():
        ones = jnp.ones((16, BLK), BF)

        def place_block(slot, carry):
            block = table[slot]
            rows = kv_ref[pl.ds(pl.multiple_of(slot * BLK, BLK), BLK), :]
            kv_c[pl.ds(pl.multiple_of(block * BLK, BLK), BLK), :] = rows
            turned = jnp.concatenate([rows.T, ones], 0)

            @pl.when(block % 2 == 0)
            def _():
                kv_t[block // 2, :, 0:BLK] = turned

            @pl.when(block % 2 == 1)
            def _():
                kv_t[block // 2, :, BLK:TILE] = turned

            return carry

        lax.fori_loop(0, blocks, place_block, 0)
        dkv_acc[...] = jnp.zeros_like(dkv_acc)

    block = table[place[0] + step]
    last = block // 2
    in_prompt = block < prompt_blocks
    seg_tile = (prompt_blocks + (block - prompt_blocks) // cont_blocks * cont_blocks) // 2
    full = jnp.where(in_prompt, last, prompt_tiles + last - seg_tile)

    def tile_of(i):
        return jnp.where(i < prompt_tiles, jnp.minimum(i, last), i - prompt_tiles + seg_tile)

    def key_rows(tile):
        return pl.ds(pl.multiple_of(tile * TILE, TILE), TILE)

    for h in range(heads):
        rq[0:size, h * BLK : (h + 1) * BLK] = q_ref[h * size : (h + 1) * size, :]
    rq[size : 2 * size, :] = jnp.zeros((size, lanes), BF)

    def scores(tile):
        return dot(kv_c[key_rows(tile), :], rq[...])

    def fold(values):
        return jnp.max(values.reshape(TILE // 8, 8, lanes), 0)

    def first_pass(i, top):
        part = scores(tile_of(i))
        s_scr[i] = part
        return jnp.maximum(top, fold(part))

    top = lax.fori_loop(0, full, first_pass, jnp.full((8, lanes), -1e30, F32))
    part = scores(last)
    key_at = last * TILE + lax.broadcasted_iota(jnp.int32, (TILE, lanes), 0)
    row_at = block * BLK + lax.rem(lax.broadcasted_iota(jnp.int32, (TILE, lanes), 1), BLK)
    part = jnp.where(key_at <= row_at, part, -1e30)
    s_scr[full] = part
    top = jnp.max(jnp.maximum(top, fold(part)), 0, keepdims=True)

    o_acc[...] = jnp.zeros_like(o_acc)

    def second_pass(i, carry):
        p = jnp.exp2(s_scr[i] - top).astype(BF)
        p_scr[i] = p
        o_acc[...] += dot(kv_t[jnp.where(i == full, last, tile_of(i)), size : 2 * size + 16, :], p)
        return carry

    lax.fori_loop(0, full + 1, second_pass, 0)

    inverse = 1.0 / o_acc[size : size + 1, :]
    mixed = o_acc[0:size, :] * inverse
    grads = []
    for h in range(heads):
        at = slice(h * BLK, (h + 1) * BLK)
        mix_ref[h * size : (h + 1) * size, :] = mixed[:, at].astype(BF)
        grads.append(do_ref[h * size : (h + 1) * size, :])
    scaled = (jnp.concatenate(grads, 1) * inverse).astype(BF)
    delta = jnp.sum(mixed * scaled.astype(F32), 0, keepdims=True)
    rd[0:size, :] = jnp.zeros((size, lanes), BF)
    rd[size : 2 * size, :] = scaled
    rqt[...] = rq[...].T
    rdt[...] = rd[...].T
    dq_acc[...] = jnp.zeros_like(dq_acc)

    def third_pass(i, carry):
        tile = jnp.where(i == full, last, tile_of(i))
        p = p_scr[i]
        d_probs = dot(kv_c[key_rows(tile), :], rd[...])
        ds = (p.astype(F32) * (d_probs - delta)).astype(BF)
        dq_acc[...] += dot(kv_t[tile, 0:size, :], ds)
        dkv_acc[key_rows(tile), :] += dot(p, rdt[...]) + dot(ds, rqt[...])
        return carry

    lax.fori_loop(0, full + 1, third_pass, 0)

    half = ROT // 2
    cosine, sine = cos_ref[...], sin_ref[...]
    for h in range(heads):
        part = dq_acc[:, h * BLK : (h + 1) * BLK] * 0.125
        first, second = part[0:half, :], part[half:ROT, :]
        turned = jnp.concatenate(
            [first * cosine + second * sine, second * cosine - first * sine, part[ROT:, :]], 0
        )
        dq_ref[h * size : (h + 1) * size, :] = turned.astype(BF)

    @pl.when((step == pl.num_programs(0) - 1) & (group == pl.num_programs(1) - 1))
    def _():
        scale = jnp.where(
            lax.broadcasted_iota(jnp.int32, (BLK, 2 * size), 1) < size, F32(LN2), F32(1.0)
        )

        def give_block(slot, carry):
            rows = dkv_acc[pl.ds(pl.multiple_of(table[slot] * BLK, BLK), BLK), :]
            dkv_ref[pl.ds(pl.multiple_of(slot * BLK, BLK), BLK), :] = (rows * scale).astype(BF)
            return carry

        lax.fori_loop(0, blocks, give_block, 0)


def attention(table, place, q_t, do_t, cosine, sine, kv_all):
    width, rows = q_t.shape
    keys = kv_all.shape[0]
    size = kv_all.shape[1] // 2
    all_heads = width // size
    blocks = keys // BLK
    heads = all_heads if keys <= 4096 else 2
    lanes = heads * BLK
    cont = min(CONT, keys // 2)
    most = (keys // 2 + cont) // TILE
    tiles = keys // TILE
    whole = lambda *shape: pl.BlockSpec(shape, lambda i, j, *_: (0,) * len(shape))
    return pl.pallas_call(
        functools.partial(attn_kernel, blocks=blocks, heads=heads, size=size),
        out_shape=(
            jax.ShapeDtypeStruct((width, rows), BF),
            jax.ShapeDtypeStruct((width, rows), BF),
            jax.ShapeDtypeStruct((keys, 2 * size), BF),
        ),
        grid_spec=pltpu.PrefetchScalarGridSpec(
            num_scalar_prefetch=2,
            grid=(rows // BLK, all_heads // heads),
            in_specs=[
                pl.BlockSpec((heads * size, BLK), lambda i, j, *_: (j, i)),
                pl.BlockSpec((heads * size, BLK), lambda i, j, *_: (j, i)),
                pl.BlockSpec((ROT // 2, BLK), lambda i, j, *_: (0, i)),
                pl.BlockSpec((ROT // 2, BLK), lambda i, j, *_: (0, i)),
                whole(keys, 2 * size),
            ],
            out_specs=[
                pl.BlockSpec((heads * size, BLK), lambda i, j, *_: (j, i)),
                pl.BlockSpec((heads * size, BLK), lambda i, j, *_: (j, i)),
                whole(keys, 2 * size),
            ],
            scratch_shapes=[
                pltpu.VMEM((keys, 2 * size), BF),
                pltpu.VMEM((tiles, 2 * size + 16, TILE), BF),
                pltpu.VMEM((most, TILE, lanes), F32),
                pltpu.VMEM((most, TILE, lanes), BF),
                pltpu.VMEM((2 * size, lanes), BF),
                pltpu.VMEM((2 * size, lanes), BF),
                pltpu.VMEM((lanes, 2 * size), BF),
                pltpu.VMEM((lanes, 2 * size), BF),
                pltpu.VMEM((size + 16, lanes), F32),
                pltpu.VMEM((size, lanes), F32),
                pltpu.VMEM((keys, 2 * size), F32),
            ],
        ),
        compiler_params=pltpu.CompilerParams(vmem_limit_bytes=60 * 1024 * 1024),
        cost_estimate=pl.CostEstimate(
            flops=8 * width * rows * keys, bytes_accessed=4 * width * rows * 4, transcendentals=0
        ),
        name="attention",
    )(table, place, q_t, do_t, cosine, sine, kv_all)


class Links:
    def __init__(self, n_grp, n_ctx):
        self.n_grp, self.n_ctx, self.n_pair = n_grp, n_ctx, n_ctx // 2
        self.small = (n_grp, n_ctx) == (4, 8)
        self.ctx = lax.axis_index("ctx")
        self.grp = lax.axis_index("grp")
        self.core = self.ctx % 2
        self.chip = self.ctx // 2
        self.groups = [[2 * z + c for z in range(self.n_pair)] for c in range(2)]

    def swap(self, value):
        return lax.ppermute(value, "ctx", [(i, i ^ 1) for i in range(self.n_ctx)])

    def permute(self, value, target):
        pairs = []
        for g in range(self.n_grp):
            for i in range(self.n_ctx):
                y, x, z, c = target(g // 2, g % 2, i // 2, i % 2)
                pairs.append((g * self.n_ctx + i, (2 * y + x) * self.n_ctx + 2 * z + c))
        return lax.ppermute(value, ("grp", "ctx"), pairs)

    def shift(self, value, k):
        return self.permute(value, lambda y, x, z, c: (y, x, (z + k) % 4, c))

    def cross(self, value, stage):
        return self.permute(
            value, lambda y, x, z, c: (y, 1 - x, z, c) if c == stage else (1 - y, x, z, c)
        )

    def bit(self, stage):
        y, x = self.grp // 2, self.grp % 2
        return jnp.where(self.core == stage, x, y)

    def spread(self, parts):
        total = lax.dynamic_index_in_dim(parts, self.chip, 0, False).astype(F32)
        for k in range(1, 4):
            out = lax.dynamic_index_in_dim(parts, (self.chip + k) % 4, 0, False)
            total = total + self.shift(out, k).astype(F32)
        return total

    def reduce(self, parts):
        if not self.small:
            moved = lax.all_to_all(parts, "ctx", 0, 0, axis_index_groups=self.groups)
            own = jnp.sum(moved.astype(F32), 0)
            return lax.psum(own.astype(BF), "grp").astype(F32)
        for stage in range(2):
            rows = parts.shape[1] // 2
            bit = self.bit(stage)
            send = lax.dynamic_slice_in_dim(parts, (1 - bit) * rows, rows, 1)
            keep = lax.dynamic_slice_in_dim(parts, bit * rows, rows, 1)
            got = self.cross(send, stage)
            parts = (keep.astype(F32) + got.astype(F32)).astype(BF)
        own = self.spread(parts).astype(BF)
        for stage in (1, 0):
            got = self.cross(own, stage)
            low = self.bit(stage) == 0
            own = jnp.concatenate([jnp.where(low, own, got), jnp.where(low, got, own)], 0)
        return own.astype(F32)

    def reduce_few(self, parts):
        if not self.small:
            return self.reduce(parts)
        own = self.spread(parts).astype(BF)
        total = own.astype(F32)
        total = total + self.permute(own, lambda y, x, z, c: (y, 1 - x, z, c)).astype(F32)
        total = total + self.permute(own, lambda y, x, z, c: (1 - y, x, z, c)).astype(F32)
        return total + self.permute(own, lambda y, x, z, c: (1 - y, 1 - x, z, c)).astype(F32)

    def gather_pairs(self, value):
        if not self.small:
            return lax.all_gather(value, "ctx", axis=0, axis_index_groups=self.groups)
        parts = [value] + [self.shift(value, k) for k in range(1, 4)]
        stacked = jnp.stack([parts[0], parts[3], parts[2], parts[1]] * 2)
        return lax.dynamic_slice_in_dim(stacked, (4 - self.chip) % 4, 4, 0)


def column_sums(values):
    return jnp.sum(values, 0)


def shards(
    layer_input,
    block_table,
    ln1_gain,
    ln1_bias,
    ln2_gain,
    ln2_bias,
    w_query,
    w_keyval,
    w_out,
    w_up,
    w_down,
    cotangent,
    *,
    n_grp,
    n_ctx,
):
    links = Links(n_grp, n_ctx)
    core, chip, n_pair = links.core, links.chip, links.n_pair
    rows, width = layer_input.shape
    size = w_keyval.shape[1] // 2
    hidden = w_up.shape[1]
    group_len = block_table.shape[1] * BLK
    part_rows = width // n_ctx
    part_hidden = hidden // n_ctx
    half_width = width // 2
    half_hidden = hidden // 2
    pair_blocks = 2 * rows // BLK
    table = block_table[0]

    def both(own, other):
        return jnp.concatenate(
            [jnp.where(core == 0, own, other), jnp.where(core == 0, other, own)], 0
        )

    def mine(value, own_core):
        return lax.dynamic_slice_in_dim(value, own_core * rows, rows, 0)

    x_two = both(layer_input, links.swap(layer_input))
    g_two = both(cotangent, links.swap(cotangent))

    canon = (
        lax.dynamic_slice_in_dim(table, chip * pair_blocks, pair_blocks)[:, None] * BLK
        + jnp.arange(BLK, dtype=jnp.int32)[None, :]
    ).reshape(2 * rows)
    prompt_len = group_len // 2
    cont_span = min(CONT, prompt_len)
    position = jnp.where(
        canon < prompt_len, canon, prompt_len + (canon - prompt_len) % cont_span
    )
    cosine, sine = rope_tables(position)

    gain_one, gain_two = ln1_gain.astype(F32), ln2_gain.astype(F32)
    x_full = x_two.astype(F32)
    shifted = x_full - jnp.mean(x_full, -1, keepdims=True)
    scale = lax.rsqrt(jnp.mean(shifted * shifted, -1, keepdims=True) + EPS)
    hat = shifted * scale
    h_one = (hat * gain_one + ln1_bias.astype(F32)).astype(BF)
    h_two = (hat * gain_two + ln2_bias.astype(F32)).astype(BF)

    kv_raw = dot(h_one, w_keyval)
    kv_low = jnp.concatenate(
        [rotate_rows(kv_raw[:, :size], cosine, sine), kv_raw[:, size:]], -1
    ).astype(BF)
    kv_all = links.gather_pairs(kv_low).reshape(group_len, 2 * size)

    up_half = lax.dynamic_index_in_dim(
        w_up.reshape(width, n_pair, 2, part_hidden), core, 2, False
    ).reshape(width, half_hidden)
    down_half = lax.dynamic_index_in_dim(
        w_down.reshape(n_pair, 2, part_hidden, width), core, 1, False
    ).reshape(half_hidden, width)
    up_val = dot(h_two, up_half)
    cdf_val = 0.5 * (1.0 + lax.erf(up_val * 0.7071067811865476))
    pdf_val = jnp.exp(-0.5 * up_val * up_val) * 0.3989422804014327
    act = (up_val * cdf_val).astype(BF)
    grad_down = dot(act, g_two, ((0,), (0,))).astype(BF)
    total_down = links.reduce(grad_down.reshape(n_pair, part_hidden, width))
    grad_act = dot(g_two, down_half, ((1,), (1,)))
    grad_up = (grad_act * (cdf_val + up_val * pdf_val)).astype(BF)
    grad_up_w = dot(h_two, grad_up, ((0,), (0,))).astype(BF)

    def parity(value, which):
        return lax.dynamic_index_in_dim(
            value.reshape(n_pair, 2, part_rows, value.shape[-1]), which, 1, False
        )

    up_own = parity(grad_up_w, core)
    up_got = links.swap(parity(grad_up_w, 1 - core))
    up_parts = jnp.concatenate(
        [jnp.where(core == 0, up_own, up_got), jnp.where(core == 0, up_got, up_own)], -1
    )
    total_up = links.reduce(up_parts)
    total_up = (
        total_up.reshape(part_rows, 2, n_pair, part_hidden)
        .transpose(0, 2, 1, 3)
        .reshape(part_rows, hidden)
    )

    query_half = lax.dynamic_slice_in_dim(w_query, core * half_width, half_width, 1)
    out_half = lax.dynamic_slice_in_dim(w_out, core * half_width, half_width, 0)
    q_raw = dot(query_half, h_one, ((0,), (1,))).reshape(-1, size, 2 * rows) * (0.125 * LOG2E)
    half = ROT // 2
    first, second = q_raw[:, :half], q_raw[:, half:ROT]
    q_t = (
        jnp.concatenate(
            [first * cosine - second * sine, second * cosine + first * sine, q_raw[:, ROT:]], 1
        )
        .astype(BF)
        .reshape(half_width, 2 * rows)
    )
    do_t = dot(out_half, g_two, ((1,), (1,)))
    place = jnp.reshape(chip * pair_blocks, (1,)).astype(jnp.int32)
    mix_t, dq_t, dkv_part = attention(table, place, q_t, do_t, cosine, sine, kv_all)

    dkv_part = dkv_part.reshape(n_pair, 2, rows, 2 * size)
    dkv_own = lax.dynamic_index_in_dim(dkv_part, core, 1, False).astype(F32)
    dkv_got = links.swap(lax.dynamic_index_in_dim(dkv_part, 1 - core, 1, False)).astype(F32)
    dkv_sum = (dkv_own + dkv_got).astype(BF)
    if links.small:
        dkv = links.spread(dkv_sum)
    else:
        dkv = jnp.sum(
            lax.all_to_all(dkv_sum, "ctx", 0, 0, axis_index_groups=links.groups).astype(F32), 0
        )
    cos_own = lax.dynamic_slice_in_dim(cosine, core * rows, rows, 1)
    sin_own = lax.dynamic_slice_in_dim(sine, core * rows, rows, 1)
    dkv_low = jnp.concatenate(
        [rotate_rows(dkv[:, :size], cos_own, -sin_own), dkv[:, size:]], -1
    ).astype(BF)

    grad_q_w = dot(h_one, dq_t, ((0,), (1,))).astype(BF)
    grad_out_w = dot(mix_t, g_two).astype(BF)
    out_parts = grad_out_w.reshape(n_pair // 2, 2, part_rows, width)

    def pack(which):
        rows_out = lax.dynamic_index_in_dim(out_parts, which, 1, False)
        rows_out = rows_out.reshape(n_pair // 2, part_rows, 2, half_width).transpose(0, 2, 1, 3)
        return jnp.concatenate(
            [parity(grad_q_w, which), rows_out.reshape(n_pair, part_rows, half_width)], -1
        )

    own, got = pack(core), links.swap(pack(1 - core))
    low = jnp.where(core == 0, own, got)
    high = jnp.where(core == 0, got, own)
    query_parts = jnp.concatenate([low[..., :half_width], high[..., :half_width]], -1)

    def unpack(value):
        value = value[..., half_width:].reshape(n_pair // 2, 2, part_rows, half_width)
        return value.transpose(0, 2, 1, 3).reshape(n_pair // 2, part_rows, width)

    late_parts = jnp.concatenate(
        [query_parts, jnp.concatenate([unpack(low), unpack(high)], 0)], -1
    )
    total_late = links.reduce(late_parts)

    out_part = dot(act, down_half) + dot(mix_t, out_half, ((0,), (0,)))
    out_got = links.swap(mine(out_part, 1 - core).astype(BF))
    layer_output = (
        layer_input.astype(F32) + mine(out_part, core) + out_got.astype(F32)
    ).astype(BF)

    d_two = dot(grad_up, up_half, ((1,), (1,)))
    d_one = dot(dq_t, query_half, ((0,), (1,)))
    d_kv = dot(dkv_low, w_keyval, ((1,), (1,)))
    row_core = lax.broadcasted_iota(jnp.int32, (2 * rows, 1), 0) // rows
    d_one = d_one + jnp.where(row_core == core, jnp.concatenate([d_kv, d_kv], 0), 0.0)
    sums = jnp.stack(
        [column_sums(d_one * hat), column_sums(d_one), column_sums(d_two * hat), column_sums(d_two)]
    )
    d_hat = d_one * gain_one + d_two * gain_two
    hat_got = links.swap(mine(d_hat, 1 - core).astype(BF))
    d_hat = mine(d_hat, core) + hat_got.astype(F32)
    hat_own = mine(hat, core)
    in_grad = cotangent.astype(F32) + mine(scale, core) * (
        d_hat
        - jnp.mean(d_hat, -1, keepdims=True)
        - hat_own * jnp.mean(d_hat * hat_own, -1, keepdims=True)
    )

    grad_kv_w = dot(mine(h_one, core), dkv_low, ((0,), (0,)))
    sum_rows = sums.reshape(4, n_pair, 2, part_rows).transpose(1, 2, 0, 3)
    sum_rows = jnp.pad(sum_rows, ((0, 0), (0, 0), (0, 12), (0, 2 * size - part_rows)))
    few = jnp.concatenate([grad_kv_w.reshape(n_pair, 2, part_rows, 2 * size), sum_rows], 2)
    few_own = lax.dynamic_index_in_dim(few, core, 1, False)
    few_got = links.swap(lax.dynamic_index_in_dim(few, 1 - core, 1, False).astype(BF))
    total_few = links.reduce_few((few_own + few_got.astype(F32)).astype(BF))
    norm_sums = total_few[part_rows : part_rows + 4, :part_rows]
    return (
        layer_output,
        in_grad,
        norm_sums[0],
        norm_sums[1],
        norm_sums[2],
        norm_sums[3],
        total_late[:, :width],
        total_few[:part_rows],
        total_late[:, width:],
        total_up,
        total_down,
    )


def solution(mesh):
    return jax.shard_map(
        functools.partial(shards, n_grp=mesh.shape["grp"], n_ctx=mesh.shape["ctx"]),
        mesh=mesh,
        in_specs=(P(("grp", "ctx"), None), P("grp", None))
        + (P(),) * 9
        + (P(("grp", "ctx"), None),),
        out_specs=(P(("grp", "ctx"), None),) * 2 + (P("ctx"),) * 4 + (P("ctx", None),) * 5,
        check_vma=False,
    )
```

```python
import functools

import jax
import jax.numpy as jnp
from jax import lax
from jax.experimental import pallas as pl
from jax.experimental.pallas import tpu as pltpu
from jax.sharding import PartitionSpec as P

ROT = 16
HALF = ROT // 2
BLK = 128
CONT = 1024
TILE = 256
LANES = 128
WIDE = 256
EPS = 1e-05
LOG2E = 1.4426950408889634
LN2 = 0.6931471805599453
BF = jnp.bfloat16
F32 = jnp.float32
MIB = 1024 * 1024
VM = pl.BlockSpec(memory_space=pltpu.VMEM)
HBM = pl.BlockSpec(memory_space=pltpu.HBM)


def dot(left, right, dims=((1,), (0,))):
    return lax.dot_general(left, right, (dims, ((), ())), preferred_element_type=F32)


def shape(dims, dtype):
    return jax.ShapeDtypeStruct(dims, dtype)


def tie(value, *others):
    return lax.optimization_barrier((value,) + others)[0]


def rope_tables(position):
    inverse = 10000.0 ** (-(2.0 * jnp.arange(HALF, dtype=F32)) / ROT)
    angles = inverse[:, None] * position.astype(F32)[None, :]
    return (jnp.cos(angles), jnp.sin(angles))


def turn(values, cosine, sine):
    first, second = values[:HALF], values[HALF:ROT]
    return jnp.concatenate(
        [first * cosine - second * sine, second * cosine + first * sine, values[ROT:]], 0
    )


def normed(values):
    shifted = values - jnp.mean(values, -1, keepdims=True)
    scale = lax.rsqrt(jnp.mean(shifted * shifted, -1, keepdims=True) + EPS)
    return (shifted * scale, scale)


def gelu_parts(value):
    cdf = 0.5 * (1.0 + lax.erf(value * 0.7071067811865476))
    pdf = jnp.exp(-0.5 * value * value) * 0.3989422804014327
    return value * cdf, cdf + value * pdf


def call(kernel, name, outs, specs, out_specs, scratch, limit, flops=1000000):
    return pl.pallas_call(
        kernel,
        out_shape=outs,
        grid_spec=pltpu.PrefetchScalarGridSpec(
            num_scalar_prefetch=1, in_specs=specs, out_specs=out_specs, scratch_shapes=scratch
        ),
        compiler_params=pltpu.CompilerParams(vmem_limit_bytes=limit * MIB),
        cost_estimate=pl.CostEstimate(flops=flops, bytes_accessed=flops // 200, transcendentals=0),
        name=name,
    )


def attn_kernel(table, place, *refs, blocks, heads, size, n_kv, per_chip, last_call, first_call):
    q_ref, do_ref, cos_ref, sin_ref = refs[:4]
    kv_refs = refs[4 : 4 + n_kv]
    refs = refs[4 + n_kv :]
    if not first_call:
        sum_ref, refs = refs[0], refs[1:]
    mix_ref, dq_ref = refs[:2]
    outs = refs[2:-11]
    kv_c, kv_t, s_scr, p_scr, rq, rd, rqt, rdt, o_acc, dq_acc, dkv_acc = refs[-11:]
    step, group = pl.program_id(0), pl.program_id(1)
    lanes = heads * BLK
    prompt_blocks = blocks // 2
    prompt_tiles = prompt_blocks * BLK // TILE
    cont_blocks = min(CONT, prompt_blocks * BLK) // BLK

    def block_rows(block):
        return pl.ds(pl.multiple_of(block * BLK, BLK), BLK)

    @pl.when((step == 0) & (group == 0))
    def _():
        ones = jnp.ones((16, BLK), BF)
        share = blocks // n_kv

        for n, kv_ref in enumerate(kv_refs):

            def place_block(at, carry, n=n, kv_ref=kv_ref):
                spot = n * share + at
                block = table[((spot // per_chip) ^ place[2]) * per_chip + spot % per_chip]
                rows = kv_ref[block_rows(at), :]
                kv_c[block_rows(block), :] = rows
                turned = jnp.concatenate([rows.T, ones], 0)

                @pl.when(block % 2 == 0)
                def _():
                    kv_t[block // 2, :, 0:BLK] = turned

                @pl.when(block % 2 == 1)
                def _():
                    kv_t[block // 2, :, BLK:TILE] = turned

                return carry

            lax.fori_loop(0, share, place_block, 0)
        dkv_acc[...] = jnp.zeros_like(dkv_acc) if first_call else sum_ref[...]

    block = table[place[0] + lax.rem(place[3] + step + place[1], per_chip)]
    last = block // 2
    in_prompt = block < prompt_blocks
    seg_tile = (prompt_blocks + (block - prompt_blocks) // cont_blocks * cont_blocks) // 2
    full = jnp.where(in_prompt, last, prompt_tiles + last - seg_tile)

    def tile_of(i):
        return jnp.where(i < prompt_tiles, jnp.minimum(i, last), i - prompt_tiles + seg_tile)

    def key_rows(tile):
        return pl.ds(pl.multiple_of(tile * TILE, TILE), TILE)

    for h in range(heads):
        rq[0:size, h * BLK : (h + 1) * BLK] = q_ref[h * size : (h + 1) * size, :]
    rq[size : 2 * size, :] = jnp.zeros((size, lanes), BF)

    def scores(tile):
        return dot(kv_c[key_rows(tile), :], rq[...])

    def fold(values):
        return jnp.max(values.reshape(TILE // 8, 8, lanes), 0)

    def first_pass(i, top):
        part = scores(tile_of(i))
        s_scr[i] = part
        return jnp.maximum(top, fold(part))

    top = lax.fori_loop(0, full, first_pass, jnp.full((8, lanes), -1e30, F32))
    part = scores(last)
    key_at = last * TILE + lax.broadcasted_iota(jnp.int32, (TILE, lanes), 0)
    row_at = block * BLK + lax.rem(lax.broadcasted_iota(jnp.int32, (TILE, lanes), 1), BLK)
    part = jnp.where(key_at <= row_at, part, -1e30)
    s_scr[full] = part
    top = jnp.max(jnp.maximum(top, fold(part)), 0, keepdims=True)

    o_acc[...] = jnp.zeros_like(o_acc)

    def second_pass(i, carry):
        p = jnp.exp2(s_scr[i] - top).astype(BF)
        p_scr[i] = p
        o_acc[...] += dot(kv_t[jnp.where(i == full, last, tile_of(i)), size : 2 * size + 16, :], p)
        return carry

    lax.fori_loop(0, full + 1, second_pass, 0)

    inverse = 1.0 / o_acc[size : size + 1, :]
    mixed = o_acc[0:size, :] * inverse
    grads = []
    for h in range(heads):
        at = slice(h * BLK, (h + 1) * BLK)
        mix_ref[h * size : (h + 1) * size, :] = mixed[:, at].astype(BF)
        grads.append(do_ref[h * size : (h + 1) * size, :])
    scaled = (jnp.concatenate(grads, 1) * inverse).astype(BF)
    delta = jnp.sum(mixed * scaled.astype(F32), 0, keepdims=True)
    rd[0:size, :] = jnp.zeros((size, lanes), BF)
    rd[size : 2 * size, :] = scaled
    rqt[...] = rq[...].T
    rdt[...] = rd[...].T
    dq_acc[...] = jnp.zeros_like(dq_acc)

    def third_pass(i, carry):
        tile = jnp.where(i == full, last, tile_of(i))
        p = p_scr[i]
        d_probs = dot(kv_c[key_rows(tile), :], rd[...])
        ds = (p.astype(F32) * (d_probs - delta)).astype(BF)
        dq_acc[...] += dot(kv_t[tile, 0:size, :], ds)
        dkv_acc[key_rows(tile), :] += dot(p, rdt[...]) + dot(ds, rqt[...])
        return carry

    lax.fori_loop(0, full + 1, third_pass, 0)

    cosine, sine = cos_ref[...], sin_ref[...]
    for h in range(heads):
        part = dq_acc[:, h * BLK : (h + 1) * BLK] * 0.125
        dq_ref[h * size : (h + 1) * size, :] = turn(part, cosine, -sine).astype(BF)

    @pl.when((step == pl.num_programs(0) - 1) & (group == pl.num_programs(1) - 1))
    def _():
        if not last_call:
            outs[0][...] = dkv_acc[...]
            return
        scale = jnp.where(
            lax.broadcasted_iota(jnp.int32, (BLK, 2 * size), 1) < size, F32(LN2), F32(1.0)
        )

        def rows_of(slot):
            return (dkv_acc[block_rows(table[slot]), :] * scale).astype(BF)

        if len(outs) == 1:

            def give_block(slot, carry):
                outs[0][block_rows(slot), :] = rows_of(slot)
                return carry

            lax.fori_loop(0, blocks, give_block, 0)
            return
        per_core = per_chip // 2
        for low in range(2):
            for high in range(2):
                chip = place[2] ^ (low + 2 * high)
                for n in range(per_core):
                    here = slice(n * BLK, (n + 1) * BLK)
                    base = chip * per_chip + n
                    outs[0][low, high, here, :] = rows_of(base + per_core - place[1])
                    outs[1][low, high, here, :] = rows_of(base + place[1])


def attention(
    table, place, q_t, do_t, cosine, sine, kvs, carried, start, count, per_chip, last_call, split
):
    width = q_t.shape[0]
    rows = count * BLK
    first_call = carried is None
    size = kvs[0].shape[1] // 2
    keys = sum(kv.shape[0] for kv in kvs)
    all_heads = width // size
    blocks = keys // BLK
    heads = all_heads if keys <= 4096 else 2
    lanes = heads * BLK
    cont = min(CONT, keys // 2)
    most = (keys // 2 + cont) // TILE
    tiles = keys // TILE

    def whole(dims):
        return pl.BlockSpec(dims, lambda i, j, *_: (0,) * len(dims))

    if not last_call:
        dkv_shapes = [shape((keys, 2 * size), F32)]
    elif split:
        dkv_shapes = [shape((2, 2, keys // 8, 2 * size), BF)] * 2
    else:
        dkv_shapes = [shape((keys, 2 * size), BF)]
    extra = [] if first_call else [carried]
    column = pl.BlockSpec((heads * size, BLK), lambda i, j, *_: (j, i + start))
    angle = pl.BlockSpec((HALF, BLK), lambda i, j, *_: (0, i + start))
    out_column = pl.BlockSpec((heads * size, BLK), lambda i, j, *_: (j, i))
    return pl.pallas_call(
        functools.partial(
            attn_kernel,
            blocks=blocks,
            heads=heads,
            size=size,
            n_kv=len(kvs),
            per_chip=per_chip,
            last_call=last_call,
            first_call=first_call,
        ),
        out_shape=[shape((width, rows), BF)] * 2 + dkv_shapes,
        grid_spec=pltpu.PrefetchScalarGridSpec(
            num_scalar_prefetch=2,
            grid=(count, all_heads // heads),
            in_specs=[column, column, angle, angle]
            + [whole(kv.shape) for kv in kvs]
            + [whole(e.shape) for e in extra],
            out_specs=[out_column, out_column] + [whole(s.shape) for s in dkv_shapes],
            scratch_shapes=[
                pltpu.VMEM((keys, 2 * size), BF),
                pltpu.VMEM((tiles, 2 * size + 16, TILE), BF),
                pltpu.VMEM((most, TILE, lanes), F32),
                pltpu.VMEM((most, TILE, lanes), BF),
                pltpu.VMEM((2 * size, lanes), BF),
                pltpu.VMEM((2 * size, lanes), BF),
                pltpu.VMEM((lanes, 2 * size), BF),
                pltpu.VMEM((lanes, 2 * size), BF),
                pltpu.VMEM((size + 16, lanes), F32),
                pltpu.VMEM((size, lanes), F32),
                pltpu.VMEM((keys, 2 * size), F32),
            ],
        ),
        compiler_params=pltpu.CompilerParams(
            vmem_limit_bytes=(24 if keys <= 4096 else 60) * MIB
        ),
        cost_estimate=pl.CostEstimate(
            flops=24 * width * rows * keys, bytes_accessed=4 * width * rows * 4, transcendentals=0
        ),
        name="attention",
    )(table, place + jnp.array([0, 0, 0, start], jnp.int32), q_t, do_t, cosine, sine, *kvs, *extra)


def prologue_kernel(
    sc, xo, xt, go, gt, g1, c1, g2, c2, w_kv, cos_ref, sin_ref, h1_ref, h2_ref, gg_ref, kv_ref
):
    rows = xo.shape[0]
    gain_one, bias_one = g1[...].astype(F32), c1[...].astype(F32)
    gain_two, bias_two = g2[...].astype(F32), c2[...].astype(F32)
    for n, (x, g) in enumerate(((xo, go), (xt, gt))):
        for t in range(rows // 128):
            here = slice(n * rows + t * 128, n * rows + (t + 1) * 128)
            hat, unused = normed(x[t * 128 : (t + 1) * 128, :].astype(F32))
            h1_ref[here, :] = (hat * gain_one + bias_one).astype(BF)
            h2_ref[here, :] = (hat * gain_two + bias_two).astype(BF)
        gg_ref[n * rows : (n + 1) * rows, :] = g[...]
    raw = dot(h1_ref[...], w_kv[...])
    kv = turn(raw.T, cos_ref[...], sin_ref[...]).T.astype(BF)
    kv_ref[pl.ds(pl.multiple_of(sc[0] * rows, rows), rows), :] = kv[:rows]
    kv_ref[pl.ds(pl.multiple_of((1 - sc[0]) * rows, rows), rows), :] = kv[rows:]


def half_copies(sc, w_query, w_out, query_s, out_s, sem):
    half = out_s.shape[0]
    at = pl.ds(pl.multiple_of(sc[0] * half, 128), half)
    return [
        pltpu.make_async_copy(w_query.at[:, at], query_s, sem.at[0]),
        pltpu.make_async_copy(w_out.at[at, :], out_s, sem.at[1]),
    ]


def project_kernel(
    sc, h_ref, g_ref, cos_ref, sin_ref, w_query, w_out, q_ref, do_ref, query_s, out_s, sem, *, size
):
    copies = half_copies(sc, w_query, w_out, query_s, out_s, sem)
    for copy in copies:
        copy.start()
    cosine, sine = cos_ref[...], sin_ref[...]
    copies[0].wait()
    raw = (dot(h_ref[...], query_s[...]) * (0.125 * LOG2E)).T
    for h in range(raw.shape[0] // size):
        at = slice(h * size, (h + 1) * size)
        q_ref[at, :] = turn(raw[at], cosine, sine).astype(BF)
    copies[1].wait()
    do_ref[...] = dot(out_s[...], g_ref[...], ((1,), (1,)))


def hidden_copies(sc, piece, w_up, w_down, up_s, down_s, sems, part, n_pair):
    copies = []
    for j in range(n_pair):
        source = pl.ds(pl.multiple_of((2 * j + sc[0]) * part + piece * LANES, LANES), LANES)
        at = slice(j * LANES, (j + 1) * LANES)
        if w_up is not None:
            copies.append(
                pltpu.make_async_copy(w_up.at[:, source], up_s.at[:, at], sems.at[0])
            )
        if w_down is not None:
            copies.append(
                pltpu.make_async_copy(w_down.at[source, :], down_s.at[at, :], sems.at[1])
            )
    return copies


def piece_of(sc, n):
    return 0 if n == 0 else (2 - sc[2] if n == 1 else 1 + sc[2])


def ffn_kernel(
    sc, h_ref, g_ref, w_up, w_down, act_ref, dup_ref, *refs, n, part, n_pair
):
    up_s, down_s, grad_s, sems = refs[-4:]
    outs = refs[:-4]
    rows, width = h_ref.shape
    copies = hidden_copies(sc, piece_of(sc, n), w_up, w_down, up_s, down_s, sems, part, n_pair)
    for copy in copies:
        copy.start()
    for copy in copies:
        copy.wait()

    def row_tile(r, carry):
        tile = pl.ds(pl.multiple_of(r * 128, 128), 128)
        act, slope = gelu_parts(dot(h_ref[tile, :], up_s[...]))
        act_ref[tile, :] = act.astype(BF)
        d_act = dot(g_ref[tile, :], down_s[...], ((1,), (1,)))
        dup_ref[tile, :] = (d_act * slope).astype(BF)
        return carry

    lax.fori_loop(0, rows // 128, row_tile, 0, unroll=2)
    up_rows = width // n_pair
    block_rows = width // WIDE * LANES

    def give(low, high, kind, first, value):
        here = slice(first, first + value.shape[0])
        if n == 0:
            outs[1 - low][high, kind * block_rows + first : kind * block_rows + here.stop, :] = value
        else:
            outs[0][kind ^ sc[3], low, high, here, :] = value

    grad_s[0 : n_pair * LANES, :] = dot(act_ref[...], g_ref[...], ((0,), (0,))).astype(BF)
    for low in range(2):
        for high in range(2):
            chip = sc[1] ^ (low + 2 * high)
            rows_at = pl.ds(pl.multiple_of(chip * LANES, LANES), LANES)
            for b in range(width // WIDE):
                give(low, high, 0, b * LANES, grad_s[rows_at, b * WIDE : (b + 1) * WIDE])
    span = n_pair * LANES
    grad_s[:, 0:span] = dot(h_ref[...], dup_ref[...], ((0,), (0,))).astype(BF)
    for low in range(2):
        for high in range(2):
            chip = sc[1] ^ (low + 2 * high)
            rows_at = pl.ds(pl.multiple_of(chip * up_rows, 64), up_rows)
            for b in range(span // WIDE):
                give(low, high, 1, b * up_rows, grad_s[rows_at, b * WIDE : (b + 1) * WIDE])


def ffn_gradients(sc, h_two, g_two, w_up, w_down, n, part, n_pair):
    rows, width = h_two.shape
    span = n_pair * LANES
    block = width // WIDE * LANES
    if n == 0:
        outs = [shape((2, 2 * block, WIDE), BF)] * 2
    else:
        outs = [shape((2, 2, 2, block, WIDE), BF)]
    return call(
        functools.partial(ffn_kernel, n=n, part=part, n_pair=n_pair),
        "ffn_gradients",
        [shape((rows, span), BF)] * 2 + outs,
        [VM, VM, HBM, HBM],
        [VM] * (2 + len(outs)),
        [
            pltpu.VMEM((width, span), BF),
            pltpu.VMEM((span, width), BF),
            pltpu.VMEM((width, width), BF),
            pltpu.SemaphoreType.DMA((2,)),
        ],
        20,
        8 * rows * width * span,
    )(sc, h_two, g_two, w_up, w_down)


def late_kernel(sc, h_ref, dq0, dq1, mix0, mix1, got0, got1, g_ref, send_ref, keep_ref, mix_s, dq_s, both_s, *, n_pair):
    half = mix0.shape[0]
    rows = mix0.shape[1]
    width = 2 * half
    own = pl.multiple_of(sc[0] * half, 128)
    other = pl.multiple_of((1 - sc[0]) * half, 128)
    mix_s[pl.ds(own, half), 0:rows] = mix0[...]
    mix_s[pl.ds(own, half), rows : 2 * rows] = mix1[...]
    mix_s[pl.ds(other, half), 0:rows] = got1[...]
    mix_s[pl.ds(other, half), rows : 2 * rows] = got0[...]
    dq_s[:, 0:rows] = dq0[...]
    dq_s[:, rows : 2 * rows] = dq1[...]
    both_s[:, 0:half] = dot(h_ref[...], dq_s[...], ((0,), (1,))).astype(BF)
    both_s[:, half:width] = dot(mix_s[...], g_ref[:, pl.ds(own, half)]).astype(BF)
    block = width // n_pair
    quarter = keep_ref.shape[3]
    unit = 48
    for low in range(2):
        for high in range(2):
            chip = sc[1] ^ (low + 2 * high)
            for first in range(2):
                ref = send_ref if first else keep_ref
                for second in range(2):
                    part = 2 * (first ^ sc[2]) + (second ^ sc[3])
                    for r in range(quarter // unit):
                        at = part * quarter + r * unit
                        col, row = at // block, at % block
                        source = pl.ds(pl.multiple_of(chip * block + row, 16), unit)
                        lane = pl.ds(pl.multiple_of(col * WIDE, WIDE), WIDE)
                        ref[second, low, high, r * unit : (r + 1) * unit, :] = both_s[source, lane]


def late_gradients(sc, h_one, dqs, mixes, gots, g_two, n_pair):
    half = dqs[0].shape[0]
    width = 2 * half
    rows = h_one.shape[0]
    quarter = width // n_pair * (width // WIDE) // 4
    return call(
        functools.partial(late_kernel, n_pair=n_pair),
        "late_gradients",
        [shape((2, 2, 2, quarter, WIDE), BF)] * 2,
        [VM] * 8,
        [VM] * 2,
        [
            pltpu.VMEM((width, rows), BF),
            pltpu.VMEM((half, rows), BF),
            pltpu.VMEM((width, width), BF),
        ],
        16,
        2 * rows * width * width,
    )(sc, h_one, *dqs, *mixes, *gots, g_two)


def out_kernel(sc, a0, a1, a2, mix0, mix1, x_ref, w_down, w_out, own_ref, send_ref, down_s, out_s, sems, *, part, n_pair):
    half = out_s.shape[0]
    rows = x_ref.shape[0]
    span = n_pair * LANES
    copies = [
        pltpu.make_async_copy(
            w_out.at[pl.ds(pl.multiple_of(sc[0] * half, 128), half), :], out_s, sems.at[0]
        )
    ]
    for n in range(3):
        copies += hidden_copies(
            sc, piece_of(sc, n), None, w_down, None, down_s.at[n], sems, part, n_pair
        )
    for copy in copies:
        copy.start()
    for copy in copies:
        copy.wait()
    for n, mix in enumerate((mix0, mix1)):
        here = slice(n * rows, (n + 1) * rows)
        total = dot(mix[...], out_s[...], ((0,), (0,)))
        for k, act in enumerate((a0, a1, a2)):
            total = total + dot(act[here, :], down_s[k])
        if n == 0:
            own_ref[...] = total + x_ref[...].astype(F32)
        else:
            send_ref[...] = total.astype(BF)


def hat_kernel(sc, d0, d1, d2, dq0, dq1, xo, xt, g1, g2, w_up, w_query, own_ref, send_ref, sum_ref, up_s, query_s, sems, *, part, n_pair):
    half = query_s.shape[1]
    rows, width = xo.shape
    copies = [
        pltpu.make_async_copy(
            w_query.at[:, pl.ds(pl.multiple_of(sc[0] * half, 128), half)], query_s, sems.at[1]
        )
    ]
    for n in range(3):
        copies += hidden_copies(
            sc, piece_of(sc, n), w_up, None, up_s.at[n], None, sems, part, n_pair
        )
    for copy in copies:
        copy.start()
    for copy in copies:
        copy.wait()
    gain_one, gain_two = g1[...].astype(F32), g2[...].astype(F32)
    sums = [jnp.zeros((1, width), F32)] * 4
    for n, (x, dq) in enumerate(((xo, dq0), (xt, dq1))):
        here = slice(n * rows, (n + 1) * rows)
        two = dot(d0[here, :], up_s[0], ((1,), (1,)))
        two = two + dot(d1[here, :], up_s[1], ((1,), (1,)))
        two = two + dot(d2[here, :], up_s[2], ((1,), (1,)))
        one = dot(dq[...], query_s[...], ((0,), (1,)))
        hat, unused = normed(x[...].astype(F32))
        for k, value in enumerate((one * hat, one, two * hat, two)):
            sums[k] = sums[k] + jnp.sum(value, 0, keepdims=True)
        total = one * gain_one + two * gain_two
        if n == 0:
            own_ref[...] = total
        else:
            send_ref[...] = total.astype(BF)
    sum_ref[...] = jnp.concatenate(sums + [jnp.zeros((4, width), F32)], 0)


def last_kernel(sc, dkv_a, dkv_b, cos_ref, sin_ref, w_kv, h_ref, x_ref, g1, hat_own, hat_got, sum_ref, g_ref, grad_ref, send_ref, keep_ref, *, n_pair):
    rows, width = x_ref.shape
    dkv = (dkv_a[...] + dkv_b[...].astype(F32)).T
    low_t = turn(dkv, cos_ref[:, 0:rows], -sin_ref[:, 0:rows]).astype(BF)
    low = low_t.T
    weight = dot(low_t, h_ref[0:rows, :]).T.astype(BF)
    d_kv = dot(low, w_kv[...], ((1,), (1,)))
    hat, scale = normed(x_ref[...].astype(F32))
    gain = g1[...].astype(F32)
    total = hat_own[...] + hat_got[...].astype(F32) + d_kv * gain
    grad_ref[...] = g_ref[...].astype(F32) + scale * (
        total
        - jnp.mean(total, -1, keepdims=True)
        - hat * jnp.mean(total * hat, -1, keepdims=True)
    )
    sums = jnp.concatenate(
        [
            sum_ref[0:1, :] + jnp.sum(d_kv * hat, 0, keepdims=True),
            sum_ref[1:2, :] + jnp.sum(d_kv, 0, keepdims=True),
            sum_ref[2:4, :],
            jnp.zeros((4, width), F32),
        ],
        0,
    ).astype(BF)
    part = width // (2 * n_pair)
    lanes = weight.shape[1]
    for chip in range(n_pair):
        rel = chip ^ sc[1]
        low_bit, high_bit = rel % 2, rel // 2
        blocks = []
        for core in range(2):
            at = (2 * chip + core) * part
            piece = weight[at : at + part, :]
            blocks.append(jnp.concatenate([piece[: part // 2], piece[part // 2 :]], 1))
            row = sums[:, at : at + part]
            blocks.append(jnp.concatenate([row, jnp.zeros((8, 2 * lanes - part), BF)], 1))
        block = jnp.concatenate(blocks, 0)

        @pl.when(low_bit == 1)
        def _():
            send_ref[high_bit] = block

        @pl.when(low_bit == 0)
        def _():
            keep_ref[high_bit] = block


def down_kernel(sc, send_ref, got_ref, out_ref, *, width):
    block = width // WIDE * LANES
    for k in range(3):
        for b in range(width // WIDE):
            here = slice(b * LANES, (b + 1) * LANES)
            if k == 0:
                at = slice(2 * block + b * LANES, 2 * block + (b + 1) * LANES)
                value = send_ref[at, :].astype(F32) + got_ref[at, :].astype(F32)
            else:
                at = pl.ds(pl.multiple_of(sc[3] * block + b * LANES, LANES), LANES)
                mine = send_ref[at, :].astype(F32)
                value = jnp.where(sc[2] == k - 1, mine, got_ref[at, :].astype(F32))
            out_ref[k * LANES : (k + 1) * LANES, b * WIDE : (b + 1) * WIDE] = value


def up_block(sc, k, b, parity, early_send, early_got, width, part):
    block = width // WIDE * LANES
    off = b * 2 * part + parity * part
    if k == 0:
        at = pl.ds(pl.multiple_of(3 * block + off, 32), part)
        return early_send[at, :].astype(F32) + early_got[at, :].astype(F32)
    at = pl.ds(pl.multiple_of((1 - sc[3]) * block + off, 32), part)
    return jnp.where(
        sc[2] == k - 1, early_send[at, :].astype(F32), early_got[at, :].astype(F32)
    )


def late_block(sc, b, parity, send, got, part, quarter):
    pieces = []
    for r in range(2):
        at = b * 2 * part + parity * part + r * (part // 2)
        first, second = at // (2 * quarter), at // quarter % 2
        rel = (second ^ sc[3]) * quarter + at % quarter
        source = pl.ds(pl.multiple_of(rel, 16), part // 2)
        pieces.append(
            jnp.where(
                first == sc[2], send[source, :].astype(F32), got[source, :].astype(F32)
            )
        )
    return jnp.concatenate(pieces, 0)


def pack_kernel(sc, early_send, early_got, last_send, last_got, out_ref, own_ref, *, width, part, quarter):
    for which, ref in ((1, out_ref), (0, own_ref)):
        parity = sc[0] if which == 0 else 1 - sc[0]
        at = 0
        for k in range(3):
            for b in range(2):
                ref[at : at + part, :] = up_block(
                    sc, k, b, parity, early_send, early_got, width, part
                ).astype(BF)
                at += part
        for b in range(width // WIDE):
            ref[at : at + part, :] = late_block(
                sc, b, parity, last_send, last_got, part, quarter
            ).astype(BF)
            at += part
        few = (last_send.shape[0] - 2 * quarter) // 2
        source = pl.ds(pl.multiple_of(2 * quarter + parity * few, 8), few)
        ref[at : at + few, :] = (
            last_send[source, :].astype(F32) + last_got[source, :].astype(F32)
        ).astype(BF)


def final_kernel(sc, own_ref, got_ref, up_ref, query_ref, proj_ref, kv_ref, norm_ref, *, part, n_pair):
    part_hidden = up_ref.shape[1] // (2 * n_pair)
    half = query_ref.shape[1] // 2
    for which, ref in enumerate((own_ref, got_ref)):
        core = sc[0] if which == 0 else 1 - sc[0]
        at = 0
        for k in range(3):
            for j in range(n_pair):
                lane = (2 * j + core) * part_hidden + k * LANES
                rows = slice((2 * k + j // 2) * part, (2 * k + j // 2 + 1) * part)
                cols = slice(j % 2 * LANES, (j % 2 + 1) * LANES)
                up_ref[:, pl.ds(pl.multiple_of(lane, LANES), LANES)] = ref[rows, cols].astype(F32)
        base = 6 * part
        for n in range(2 * half // LANES):
            rows = slice(base + n // 2 * part, base + (n // 2 + 1) * part)
            value = ref[rows, n % 2 * LANES : (n % 2 + 1) * LANES].astype(F32)
            to, m = (query_ref, n) if n < half // LANES else (proj_ref, n - half // LANES)
            to[:, pl.ds(pl.multiple_of(core * half + m * LANES, LANES), LANES)] = value
    base = 9 * part
    few = own_ref[base:, :].astype(F32) + got_ref[base:, :].astype(F32)
    kv_ref[0 : part // 2, :] = few[0 : part // 2, 0:LANES]
    kv_ref[part // 2 : part, :] = few[0 : part // 2, LANES:WIDE]
    norm_ref[...] = few[part // 2 : part // 2 + 8, :]


class Links:
    def __init__(self, n_grp, n_ctx):
        self.n_grp, self.n_ctx, self.n_pair = n_grp, n_ctx, n_ctx // 2
        self.small = (n_grp, n_ctx) == (4, 8)
        self.ctx = lax.axis_index("ctx")
        self.grp = lax.axis_index("grp")
        self.core = self.ctx % 2
        self.chip = self.ctx // 2
        self.groups = [[2 * z + c for z in range(self.n_pair)] for c in range(2)]

    def swap(self, value):
        return lax.ppermute(value, "ctx", [(i, i ^ 1) for i in range(self.n_ctx)])

    def permute(self, value, target):
        pairs = []
        for g in range(self.n_grp):
            for i in range(self.n_ctx):
                y, x, z, c = target(g // 2, g % 2, i // 2, i % 2)
                pairs.append((g * self.n_ctx + i, (2 * y + x) * self.n_ctx + 2 * z + c))
        return lax.ppermute(value, ("grp", "ctx"), pairs)

    def cross(self, value, stage):
        return self.permute(
            value, lambda y, x, z, c: (y, 1 - x, z, c) if c == stage else (1 - y, x, z, c)
        )

    def bit(self, stage):
        y, x = self.grp // 2, self.grp % 2
        return jnp.where(self.core == stage, x, y)

    def flip(self, value, bit):
        return self.permute(value, lambda y, x, z, c: (y, x, z ^ bit, c))

    def reduce(self, parts):
        moved = lax.all_to_all(parts, "ctx", 0, 0, axis_index_groups=self.groups)
        return lax.psum(jnp.sum(moved.astype(F32), 0).astype(BF), "grp")


def add(keep, got):
    return keep.astype(F32) + got.astype(F32)


def low(value):
    return value.astype(BF)


def shards_small(
    layer_input, block_table, ln1_gain, ln1_bias, ln2_gain, ln2_bias,
    w_query, w_keyval, w_out, w_up, w_down, cotangent, *, n_grp, n_ctx,
):
    links = Links(n_grp, n_ctx)
    core, chip, n_pair = links.core, links.chip, links.n_pair
    rows, width = layer_input.shape
    lanes = w_keyval.shape[1]
    size = lanes // 2
    hidden = w_up.shape[1]
    group_len = block_table.shape[1] * BLK
    part, part_hidden = width // n_ctx, hidden // n_ctx
    half = width // 2
    per_chip = 2 * rows // BLK
    table = block_table[0]
    sc = jnp.stack([core, chip, links.bit(0), links.bit(1)]).astype(jnp.int32)
    g1, c1, g2, c2 = (v.reshape(1, width) for v in (ln1_gain, ln1_bias, ln2_gain, ln2_bias))

    x_other, g_other = links.swap(layer_input), links.swap(cotangent)
    own_slots = lax.dynamic_slice_in_dim(table, chip * per_chip, per_chip).reshape(2, -1)
    slots = jnp.concatenate([own_slots[core], own_slots[1 - core]])
    canon = (slots[:, None] * BLK + jnp.arange(BLK, dtype=jnp.int32)[None, :]).reshape(2 * rows)
    prompt_len = group_len // 2
    cont_span = min(CONT, prompt_len)
    position = jnp.where(
        canon < prompt_len, canon, prompt_len + (canon - prompt_len) % cont_span
    )
    cosine, sine = rope_tables(position)

    h_one, h_two, g_two, kv_low = call(
        prologue_kernel,
        "prologue",
        [shape((2 * rows, width), BF)] * 3 + [shape((2 * rows, lanes), BF)],
        [VM] * 11,
        [VM] * 4,
        [],
        16,
    )(sc, layer_input, x_other, cotangent, g_other, g1, c1, g2, c2, w_keyval, cosine, sine)

    kv_got = links.flip(kv_low, 1)
    ffn = functools.partial(
        ffn_gradients, sc, w_up=w_up, w_down=w_down, part=part_hidden, n_pair=n_pair
    )
    act_0, dup_0, a_send, a_keep = ffn(h_two, g_two, n=0)
    a_got = links.flip(a_send, 1)
    kv_near = jnp.concatenate([kv_low, kv_got], 0)
    kv_far = links.flip(kv_near, 2)
    act_1, dup_1, b_send = ffn(tie(h_two, a_keep, kv_near), g_two, n=1)
    b_got = links.cross(b_send, 0)
    act_2, dup_2, b_keep = ffn(tie(h_two, b_send), g_two, n=2)

    q_t, do_t = call(
        functools.partial(project_kernel, size=size),
        "project",
        [shape((half, 2 * rows), BF), shape((half, 2 * rows), F32)],
        [VM] * 4 + [HBM] * 2,
        [VM] * 2,
        [
            pltpu.VMEM((width, half), BF),
            pltpu.VMEM((half, width), BF),
            pltpu.SemaphoreType.DMA((2,)),
        ],
        16,
    )(sc, tie(h_one, b_keep), g_two, cosine, sine, w_query, w_out)

    place = jnp.stack([chip * per_chip, core * (rows // BLK), chip, 0 * chip]).astype(jnp.int32)
    count = rows // BLK
    attend = functools.partial(
        attention, table, place, do_t=do_t, cosine=cosine, sine=sine, kvs=(kv_near, kv_far),
        count=count, per_chip=per_chip, split=True,
    )
    mix_0, dq_0, carried = attend(q_t=q_t, carried=None, start=0, last_call=False)
    mix_0_got = links.swap(mix_0)
    a_sum = add(a_keep, tie(a_got, carried))
    a_got_2 = links.flip(low(a_sum[1]), 2)
    b_sum = add(b_keep, tie(b_got, carried))
    b_got_2 = links.cross(low(b_sum[1]), 1)
    mix_1, dq_1, dkv_send, dkv_keep = attend(
        q_t=tie(q_t, a_got, b_got), carried=carried, start=count, last_call=True
    )

    dkv_got = links.swap(dkv_send)
    mix_1_got = links.swap(mix_1)
    late_send, late_keep = late_gradients(
        sc, h_one, (dq_0, dq_1), (mix_0, mix_1), (mix_0_got, mix_1_got), g_two, n_pair
    )
    late_got = links.cross(late_send, 0)
    dkv_sum = add(dkv_keep, dkv_got)
    dkv_got_2 = links.flip(low(dkv_sum[1]), 1)
    b_sum = add(b_sum[0], tie(b_got_2, late_send))
    b_got_3 = links.flip(low(b_sum[1]), 1)

    w_specs = [HBM] * 2
    out_own, out_send = call(
        functools.partial(out_kernel, part=part_hidden, n_pair=n_pair),
        "outputs",
        [shape((rows, width), F32), shape((rows, width), BF)],
        [VM] * 6 + w_specs,
        [VM] * 2,
        [
            pltpu.VMEM((3, n_pair * LANES, width), BF),
            pltpu.VMEM((half, width), BF),
            pltpu.SemaphoreType.DMA((2,)),
        ],
        16,
    )(sc, act_0, act_1, tie(act_2, late_send, dkv_got), mix_0, mix_1, layer_input, w_down, w_out)
    out_got = links.swap(out_send)
    dkv_sum = add(dkv_sum[0], tie(dkv_got_2, out_send))
    dkv_got_3 = links.flip(low(dkv_sum[1]), 2)
    hat_own, hat_send, sums = call(
        functools.partial(hat_kernel, part=part_hidden, n_pair=n_pair),
        "norms",
        [shape((rows, width), F32), shape((rows, width), BF), shape((8, width), F32)],
        [VM] * 9 + w_specs,
        [VM] * 3,
        [
            pltpu.VMEM((3, width, n_pair * LANES), BF),
            pltpu.VMEM((width, half), BF),
            pltpu.SemaphoreType.DMA((2,)),
        ],
        24,
    )(
        sc, dup_0, dup_1, tie(dup_2, out_send, dkv_got_2), dq_0, dq_1, layer_input, x_other, g1, g2,
        w_up, w_query,
    )
    hat_got = links.swap(hat_send)
    layer_output = low(out_own + out_got.astype(F32))

    late_sum = add(late_keep, tie(late_got, hat_send))
    late_got_2 = links.cross(low(late_sum[1]), 1)
    b_sum = add(b_sum[0], tie(b_got_3, hat_send))
    b_got_4 = links.flip(low(b_sum[1]), 2)
    a_sum = add(a_sum[0], tie(a_got_2, hat_send))

    few = part // 2 + 8
    in_grad, few_send, few_keep = call(
        functools.partial(last_kernel, n_pair=n_pair),
        "last",
        [shape((rows, width), F32)] + [shape((2, 2 * few, 2 * lanes), BF)] * 2,
        [VM] * 12,
        [VM] * 3,
        [],
        16,
    )(
        sc, dkv_sum[0], dkv_got_3, cosine, sine, w_keyval, h_one, layer_input, g1, hat_own, hat_got,
        sums, cotangent,
    )

    late_sum = add(late_sum[0], tie(late_got_2, few_send))
    quarter = late_sum.shape[2]
    last = jnp.concatenate([late_sum, jnp.stack([few_keep, few_send]).astype(F32)], 2)
    last_got = links.flip(low(last[1]), 1)
    early = jnp.concatenate([low(add(b_sum[0], tie(b_got_4, last_got))), low(a_sum)], 0)
    block = early.shape[0] // 3
    early_got = links.cross(early, 1)
    last = add(last[0], last_got)
    last_got = links.flip(low(last[1]), 2)
    early = jnp.concatenate(
        [early[:block], early_got[:block], low(add(early[block:], early_got[block:]))], 0
    )
    early_got = links.cross(early, 0)
    last = low(add(last[0], last_got))
    last_got = links.cross(last, 1)
    last = jnp.concatenate(
        [last[:quarter], last_got[:quarter], low(add(last[quarter:], last_got[quarter:]))], 0
    )
    last_got = links.cross(last, 0)
    total_down = call(
        functools.partial(down_kernel, width=width),
        "down", shape((part_hidden, width), F32), [VM] * 2, VM, [], 8,
    )(sc, early, early_got)
    size_out = 9 * part + few
    other, own = call(
        functools.partial(pack_kernel, width=width, part=part, quarter=quarter),
        "pack", [shape((size_out, WIDE), BF)] * 2, [VM] * 4, [VM] * 2, [], 8,
    )(sc, early, early_got, last, last_got)
    got = links.swap(other)
    total_up, total_query, total_out, total_kv, norm = call(
        functools.partial(final_kernel, part=part, n_pair=n_pair),
        "final",
        [
            shape((part, hidden), F32),
            shape((part, width), F32),
            shape((part, width), F32),
            shape((part, lanes), F32),
            shape((8, WIDE), F32),
        ],
        [VM] * 2,
        [VM] * 5,
        [],
        8,
    )(sc, own, got)
    norms = [norm[n, :part] for n in range(4)]
    return (layer_output, in_grad, *norms, total_query, total_kv, total_out, total_up, total_down)


def rotate_rows(values, cosine, sine):
    return turn(values.T, cosine, sine).T


def shards(
    layer_input, block_table, ln1_gain, ln1_bias, ln2_gain, ln2_bias,
    w_query, w_keyval, w_out, w_up, w_down, cotangent, *, n_grp, n_ctx,
):
    links = Links(n_grp, n_ctx)
    core, chip, n_pair = links.core, links.chip, links.n_pair
    rows, width = layer_input.shape
    size = w_keyval.shape[1] // 2
    hidden = w_up.shape[1]
    group_len = block_table.shape[1] * BLK
    part_rows, part_hidden = width // n_ctx, hidden // n_ctx
    half_width, half_hidden = width // 2, hidden // 2
    per_chip = 2 * rows // BLK
    table = block_table[0]

    def both(own, other):
        return jnp.concatenate(
            [jnp.where(core == 0, own, other), jnp.where(core == 0, other, own)], 0
        )

    def mine(value, own_core):
        return lax.dynamic_slice_in_dim(value, own_core * rows, rows, 0)

    x_two = both(layer_input, links.swap(layer_input))
    g_two = both(cotangent, links.swap(cotangent))
    canon = (
        lax.dynamic_slice_in_dim(table, chip * per_chip, per_chip)[:, None] * BLK
        + jnp.arange(BLK, dtype=jnp.int32)[None, :]
    ).reshape(2 * rows)
    prompt_len = group_len // 2
    cont_span = min(CONT, prompt_len)
    position = jnp.where(
        canon < prompt_len, canon, prompt_len + (canon - prompt_len) % cont_span
    )
    cosine, sine = rope_tables(position)
    gain_one, gain_two = ln1_gain.astype(F32), ln2_gain.astype(F32)
    hat, scale = normed(x_two.astype(F32))
    h_one = low(hat * gain_one + ln1_bias.astype(F32))
    h_two = low(hat * gain_two + ln2_bias.astype(F32))
    kv_raw = dot(h_one, w_keyval)
    kv_low = low(
        jnp.concatenate([rotate_rows(kv_raw[:, :size], cosine, sine), kv_raw[:, size:]], -1)
    )
    kv_all = lax.all_gather(kv_low, "ctx", axis=0, axis_index_groups=links.groups, tiled=True)

    up_half = lax.dynamic_index_in_dim(
        w_up.reshape(width, n_pair, 2, part_hidden), core, 2, False
    ).reshape(width, half_hidden)
    down_half = lax.dynamic_index_in_dim(
        w_down.reshape(n_pair, 2, part_hidden, width), core, 1, False
    ).reshape(half_hidden, width)
    act, slope = gelu_parts(dot(h_two, up_half))
    act = low(act)
    grad_down = low(dot(act, g_two, ((0,), (0,))))
    total_down = links.reduce(grad_down.reshape(n_pair, part_hidden, width))
    grad_up = low(dot(g_two, down_half, ((1,), (1,))) * slope)
    grad_up_w = low(dot(h_two, grad_up, ((0,), (0,))))
    total_up = links.reduce(grad_up_w.reshape(n_pair, 2 * part_rows, half_hidden))

    query_half = lax.dynamic_slice_in_dim(w_query, core * half_width, half_width, 1)
    out_half = lax.dynamic_slice_in_dim(w_out, core * half_width, half_width, 0)
    q_raw = dot(query_half, h_one, ((0,), (1,))) * (0.125 * LOG2E)
    q_t = low(
        jax.vmap(turn, (0, None, None))(q_raw.reshape(-1, size, 2 * rows), cosine, sine)
    ).reshape(half_width, 2 * rows)
    do_t = dot(out_half, g_two, ((1,), (1,)))
    place = jnp.stack([chip * per_chip, 0 * chip, 0 * chip, 0 * chip]).astype(jnp.int32)
    mix_t, dq_t, dkv_part = attention(
        table, place, q_t, do_t, cosine, sine, (kv_all,), None, 0, per_chip, per_chip, True, False
    )

    dkv_part = dkv_part.reshape(n_pair, 2, rows, 2 * size)
    dkv_own = lax.dynamic_index_in_dim(dkv_part, core, 1, False)
    dkv_got = links.swap(lax.dynamic_index_in_dim(dkv_part, 1 - core, 1, False))
    moved = lax.all_to_all(
        low(add(dkv_own, dkv_got)), "ctx", 0, 0, axis_index_groups=links.groups
    )
    dkv = jnp.sum(moved.astype(F32), 0)
    cos_own = lax.dynamic_slice_in_dim(cosine, core * rows, rows, 1)
    sin_own = lax.dynamic_slice_in_dim(sine, core * rows, rows, 1)
    dkv_low = low(
        jnp.concatenate([rotate_rows(dkv[:, :size], cos_own, -sin_own), dkv[:, size:]], -1)
    )

    mix_got = links.swap(mix_t)
    mix_all = jnp.concatenate(
        [jnp.where(core == 0, mix_t, mix_got), jnp.where(core == 0, mix_got, mix_t)], 0
    )
    g_half = lax.dynamic_slice_in_dim(g_two, core * half_width, half_width, 1)
    grad_q_w = low(dot(h_one, dq_t, ((0,), (1,))))
    grad_out_w = low(dot(mix_all, g_half))
    late = jnp.concatenate([grad_q_w, grad_out_w], 1).reshape(n_pair, 2 * part_rows, width)
    total_late = links.reduce(late)

    out_part = dot(act, down_half) + dot(mix_t, out_half, ((0,), (0,)))
    out_got = links.swap(low(mine(out_part, 1 - core)))
    layer_output = low(layer_input.astype(F32) + mine(out_part, core) + out_got.astype(F32))

    d_two = dot(grad_up, up_half, ((1,), (1,)))
    d_one = dot(dq_t, query_half, ((0,), (1,)))
    d_kv = dot(dkv_low, w_keyval, ((1,), (1,)))
    row_core = lax.broadcasted_iota(jnp.int32, (2 * rows, 1), 0) // rows
    d_one = d_one + jnp.where(row_core == core, jnp.concatenate([d_kv, d_kv], 0), 0.0)
    sums = jnp.stack([jnp.sum(v, 0) for v in (d_one * hat, d_one, d_two * hat, d_two)])
    d_hat = d_one * gain_one + d_two * gain_two
    hat_got = links.swap(low(mine(d_hat, 1 - core)))
    d_hat = mine(d_hat, core) + hat_got.astype(F32)
    hat_own = mine(hat, core)
    in_grad = cotangent.astype(F32) + mine(scale, core) * (
        d_hat
        - jnp.mean(d_hat, -1, keepdims=True)
        - hat_own * jnp.mean(d_hat * hat_own, -1, keepdims=True)
    )

    grad_kv_w = dot(mine(h_one, core), dkv_low, ((0,), (0,)))
    sum_rows = sums.reshape(4, n_pair, 2, part_rows).transpose(1, 2, 0, 3)
    sum_rows = jnp.pad(sum_rows, ((0, 0), (0, 0), (0, 0), (0, 2 * size - part_rows)))
    few = jnp.concatenate([grad_kv_w.reshape(n_pair, 2, part_rows, 2 * size), sum_rows], 2)
    few = links.reduce(low(few).reshape(n_pair, 2 * (part_rows + 4), 2 * size))
    few = few.reshape(2, part_rows + 4, 2 * size)
    few_got = links.swap(lax.dynamic_index_in_dim(few, 1 - core, 0, False))
    few = add(lax.dynamic_index_in_dim(few, core, 0, False), few_got)

    halves = jnp.concatenate(
        [total_up.reshape(2, part_rows, half_hidden), total_late.reshape(2, part_rows, width)], -1
    )
    own = lax.dynamic_index_in_dim(halves, core, 0, False)
    got = links.swap(lax.dynamic_index_in_dim(halves, 1 - core, 0, False))
    sides = jnp.stack([jnp.where(core == 0, own, got), jnp.where(core == 0, got, own)]).astype(F32)
    ups = sides[:, :, :half_hidden].reshape(2, part_rows, n_pair, part_hidden)
    total_up = ups.transpose(1, 2, 0, 3).reshape(part_rows, hidden)
    lates = sides[:, :, half_hidden:]
    total_query = lates[:, :, :half_width].transpose(1, 0, 2).reshape(part_rows, width)
    total_out = lates[:, :, half_width:].transpose(1, 0, 2).reshape(part_rows, width)
    norms = [few[part_rows + n, :part_rows] for n in range(4)]
    total_kv = few[:part_rows]
    total_down = total_down.astype(F32)
    return (layer_output, in_grad, *norms, total_query, total_kv, total_out, total_up, total_down)


def solution(mesh):
    n_grp, n_ctx = mesh.shape["grp"], mesh.shape["ctx"]
    body = shards_small if (n_grp, n_ctx) == (4, 8) else shards
    return jax.shard_map(
        functools.partial(body, n_grp=n_grp, n_ctx=n_ctx),
        mesh=mesh,
        in_specs=(P(("grp", "ctx"), None), P("grp", None))
        + (P(),) * 9
        + (P(("grp", "ctx"), None),),
        out_specs=(P(("grp", "ctx"), None),) * 2 + (P("ctx"),) * 4 + (P("ctx", None),) * 5,
        check_vma=False,
    )
```

```python
import functools

import jax
import jax.numpy as jnp
from jax import lax
from jax.experimental import pallas as pl
from jax.experimental.pallas import tpu as pltpu
from jax.sharding import PartitionSpec as P

ROT = 16
HALF = ROT // 2
BLK = 128
CONT = 1024
TILE = 256
LANES = 128
WIDE = 256
EPS = 1e-05
LOG2E = 1.4426950408889634
LN2 = 0.6931471805599453
BF = jnp.bfloat16
F32 = jnp.float32
MIB = 1024 * 1024
VM = pl.BlockSpec(memory_space=pltpu.VMEM)
HBM = pl.BlockSpec(memory_space=pltpu.HBM)


def dot(left, right, dims=((1,), (0,))):
    return lax.dot_general(left, right, (dims, ((), ())), preferred_element_type=F32)


def shape(dims, dtype):
    return jax.ShapeDtypeStruct(dims, dtype)


def tie(value, *others):
    return lax.optimization_barrier((value,) + others)[0]


def rope_tables(position):
    inverse = 10000.0 ** (-(2.0 * jnp.arange(HALF, dtype=F32)) / ROT)
    angles = inverse[:, None] * position.astype(F32)[None, :]
    return (jnp.cos(angles), jnp.sin(angles))


def turn(values, cosine, sine):
    first, second = values[:HALF], values[HALF:ROT]
    return jnp.concatenate(
        [first * cosine - second * sine, second * cosine + first * sine, values[ROT:]], 0
    )


def normed(values):
    shifted = values - jnp.mean(values, -1, keepdims=True)
    scale = lax.rsqrt(jnp.mean(shifted * shifted, -1, keepdims=True) + EPS)
    return (shifted * scale, scale)


def gelu_parts(value):
    cdf = 0.5 * (1.0 + lax.erf(value * 0.7071067811865476))
    pdf = jnp.exp(-0.5 * value * value) * 0.3989422804014327
    return value * cdf, cdf + value * pdf


def call(kernel, name, outs, specs, out_specs, scratch, limit, flops=1000000):
    return pl.pallas_call(
        kernel,
        out_shape=outs,
        grid_spec=pltpu.PrefetchScalarGridSpec(
            num_scalar_prefetch=1, in_specs=specs, out_specs=out_specs, scratch_shapes=scratch
        ),
        compiler_params=pltpu.CompilerParams(vmem_limit_bytes=limit * MIB),
        cost_estimate=pl.CostEstimate(flops=flops, bytes_accessed=flops // 200, transcendentals=0),
        name=name,
    )


def attn_kernel(table, place, *refs, blocks, heads, size, n_kv, per_chip, last_call, first_call):
    q_ref, do_ref, cos_ref, sin_ref = refs[:4]
    kv_refs = refs[4 : 4 + n_kv]
    refs = refs[4 + n_kv :]
    if not first_call:
        sum_ref, refs = refs[0], refs[1:]
    mix_ref, dq_ref = refs[:2]
    outs = refs[2:-11]
    kv_c, kv_t, s_scr, p_scr, rq, rd, rqt, rdt, o_acc, dq_acc, dkv_acc = refs[-11:]
    step, group = pl.program_id(0), pl.program_id(1)
    lanes = heads * BLK
    prompt_blocks = blocks // 2
    prompt_tiles = prompt_blocks * BLK // TILE
    cont_blocks = min(CONT, prompt_blocks * BLK) // BLK

    def block_rows(block):
        return pl.ds(pl.multiple_of(block * BLK, BLK), BLK)

    @pl.when((step == 0) & (group == 0))
    def _():
        ones = jnp.ones((16, BLK), BF)
        share = blocks // n_kv

        for n, kv_ref in enumerate(kv_refs):

            def place_block(at, carry, n=n, kv_ref=kv_ref):
                spot = n * share + at
                block = table[((spot // per_chip) ^ place[2]) * per_chip + spot % per_chip]
                rows = kv_ref[block_rows(at), :]
                kv_c[block_rows(block), :] = rows
                turned = jnp.concatenate([rows.T, ones], 0)

                @pl.when(block % 2 == 0)
                def _():
                    kv_t[block // 2, :, 0:BLK] = turned

                @pl.when(block % 2 == 1)
                def _():
                    kv_t[block // 2, :, BLK:TILE] = turned

                return carry

            lax.fori_loop(0, share, place_block, 0)
        dkv_acc[...] = jnp.zeros_like(dkv_acc) if first_call else sum_ref[...]

    block = table[place[0] + lax.rem(place[3] + step + place[1], per_chip)]
    last = block // 2
    in_prompt = block < prompt_blocks
    seg_tile = (prompt_blocks + (block - prompt_blocks) // cont_blocks * cont_blocks) // 2
    full = jnp.where(in_prompt, last, prompt_tiles + last - seg_tile)

    def tile_of(i):
        return jnp.where(i < prompt_tiles, jnp.minimum(i, last), i - prompt_tiles + seg_tile)

    def key_rows(tile):
        return pl.ds(pl.multiple_of(tile * TILE, TILE), TILE)

    for h in range(heads):
        rq[0:size, h * BLK : (h + 1) * BLK] = q_ref[h * size : (h + 1) * size, :]
    rq[size : 2 * size, :] = jnp.zeros((size, lanes), BF)

    def scores(tile):
        return dot(kv_c[key_rows(tile), :], rq[...])

    def fold(values):
        return jnp.max(values.reshape(TILE // 8, 8, lanes), 0)

    def first_pass(i, top):
        part = scores(tile_of(i))
        s_scr[i] = part
        return jnp.maximum(top, fold(part))

    top = lax.fori_loop(0, full, first_pass, jnp.full((8, lanes), -1e30, F32))
    part = scores(last)
    key_at = last * TILE + lax.broadcasted_iota(jnp.int32, (TILE, lanes), 0)
    row_at = block * BLK + lax.rem(lax.broadcasted_iota(jnp.int32, (TILE, lanes), 1), BLK)
    part = jnp.where(key_at <= row_at, part, -1e30)
    s_scr[full] = part
    top = jnp.max(jnp.maximum(top, fold(part)), 0, keepdims=True)

    o_acc[...] = jnp.zeros_like(o_acc)

    def second_pass(i, carry):
        p = jnp.exp2(s_scr[i] - top).astype(BF)
        p_scr[i] = p
        o_acc[...] += dot(kv_t[jnp.where(i == full, last, tile_of(i)), size : 2 * size + 16, :], p)
        return carry

    lax.fori_loop(0, full + 1, second_pass, 0)

    inverse = 1.0 / o_acc[size : size + 1, :]
    mixed = o_acc[0:size, :] * inverse
    grads = []
    for h in range(heads):
        at = slice(h * BLK, (h + 1) * BLK)
        mix_ref[h * size : (h + 1) * size, :] = mixed[:, at].astype(BF)
        grads.append(do_ref[h * size : (h + 1) * size, :])
    scaled = (jnp.concatenate(grads, 1) * inverse).astype(BF)
    delta = jnp.sum(mixed * scaled.astype(F32), 0, keepdims=True)
    rd[0:size, :] = jnp.zeros((size, lanes), BF)
    rd[size : 2 * size, :] = scaled
    rqt[...] = rq[...].T
    rdt[...] = rd[...].T
    dq_acc[...] = jnp.zeros_like(dq_acc)

    def third_pass(i, carry):
        tile = jnp.where(i == full, last, tile_of(i))
        p = p_scr[i]
        d_probs = dot(kv_c[key_rows(tile), :], rd[...])
        ds = (p.astype(F32) * (d_probs - delta)).astype(BF)
        dq_acc[...] += dot(kv_t[tile, 0:size, :], ds)
        dkv_acc[key_rows(tile), :] += dot(p, rdt[...]) + dot(ds, rqt[...])
        return carry

    lax.fori_loop(0, full + 1, third_pass, 0)

    cosine, sine = cos_ref[...], sin_ref[...]
    for h in range(heads):
        part = dq_acc[:, h * BLK : (h + 1) * BLK] * 0.125
        dq_ref[h * size : (h + 1) * size, :] = turn(part, cosine, -sine).astype(BF)

    @pl.when((step == pl.num_programs(0) - 1) & (group == pl.num_programs(1) - 1))
    def _():
        if not last_call:
            outs[0][...] = dkv_acc[...]
            return
        scale = jnp.where(
            lax.broadcasted_iota(jnp.int32, (BLK, 2 * size), 1) < size, F32(LN2), F32(1.0)
        )

        def rows_of(slot):
            return (dkv_acc[block_rows(table[slot]), :] * scale).astype(BF)

        if len(outs) == 1:

            def give_block(slot, carry):
                outs[0][block_rows(slot), :] = rows_of(slot)
                return carry

            lax.fori_loop(0, blocks, give_block, 0)
            return
        per_core = per_chip // 2
        for low in range(2):
            for high in range(2):
                chip = place[2] ^ (low + 2 * high)
                for n in range(per_core):
                    here = slice(n * BLK, (n + 1) * BLK)
                    base = chip * per_chip + n
                    outs[0][low, high, here, :] = rows_of(base + per_core - place[1])
                    outs[1][low, high, here, :] = rows_of(base + place[1])


def attention(
    table, place, q_t, do_t, cosine, sine, kvs, carried, start, count, per_chip, last_call, split
):
    width = q_t.shape[0]
    rows = count * BLK
    first_call = carried is None
    size = kvs[0].shape[1] // 2
    keys = sum(kv.shape[0] for kv in kvs)
    all_heads = width // size
    blocks = keys // BLK
    heads = all_heads if keys <= 4096 else 2
    lanes = heads * BLK
    cont = min(CONT, keys // 2)
    most = (keys // 2 + cont) // TILE
    tiles = keys // TILE

    def whole(dims):
        return pl.BlockSpec(dims, lambda i, j, *_: (0,) * len(dims))

    if not last_call:
        dkv_shapes = [shape((keys, 2 * size), F32)]
    elif split:
        dkv_shapes = [shape((2, 2, keys // 8, 2 * size), BF)] * 2
    else:
        dkv_shapes = [shape((keys, 2 * size), BF)]
    extra = [] if first_call else [carried]
    column = pl.BlockSpec((heads * size, BLK), lambda i, j, *_: (j, i + start))
    angle = pl.BlockSpec((HALF, BLK), lambda i, j, *_: (0, i + start))
    out_column = pl.BlockSpec((heads * size, BLK), lambda i, j, *_: (j, i))
    return pl.pallas_call(
        functools.partial(
            attn_kernel,
            blocks=blocks,
            heads=heads,
            size=size,
            n_kv=len(kvs),
            per_chip=per_chip,
            last_call=last_call,
            first_call=first_call,
        ),
        out_shape=[shape((width, rows), BF)] * 2 + dkv_shapes,
        grid_spec=pltpu.PrefetchScalarGridSpec(
            num_scalar_prefetch=2,
            grid=(count, all_heads // heads),
            in_specs=[column, column, angle, angle]
            + [whole(kv.shape) for kv in kvs]
            + [whole(e.shape) for e in extra],
            out_specs=[out_column, out_column] + [whole(s.shape) for s in dkv_shapes],
            scratch_shapes=[
                pltpu.VMEM((keys, 2 * size), BF),
                pltpu.VMEM((tiles, 2 * size + 16, TILE), BF),
                pltpu.VMEM((most, TILE, lanes), F32),
                pltpu.VMEM((most, TILE, lanes), BF),
                pltpu.VMEM((2 * size, lanes), BF),
                pltpu.VMEM((2 * size, lanes), BF),
                pltpu.VMEM((lanes, 2 * size), BF),
                pltpu.VMEM((lanes, 2 * size), BF),
                pltpu.VMEM((size + 16, lanes), F32),
                pltpu.VMEM((size, lanes), F32),
                pltpu.VMEM((keys, 2 * size), F32),
            ],
        ),
        compiler_params=pltpu.CompilerParams(
            vmem_limit_bytes=(24 if keys <= 4096 else 60) * MIB
        ),
        cost_estimate=pl.CostEstimate(
            flops=24 * width * rows * keys, bytes_accessed=4 * width * rows * 4, transcendentals=0
        ),
        name="attention",
    )(table, place + jnp.array([0, 0, 0, start], jnp.int32), q_t, do_t, cosine, sine, *kvs, *extra)


def prologue_kernel(
    sc, x_hbm, xt, g_hbm, gt, gains, w_hbm, cos_ref, sin_ref, h1_ref, h2_ref, gg_ref, kv_ref, xo, w_kv, sem
):
    rows = xt.shape[0]
    copies = [
        pltpu.make_async_copy(x_hbm, xo, sem.at[0]),
        pltpu.make_async_copy(w_hbm, w_kv, sem.at[1]),
        pltpu.make_async_copy(g_hbm, gg_ref.at[0:rows, :], sem.at[2]),
    ]
    for copy in copies:
        copy.start()
    gg_ref[rows : 2 * rows, :] = gt[...]
    gain_one, bias_one = gains[0:1, :].astype(F32), gains[1:2, :].astype(F32)
    gain_two, bias_two = gains[2:3, :].astype(F32), gains[3:4, :].astype(F32)
    for n, x in ((1, xt), (0, xo)):
        if n == 0:
            copies[0].wait()
        for t in range(rows // 128):
            here = slice(n * rows + t * 128, n * rows + (t + 1) * 128)
            hat, unused = normed(x[t * 128 : (t + 1) * 128, :].astype(F32))
            h1_ref[here, :] = (hat * gain_one + bias_one).astype(BF)
            h2_ref[here, :] = (hat * gain_two + bias_two).astype(BF)
    copies[1].wait()
    raw = dot(h1_ref[...], w_kv[...])
    kv = turn(raw.T, cos_ref[...], sin_ref[...]).T.astype(BF)
    kv_ref[pl.ds(pl.multiple_of(sc[0] * rows, rows), rows), :] = kv[:rows]
    kv_ref[pl.ds(pl.multiple_of((1 - sc[0]) * rows, rows), rows), :] = kv[rows:]
    copies[2].wait()


def half_copies(sc, w_query, w_out, query_s, out_s, sem):
    half = out_s.shape[0]
    at = pl.ds(pl.multiple_of(sc[0] * half, 128), half)
    return [
        pltpu.make_async_copy(w_query.at[:, at], query_s, sem.at[0]),
        pltpu.make_async_copy(w_out.at[at, :], out_s, sem.at[1]),
    ]


def project_kernel(
    sc, h_ref, g_ref, cos_ref, sin_ref, w_query, w_out, q_ref, do_ref, query_s, out_s, sem, *, size
):
    copies = half_copies(sc, w_query, w_out, query_s, out_s, sem)
    for copy in copies:
        copy.start()
    cosine, sine = cos_ref[...], sin_ref[...]
    copies[0].wait()
    raw = (dot(h_ref[...], query_s[...]) * (0.125 * LOG2E)).T
    for h in range(raw.shape[0] // size):
        at = slice(h * size, (h + 1) * size)
        q_ref[at, :] = turn(raw[at], cosine, sine).astype(BF)
    copies[1].wait()
    do_ref[...] = dot(out_s[...], g_ref[...], ((1,), (1,)))


def hidden_copies(sc, piece, w_up, w_down, up_s, down_s, sems, part, n_pair):
    copies = []
    for j in range(n_pair):
        source = pl.ds(pl.multiple_of((2 * j + sc[0]) * part + piece * LANES, LANES), LANES)
        at = slice(j * LANES, (j + 1) * LANES)
        if w_up is not None:
            copies.append(
                pltpu.make_async_copy(w_up.at[:, source], up_s.at[:, at], sems.at[0])
            )
        if w_down is not None:
            copies.append(
                pltpu.make_async_copy(w_down.at[source, :], down_s.at[at, :], sems.at[1])
            )
    return copies


def piece_of(sc, n):
    return 0 if n == 0 else (2 - sc[2] if n == 1 else 1 + sc[2])


def ffn_kernel(
    sc, h_ref, g_ref, w_up, w_down, act_ref, dup_ref, *refs, n, part, n_pair
):
    up_s, down_s, grad_s, sems = refs[-4:]
    outs = refs[:-4]
    rows, width = h_ref.shape
    copies = hidden_copies(sc, piece_of(sc, n), w_up, w_down, up_s, down_s, sems, part, n_pair)
    for copy in copies[0::2] + copies[1::2]:
        copy.start()
    for copy in copies[0::2] + copies[1::2]:
        copy.wait()

    def row_tile(r, carry):
        tile = pl.ds(pl.multiple_of(r * 128, 128), 128)
        act, slope = gelu_parts(dot(h_ref[tile, :], up_s[...]))
        act_ref[tile, :] = act.astype(BF)
        d_act = dot(g_ref[tile, :], down_s[...], ((1,), (1,)))
        dup_ref[tile, :] = (d_act * slope).astype(BF)
        return carry

    lax.fori_loop(0, rows // 128, row_tile, 0, unroll=2)
    up_rows = width // n_pair
    block_rows = width // WIDE * LANES

    def give(low, high, kind, first, value):
        here = slice(first, first + value.shape[0])
        if n == 0:
            outs[1 - low][high, kind * block_rows + first : kind * block_rows + here.stop, :] = value
        else:
            outs[0][kind ^ sc[3], low, high, here, :] = value

    grad_s[0 : n_pair * LANES, :] = dot(act_ref[...], g_ref[...], ((0,), (0,))).astype(BF)
    for low in range(2):
        for high in range(2):
            chip = sc[1] ^ (low + 2 * high)
            rows_at = pl.ds(pl.multiple_of(chip * LANES, LANES), LANES)
            for b in range(width // WIDE):
                give(low, high, 0, b * LANES, grad_s[rows_at, b * WIDE : (b + 1) * WIDE])
    span = n_pair * LANES
    grad_s[:, 0:span] = dot(h_ref[...], dup_ref[...], ((0,), (0,))).astype(BF)
    for low in range(2):
        for high in range(2):
            chip = sc[1] ^ (low + 2 * high)
            rows_at = pl.ds(pl.multiple_of(chip * up_rows, 64), up_rows)
            for b in range(span // WIDE):
                give(low, high, 1, b * up_rows, grad_s[rows_at, b * WIDE : (b + 1) * WIDE])


def ffn_gradients(sc, h_two, g_two, w_up, w_down, n, part, n_pair):
    rows, width = h_two.shape
    span = n_pair * LANES
    block = width // WIDE * LANES
    if n == 0:
        outs = [shape((2, 2 * block, WIDE), BF)] * 2
    else:
        outs = [shape((2, 2, 2, block, WIDE), BF)]
    return call(
        functools.partial(ffn_kernel, n=n, part=part, n_pair=n_pair),
        "ffn_gradients",
        [shape((rows, span), BF)] * 2 + outs,
        [VM, VM, HBM, HBM],
        [VM] * (2 + len(outs)),
        [
            pltpu.VMEM((width, span), BF),
            pltpu.VMEM((span, width), BF),
            pltpu.VMEM((width, width), BF),
            pltpu.SemaphoreType.DMA((2,)),
        ],
        56,
        8 * rows * width * span,
    )(sc, h_two, g_two, w_up, w_down)


def late_kernel(sc, h_ref, dq0, dq1, mix0, mix1, got0, got1, g_ref, send_ref, keep_ref, mix_s, dq_s, both_s, *, n_pair):
    half = mix0.shape[0]
    rows = mix0.shape[1]
    width = 2 * half
    own = pl.multiple_of(sc[0] * half, 128)
    other = pl.multiple_of((1 - sc[0]) * half, 128)
    mix_s[pl.ds(own, half), 0:rows] = mix0[...]
    mix_s[pl.ds(own, half), rows : 2 * rows] = mix1[...]
    mix_s[pl.ds(other, half), 0:rows] = got1[...]
    mix_s[pl.ds(other, half), rows : 2 * rows] = got0[...]
    dq_s[:, 0:rows] = dq0[...]
    dq_s[:, rows : 2 * rows] = dq1[...]
    both_s[:, 0:half] = dot(h_ref[...], dq_s[...], ((0,), (1,))).astype(BF)
    both_s[:, half:width] = dot(mix_s[...], g_ref[:, pl.ds(own, half)]).astype(BF)
    block = width // n_pair
    quarter = keep_ref.shape[3]
    unit = 48
    for low in range(2):
        for high in range(2):
            chip = sc[1] ^ (low + 2 * high)
            for first in range(2):
                ref = send_ref if first else keep_ref
                for second in range(2):
                    part = 2 * (first ^ sc[2]) + (second ^ sc[3])
                    for r in range(quarter // unit):
                        at = part * quarter + r * unit
                        col, row = at // block, at % block
                        source = pl.ds(pl.multiple_of(chip * block + row, 16), unit)
                        lane = pl.ds(pl.multiple_of(col * WIDE, WIDE), WIDE)
                        ref[second, low, high, r * unit : (r + 1) * unit, :] = both_s[source, lane]


def late_gradients(sc, h_one, dqs, mixes, gots, g_two, n_pair):
    half = dqs[0].shape[0]
    width = 2 * half
    rows = h_one.shape[0]
    quarter = width // n_pair * (width // WIDE) // 4
    return call(
        functools.partial(late_kernel, n_pair=n_pair),
        "late_gradients",
        [shape((2, 2, 2, quarter, WIDE), BF)] * 2,
        [VM] * 8,
        [VM] * 2,
        [
            pltpu.VMEM((width, rows), BF),
            pltpu.VMEM((half, rows), BF),
            pltpu.VMEM((width, width), BF),
        ],
        16,
        2 * rows * width * width,
    )(sc, h_one, *dqs, *mixes, *gots, g_two)


def out_kernel(sc, a0, a1, a2, mix0, mix1, x_ref, w_down, w_out, own_ref, send_ref, down_s, out_s, sems, *, part, n_pair):
    half = out_s.shape[0]
    rows = x_ref.shape[0]
    span = n_pair * LANES
    copies = [
        pltpu.make_async_copy(
            w_out.at[pl.ds(pl.multiple_of(sc[0] * half, 128), half), :], out_s, sems.at[0]
        )
    ]
    for n in range(3):
        copies += hidden_copies(
            sc, piece_of(sc, n), None, w_down, None, down_s.at[n], sems, part, n_pair
        )
    for copy in copies:
        copy.start()
    for copy in copies:
        copy.wait()
    for n, mix in enumerate((mix0, mix1)):
        here = slice(n * rows, (n + 1) * rows)
        total = dot(mix[...], out_s[...], ((0,), (0,)))
        for k, act in enumerate((a0, a1, a2)):
            total = total + dot(act[here, :], down_s[k])
        if n == 0:
            own_ref[...] = total + x_ref[...].astype(F32)
        else:
            send_ref[...] = total.astype(BF)


def hat_kernel(sc, d0, d1, d2, dq0, dq1, xo, xt, gains, w_up, w_query, own_ref, send_ref, sum_ref, up_s, query_s, sems, *, part, n_pair):
    half = query_s.shape[1]
    rows, width = xo.shape
    copies = [
        pltpu.make_async_copy(
            w_query.at[:, pl.ds(pl.multiple_of(sc[0] * half, 128), half)], query_s, sems.at[1]
        )
    ]
    for n in range(3):
        copies += hidden_copies(
            sc, piece_of(sc, n), w_up, None, up_s.at[n], None, sems, part, n_pair
        )
    for copy in copies:
        copy.start()
    for copy in copies:
        copy.wait()
    gain_one, gain_two = gains[0:1, :].astype(F32), gains[2:3, :].astype(F32)
    sums = [jnp.zeros((1, width), F32)] * 4
    for n, (x, dq) in enumerate(((xo, dq0), (xt, dq1))):
        here = slice(n * rows, (n + 1) * rows)
        two = dot(d0[here, :], up_s[0], ((1,), (1,)))
        two = two + dot(d1[here, :], up_s[1], ((1,), (1,)))
        two = two + dot(d2[here, :], up_s[2], ((1,), (1,)))
        one = dot(dq[...], query_s[...], ((0,), (1,)))
        hat, unused = normed(x[...].astype(F32))
        for k, value in enumerate((one * hat, one, two * hat, two)):
            sums[k] = sums[k] + jnp.sum(value, 0, keepdims=True)
        total = one * gain_one + two * gain_two
        if n == 0:
            own_ref[...] = total
        else:
            send_ref[...] = total.astype(BF)
    sum_ref[...] = jnp.concatenate(sums + [jnp.zeros((4, width), F32)], 0)


def last_kernel(sc, dkv_a, dkv_b, cos_ref, sin_ref, w_kv, h_ref, x_ref, gains, hat_own, hat_got, sum_ref, g_ref, grad_ref, send_ref, keep_ref, *, n_pair):
    rows, width = x_ref.shape
    dkv = (dkv_a[...].astype(F32) + dkv_b[...].astype(F32)).T
    low_t = turn(dkv, cos_ref[:, 0:rows], -sin_ref[:, 0:rows]).astype(BF)
    low = low_t.T
    weight = dot(low_t, h_ref[0:rows, :]).T.astype(BF)
    d_kv = dot(low, w_kv[...], ((1,), (1,)))
    hat, scale = normed(x_ref[...].astype(F32))
    gain = gains[0:1, :].astype(F32)
    total = hat_own[...] + hat_got[...].astype(F32) + d_kv * gain
    grad_ref[...] = g_ref[...].astype(F32) + scale * (
        total
        - jnp.mean(total, -1, keepdims=True)
        - hat * jnp.mean(total * hat, -1, keepdims=True)
    )
    sums = jnp.concatenate(
        [
            sum_ref[0:1, :] + jnp.sum(d_kv * hat, 0, keepdims=True),
            sum_ref[1:2, :] + jnp.sum(d_kv, 0, keepdims=True),
            sum_ref[2:4, :],
            jnp.zeros((4, width), F32),
        ],
        0,
    ).astype(BF)
    part = width // (2 * n_pair)
    lanes = weight.shape[1]
    for chip in range(n_pair):
        rel = chip ^ sc[1]
        low_bit, high_bit = rel % 2, rel // 2
        blocks = []
        for core in range(2):
            at = (2 * chip + core) * part
            piece = weight[at : at + part, :]
            blocks.append(jnp.concatenate([piece[: part // 2], piece[part // 2 :]], 1))
            row = sums[:, at : at + part]
            blocks.append(jnp.concatenate([row, jnp.zeros((8, 2 * lanes - part), BF)], 1))
        block = jnp.concatenate(blocks, 0)

        @pl.when(low_bit == 1)
        def _():
            send_ref[high_bit] = block

        @pl.when(low_bit == 0)
        def _():
            keep_ref[high_bit] = block


def down_kernel(sc, send_ref, got_ref, out_ref, *, width):
    block = width // WIDE * LANES
    for k in range(3):
        for b in range(width // WIDE):
            here = slice(b * LANES, (b + 1) * LANES)
            if k == 0:
                at = slice(2 * block + b * LANES, 2 * block + (b + 1) * LANES)
                value = send_ref[at, :].astype(F32) + got_ref[at, :].astype(F32)
            else:
                at = pl.ds(pl.multiple_of(sc[3] * block + b * LANES, LANES), LANES)
                mine = send_ref[at, :].astype(F32)
                value = jnp.where(sc[2] == k - 1, mine, got_ref[at, :].astype(F32))
            out_ref[k * LANES : (k + 1) * LANES, b * WIDE : (b + 1) * WIDE] = value


def up_block(sc, k, b, parity, early_send, early_got, width, part):
    block = width // WIDE * LANES
    off = b * 2 * part + parity * part
    if k == 0:
        at = pl.ds(pl.multiple_of(3 * block + off, 32), part)
        return early_send[at, :].astype(F32) + early_got[at, :].astype(F32)
    at = pl.ds(pl.multiple_of((1 - sc[3]) * block + off, 32), part)
    return jnp.where(
        sc[2] == k - 1, early_send[at, :].astype(F32), early_got[at, :].astype(F32)
    )


def late_block(sc, b, parity, send, got, part, quarter):
    pieces = []
    for r in range(2):
        at = b * 2 * part + parity * part + r * (part // 2)
        first, second = at // (2 * quarter), at // quarter % 2
        rel = (second ^ sc[3]) * quarter + at % quarter
        source = pl.ds(pl.multiple_of(rel, 16), part // 2)
        pieces.append(
            jnp.where(
                first == sc[2], send[source, :].astype(F32), got[source, :].astype(F32)
            )
        )
    return jnp.concatenate(pieces, 0)


def pack_kernel(sc, early_send, early_got, last_send, last_got, out_ref, own_ref, *, width, part, quarter):
    for which, ref in ((1, out_ref), (0, own_ref)):
        parity = sc[0] if which == 0 else 1 - sc[0]
        at = 0
        for k in range(3):
            for b in range(2):
                ref[at : at + part, :] = up_block(
                    sc, k, b, parity, early_send, early_got, width, part
                ).astype(BF)
                at += part
        for b in range(width // WIDE):
            ref[at : at + part, :] = late_block(
                sc, b, parity, last_send, last_got, part, quarter
            ).astype(BF)
            at += part
        few = (last_send.shape[0] - 2 * quarter) // 2
        source = pl.ds(pl.multiple_of(2 * quarter + parity * few, 8), few)
        ref[at : at + few, :] = (
            last_send[source, :].astype(F32) + last_got[source, :].astype(F32)
        ).astype(BF)


def final_kernel(sc, own_ref, got_ref, up_ref, query_ref, proj_ref, kv_ref, norm_ref, *, part, n_pair):
    part_hidden = up_ref.shape[1] // (2 * n_pair)
    half = query_ref.shape[1] // 2
    for which, ref in enumerate((own_ref, got_ref)):
        core = sc[0] if which == 0 else 1 - sc[0]
        at = 0
        for k in range(3):
            for j in range(n_pair):
                lane = (2 * j + core) * part_hidden + k * LANES
                rows = slice((2 * k + j // 2) * part, (2 * k + j // 2 + 1) * part)
                cols = slice(j % 2 * LANES, (j % 2 + 1) * LANES)
                up_ref[:, pl.ds(pl.multiple_of(lane, LANES), LANES)] = ref[rows, cols].astype(F32)
        base = 6 * part
        for n in range(2 * half // LANES):
            rows = slice(base + n // 2 * part, base + (n // 2 + 1) * part)
            value = ref[rows, n % 2 * LANES : (n % 2 + 1) * LANES].astype(F32)
            to, m = (query_ref, n) if n < half // LANES else (proj_ref, n - half // LANES)
            to[:, pl.ds(pl.multiple_of(core * half + m * LANES, LANES), LANES)] = value
    base = 9 * part
    few = own_ref[base:, :].astype(F32) + got_ref[base:, :].astype(F32)
    kv_ref[0 : part // 2, :] = few[0 : part // 2, 0:LANES]
    kv_ref[part // 2 : part, :] = few[0 : part // 2, LANES:WIDE]
    norm_ref[...] = few[part // 2 : part // 2 + 8, :]


class Links:
    def __init__(self, n_grp, n_ctx):
        self.n_grp, self.n_ctx, self.n_pair = n_grp, n_ctx, n_ctx // 2
        self.small = (n_grp, n_ctx) == (4, 8)
        self.ctx = lax.axis_index("ctx")
        self.grp = lax.axis_index("grp")
        self.core = self.ctx % 2
        self.chip = self.ctx // 2
        self.groups = [[2 * z + c for z in range(self.n_pair)] for c in range(2)]

    def swap(self, value):
        return lax.ppermute(value, "ctx", [(i, i ^ 1) for i in range(self.n_ctx)])

    def permute(self, value, target):
        pairs = []
        for g in range(self.n_grp):
            for i in range(self.n_ctx):
                y, x, z, c = target(g // 2, g % 2, i // 2, i % 2)
                pairs.append((g * self.n_ctx + i, (2 * y + x) * self.n_ctx + 2 * z + c))
        return lax.ppermute(value, ("grp", "ctx"), pairs)

    def cross(self, value, stage):
        return self.permute(
            value, lambda y, x, z, c: (y, 1 - x, z, c) if c == stage else (1 - y, x, z, c)
        )

    def bit(self, stage):
        y, x = self.grp // 2, self.grp % 2
        return jnp.where(self.core == stage, x, y)

    def flip(self, value, bit):
        return self.permute(value, lambda y, x, z, c: (y, x, z ^ bit, c))

    def reduce(self, parts):
        moved = lax.all_to_all(parts, "ctx", 0, 0, axis_index_groups=self.groups)
        return lax.psum(jnp.sum(moved.astype(F32), 0).astype(BF), "grp")


def add(keep, got):
    return (keep.astype(F32) + got.astype(F32)).astype(BF)


def low(value):
    return value.astype(BF)


def shards_small(
    layer_input, block_table, ln1_gain, ln1_bias, ln2_gain, ln2_bias,
    w_query, w_keyval, w_out, w_up, w_down, cotangent, *, n_grp, n_ctx,
):
    links = Links(n_grp, n_ctx)
    core, chip, n_pair = links.core, links.chip, links.n_pair
    rows, width = layer_input.shape
    lanes = w_keyval.shape[1]
    size = lanes // 2
    hidden = w_up.shape[1]
    group_len = block_table.shape[1] * BLK
    part, part_hidden = width // n_ctx, hidden // n_ctx
    half = width // 2
    per_chip = 2 * rows // BLK
    table = block_table[0]
    sc = jnp.stack([core, chip, links.bit(0), links.bit(1)]).astype(jnp.int32)
    gains = jnp.stack([ln1_gain, ln1_bias, ln2_gain, ln2_bias])

    x_other, g_other = links.swap(layer_input), links.swap(cotangent)
    own_slots = lax.dynamic_slice_in_dim(table, chip * per_chip, per_chip).reshape(2, -1)
    slots = jnp.concatenate([own_slots[core], own_slots[1 - core]])
    canon = (slots[:, None] * BLK + jnp.arange(BLK, dtype=jnp.int32)[None, :]).reshape(2 * rows)
    prompt_len = group_len // 2
    cont_span = min(CONT, prompt_len)
    position = jnp.where(
        canon < prompt_len, canon, prompt_len + (canon - prompt_len) % cont_span
    )
    cosine, sine = rope_tables(position)

    h_one, h_two, g_two, kv_low = call(
        prologue_kernel,
        "prologue",
        [shape((2 * rows, width), BF)] * 3 + [shape((2 * rows, lanes), BF)],
        [HBM, VM, HBM, VM, VM, HBM, VM, VM],
        [VM] * 4,
        [
            pltpu.VMEM((rows, width), BF),
            pltpu.VMEM((width, lanes), BF),
            pltpu.SemaphoreType.DMA((3,)),
        ],
        16,
    )(sc, layer_input, x_other, cotangent, g_other, gains, w_keyval, cosine, sine)

    kv_got = links.flip(kv_low, 1)
    ffn = functools.partial(
        ffn_gradients, sc, w_up=w_up, w_down=w_down, part=part_hidden, n_pair=n_pair
    )
    act_0, dup_0, a_send, a_keep = ffn(h_two, g_two, n=0)
    a_got = links.flip(a_send, 1)
    kv_near = jnp.concatenate([kv_low, kv_got], 0)
    kv_far = links.flip(kv_near, 2)
    act_1, dup_1, b_send = ffn(tie(h_two, a_keep, kv_near), g_two, n=1)
    b_got = links.cross(b_send, 0)
    act_2, dup_2, b_keep = ffn(tie(h_two, b_send), g_two, n=2)

    q_t, do_t = call(
        functools.partial(project_kernel, size=size),
        "project",
        [shape((half, 2 * rows), BF), shape((half, 2 * rows), F32)],
        [VM] * 4 + [HBM] * 2,
        [VM] * 2,
        [
            pltpu.VMEM((width, half), BF),
            pltpu.VMEM((half, width), BF),
            pltpu.SemaphoreType.DMA((2,)),
        ],
        16,
    )(sc, tie(h_one, b_keep), g_two, cosine, sine, w_query, w_out)

    place = jnp.stack([chip * per_chip, core * (rows // BLK), chip, 0 * chip]).astype(jnp.int32)
    count = rows // BLK
    attend = functools.partial(
        attention, table, place, do_t=do_t, cosine=cosine, sine=sine, kvs=(kv_near, kv_far),
        count=count, per_chip=per_chip, split=True,
    )
    mix_0, dq_0, carried = attend(q_t=q_t, carried=None, start=0, last_call=False)
    mix_0_got = links.swap(mix_0)
    a_got, b_got = tie(a_got, carried), tie(b_got, carried)
    a_send = add(a_keep[1], a_got[1])
    a_got_2 = links.flip(a_send, 2)
    b_send = add(b_keep[1], b_got[1])
    b_got_2 = links.cross(b_send, 1)
    mix_1, dq_1, dkv_send, dkv_keep = attend(
        q_t=tie(q_t, a_send, b_send), carried=carried, start=count, last_call=True
    )
    a_keep, b_keep = add(a_keep[0], a_got[0]), add(b_keep[0], b_got[0])

    dkv_got = links.swap(dkv_send)
    mix_1_got = links.swap(mix_1)
    late_send, late_keep = late_gradients(
        sc, h_one, (dq_0, dq_1), (mix_0, mix_1), (mix_0_got, mix_1_got), g_two, n_pair
    )
    late_got = links.cross(late_send, 0)
    dkv_got_2 = links.flip(add(dkv_keep[1], dkv_got[1]), 1)
    dkv_keep = add(dkv_keep[0], dkv_got[0])
    b_got_2 = tie(b_got_2, late_send)
    b_got_3 = links.flip(add(b_keep[1], b_got_2[1]), 1)
    b_keep = add(b_keep[0], b_got_2[0])

    w_specs = [HBM] * 2
    out_own, out_send = call(
        functools.partial(out_kernel, part=part_hidden, n_pair=n_pair),
        "outputs",
        [shape((rows, width), F32), shape((rows, width), BF)],
        [VM] * 6 + w_specs,
        [VM] * 2,
        [
            pltpu.VMEM((3, n_pair * LANES, width), BF),
            pltpu.VMEM((half, width), BF),
            pltpu.SemaphoreType.DMA((2,)),
        ],
        56,
    )(sc, act_0, act_1, tie(act_2, late_send, dkv_got), mix_0, mix_1, layer_input, w_down, w_out)
    out_got = links.swap(out_send)
    dkv_got_2 = tie(dkv_got_2, out_send)
    dkv_got_3 = links.flip(add(dkv_keep[1], dkv_got_2[1]), 2)
    dkv_keep = add(dkv_keep[0], dkv_got_2[0])
    hat_own, hat_send, sums = call(
        functools.partial(hat_kernel, part=part_hidden, n_pair=n_pair),
        "norms",
        [shape((rows, width), F32), shape((rows, width), BF), shape((8, width), F32)],
        [VM] * 8 + w_specs,
        [VM] * 3,
        [
            pltpu.VMEM((3, width, n_pair * LANES), BF),
            pltpu.VMEM((width, half), BF),
            pltpu.SemaphoreType.DMA((2,)),
        ],
        56,
    )(
        sc, dup_0, dup_1, tie(dup_2, out_send, dkv_got_2), dq_0, dq_1, layer_input, x_other, gains,
        w_up, w_query,
    )
    hat_got = links.swap(hat_send)
    layer_output = low(out_own + out_got.astype(F32))

    late_got = tie(late_got, hat_send)
    late_got_2 = links.cross(add(late_keep[1], late_got[1]), 1)
    late_keep = add(late_keep[0], late_got[0])
    b_got_3 = tie(b_got_3, hat_send)
    b_got_4 = links.flip(add(b_keep[1], b_got_3[1]), 2)
    b_keep = add(b_keep[0], b_got_3[0])
    a_sum = add(a_keep, tie(a_got_2, hat_send))

    few = part // 2 + 8
    in_grad, few_send, few_keep = call(
        functools.partial(last_kernel, n_pair=n_pair),
        "last",
        [shape((rows, width), F32)] + [shape((2, 2 * few, 2 * lanes), BF)] * 2,
        [VM] * 12,
        [VM] * 3,
        [],
        16,
    )(
        sc, dkv_keep, dkv_got_3, cosine, sine, w_keyval, h_one, layer_input, gains, hat_own, hat_got,
        sums, cotangent,
    )

    late_got_2 = tie(late_got_2, few_send)
    quarter = late_keep.shape[2]
    last_send = jnp.concatenate([add(late_keep[1], late_got_2[1]), few_send], 1)
    last_got = links.flip(last_send, 1)
    last_keep = jnp.concatenate([add(late_keep[0], late_got_2[0]), few_keep], 1)
    early = jnp.concatenate([add(b_keep, tie(b_got_4, last_send)), a_sum], 0)
    block = early.shape[0] // 3
    early_got = links.cross(early, 1)
    last_got_2 = links.flip(add(last_keep[1], last_got[1]), 2)
    last_keep = add(last_keep[0], last_got[0])
    early = jnp.concatenate(
        [early[:block], early_got[:block], add(early[block:], early_got[block:])], 0
    )
    early_got = links.cross(early, 0)
    last = add(last_keep, last_got_2)
    last_got = links.cross(last, 1)
    last = jnp.concatenate(
        [last[:quarter], last_got[:quarter], add(last[quarter:], last_got[quarter:])], 0
    )
    last_got = links.cross(last, 0)
    total_down = call(
        functools.partial(down_kernel, width=width),
        "down", shape((part_hidden, width), F32), [VM] * 2, VM, [], 8,
    )(sc, early, early_got)
    size_out = 9 * part + few
    other, own = call(
        functools.partial(pack_kernel, width=width, part=part, quarter=quarter),
        "pack", [shape((size_out, WIDE), BF)] * 2, [VM] * 4, [VM] * 2, [], 8,
    )(sc, early, early_got, last, last_got)
    got = links.swap(other)
    total_up, total_query, total_out, total_kv, norm = call(
        functools.partial(final_kernel, part=part, n_pair=n_pair),
        "final",
        [
            shape((part, hidden), F32),
            shape((part, width), F32),
            shape((part, width), F32),
            shape((part, lanes), F32),
            shape((8, WIDE), F32),
        ],
        [VM] * 2,
        [VM] * 5,
        [],
        8,
    )(sc, own, got)
    norms = [norm[n, :part] for n in range(4)]
    return (layer_output, in_grad, *norms, total_query, total_kv, total_out, total_up, total_down)


def rotate_rows(values, cosine, sine):
    return turn(values.T, cosine, sine).T


def shards(
    layer_input, block_table, ln1_gain, ln1_bias, ln2_gain, ln2_bias,
    w_query, w_keyval, w_out, w_up, w_down, cotangent, *, n_grp, n_ctx,
):
    links = Links(n_grp, n_ctx)
    core, chip, n_pair = links.core, links.chip, links.n_pair
    rows, width = layer_input.shape
    size = w_keyval.shape[1] // 2
    hidden = w_up.shape[1]
    group_len = block_table.shape[1] * BLK
    part_rows, part_hidden = width // n_ctx, hidden // n_ctx
    half_width, half_hidden = width // 2, hidden // 2
    per_chip = 2 * rows // BLK
    table = block_table[0]

    def both(own, other):
        return jnp.concatenate(
            [jnp.where(core == 0, own, other), jnp.where(core == 0, other, own)], 0
        )

    def mine(value, own_core):
        return lax.dynamic_slice_in_dim(value, own_core * rows, rows, 0)

    x_two = both(layer_input, links.swap(layer_input))
    g_two = both(cotangent, links.swap(cotangent))
    canon = (
        lax.dynamic_slice_in_dim(table, chip * per_chip, per_chip)[:, None] * BLK
        + jnp.arange(BLK, dtype=jnp.int32)[None, :]
    ).reshape(2 * rows)
    prompt_len = group_len // 2
    cont_span = min(CONT, prompt_len)
    position = jnp.where(
        canon < prompt_len, canon, prompt_len + (canon - prompt_len) % cont_span
    )
    cosine, sine = rope_tables(position)
    gain_one, gain_two = ln1_gain.astype(F32), ln2_gain.astype(F32)
    hat, scale = normed(x_two.astype(F32))
    h_one = low(hat * gain_one + ln1_bias.astype(F32))
    h_two = low(hat * gain_two + ln2_bias.astype(F32))
    kv_raw = dot(h_one, w_keyval)
    kv_low = low(
        jnp.concatenate([rotate_rows(kv_raw[:, :size], cosine, sine), kv_raw[:, size:]], -1)
    )
    kv_all = lax.all_gather(kv_low, "ctx", axis=0, axis_index_groups=links.groups, tiled=True)

    up_half = lax.dynamic_index_in_dim(
        w_up.reshape(width, n_pair, 2, part_hidden), core, 2, False
    ).reshape(width, half_hidden)
    down_half = lax.dynamic_index_in_dim(
        w_down.reshape(n_pair, 2, part_hidden, width), core, 1, False
    ).reshape(half_hidden, width)
    act, slope = gelu_parts(dot(h_two, up_half))
    act = low(act)
    grad_down = low(dot(act, g_two, ((0,), (0,))))
    total_down = links.reduce(grad_down.reshape(n_pair, part_hidden, width))
    grad_up = low(dot(g_two, down_half, ((1,), (1,))) * slope)
    grad_up_w = low(dot(h_two, grad_up, ((0,), (0,))))
    total_up = links.reduce(grad_up_w.reshape(n_pair, 2 * part_rows, half_hidden))

    query_half = lax.dynamic_slice_in_dim(w_query, core * half_width, half_width, 1)
    out_half = lax.dynamic_slice_in_dim(w_out, core * half_width, half_width, 0)
    q_raw = dot(query_half, h_one, ((0,), (1,))) * (0.125 * LOG2E)
    q_t = low(
        jax.vmap(turn, (0, None, None))(q_raw.reshape(-1, size, 2 * rows), cosine, sine)
    ).reshape(half_width, 2 * rows)
    do_t = dot(out_half, g_two, ((1,), (1,)))
    place = jnp.stack([chip * per_chip, 0 * chip, 0 * chip, 0 * chip]).astype(jnp.int32)
    mix_t, dq_t, dkv_part = attention(
        table, place, q_t, do_t, cosine, sine, (kv_all,), None, 0, per_chip, per_chip, True, False
    )

    dkv_part = dkv_part.reshape(n_pair, 2, rows, 2 * size)
    dkv_own = lax.dynamic_index_in_dim(dkv_part, core, 1, False)
    dkv_got = links.swap(lax.dynamic_index_in_dim(dkv_part, 1 - core, 1, False))
    moved = lax.all_to_all(
        add(dkv_own, dkv_got), "ctx", 0, 0, axis_index_groups=links.groups
    )
    dkv = jnp.sum(moved.astype(F32), 0)
    cos_own = lax.dynamic_slice_in_dim(cosine, core * rows, rows, 1)
    sin_own = lax.dynamic_slice_in_dim(sine, core * rows, rows, 1)
    dkv_low = low(
        jnp.concatenate([rotate_rows(dkv[:, :size], cos_own, -sin_own), dkv[:, size:]], -1)
    )

    mix_got = links.swap(mix_t)
    mix_all = jnp.concatenate(
        [jnp.where(core == 0, mix_t, mix_got), jnp.where(core == 0, mix_got, mix_t)], 0
    )
    g_half = lax.dynamic_slice_in_dim(g_two, core * half_width, half_width, 1)
    grad_q_w = low(dot(h_one, dq_t, ((0,), (1,))))
    grad_out_w = low(dot(mix_all, g_half))
    late = jnp.concatenate([grad_q_w, grad_out_w], 1).reshape(n_pair, 2 * part_rows, width)
    total_late = links.reduce(late)

    out_part = dot(act, down_half) + dot(mix_t, out_half, ((0,), (0,)))
    out_got = links.swap(low(mine(out_part, 1 - core)))
    layer_output = low(layer_input.astype(F32) + mine(out_part, core) + out_got.astype(F32))

    d_two = dot(grad_up, up_half, ((1,), (1,)))
    d_one = dot(dq_t, query_half, ((0,), (1,)))
    d_kv = dot(dkv_low, w_keyval, ((1,), (1,)))
    row_core = lax.broadcasted_iota(jnp.int32, (2 * rows, 1), 0) // rows
    d_one = d_one + jnp.where(row_core == core, jnp.concatenate([d_kv, d_kv], 0), 0.0)
    sums = jnp.stack([jnp.sum(v, 0) for v in (d_one * hat, d_one, d_two * hat, d_two)])
    d_hat = d_one * gain_one + d_two * gain_two
    hat_got = links.swap(low(mine(d_hat, 1 - core)))
    d_hat = mine(d_hat, core) + hat_got.astype(F32)
    hat_own = mine(hat, core)
    in_grad = cotangent.astype(F32) + mine(scale, core) * (
        d_hat
        - jnp.mean(d_hat, -1, keepdims=True)
        - hat_own * jnp.mean(d_hat * hat_own, -1, keepdims=True)
    )

    grad_kv_w = dot(mine(h_one, core), dkv_low, ((0,), (0,)))
    sum_rows = sums.reshape(4, n_pair, 2, part_rows).transpose(1, 2, 0, 3)
    sum_rows = jnp.pad(sum_rows, ((0, 0), (0, 0), (0, 0), (0, 2 * size - part_rows)))
    few = jnp.concatenate([grad_kv_w.reshape(n_pair, 2, part_rows, 2 * size), sum_rows], 2)
    few = links.reduce(low(few).reshape(n_pair, 2 * (part_rows + 4), 2 * size))
    few = few.reshape(2, part_rows + 4, 2 * size)
    few_got = links.swap(lax.dynamic_index_in_dim(few, 1 - core, 0, False))
    few = lax.dynamic_index_in_dim(few, core, 0, False).astype(F32) + few_got.astype(F32)

    halves = jnp.concatenate(
        [total_up.reshape(2, part_rows, half_hidden), total_late.reshape(2, part_rows, width)], -1
    )
    own = lax.dynamic_index_in_dim(halves, core, 0, False)
    got = links.swap(lax.dynamic_index_in_dim(halves, 1 - core, 0, False))
    sides = jnp.stack([jnp.where(core == 0, own, got), jnp.where(core == 0, got, own)]).astype(F32)
    ups = sides[:, :, :half_hidden].reshape(2, part_rows, n_pair, part_hidden)
    total_up = ups.transpose(1, 2, 0, 3).reshape(part_rows, hidden)
    lates = sides[:, :, half_hidden:]
    total_query = lates[:, :, :half_width].transpose(1, 0, 2).reshape(part_rows, width)
    total_out = lates[:, :, half_width:].transpose(1, 0, 2).reshape(part_rows, width)
    norms = [few[part_rows + n, :part_rows] for n in range(4)]
    total_kv = few[:part_rows]
    total_down = total_down.astype(F32)
    return (layer_output, in_grad, *norms, total_query, total_kv, total_out, total_up, total_down)


def solution(mesh):
    n_grp, n_ctx = mesh.shape["grp"], mesh.shape["ctx"]
    body = shards_small if (n_grp, n_ctx) == (4, 8) else shards
    return jax.shard_map(
        functools.partial(body, n_grp=n_grp, n_ctx=n_ctx),
        mesh=mesh,
        in_specs=(P(("grp", "ctx"), None), P("grp", None))
        + (P(),) * 9
        + (P(("grp", "ctx"), None),),
        out_specs=(P(("grp", "ctx"), None),) * 2 + (P("ctx"),) * 4 + (P("ctx", None),) * 5,
        check_vma=False,
    )
```

```python
import functools

import jax
import jax.numpy as jnp
from jax import lax
from jax.experimental import pallas as pl
from jax.experimental.pallas import tpu as pltpu
from jax.sharding import PartitionSpec as P

ROT = 16
HALF = ROT // 2
BLK = 128
CONT = 1024
TILE = 256
LANES = 128
WIDE = 256
EPS = 1e-05
LOG2E = 1.4426950408889634
LN2 = 0.6931471805599453
BF = jnp.bfloat16
F32 = jnp.float32
MIB = 1024 * 1024
VM = pl.BlockSpec(memory_space=pltpu.VMEM)
HBM = pl.BlockSpec(memory_space=pltpu.HBM)


def dot(left, right, dims=((1,), (0,))):
    return lax.dot_general(left, right, (dims, ((), ())), preferred_element_type=F32)


def shape(dims, dtype):
    return jax.ShapeDtypeStruct(dims, dtype)


def tie(value, *others):
    return lax.optimization_barrier((value,) + others)[0]


def meet(*values):
    return lax.optimization_barrier(values)


def rope_tables(position):
    inverse = 10000.0 ** (-(2.0 * jnp.arange(HALF, dtype=F32)) / ROT)
    angles = inverse[:, None] * position.astype(F32)[None, :]
    return (jnp.cos(angles), jnp.sin(angles))


def turn(values, cosine, sine):
    first, second = values[:HALF], values[HALF:ROT]
    return jnp.concatenate(
        [first * cosine - second * sine, second * cosine + first * sine, values[ROT:]], 0
    )


def normed(values):
    shifted = values - jnp.mean(values, -1, keepdims=True)
    scale = lax.rsqrt(jnp.mean(shifted * shifted, -1, keepdims=True) + EPS)
    return (shifted * scale, scale)


def gelu_parts(value):
    cdf = 0.5 * (1.0 + lax.erf(value * 0.7071067811865476))
    pdf = jnp.exp(-0.5 * value * value) * 0.3989422804014327
    return value * cdf, cdf + value * pdf


def call(kernel, name, outs, specs, out_specs, scratch, limit, flops=1000):
    made = pl.pallas_call(
        kernel,
        out_shape=outs,
        grid_spec=pltpu.PrefetchScalarGridSpec(
            num_scalar_prefetch=1, in_specs=specs, out_specs=out_specs, scratch_shapes=scratch
        ),
        compiler_params=pltpu.CompilerParams(vmem_limit_bytes=limit * MIB),
        cost_estimate=pl.CostEstimate(flops=flops, bytes_accessed=flops, transcendentals=0),
        name=name,
    )

    def placed(scalars, *values):
        return made(
            scalars,
            *(
                pltpu.with_memory_space_constraint(v, pltpu.HBM) if spec is HBM else v
                for v, spec in zip(values, specs)
            ),
        )

    return placed


def attn_kernel(table, place, *refs, blocks, heads, size, n_kv, per_chip, last_call, first_call):
    q_ref, do_ref, cos_ref, sin_ref = refs[:4]
    kv_refs = refs[4 : 4 + n_kv]
    refs = refs[4 + n_kv :]
    if not first_call:
        sum_ref, refs = refs[0], refs[1:]
    mix_ref, dq_ref = refs[:2]
    outs = refs[2:-11]
    kv_c, kv_t, s_scr, p_scr, rq, rd, rqt, rdt, o_acc, dq_acc, dkv_acc = refs[-11:]
    step, group = pl.program_id(0), pl.program_id(1)
    lanes = heads * BLK
    prompt_blocks = blocks // 2
    prompt_tiles = prompt_blocks * BLK // TILE
    cont_blocks = min(CONT, prompt_blocks * BLK) // BLK

    def block_rows(block):
        return pl.ds(pl.multiple_of(block * BLK, BLK), BLK)

    @pl.when((step == 0) & (group == 0))
    def _():
        ones = jnp.ones((16, BLK), BF)
        share = blocks // n_kv

        for n, kv_ref in enumerate(kv_refs):

            def place_block(at, carry, n=n, kv_ref=kv_ref):
                spot = n * share + at
                block = table[((spot // per_chip) ^ place[2]) * per_chip + spot % per_chip]
                rows = kv_ref[block_rows(at), :]
                kv_c[block_rows(block), :] = rows
                turned = jnp.concatenate([rows.T, ones], 0)

                @pl.when(block % 2 == 0)
                def _():
                    kv_t[block // 2, :, 0:BLK] = turned

                @pl.when(block % 2 == 1)
                def _():
                    kv_t[block // 2, :, BLK:TILE] = turned

                return carry

            lax.fori_loop(0, share, place_block, 0)
        dkv_acc[...] = jnp.zeros_like(dkv_acc) if first_call else sum_ref[...]

    block = table[place[0] + lax.rem(place[3] + step + place[1], per_chip)]
    last = block // 2
    in_prompt = block < prompt_blocks
    seg_tile = (prompt_blocks + (block - prompt_blocks) // cont_blocks * cont_blocks) // 2
    full = jnp.where(in_prompt, last, prompt_tiles + last - seg_tile)

    def tile_of(i):
        return jnp.where(i < prompt_tiles, jnp.minimum(i, last), i - prompt_tiles + seg_tile)

    def key_rows(tile):
        return pl.ds(pl.multiple_of(tile * TILE, TILE), TILE)

    for h in range(heads):
        rq[0:size, h * BLK : (h + 1) * BLK] = q_ref[h * size : (h + 1) * size, :]
    rq[size : 2 * size, :] = jnp.zeros((size, lanes), BF)

    def scores(tile):
        return dot(kv_c[key_rows(tile), :], rq[...])

    def fold(values):
        return jnp.max(values.reshape(TILE // 8, 8, lanes), 0)

    def first_pass(i, top):
        part = scores(tile_of(i))
        s_scr[i] = part
        return jnp.maximum(top, fold(part))

    top = lax.fori_loop(0, full, first_pass, jnp.full((8, lanes), -1e30, F32))
    part = scores(last)
    key_at = last * TILE + lax.broadcasted_iota(jnp.int32, (TILE, lanes), 0)
    row_at = block * BLK + lax.rem(lax.broadcasted_iota(jnp.int32, (TILE, lanes), 1), BLK)
    part = jnp.where(key_at <= row_at, part, -1e30)
    s_scr[full] = part
    top = jnp.max(jnp.maximum(top, fold(part)), 0, keepdims=True)

    o_acc[...] = jnp.zeros_like(o_acc)

    def second_pass(i, carry):
        p = jnp.exp2(s_scr[i] - top).astype(BF)
        p_scr[i] = p
        o_acc[...] += dot(kv_t[jnp.where(i == full, last, tile_of(i)), size : 2 * size + 16, :], p)
        return carry

    lax.fori_loop(0, full + 1, second_pass, 0)

    inverse = 1.0 / o_acc[size : size + 1, :]
    mixed = o_acc[0:size, :] * inverse
    grads = []
    for h in range(heads):
        at = slice(h * BLK, (h + 1) * BLK)
        mix_ref[h * size : (h + 1) * size, :] = mixed[:, at].astype(BF)
        grads.append(do_ref[h * size : (h + 1) * size, :])
    scaled = (jnp.concatenate(grads, 1) * inverse).astype(BF)
    delta = jnp.sum(mixed * scaled.astype(F32), 0, keepdims=True)
    rd[0:size, :] = jnp.zeros((size, lanes), BF)
    rd[size : 2 * size, :] = scaled
    rqt[...] = rq[...].T
    rdt[...] = rd[...].T
    dq_acc[...] = jnp.zeros_like(dq_acc)

    def third_pass(i, carry):
        tile = jnp.where(i == full, last, tile_of(i))
        p = p_scr[i]
        d_probs = dot(kv_c[key_rows(tile), :], rd[...])
        ds = (p.astype(F32) * (d_probs - delta)).astype(BF)
        dq_acc[...] += dot(kv_t[tile, 0:size, :], ds)
        dkv_acc[key_rows(tile), :] += dot(p, rdt[...]) + dot(ds, rqt[...])
        return carry

    lax.fori_loop(0, full + 1, third_pass, 0)

    cosine, sine = cos_ref[...], sin_ref[...]
    for h in range(heads):
        part = dq_acc[:, h * BLK : (h + 1) * BLK] * 0.125
        dq_ref[h * size : (h + 1) * size, :] = turn(part, cosine, -sine).astype(BF)

    @pl.when((step == pl.num_programs(0) - 1) & (group == pl.num_programs(1) - 1))
    def _():
        if not last_call:
            outs[0][...] = dkv_acc[...]
            return
        scale = jnp.where(
            lax.broadcasted_iota(jnp.int32, (BLK, 2 * size), 1) < size, F32(LN2), F32(1.0)
        )

        def rows_of(slot):
            return (dkv_acc[block_rows(table[slot]), :] * scale).astype(BF)

        if len(outs) == 1:

            def give_block(slot, carry):
                outs[0][block_rows(slot), :] = rows_of(slot)
                return carry

            lax.fori_loop(0, blocks, give_block, 0)
            return
        per_core = per_chip // 2
        for low in range(2):
            for high in range(2):
                chip = place[2] ^ (low + 2 * high)
                for n in range(per_core):
                    here = slice(n * BLK, (n + 1) * BLK)
                    base = chip * per_chip + n
                    outs[0][low, high, here, :] = rows_of(base + per_core - place[1])
                    outs[1][low, high, here, :] = rows_of(base + place[1])


def attention(
    table, place, q_t, do_t, cosine, sine, kvs, carried, start, count, per_chip, last_call, split
):
    width = q_t.shape[0]
    rows = count * BLK
    first_call = carried is None
    size = kvs[0].shape[1] // 2
    keys = sum(kv.shape[0] for kv in kvs)
    all_heads = width // size
    blocks = keys // BLK
    heads = all_heads if keys <= 4096 else 2
    lanes = heads * BLK
    cont = min(CONT, keys // 2)
    most = (keys // 2 + cont) // TILE
    tiles = keys // TILE

    def whole(dims):
        return pl.BlockSpec(dims, lambda i, j, *_: (0,) * len(dims))

    if not last_call:
        dkv_shapes = [shape((keys, 2 * size), F32)]
    elif split:
        dkv_shapes = [shape((2, 2, keys // 8, 2 * size), BF)] * 2
    else:
        dkv_shapes = [shape((keys, 2 * size), BF)]
    extra = [] if first_call else [carried]
    column = pl.BlockSpec((heads * size, BLK), lambda i, j, *_: (j, i + start))
    angle = pl.BlockSpec((HALF, BLK), lambda i, j, *_: (0, i + start))
    out_column = pl.BlockSpec((heads * size, BLK), lambda i, j, *_: (j, i))
    return pl.pallas_call(
        functools.partial(
            attn_kernel,
            blocks=blocks,
            heads=heads,
            size=size,
            n_kv=len(kvs),
            per_chip=per_chip,
            last_call=last_call,
            first_call=first_call,
        ),
        out_shape=[shape((width, rows), BF)] * 2 + dkv_shapes,
        grid_spec=pltpu.PrefetchScalarGridSpec(
            num_scalar_prefetch=2,
            grid=(count, all_heads // heads),
            in_specs=[column, column, angle, angle]
            + [whole(kv.shape) for kv in kvs]
            + [whole(e.shape) for e in extra],
            out_specs=[out_column, out_column] + [whole(s.shape) for s in dkv_shapes],
            scratch_shapes=[
                pltpu.VMEM((keys, 2 * size), BF),
                pltpu.VMEM((tiles, 2 * size + 16, TILE), BF),
                pltpu.VMEM((most, TILE, lanes), F32),
                pltpu.VMEM((most, TILE, lanes), BF),
                pltpu.VMEM((2 * size, lanes), BF),
                pltpu.VMEM((2 * size, lanes), BF),
                pltpu.VMEM((lanes, 2 * size), BF),
                pltpu.VMEM((lanes, 2 * size), BF),
                pltpu.VMEM((size + 16, lanes), F32),
                pltpu.VMEM((size, lanes), F32),
                pltpu.VMEM((keys, 2 * size), F32),
            ],
        ),
        compiler_params=pltpu.CompilerParams(
            vmem_limit_bytes=(24 if keys <= 4096 else 60) * MIB
        ),
        cost_estimate=pl.CostEstimate(
            flops=1000, bytes_accessed=1000, transcendentals=0
        ),
        name="attention",
    )(table, place + jnp.array([0, 0, 0, start], jnp.int32), q_t, do_t, cosine, sine, *kvs, *extra)


def prologue_kernel(
    sc, x_hbm, xt_hbm, g_hbm, gt_hbm, gains, w_hbm, cos_ref, sin_ref, h1_ref, h2_ref, gg_ref, kv_ref, xo, xt, w_kv, sem
):
    rows = xt.shape[0]
    copies = [
        pltpu.make_async_copy(x_hbm, xo, sem.at[0]),
        pltpu.make_async_copy(xt_hbm, xt, sem.at[1]),
        pltpu.make_async_copy(w_hbm, w_kv, sem.at[2]),
        pltpu.make_async_copy(g_hbm, gg_ref.at[0:rows, :], sem.at[3]),
        pltpu.make_async_copy(gt_hbm, gg_ref.at[rows : 2 * rows, :], sem.at[4]),
    ]
    for copy in copies:
        copy.start()
    gain_one, bias_one = gains[0:1, :].astype(F32), gains[1:2, :].astype(F32)
    gain_two, bias_two = gains[2:3, :].astype(F32), gains[3:4, :].astype(F32)
    for n, x in enumerate((xo, xt)):
        copies[n].wait()
        for t in range(rows // 128):
            here = slice(n * rows + t * 128, n * rows + (t + 1) * 128)
            hat, unused = normed(x[t * 128 : (t + 1) * 128, :].astype(F32))
            h1_ref[here, :] = (hat * gain_one + bias_one).astype(BF)
            h2_ref[here, :] = (hat * gain_two + bias_two).astype(BF)
    copies[2].wait()
    raw = dot(h1_ref[...], w_kv[...])
    kv = turn(raw.T, cos_ref[...], sin_ref[...]).T.astype(BF)
    kv_ref[pl.ds(pl.multiple_of(sc[0] * rows, rows), rows), :] = kv[:rows]
    kv_ref[pl.ds(pl.multiple_of((1 - sc[0]) * rows, rows), rows), :] = kv[rows:]
    copies[3].wait()
    copies[4].wait()


def half_copies(sc, w_query, w_out, query_s, out_s, sem):
    half = out_s.shape[0]
    at = pl.ds(pl.multiple_of(sc[0] * half, 128), half)
    return [
        pltpu.make_async_copy(w_query.at[:, at], query_s, sem.at[0]),
        pltpu.make_async_copy(w_out.at[at, :], out_s, sem.at[1]),
    ]


def project_kernel(
    sc, h_ref, g_ref, cos_ref, sin_ref, w_query, w_out, q_ref, do_ref, query_s, out_s, sem, *, size
):
    copies = half_copies(sc, w_query, w_out, query_s, out_s, sem)
    for copy in copies:
        copy.start()
    cosine, sine = cos_ref[...], sin_ref[...]
    copies[0].wait()
    raw = (dot(h_ref[...], query_s[...]) * (0.125 * LOG2E)).T
    for h in range(raw.shape[0] // size):
        at = slice(h * size, (h + 1) * size)
        q_ref[at, :] = turn(raw[at], cosine, sine).astype(BF)
    copies[1].wait()
    do_ref[...] = dot(out_s[...], g_ref[...], ((1,), (1,)))


def hidden_copies(sc, piece, w_up, w_down, up_s, down_s, sems, part, n_pair):
    copies = []
    for j in range(n_pair):
        source = pl.ds(pl.multiple_of((2 * j + sc[0]) * part + piece * LANES, LANES), LANES)
        at = slice(j * LANES, (j + 1) * LANES)
        if w_up is not None:
            copies.append(
                pltpu.make_async_copy(w_up.at[:, source], up_s.at[:, at], sems.at[0])
            )
        if w_down is not None:
            copies.append(
                pltpu.make_async_copy(w_down.at[source, :], down_s.at[at, :], sems.at[1])
            )
    return copies


def piece_of(sc, n):
    return 0 if n == 0 else (2 - sc[2] if n == 1 else 1 + sc[2])


def ffn_kernel(
    sc, h_ref, g_ref, w_up, w_down, act_ref, dup_ref, *refs, n, part, n_pair
):
    up_s, down_s, grad_s, sems = refs[-4:]
    outs = refs[:-4]
    rows, width = h_ref.shape
    copies = hidden_copies(sc, piece_of(sc, n), w_up, w_down, up_s, down_s, sems, part, n_pair)
    for copy in copies[0::2] + copies[1::2]:
        copy.start()
    for copy in copies[0::2] + copies[1::2]:
        copy.wait()

    def row_tile(r, carry):
        tile = pl.ds(pl.multiple_of(r * 128, 128), 128)
        act, slope = gelu_parts(dot(h_ref[tile, :], up_s[...]))
        act_ref[tile, :] = act.astype(BF)
        d_act = dot(g_ref[tile, :], down_s[...], ((1,), (1,)))
        dup_ref[tile, :] = (d_act * slope).astype(BF)
        return carry

    lax.fori_loop(0, rows // 128, row_tile, 0, unroll=2)
    up_rows = width // n_pair
    block_rows = width // WIDE * LANES

    def give(low, high, kind, first, value):
        here = slice(first, first + value.shape[0])
        if n == 0:
            outs[1 - low][high, kind * block_rows + first : kind * block_rows + here.stop, :] = value
        else:
            outs[0][kind ^ sc[3], low, high, here, :] = value

    grad_s[0 : n_pair * LANES, :] = dot(act_ref[...], g_ref[...], ((0,), (0,))).astype(BF)
    for low in range(2):
        for high in range(2):
            chip = sc[1] ^ (low + 2 * high)
            rows_at = pl.ds(pl.multiple_of(chip * LANES, LANES), LANES)
            for b in range(width // WIDE):
                give(low, high, 0, b * LANES, grad_s[rows_at, b * WIDE : (b + 1) * WIDE])
    span = n_pair * LANES
    grad_s[:, 0:span] = dot(h_ref[...], dup_ref[...], ((0,), (0,))).astype(BF)
    for low in range(2):
        for high in range(2):
            chip = sc[1] ^ (low + 2 * high)
            rows_at = pl.ds(pl.multiple_of(chip * up_rows, 64), up_rows)
            for b in range(span // WIDE):
                give(low, high, 1, b * up_rows, grad_s[rows_at, b * WIDE : (b + 1) * WIDE])


def ffn_gradients(sc, h_two, g_two, w_up, w_down, n, part, n_pair):
    rows, width = h_two.shape
    span = n_pair * LANES
    block = width // WIDE * LANES
    if n == 0:
        outs = [shape((2, 2 * block, WIDE), BF)] * 2
    else:
        outs = [shape((2, 2, 2, block, WIDE), BF)]
    return call(
        functools.partial(ffn_kernel, n=n, part=part, n_pair=n_pair),
        "ffn_gradients",
        [shape((rows, span), BF)] * 2 + outs,
        [VM, VM, HBM, HBM],
        [VM] * (2 + len(outs)),
        [
            pltpu.VMEM((width, span), BF),
            pltpu.VMEM((span, width), BF),
            pltpu.VMEM((width, width), BF),
            pltpu.SemaphoreType.DMA((2,)),
        ],
        56,
    )(sc, h_two, g_two, w_up, w_down)


def late_kernel(sc, h_ref, dq0, dq1, mix0, mix1, got0, got1, g_ref, send_ref, keep_ref, mix_s, dq_s, both_s, *, n_pair):
    half = mix0.shape[0]
    rows = mix0.shape[1]
    width = 2 * half
    own = pl.multiple_of(sc[0] * half, 128)
    other = pl.multiple_of((1 - sc[0]) * half, 128)
    mix_s[pl.ds(own, half), 0:rows] = mix0[...]
    mix_s[pl.ds(own, half), rows : 2 * rows] = mix1[...]
    mix_s[pl.ds(other, half), 0:rows] = got1[...]
    mix_s[pl.ds(other, half), rows : 2 * rows] = got0[...]
    dq_s[:, 0:rows] = dq0[...]
    dq_s[:, rows : 2 * rows] = dq1[...]
    both_s[:, 0:half] = dot(h_ref[...], dq_s[...], ((0,), (1,))).astype(BF)
    both_s[:, half:width] = dot(mix_s[...], g_ref[:, pl.ds(own, half)]).astype(BF)
    block = width // n_pair
    quarter = keep_ref.shape[3]
    unit = 48
    for low in range(2):
        for high in range(2):
            chip = sc[1] ^ (low + 2 * high)
            for first in range(2):
                ref = send_ref if first else keep_ref
                for second in range(2):
                    part = 2 * (first ^ sc[2]) + (second ^ sc[3])
                    for r in range(quarter // unit):
                        at = part * quarter + r * unit
                        col, row = at // block, at % block
                        source = pl.ds(pl.multiple_of(chip * block + row, 16), unit)
                        lane = pl.ds(pl.multiple_of(col * WIDE, WIDE), WIDE)
                        ref[second, low, high, r * unit : (r + 1) * unit, :] = both_s[source, lane]


def late_gradients(sc, h_one, dqs, mixes, gots, g_two, n_pair):
    half = dqs[0].shape[0]
    width = 2 * half
    rows = h_one.shape[0]
    quarter = width // n_pair * (width // WIDE) // 4
    return call(
        functools.partial(late_kernel, n_pair=n_pair),
        "late_gradients",
        [shape((2, 2, 2, quarter, WIDE), BF)] * 2,
        [VM] * 8,
        [VM] * 2,
        [
            pltpu.VMEM((width, rows), BF),
            pltpu.VMEM((half, rows), BF),
            pltpu.VMEM((width, width), BF),
        ],
        16,
    )(sc, h_one, *dqs, *mixes, *gots, g_two)


def out_kernel(sc, a0, a1, a2, mix0, mix1, x_ref, w_down, w_out, own_ref, send_ref, down_s, out_s, sems, *, part, n_pair):
    half = out_s.shape[0]
    rows = x_ref.shape[0]
    span = n_pair * LANES
    copies = [
        pltpu.make_async_copy(
            w_out.at[pl.ds(pl.multiple_of(sc[0] * half, 128), half), :], out_s, sems.at[0]
        )
    ]
    for n in range(3):
        copies += hidden_copies(
            sc, piece_of(sc, n), None, w_down, None, down_s.at[n], sems, part, n_pair
        )
    for copy in copies:
        copy.start()
    for copy in copies:
        copy.wait()
    for n, mix in enumerate((mix0, mix1)):
        here = slice(n * rows, (n + 1) * rows)
        total = dot(mix[...], out_s[...], ((0,), (0,)))
        for k, act in enumerate((a0, a1, a2)):
            total = total + dot(act[here, :], down_s[k])
        if n == 0:
            own_ref[...] = total + x_ref[...].astype(F32)
        else:
            send_ref[...] = total.astype(BF)


def hat_kernel(sc, d0, d1, d2, dq0, dq1, xo, xt, gains, w_up, w_query, own_ref, send_ref, sum_ref, up_s, query_s, sems, *, part, n_pair):
    half = query_s.shape[1]
    rows, width = xo.shape
    copies = [
        pltpu.make_async_copy(
            w_query.at[:, pl.ds(pl.multiple_of(sc[0] * half, 128), half)], query_s, sems.at[1]
        )
    ]
    for n in range(3):
        copies += hidden_copies(
            sc, piece_of(sc, n), w_up, None, up_s.at[n], None, sems, part, n_pair
        )
    for copy in copies:
        copy.start()
    for copy in copies:
        copy.wait()
    gain_one, gain_two = gains[0:1, :].astype(F32), gains[2:3, :].astype(F32)
    sums = [jnp.zeros((1, width), F32)] * 4
    for n, (x, dq) in enumerate(((xo, dq0), (xt, dq1))):
        here = slice(n * rows, (n + 1) * rows)
        two = dot(d0[here, :], up_s[0], ((1,), (1,)))
        two = two + dot(d1[here, :], up_s[1], ((1,), (1,)))
        two = two + dot(d2[here, :], up_s[2], ((1,), (1,)))
        one = dot(dq[...], query_s[...], ((0,), (1,)))
        hat, unused = normed(x[...].astype(F32))
        for k, value in enumerate((one * hat, one, two * hat, two)):
            sums[k] = sums[k] + jnp.sum(value, 0, keepdims=True)
        total = one * gain_one + two * gain_two
        if n == 0:
            own_ref[...] = total
        else:
            send_ref[...] = total.astype(BF)
    sum_ref[...] = jnp.concatenate(sums + [jnp.zeros((4, width), F32)], 0)


def last_kernel(sc, dkv_a, dkv_b, cos_ref, sin_ref, w_kv, h_ref, x_ref, gains, hat_own, hat_got, sum_ref, g_ref, grad_ref, send_ref, keep_ref, *, n_pair):
    rows, width = x_ref.shape
    dkv = (dkv_a[...].astype(F32) + dkv_b[...].astype(F32)).T
    low_t = turn(dkv, cos_ref[:, 0:rows], -sin_ref[:, 0:rows]).astype(BF)
    low = low_t.T
    weight = dot(low_t, h_ref[0:rows, :]).T.astype(BF)
    d_kv = dot(low, w_kv[...], ((1,), (1,)))
    hat, scale = normed(x_ref[...].astype(F32))
    gain = gains[0:1, :].astype(F32)
    total = hat_own[...] + hat_got[...].astype(F32) + d_kv * gain
    grad_ref[...] = g_ref[...].astype(F32) + scale * (
        total
        - jnp.mean(total, -1, keepdims=True)
        - hat * jnp.mean(total * hat, -1, keepdims=True)
    )
    sums = jnp.concatenate(
        [
            sum_ref[0:1, :] + jnp.sum(d_kv * hat, 0, keepdims=True),
            sum_ref[1:2, :] + jnp.sum(d_kv, 0, keepdims=True),
            sum_ref[2:4, :],
            jnp.zeros((4, width), F32),
        ],
        0,
    ).astype(BF)
    part = width // (2 * n_pair)
    lanes = weight.shape[1]
    for chip in range(n_pair):
        rel = chip ^ sc[1]
        low_bit, high_bit = rel % 2, rel // 2
        blocks = []
        for core in range(2):
            at = (2 * chip + core) * part
            piece = weight[at : at + part, :]
            blocks.append(jnp.concatenate([piece[: part // 2], piece[part // 2 :]], 1))
            row = sums[:, at : at + part]
            blocks.append(jnp.concatenate([row, jnp.zeros((8, 2 * lanes - part), BF)], 1))
        block = jnp.concatenate(blocks, 0)

        @pl.when(low_bit == 1)
        def _():
            send_ref[high_bit] = block

        @pl.when(low_bit == 0)
        def _():
            keep_ref[high_bit] = block


def down_kernel(sc, a_send, a_got, send_ref, got_ref, out_ref, *, width):
    block = width // WIDE * LANES
    for k in range(3):
        for b in range(width // WIDE):
            here = slice(b * LANES, (b + 1) * LANES)
            if k == 0:
                value = a_send[here, :].astype(F32) + a_got[here, :].astype(F32)
            else:
                at = pl.ds(pl.multiple_of(sc[3] * block + b * LANES, LANES), LANES)
                mine = send_ref[at, :].astype(F32)
                value = jnp.where(sc[2] == k - 1, mine, got_ref[at, :].astype(F32))
            out_ref[k * LANES : (k + 1) * LANES, b * WIDE : (b + 1) * WIDE] = value


def up_block(sc, k, b, parity, a_send, a_got, b_send, b_got, width, part):
    block = width // WIDE * LANES
    off = b * 2 * part + parity * part
    if k == 0:
        at = pl.ds(pl.multiple_of(block + off, 32), part)
        return a_send[at, :].astype(F32) + a_got[at, :].astype(F32)
    at = pl.ds(pl.multiple_of((1 - sc[3]) * block + off, 32), part)
    return jnp.where(
        sc[2] == k - 1, b_send[at, :].astype(F32), b_got[at, :].astype(F32)
    )


def late_block(sc, b, parity, send, got, part, quarter):
    pieces = []
    for r in range(2):
        at = b * 2 * part + parity * part + r * (part // 2)
        first, second = at // (2 * quarter), at // quarter % 2
        rel = (second ^ sc[3]) * quarter + at % quarter
        source = pl.ds(pl.multiple_of(rel, 16), part // 2)
        pieces.append(
            jnp.where(
                first == sc[2], send[source, :].astype(F32), got[source, :].astype(F32)
            )
        )
    return jnp.concatenate(pieces, 0)


def pack_kernel(sc, a_send, a_got, b_send, b_got, last_send, last_got, out_ref, own_ref, *, width, part, quarter):
    for which, ref in ((1, out_ref), (0, own_ref)):
        parity = sc[0] if which == 0 else 1 - sc[0]
        at = 0
        for k in range(3):
            for b in range(2):
                ref[at : at + part, :] = up_block(
                    sc, k, b, parity, a_send, a_got, b_send, b_got, width, part
                ).astype(BF)
                at += part
        for b in range(width // WIDE):
            ref[at : at + part, :] = late_block(
                sc, b, parity, last_send, last_got, part, quarter
            ).astype(BF)
            at += part
        few = (last_send.shape[0] - 2 * quarter) // 2
        source = pl.ds(pl.multiple_of(2 * quarter + parity * few, 8), few)
        ref[at : at + few, :] = (
            last_send[source, :].astype(F32) + last_got[source, :].astype(F32)
        ).astype(BF)


def final_kernel(sc, own_ref, got_ref, up_ref, query_ref, proj_ref, kv_ref, norm_ref, *, part, n_pair):
    part_hidden = up_ref.shape[1] // (2 * n_pair)
    half = query_ref.shape[1] // 2
    for which, ref in enumerate((own_ref, got_ref)):
        core = sc[0] if which == 0 else 1 - sc[0]
        at = 0
        for k in range(3):
            for j in range(n_pair):
                lane = (2 * j + core) * part_hidden + k * LANES
                rows = slice((2 * k + j // 2) * part, (2 * k + j // 2 + 1) * part)
                cols = slice(j % 2 * LANES, (j % 2 + 1) * LANES)
                up_ref[:, pl.ds(pl.multiple_of(lane, LANES), LANES)] = ref[rows, cols].astype(F32)
        base = 6 * part
        for n in range(2 * half // LANES):
            rows = slice(base + n // 2 * part, base + (n // 2 + 1) * part)
            value = ref[rows, n % 2 * LANES : (n % 2 + 1) * LANES].astype(F32)
            to, m = (query_ref, n) if n < half // LANES else (proj_ref, n - half // LANES)
            to[:, pl.ds(pl.multiple_of(core * half + m * LANES, LANES), LANES)] = value
    base = 9 * part
    few = own_ref[base:, :].astype(F32) + got_ref[base:, :].astype(F32)
    kv_ref[0 : part // 2, :] = few[0 : part // 2, 0:LANES]
    kv_ref[part // 2 : part, :] = few[0 : part // 2, LANES:WIDE]
    norm_ref[...] = few[part // 2 : part // 2 + 8, :]


class Links:
    def __init__(self, n_grp, n_ctx):
        self.n_grp, self.n_ctx, self.n_pair = n_grp, n_ctx, n_ctx // 2
        self.small = (n_grp, n_ctx) == (4, 8)
        self.ctx = lax.axis_index("ctx")
        self.grp = lax.axis_index("grp")
        self.core = self.ctx % 2
        self.chip = self.ctx // 2
        self.groups = [[2 * z + c for z in range(self.n_pair)] for c in range(2)]

    def swap(self, value):
        return lax.ppermute(value, "ctx", [(i, i ^ 1) for i in range(self.n_ctx)])

    def permute(self, value, target):
        pairs = []
        for g in range(self.n_grp):
            for i in range(self.n_ctx):
                y, x, z, c = target(g // 2, g % 2, i // 2, i % 2)
                pairs.append((g * self.n_ctx + i, (2 * y + x) * self.n_ctx + 2 * z + c))
        return lax.ppermute(value, ("grp", "ctx"), pairs)

    def cross(self, value, stage):
        return self.permute(
            value, lambda y, x, z, c: (y, 1 - x, z, c) if c == stage else (1 - y, x, z, c)
        )

    def bit(self, stage):
        y, x = self.grp // 2, self.grp % 2
        return jnp.where(self.core == stage, x, y)

    def flip(self, value, bit):
        return self.permute(value, lambda y, x, z, c: (y, x, z ^ bit, c))

    def reduce(self, parts):
        moved = lax.all_to_all(parts, "ctx", 0, 0, axis_index_groups=self.groups)
        return lax.psum(jnp.sum(moved.astype(F32), 0).astype(BF), "grp")


def add(keep, got):
    return (keep.astype(F32) + got.astype(F32)).astype(BF)


def low(value):
    return value.astype(BF)


def shards_small(
    layer_input, block_table, ln1_gain, ln1_bias, ln2_gain, ln2_bias,
    w_query, w_keyval, w_out, w_up, w_down, cotangent, *, n_grp, n_ctx,
):
    links = Links(n_grp, n_ctx)
    core, chip, n_pair = links.core, links.chip, links.n_pair
    rows, width = layer_input.shape
    lanes = w_keyval.shape[1]
    size = lanes // 2
    hidden = w_up.shape[1]
    group_len = block_table.shape[1] * BLK
    part, part_hidden = width // n_ctx, hidden // n_ctx
    half = width // 2
    per_chip = 2 * rows // BLK
    table = block_table[0]
    sc = jnp.stack([core, chip, links.bit(0), links.bit(1)]).astype(jnp.int32)
    gains = jnp.concatenate([ln1_gain, ln1_bias, ln2_gain, ln2_bias]).reshape(4, width)

    x_other, g_other = links.swap(layer_input), links.swap(cotangent)
    own_slots = lax.dynamic_slice_in_dim(table, chip * per_chip, per_chip).reshape(2, -1)
    slots = jnp.concatenate([own_slots[core], own_slots[1 - core]])
    canon = (slots[:, None] * BLK + jnp.arange(BLK, dtype=jnp.int32)[None, :]).reshape(2 * rows)
    prompt_len = group_len // 2
    cont_span = min(CONT, prompt_len)
    position = jnp.where(
        canon < prompt_len, canon, prompt_len + (canon - prompt_len) % cont_span
    )
    cosine, sine = rope_tables(position)

    h_one, h_two, g_two, kv_low = call(
        prologue_kernel,
        "prologue",
        [shape((2 * rows, width), BF)] * 3 + [shape((2 * rows, lanes), BF)],
        [HBM] * 4 + [VM, HBM, VM, VM],
        [VM] * 4,
        [
            pltpu.VMEM((rows, width), BF),
            pltpu.VMEM((rows, width), BF),
            pltpu.VMEM((width, lanes), BF),
            pltpu.SemaphoreType.DMA((5,)),
        ],
        56,
    )(sc, layer_input, x_other, cotangent, g_other, gains, w_keyval, cosine, sine)

    kv_got = links.flip(kv_low, 1)
    ffn = functools.partial(
        ffn_gradients, sc, w_up=w_up, w_down=w_down, part=part_hidden, n_pair=n_pair
    )
    act_1, dup_1, b_send = ffn(h_two, g_two, n=1)
    b_send, kv_got = meet(b_send, kv_got)
    kv_near = jnp.concatenate([kv_low, kv_got], 0)
    kv_far = links.flip(kv_near, 2)
    b_got = links.cross(b_send, 0)
    act_2, dup_2, b_keep = ffn(tie(h_two, b_send, kv_near), g_two, n=2)
    act_0, dup_0, a_send, a_keep = ffn(tie(h_two, b_keep), g_two, n=0)
    a_send, kv_far = meet(a_send, kv_far)
    a_got = links.flip(a_send, 1)

    q_t, do_t = call(
        functools.partial(project_kernel, size=size),
        "project",
        [shape((half, 2 * rows), BF), shape((half, 2 * rows), F32)],
        [VM] * 4 + [HBM] * 2,
        [VM] * 2,
        [
            pltpu.VMEM((width, half), BF),
            pltpu.VMEM((half, width), BF),
            pltpu.SemaphoreType.DMA((2,)),
        ],
        16,
    )(sc, tie(h_one, a_send), g_two, cosine, sine, w_query, w_out)
    q_t, b_got = meet(q_t, b_got)
    b_send = add(b_keep[1], b_got[1])
    b_got_2 = links.cross(b_send, 1)

    place = jnp.stack([chip * per_chip, core * (rows // BLK), chip, 0 * chip]).astype(jnp.int32)
    count = rows // BLK
    attend = functools.partial(
        attention, table, place, do_t=do_t, cosine=cosine, sine=sine, kvs=(kv_near, kv_far),
        count=count, per_chip=per_chip, split=True,
    )
    mix_0, dq_0, carried = attend(
        q_t=tie(q_t, b_send), carried=None, start=0, last_call=False
    )
    carried, a_got, b_got_2, b_got = meet(carried, a_got, b_got_2, b_got)
    mix_0_got = links.swap(mix_0)
    b_keep = add(b_keep[0], b_got[0])
    b_send = add(b_keep[1], b_got_2[1])
    b_got_3 = links.flip(b_send, 1)
    a_send = add(a_keep[1], tie(a_got, b_send)[1])
    a_got_2 = links.flip(a_send, 2)
    mix_1, dq_1, dkv_send, dkv_keep = attend(
        q_t=tie(q_t, a_send, b_send, carried), carried=carried, start=count, last_call=True
    )
    mix_1, dkv_send, mix_0_got, a_got_2 = meet(mix_1, dkv_send, mix_0_got, a_got_2)
    dkv_got = links.swap(dkv_send)
    mix_1_got = links.swap(mix_1)
    dkv_got, mix_1_got = meet(dkv_got, mix_1_got)
    dkv_send = add(dkv_keep[1], dkv_got[1])
    dkv_got_2 = links.flip(dkv_send, 1)
    late_send, late_keep = late_gradients(
        sc, tie(h_one, dkv_send), (dq_0, dq_1), (mix_0, mix_1), (mix_0_got, mix_1_got), g_two, n_pair
    )
    late_send, dkv_got, dkv_got_2 = meet(late_send, dkv_got, dkv_got_2)
    late_got = links.cross(late_send, 0)
    dkv_keep = add(dkv_keep[0], dkv_got[0])
    dkv_send = add(dkv_keep[1], dkv_got_2[1])
    dkv_got_3 = links.flip(dkv_send, 2)
    b_got_3 = links.flip(tie(b_send, dkv_send), 1)

    w_specs = [HBM] * 2
    hat_own, hat_send, sums = call(
        functools.partial(hat_kernel, part=part_hidden, n_pair=n_pair),
        "norms",
        [shape((rows, width), F32), shape((rows, width), BF), shape((8, width), F32)],
        [VM] * 8 + w_specs,
        [VM] * 3,
        [
            pltpu.VMEM((3, width, n_pair * LANES), BF),
            pltpu.VMEM((width, half), BF),
            pltpu.SemaphoreType.DMA((2,)),
        ],
        56,
    )(
        sc, dup_0, dup_1, tie(dup_2, late_send, dkv_send), dq_0, dq_1, layer_input, x_other, gains,
        w_up, w_query,
    )
    hat_send, dkv_got_2, dkv_got_3, late_got = meet(hat_send, dkv_got_2, dkv_got_3, late_got)
    hat_got = links.swap(hat_send)
    dkv_keep = add(dkv_keep[0], dkv_got_2[0])
    late_send = add(late_keep[1], late_got[1])
    late_got_2 = links.cross(late_send, 1)
    late_send, hat_got = meet(late_send, hat_got)

    few = part // 2 + 8
    in_grad, few_send, few_keep = call(
        functools.partial(last_kernel, n_pair=n_pair),
        "last",
        [shape((rows, width), F32)] + [shape((2, 2 * few, 2 * lanes), BF)] * 2,
        [VM] * 12,
        [VM] * 3,
        [],
        16,
    )(
        sc, dkv_keep, tie(dkv_got_3, late_send), cosine, sine, w_keyval, h_one, layer_input,
        gains, hat_own, hat_got, sums, cotangent,
    )
    few_send, late_got, late_got_2, b_got_2, b_got_3 = meet(
        few_send, late_got, late_got_2, b_got_2, b_got_3
    )
    late_keep = add(late_keep[0], late_got[0])
    quarter = late_keep.shape[2]
    last_send = jnp.concatenate([add(late_keep[1], late_got_2[1]), few_send], 1)
    last_got = links.flip(last_send, 1)
    b_keep = add(b_keep[0], b_got_2[0])
    b_send = add(b_keep[1], b_got_3[1])
    b_got_4 = links.flip(b_send, 2)
    a_sum = add(add(a_keep[0], a_got[0]), a_got_2)
    a_got = links.cross(a_sum, 1)

    out_own, out_send = call(
        functools.partial(out_kernel, part=part_hidden, n_pair=n_pair),
        "outputs",
        [shape((rows, width), F32), shape((rows, width), BF)],
        [VM] * 6 + w_specs,
        [VM] * 2,
        [
            pltpu.VMEM((3, n_pair * LANES, width), BF),
            pltpu.VMEM((half, width), BF),
            pltpu.SemaphoreType.DMA((2,)),
        ],
        56,
    )(
        sc, act_0, act_1, tie(act_2, last_send, b_send, a_sum), mix_0, mix_1,
        layer_input, w_down, w_out,
    )
    out_send, last_got, a_got = meet(out_send, last_got, a_got)
    out_got = links.swap(out_send)
    last_keep = jnp.concatenate([add(late_keep[0], late_got_2[0]), few_keep], 1)
    last_send = add(last_keep[1], last_got[1])
    last_got_2 = links.flip(last_send, 2)
    a_sum = add(a_sum, a_got)
    a_got = links.cross(a_sum, 0)
    out_got, b_got_4 = meet(out_got, b_got_3, b_got_4, a_sum, last_send)[::2][:2]
    layer_output = low(out_own + out_got.astype(F32))
    b_sum = add(add(b_keep[0], b_got_3[0]), b_got_4)
    b_got = links.cross(b_sum, 1)
    last_keep = add(last_keep[0], last_got[0])
    b_got, layer_output = meet(b_got, layer_output)
    b_sum = jnp.concatenate([b_sum, b_got], 0)
    b_got = links.cross(b_sum, 0)
    last_got_2 = meet(last_got_2, b_sum)[0]
    last = add(last_keep, last_got_2)
    last_got = links.cross(last, 1)
    last = jnp.concatenate(
        [last[:quarter], last_got[:quarter], add(last[quarter:], last_got[quarter:])], 0
    )
    last_got = links.cross(last, 0)
    total_down = call(
        functools.partial(down_kernel, width=width),
        "down", shape((part_hidden, width), F32), [VM] * 4, VM, [], 8,
    )(sc, tie(a_sum, last), a_got, b_sum, b_got)
    total_down, last_got = meet(total_down, last_got)
    size_out = 9 * part + few
    other, own = call(
        functools.partial(pack_kernel, width=width, part=part, quarter=quarter),
        "pack", [shape((size_out, WIDE), BF)] * 2, [VM] * 6, [VM] * 2, [], 8,
    )(sc, a_sum, a_got, b_sum, b_got, last, last_got)
    got = links.swap(other)
    total_up, total_query, total_out, total_kv, norm = call(
        functools.partial(final_kernel, part=part, n_pair=n_pair),
        "final",
        [
            shape((part, hidden), F32),
            shape((part, width), F32),
            shape((part, width), F32),
            shape((part, lanes), F32),
            shape((8, WIDE), F32),
        ],
        [VM] * 2,
        [VM] * 5,
        [],
        8,
    )(sc, own, got)
    norms = [norm[n, :part] for n in range(4)]
    return (layer_output, in_grad, *norms, total_query, total_kv, total_out, total_up, total_down)


def rotate_rows(values, cosine, sine):
    return turn(values.T, cosine, sine).T


def shards(
    layer_input, block_table, ln1_gain, ln1_bias, ln2_gain, ln2_bias,
    w_query, w_keyval, w_out, w_up, w_down, cotangent, *, n_grp, n_ctx,
):
    links = Links(n_grp, n_ctx)
    core, chip, n_pair = links.core, links.chip, links.n_pair
    rows, width = layer_input.shape
    size = w_keyval.shape[1] // 2
    hidden = w_up.shape[1]
    group_len = block_table.shape[1] * BLK
    part_rows, part_hidden = width // n_ctx, hidden // n_ctx
    half_width, half_hidden = width // 2, hidden // 2
    per_chip = 2 * rows // BLK
    table = block_table[0]

    def both(own, other):
        return jnp.concatenate(
            [jnp.where(core == 0, own, other), jnp.where(core == 0, other, own)], 0
        )

    def mine(value, own_core):
        return lax.dynamic_slice_in_dim(value, own_core * rows, rows, 0)

    x_two = both(layer_input, links.swap(layer_input))
    g_two = both(cotangent, links.swap(cotangent))
    canon = (
        lax.dynamic_slice_in_dim(table, chip * per_chip, per_chip)[:, None] * BLK
        + jnp.arange(BLK, dtype=jnp.int32)[None, :]
    ).reshape(2 * rows)
    prompt_len = group_len // 2
    cont_span = min(CONT, prompt_len)
    position = jnp.where(
        canon < prompt_len, canon, prompt_len + (canon - prompt_len) % cont_span
    )
    cosine, sine = rope_tables(position)
    gain_one, gain_two = ln1_gain.astype(F32), ln2_gain.astype(F32)
    hat, scale = normed(x_two.astype(F32))
    h_one = low(hat * gain_one + ln1_bias.astype(F32))
    h_two = low(hat * gain_two + ln2_bias.astype(F32))
    kv_raw = dot(h_one, w_keyval)
    kv_low = low(
        jnp.concatenate([rotate_rows(kv_raw[:, :size], cosine, sine), kv_raw[:, size:]], -1)
    )
    kv_all = lax.all_gather(kv_low, "ctx", axis=0, axis_index_groups=links.groups, tiled=True)

    up_half = lax.dynamic_index_in_dim(
        w_up.reshape(width, n_pair, 2, part_hidden), core, 2, False
    ).reshape(width, half_hidden)
    down_half = lax.dynamic_index_in_dim(
        w_down.reshape(n_pair, 2, part_hidden, width), core, 1, False
    ).reshape(half_hidden, width)
    act, slope = gelu_parts(dot(h_two, up_half))
    act = low(act)
    grad_down = low(dot(act, g_two, ((0,), (0,))))
    total_down = links.reduce(grad_down.reshape(n_pair, part_hidden, width))
    grad_up = low(dot(g_two, down_half, ((1,), (1,))) * slope)
    grad_up_w = low(dot(h_two, grad_up, ((0,), (0,))))
    total_up = links.reduce(grad_up_w.reshape(n_pair, 2 * part_rows, half_hidden))

    query_half = lax.dynamic_slice_in_dim(w_query, core * half_width, half_width, 1)
    out_half = lax.dynamic_slice_in_dim(w_out, core * half_width, half_width, 0)
    q_raw = dot(query_half, h_one, ((0,), (1,))) * (0.125 * LOG2E)
    q_t = low(
        jax.vmap(turn, (0, None, None))(q_raw.reshape(-1, size, 2 * rows), cosine, sine)
    ).reshape(half_width, 2 * rows)
    do_t = dot(out_half, g_two, ((1,), (1,)))
    place = jnp.stack([chip * per_chip, 0 * chip, 0 * chip, 0 * chip]).astype(jnp.int32)
    mix_t, dq_t, dkv_part = attention(
        table, place, q_t, do_t, cosine, sine, (kv_all,), None, 0, per_chip, per_chip, True, False
    )

    dkv_part = dkv_part.reshape(n_pair, 2, rows, 2 * size)
    dkv_own = lax.dynamic_index_in_dim(dkv_part, core, 1, False)
    dkv_got = links.swap(lax.dynamic_index_in_dim(dkv_part, 1 - core, 1, False))
    moved = lax.all_to_all(
        add(dkv_own, dkv_got), "ctx", 0, 0, axis_index_groups=links.groups
    )
    dkv = jnp.sum(moved.astype(F32), 0)
    cos_own = lax.dynamic_slice_in_dim(cosine, core * rows, rows, 1)
    sin_own = lax.dynamic_slice_in_dim(sine, core * rows, rows, 1)
    dkv_low = low(
        jnp.concatenate([rotate_rows(dkv[:, :size], cos_own, -sin_own), dkv[:, size:]], -1)
    )

    mix_got = links.swap(mix_t)
    mix_all = jnp.concatenate(
        [jnp.where(core == 0, mix_t, mix_got), jnp.where(core == 0, mix_got, mix_t)], 0
    )
    g_half = lax.dynamic_slice_in_dim(g_two, core * half_width, half_width, 1)
    grad_q_w = low(dot(h_one, dq_t, ((0,), (1,))))
    grad_out_w = low(dot(mix_all, g_half))
    late = jnp.concatenate([grad_q_w, grad_out_w], 1).reshape(n_pair, 2 * part_rows, width)
    total_late = links.reduce(late)

    out_part = dot(act, down_half) + dot(mix_t, out_half, ((0,), (0,)))
    out_got = links.swap(low(mine(out_part, 1 - core)))
    layer_output = low(layer_input.astype(F32) + mine(out_part, core) + out_got.astype(F32))

    d_two = dot(grad_up, up_half, ((1,), (1,)))
    d_one = dot(dq_t, query_half, ((0,), (1,)))
    d_kv = dot(dkv_low, w_keyval, ((1,), (1,)))
    row_core = lax.broadcasted_iota(jnp.int32, (2 * rows, 1), 0) // rows
    d_one = d_one + jnp.where(row_core == core, jnp.concatenate([d_kv, d_kv], 0), 0.0)
    sums = jnp.stack([jnp.sum(v, 0) for v in (d_one * hat, d_one, d_two * hat, d_two)])
    d_hat = d_one * gain_one + d_two * gain_two
    hat_got = links.swap(low(mine(d_hat, 1 - core)))
    d_hat = mine(d_hat, core) + hat_got.astype(F32)
    hat_own = mine(hat, core)
    in_grad = cotangent.astype(F32) + mine(scale, core) * (
        d_hat
        - jnp.mean(d_hat, -1, keepdims=True)
        - hat_own * jnp.mean(d_hat * hat_own, -1, keepdims=True)
    )

    grad_kv_w = dot(mine(h_one, core), dkv_low, ((0,), (0,)))
    sum_rows = sums.reshape(4, n_pair, 2, part_rows).transpose(1, 2, 0, 3)
    sum_rows = jnp.pad(sum_rows, ((0, 0), (0, 0), (0, 0), (0, 2 * size - part_rows)))
    few = jnp.concatenate([grad_kv_w.reshape(n_pair, 2, part_rows, 2 * size), sum_rows], 2)
    few = links.reduce(low(few).reshape(n_pair, 2 * (part_rows + 4), 2 * size))
    few = few.reshape(2, part_rows + 4, 2 * size)
    few_got = links.swap(lax.dynamic_index_in_dim(few, 1 - core, 0, False))
    few = lax.dynamic_index_in_dim(few, core, 0, False).astype(F32) + few_got.astype(F32)

    halves = jnp.concatenate(
        [total_up.reshape(2, part_rows, half_hidden), total_late.reshape(2, part_rows, width)], -1
    )
    own = lax.dynamic_index_in_dim(halves, core, 0, False)
    got = links.swap(lax.dynamic_index_in_dim(halves, 1 - core, 0, False))
    sides = jnp.stack([jnp.where(core == 0, own, got), jnp.where(core == 0, got, own)]).astype(F32)
    ups = sides[:, :, :half_hidden].reshape(2, part_rows, n_pair, part_hidden)
    total_up = ups.transpose(1, 2, 0, 3).reshape(part_rows, hidden)
    lates = sides[:, :, half_hidden:]
    total_query = lates[:, :, :half_width].transpose(1, 0, 2).reshape(part_rows, width)
    total_out = lates[:, :, half_width:].transpose(1, 0, 2).reshape(part_rows, width)
    norms = [few[part_rows + n, :part_rows] for n in range(4)]
    total_kv = few[:part_rows]
    total_down = total_down.astype(F32)
    return (layer_output, in_grad, *norms, total_query, total_kv, total_out, total_up, total_down)


def solution(mesh):
    n_grp, n_ctx = mesh.shape["grp"], mesh.shape["ctx"]
    body = shards_small if (n_grp, n_ctx) == (4, 8) else shards
    return jax.shard_map(
        functools.partial(body, n_grp=n_grp, n_ctx=n_ctx),
        mesh=mesh,
        in_specs=(P(("grp", "ctx"), None), P("grp", None))
        + (P(),) * 9
        + (P(("grp", "ctx"), None),),
        out_specs=(P(("grp", "ctx"), None),) * 2 + (P("ctx"),) * 4 + (P("ctx", None),) * 5,
        check_vma=False,
    )
```

```python
import functools

import jax
import jax.numpy as jnp
from jax import lax
from jax.experimental import pallas as pl
from jax.experimental.pallas import tpu as pltpu
from jax.sharding import PartitionSpec as P

ROT = 16
HALF = ROT // 2
BLK = 128
CONT = 1024
TILE = 256
LANES = 128
WIDE = 256
EPS = 1e-05
LOG2E = 1.4426950408889634
LN2 = 0.6931471805599453
BF = jnp.bfloat16
F32 = jnp.float32
MIB = 1024 * 1024
VM = pl.BlockSpec(memory_space=pltpu.VMEM)
HBM = pl.BlockSpec(memory_space=pltpu.HBM)


def dot(left, right, dims=((1,), (0,))):
    return lax.dot_general(left, right, (dims, ((), ())), preferred_element_type=F32)


def shape(dims, dtype):
    return jax.ShapeDtypeStruct(dims, dtype)


def tie(value, *others):
    return lax.optimization_barrier((value,) + others)[0]


def meet(*values):
    return lax.optimization_barrier(values)


def rope_tables(position):
    inverse = 10000.0 ** (-(2.0 * jnp.arange(HALF, dtype=F32)) / ROT)
    angles = inverse[:, None] * position.astype(F32)[None, :]
    return (jnp.cos(angles), jnp.sin(angles))


def turn(values, cosine, sine):
    first, second = values[:HALF], values[HALF:ROT]
    return jnp.concatenate(
        [first * cosine - second * sine, second * cosine + first * sine, values[ROT:]], 0
    )


def normed(values):
    shifted = values - jnp.mean(values, -1, keepdims=True)
    scale = lax.rsqrt(jnp.mean(shifted * shifted, -1, keepdims=True) + EPS)
    return (shifted * scale, scale)


def gelu_parts(value):
    cdf = 0.5 * (1.0 + lax.erf(value * 0.7071067811865476))
    pdf = jnp.exp(-0.5 * value * value) * 0.3989422804014327
    return value * cdf, cdf + value * pdf


def call(kernel, name, outs, specs, out_specs, scratch, limit, flops=1000):
    made = pl.pallas_call(
        kernel,
        out_shape=outs,
        grid_spec=pltpu.PrefetchScalarGridSpec(
            num_scalar_prefetch=1, in_specs=specs, out_specs=out_specs, scratch_shapes=scratch
        ),
        compiler_params=pltpu.CompilerParams(vmem_limit_bytes=limit * MIB),
        cost_estimate=pl.CostEstimate(flops=flops, bytes_accessed=flops, transcendentals=0),
        name=name,
    )

    def placed(scalars, *values):
        return made(
            scalars,
            *(
                pltpu.with_memory_space_constraint(v, pltpu.HBM) if spec is HBM else v
                for v, spec in zip(values, specs)
            ),
        )

    return placed


def attn_kernel(
    table, place, *refs, blocks, heads, size, n_kv, per_chip, start, last_call, first_call
):
    q_ref, do_ref, cos_ref, sin_ref = refs[:4]
    kv_refs = refs[4 : 4 + n_kv]
    refs = refs[4 + n_kv :]
    if not first_call:
        sum_ref, refs = refs[0], refs[1:]
    mix_ref, dq_ref = refs[:2]
    outs = refs[2:-11]
    kv_c, kv_t, s_scr, p_scr, rq, rd, rqt, rdt, o_acc, dq_acc, dkv_acc = refs[-11:]
    step, group = pl.program_id(0), pl.program_id(1)
    lanes = heads * BLK
    prompt_blocks = blocks // 2
    prompt_tiles = prompt_blocks * BLK // TILE
    cont_blocks = min(CONT, prompt_blocks * BLK) // BLK

    def block_rows(block):
        return pl.ds(pl.multiple_of(block * BLK, BLK), BLK)

    @pl.when((step == 0) & (group == 0))
    def _():
        ones = jnp.ones((16, BLK), BF)
        share = blocks // n_kv

        for n, kv_ref in enumerate(kv_refs):

            def place_block(at, carry, n=n, kv_ref=kv_ref):
                spot = n * share + at
                block = table[((spot // per_chip) ^ place[2]) * per_chip + spot % per_chip]
                rows = kv_ref[block_rows(at), :]
                kv_c[block_rows(block), :] = rows
                turned = jnp.concatenate([rows.T, ones], 0)

                @pl.when(block % 2 == 0)
                def _():
                    kv_t[block // 2, :, 0:BLK] = turned

                @pl.when(block % 2 == 1)
                def _():
                    kv_t[block // 2, :, BLK:TILE] = turned

                return carry

            lax.fori_loop(0, share, place_block, 0)
        dkv_acc[...] = jnp.zeros_like(dkv_acc) if first_call else sum_ref[...]

    block = table[place[0] + place[4 + start + step]]
    last = block // 2
    in_prompt = block < prompt_blocks
    seg_tile = (prompt_blocks + (block - prompt_blocks) // cont_blocks * cont_blocks) // 2
    full = jnp.where(in_prompt, last, prompt_tiles + last - seg_tile)

    def tile_of(i):
        return jnp.where(i < prompt_tiles, jnp.minimum(i, last), i - prompt_tiles + seg_tile)

    def key_rows(tile):
        return pl.ds(pl.multiple_of(tile * TILE, TILE), TILE)

    for h in range(heads):
        rq[0:size, h * BLK : (h + 1) * BLK] = q_ref[h * size : (h + 1) * size, :]
    rq[size : 2 * size, :] = jnp.zeros((size, lanes), BF)

    def scores(tile):
        return dot(kv_c[key_rows(tile), :], rq[...])

    def fold(values):
        return jnp.max(values.reshape(TILE // 8, 8, lanes), 0)

    def first_pass(i, top):
        part = scores(tile_of(i))
        s_scr[i] = part
        return jnp.maximum(top, fold(part))

    top = lax.fori_loop(0, full, first_pass, jnp.full((8, lanes), -1e30, F32))
    part = scores(last)
    key_at = last * TILE + lax.broadcasted_iota(jnp.int32, (TILE, lanes), 0)
    row_at = block * BLK + lax.rem(lax.broadcasted_iota(jnp.int32, (TILE, lanes), 1), BLK)
    part = jnp.where(key_at <= row_at, part, -1e30)
    s_scr[full] = part
    top = jnp.max(jnp.maximum(top, fold(part)), 0, keepdims=True)

    o_acc[...] = jnp.zeros_like(o_acc)

    def second_pass(i, carry):
        p = jnp.exp2(s_scr[i] - top).astype(BF)
        p_scr[i] = p
        o_acc[...] += dot(kv_t[jnp.where(i == full, last, tile_of(i)), size : 2 * size + 16, :], p)
        return carry

    lax.fori_loop(0, full + 1, second_pass, 0)

    inverse = 1.0 / o_acc[size : size + 1, :]
    mixed = o_acc[0:size, :] * inverse
    grads = []
    for h in range(heads):
        at = slice(h * BLK, (h + 1) * BLK)
        mix_ref[h * size : (h + 1) * size, :] = mixed[:, at].astype(BF)
        grads.append(do_ref[h * size : (h + 1) * size, :])
    scaled = (jnp.concatenate(grads, 1) * inverse).astype(BF)
    delta = jnp.sum(mixed * scaled.astype(F32), 0, keepdims=True)
    rd[0:size, :] = jnp.zeros((size, lanes), BF)
    rd[size : 2 * size, :] = scaled
    rqt[...] = rq[...].T
    rdt[...] = rd[...].T
    dq_acc[...] = jnp.zeros_like(dq_acc)

    def third_pass(i, carry):
        tile = jnp.where(i == full, last, tile_of(i))
        p = p_scr[i]
        d_probs = dot(kv_c[key_rows(tile), :], rd[...])
        ds = (p.astype(F32) * (d_probs - delta)).astype(BF)
        dq_acc[...] += dot(kv_t[tile, 0:size, :], ds)
        dkv_acc[key_rows(tile), :] += dot(p, rdt[...]) + dot(ds, rqt[...])
        return carry

    lax.fori_loop(0, full + 1, third_pass, 0)

    cosine, sine = cos_ref[...], sin_ref[...]
    for h in range(heads):
        part = dq_acc[:, h * BLK : (h + 1) * BLK] * 0.125
        dq_ref[h * size : (h + 1) * size, :] = turn(part, cosine, -sine).astype(BF)

    @pl.when((step == pl.num_programs(0) - 1) & (group == pl.num_programs(1) - 1))
    def _():
        if not last_call:
            outs[0][...] = dkv_acc[...]
            return
        scale = jnp.where(
            lax.broadcasted_iota(jnp.int32, (BLK, 2 * size), 1) < size, F32(LN2), F32(1.0)
        )

        def rows_of(slot):
            return (dkv_acc[block_rows(table[slot]), :] * scale).astype(BF)

        if len(outs) == 1:

            def give_block(slot, carry):
                outs[0][block_rows(slot), :] = rows_of(slot)
                return carry

            lax.fori_loop(0, blocks, give_block, 0)
            return
        per_core = per_chip // 2
        for low in range(2):
            for high in range(2):
                chip = place[2] ^ (low + 2 * high)
                for n in range(per_core):
                    here = slice(n * BLK, (n + 1) * BLK)
                    base = chip * per_chip + n
                    outs[0][low, high, here, :] = rows_of(base + per_core - place[1])
                    outs[1][low, high, here, :] = rows_of(base + place[1])


def attention(
    table, place, q_t, do_t, cosine, sine, kvs, carried, start, count, per_chip, last_call, split
):
    width = q_t.shape[0]
    rows = count * BLK
    first_call = carried is None
    size = kvs[0].shape[1] // 2
    keys = sum(kv.shape[0] for kv in kvs)
    all_heads = width // size
    blocks = keys // BLK
    heads = all_heads if keys <= 4096 else 2
    lanes = heads * BLK
    cont = min(CONT, keys // 2)
    most = (keys // 2 + cont) // TILE
    tiles = keys // TILE

    def whole(dims):
        return pl.BlockSpec(dims, lambda i, j, *_: (0,) * len(dims))

    if not last_call:
        dkv_shapes = [shape((keys, 2 * size), F32)]
    elif split:
        dkv_shapes = [shape((2, 2, keys // 8, 2 * size), BF)] * 2
    else:
        dkv_shapes = [shape((keys, 2 * size), BF)]
    extra = [] if first_call else [carried]

    def column_of(i, scalars):
        return lax.rem(scalars[4 + start + i] + per_chip - scalars[1], per_chip)

    column = pl.BlockSpec((heads * size, BLK), lambda i, j, _, scalars: (j, column_of(i, scalars)))
    angle = pl.BlockSpec((HALF, BLK), lambda i, j, _, scalars: (0, column_of(i, scalars)))
    out_column = pl.BlockSpec((heads * size, BLK), lambda i, j, *_: (j, i))
    return pl.pallas_call(
        functools.partial(
            attn_kernel,
            blocks=blocks,
            heads=heads,
            size=size,
            n_kv=len(kvs),
            per_chip=per_chip,
            start=start,
            last_call=last_call,
            first_call=first_call,
        ),
        out_shape=[shape((width, rows), BF)] * 2 + dkv_shapes,
        grid_spec=pltpu.PrefetchScalarGridSpec(
            num_scalar_prefetch=2,
            grid=(count, all_heads // heads),
            in_specs=[column, column, angle, angle]
            + [whole(kv.shape) for kv in kvs]
            + [whole(e.shape) for e in extra],
            out_specs=[out_column, out_column] + [whole(s.shape) for s in dkv_shapes],
            scratch_shapes=[
                pltpu.VMEM((keys, 2 * size), BF),
                pltpu.VMEM((tiles, 2 * size + 16, TILE), BF),
                pltpu.VMEM((most, TILE, lanes), F32),
                pltpu.VMEM((most, TILE, lanes), BF),
                pltpu.VMEM((2 * size, lanes), BF),
                pltpu.VMEM((2 * size, lanes), BF),
                pltpu.VMEM((lanes, 2 * size), BF),
                pltpu.VMEM((lanes, 2 * size), BF),
                pltpu.VMEM((size + 16, lanes), F32),
                pltpu.VMEM((size, lanes), F32),
                pltpu.VMEM((keys, 2 * size), F32),
            ],
        ),
        compiler_params=pltpu.CompilerParams(
            vmem_limit_bytes=(24 if keys <= 4096 else 60) * MIB
        ),
        cost_estimate=pl.CostEstimate(
            flops=1000, bytes_accessed=1000, transcendentals=0
        ),
        name="attention",
    )(table, place, q_t, do_t, cosine, sine, *kvs, *extra)


def prologue_kernel(
    sc, x_hbm, xt_hbm, g_hbm, gt_hbm, gains, w_hbm, cos_ref, sin_ref, h1_ref, h2_ref, gg_ref, kv_ref, xo, xt, w_kv, sem
):
    rows = xt.shape[0]
    copies = [
        pltpu.make_async_copy(x_hbm, xo, sem.at[0]),
        pltpu.make_async_copy(xt_hbm, xt, sem.at[1]),
        pltpu.make_async_copy(w_hbm, w_kv, sem.at[2]),
        pltpu.make_async_copy(g_hbm, gg_ref.at[0:rows, :], sem.at[3]),
        pltpu.make_async_copy(gt_hbm, gg_ref.at[rows : 2 * rows, :], sem.at[4]),
    ]
    for copy in copies:
        copy.start()
    gain_one, bias_one = gains[0:1, :].astype(F32), gains[1:2, :].astype(F32)
    gain_two, bias_two = gains[2:3, :].astype(F32), gains[3:4, :].astype(F32)
    for n, x in enumerate((xo, xt)):
        copies[n].wait()
        for t in range(rows // 128):
            here = slice(n * rows + t * 128, n * rows + (t + 1) * 128)
            hat, unused = normed(x[t * 128 : (t + 1) * 128, :].astype(F32))
            h1_ref[here, :] = (hat * gain_one + bias_one).astype(BF)
            h2_ref[here, :] = (hat * gain_two + bias_two).astype(BF)
    copies[2].wait()
    raw = dot(h1_ref[...], w_kv[...])
    kv = turn(raw.T, cos_ref[...], sin_ref[...]).T.astype(BF)
    kv_ref[pl.ds(pl.multiple_of(sc[0] * rows, rows), rows), :] = kv[:rows]
    kv_ref[pl.ds(pl.multiple_of((1 - sc[0]) * rows, rows), rows), :] = kv[rows:]
    copies[3].wait()
    copies[4].wait()


def half_copies(sc, w_query, w_out, query_s, out_s, sem):
    half = out_s.shape[0]
    at = pl.ds(pl.multiple_of(sc[0] * half, 128), half)
    return [
        pltpu.make_async_copy(w_query.at[:, at], query_s, sem.at[0]),
        pltpu.make_async_copy(w_out.at[at, :], out_s, sem.at[1]),
    ]


def project_kernel(
    sc, h_ref, g_ref, cos_ref, sin_ref, w_query, w_out, q_ref, do_ref, query_s, out_s, sem, *, size
):
    copies = half_copies(sc, w_query, w_out, query_s, out_s, sem)
    for copy in copies:
        copy.start()
    cosine, sine = cos_ref[...], sin_ref[...]
    copies[0].wait()
    raw = (dot(h_ref[...], query_s[...]) * (0.125 * LOG2E)).T
    for h in range(raw.shape[0] // size):
        at = slice(h * size, (h + 1) * size)
        q_ref[at, :] = turn(raw[at], cosine, sine).astype(BF)
    copies[1].wait()
    do_ref[...] = dot(out_s[...], g_ref[...], ((1,), (1,)))


def hidden_copies(sc, piece, w_up, w_down, up_s, down_s, sems, part, n_pair):
    copies = []
    for j in range(n_pair):
        source = pl.ds(pl.multiple_of((2 * j + sc[0]) * part + piece * LANES, LANES), LANES)
        at = slice(j * LANES, (j + 1) * LANES)
        if w_up is not None:
            copies.append(
                pltpu.make_async_copy(w_up.at[:, source], up_s.at[:, at], sems.at[0])
            )
        if w_down is not None:
            copies.append(
                pltpu.make_async_copy(w_down.at[source, :], down_s.at[at, :], sems.at[1])
            )
    return copies


def piece_of(sc, n):
    return 0 if n == 0 else (2 - sc[2] if n == 1 else 1 + sc[2])


def ffn_kernel(
    sc, h_ref, g_ref, w_up, w_down, act_ref, dup_ref, *refs, n, part, n_pair
):
    up_s, down_s, grad_s, sems = refs[-4:]
    outs = refs[:-4]
    rows, width = h_ref.shape
    copies = hidden_copies(sc, piece_of(sc, n), w_up, w_down, up_s, down_s, sems, part, n_pair)
    for copy in copies[0::2] + copies[1::2]:
        copy.start()
    for copy in copies[0::2] + copies[1::2]:
        copy.wait()

    def row_tile(r, carry):
        tile = pl.ds(pl.multiple_of(r * 128, 128), 128)
        act, slope = gelu_parts(dot(h_ref[tile, :], up_s[...]))
        act_ref[tile, :] = act.astype(BF)
        d_act = dot(g_ref[tile, :], down_s[...], ((1,), (1,)))
        dup_ref[tile, :] = (d_act * slope).astype(BF)
        return carry

    lax.fori_loop(0, rows // 128, row_tile, 0, unroll=2)
    up_rows = width // n_pair
    block_rows = width // WIDE * LANES

    def give(low, high, kind, first, value):
        here = slice(first, first + value.shape[0])
        if n == 0:
            outs[1 - low][high, kind * block_rows + first : kind * block_rows + here.stop, :] = value
        else:
            outs[0][kind ^ sc[3], low, high, here, :] = value

    grad_s[0 : n_pair * LANES, :] = dot(act_ref[...], g_ref[...], ((0,), (0,))).astype(BF)
    for low in range(2):
        for high in range(2):
            chip = sc[1] ^ (low + 2 * high)
            rows_at = pl.ds(pl.multiple_of(chip * LANES, LANES), LANES)
            for b in range(width // WIDE):
                give(low, high, 0, b * LANES, grad_s[rows_at, b * WIDE : (b + 1) * WIDE])
    span = n_pair * LANES
    grad_s[:, 0:span] = dot(h_ref[...], dup_ref[...], ((0,), (0,))).astype(BF)
    for low in range(2):
        for high in range(2):
            chip = sc[1] ^ (low + 2 * high)
            rows_at = pl.ds(pl.multiple_of(chip * up_rows, 64), up_rows)
            for b in range(span // WIDE):
                give(low, high, 1, b * up_rows, grad_s[rows_at, b * WIDE : (b + 1) * WIDE])


def ffn_gradients(sc, h_two, g_two, w_up, w_down, n, part, n_pair):
    rows, width = h_two.shape
    span = n_pair * LANES
    block = width // WIDE * LANES
    if n == 0:
        outs = [shape((2, 2 * block, WIDE), BF)] * 2
    else:
        outs = [shape((2, 2, 2, block, WIDE), BF)]
    return call(
        functools.partial(ffn_kernel, n=n, part=part, n_pair=n_pair),
        "ffn_gradients",
        [shape((rows, span), BF)] * 2 + outs,
        [VM, VM, HBM, HBM],
        [VM] * (2 + len(outs)),
        [
            pltpu.VMEM((width, span), BF),
            pltpu.VMEM((span, width), BF),
            pltpu.VMEM((width, width), BF),
            pltpu.SemaphoreType.DMA((2,)),
        ],
        56,
    )(sc, h_two, g_two, w_up, w_down)


def late_kernel(
    sc, h_ref, dq0, dq1, mix0, mix1, got0, got1, g_ref, send_ref, keep_ref, mix_ref, dq_s, mix_s, both_s,
    *, n_pair
):
    half = mix0.shape[0]
    rows = mix0.shape[1]
    width = 2 * half
    count = rows // BLK
    own = pl.multiple_of(sc[0] * half, 128)
    other = pl.multiple_of((1 - sc[0]) * half, 128)
    for n, (mix, got, dq) in enumerate(((mix0, got0, dq0), (mix1, got1, dq1))):
        for k in range(count):
            source = slice(k * BLK, (k + 1) * BLK)
            at = pl.ds(pl.multiple_of(sc[4 + n * count + k] * BLK, BLK), BLK)
            mix_ref[:, at] = mix[:, source]
            mix_s[pl.ds(own, half), at] = mix[:, source]
            mix_s[pl.ds(other, half), at] = got[:, source]
            dq_s[:, at] = dq[:, source]
    both_s[:, 0:half] = dot(h_ref[...], dq_s[...], ((0,), (1,))).astype(BF)
    both_s[:, half:width] = dot(mix_s[...], g_ref[:, pl.ds(own, half)]).astype(BF)
    block = width // n_pair
    quarter = keep_ref.shape[3]
    unit = 48
    for low in range(2):
        for high in range(2):
            chip = sc[1] ^ (low + 2 * high)
            for first in range(2):
                ref = send_ref if first else keep_ref
                for second in range(2):
                    part = 2 * (first ^ sc[2]) + (second ^ sc[3])
                    for r in range(quarter // unit):
                        at = part * quarter + r * unit
                        col, row = at // block, at % block
                        source = pl.ds(pl.multiple_of(chip * block + row, 16), unit)
                        lane = pl.ds(pl.multiple_of(col * WIDE, WIDE), WIDE)
                        ref[second, low, high, r * unit : (r + 1) * unit, :] = both_s[source, lane]


def late_gradients(sc, h_one, dqs, mixes, gots, g_two, n_pair):
    half = dqs[0].shape[0]
    width = 2 * half
    rows = h_one.shape[0]
    quarter = width // n_pair * (width // WIDE) // 4
    return call(
        functools.partial(late_kernel, n_pair=n_pair),
        "late_gradients",
        [shape((2, 2, 2, quarter, WIDE), BF)] * 2 + [shape((half, rows), BF)] * 2,
        [VM] * 8,
        [VM] * 4,
        [
            pltpu.VMEM((width, rows), BF),
            pltpu.VMEM((width, width), BF),
        ],
        16,
    )(sc, h_one, *dqs, *mixes, *gots, g_two)


def out_kernel(sc, a0, a1, a2, mix_ref, x_ref, w_down, w_out, own_ref, send_ref, down_s, out_s, sems, *, part, n_pair):
    half = out_s.shape[0]
    rows = x_ref.shape[0]
    span = n_pair * LANES
    copies = [
        pltpu.make_async_copy(
            w_out.at[pl.ds(pl.multiple_of(sc[0] * half, 128), half), :], out_s, sems.at[0]
        )
    ]
    for n in range(3):
        copies += hidden_copies(
            sc, piece_of(sc, n), None, w_down, None, down_s.at[n], sems, part, n_pair
        )
    for copy in copies:
        copy.start()
    for copy in copies:
        copy.wait()
    for n in range(2):
        here = slice(n * rows, (n + 1) * rows)
        total = dot(mix_ref[:, here], out_s[...], ((0,), (0,)))
        for k, act in enumerate((a0, a1, a2)):
            total = total + dot(act[here, :], down_s[k])
        if n == 0:
            own_ref[...] = total + x_ref[...].astype(F32)
        else:
            send_ref[...] = total.astype(BF)


def hat_kernel(sc, d0, d1, d2, dq_ref, xo, xt, gains, w_up, w_query, own_ref, send_ref, sum_ref, up_s, query_s, sems, *, part, n_pair):
    half = query_s.shape[1]
    rows, width = xo.shape
    copies = [
        pltpu.make_async_copy(
            w_query.at[:, pl.ds(pl.multiple_of(sc[0] * half, 128), half)], query_s, sems.at[1]
        )
    ]
    for n in range(3):
        copies += hidden_copies(
            sc, piece_of(sc, n), w_up, None, up_s.at[n], None, sems, part, n_pair
        )
    for copy in copies:
        copy.start()
    for copy in copies:
        copy.wait()
    gain_one, gain_two = gains[0:1, :].astype(F32), gains[2:3, :].astype(F32)
    sums = [jnp.zeros((1, width), F32)] * 4
    for n, x in enumerate((xo, xt)):
        here = slice(n * rows, (n + 1) * rows)
        two = dot(d0[here, :], up_s[0], ((1,), (1,)))
        two = two + dot(d1[here, :], up_s[1], ((1,), (1,)))
        two = two + dot(d2[here, :], up_s[2], ((1,), (1,)))
        one = dot(dq_ref[:, here], query_s[...], ((0,), (1,)))
        hat, unused = normed(x[...].astype(F32))
        for k, value in enumerate((one * hat, one, two * hat, two)):
            sums[k] = sums[k] + jnp.sum(value, 0, keepdims=True)
        total = one * gain_one + two * gain_two
        if n == 0:
            own_ref[...] = total
        else:
            send_ref[...] = total.astype(BF)
    sum_ref[...] = jnp.concatenate(sums + [jnp.zeros((4, width), F32)], 0)


def last_kernel(sc, dkv_a, dkv_b, dkv_c, dkv_d, cos_ref, sin_ref, w_kv, h_ref, x_ref, gains, hat_own, hat_got, sum_ref, g_ref, grad_ref, send_ref, keep_ref, *, n_pair):
    rows, width = x_ref.shape
    dkv = sum(ref[...].astype(F32) for ref in (dkv_a, dkv_b, dkv_c, dkv_d)).T
    low_t = turn(dkv, cos_ref[:, 0:rows], -sin_ref[:, 0:rows]).astype(BF)
    low = low_t.T
    weight = dot(low_t, h_ref[0:rows, :]).T.astype(BF)
    d_kv = dot(low, w_kv[...], ((1,), (1,)))
    hat, scale = normed(x_ref[...].astype(F32))
    gain = gains[0:1, :].astype(F32)
    total = hat_own[...] + hat_got[...].astype(F32) + d_kv * gain
    grad_ref[...] = g_ref[...].astype(F32) + scale * (
        total
        - jnp.mean(total, -1, keepdims=True)
        - hat * jnp.mean(total * hat, -1, keepdims=True)
    )
    sums = jnp.concatenate(
        [
            sum_ref[0:1, :] + jnp.sum(d_kv * hat, 0, keepdims=True),
            sum_ref[1:2, :] + jnp.sum(d_kv, 0, keepdims=True),
            sum_ref[2:4, :],
            jnp.zeros((4, width), F32),
        ],
        0,
    ).astype(BF)
    part = width // (2 * n_pair)
    lanes = weight.shape[1]
    for chip in range(n_pair):
        rel = chip ^ sc[1]
        low_bit, high_bit = rel % 2, rel // 2
        blocks = []
        for core in range(2):
            at = (2 * chip + core) * part
            piece = weight[at : at + part, :]
            blocks.append(jnp.concatenate([piece[: part // 2], piece[part // 2 :]], 1))
            row = sums[:, at : at + part]
            blocks.append(jnp.concatenate([row, jnp.zeros((8, 2 * lanes - part), BF)], 1))
        block = jnp.concatenate(blocks, 0)

        @pl.when(low_bit == 1)
        def _():
            send_ref[high_bit] = block

        @pl.when(low_bit == 0)
        def _():
            keep_ref[high_bit] = block


def down_kernel(sc, a_send, a_got, send_ref, got_ref, out_ref, *, width):
    block = width // WIDE * LANES
    for k in range(3):
        for b in range(width // WIDE):
            here = slice(b * LANES, (b + 1) * LANES)
            if k == 0:
                value = a_send[here, :].astype(F32) + a_got[here, :].astype(F32)
            else:
                at = pl.ds(pl.multiple_of(sc[3] * block + b * LANES, LANES), LANES)
                mine = send_ref[at, :].astype(F32)
                value = jnp.where(sc[2] == k - 1, mine, got_ref[at, :].astype(F32))
            out_ref[k * LANES : (k + 1) * LANES, b * WIDE : (b + 1) * WIDE] = value


def up_block(sc, k, b, parity, a_send, a_got, b_send, b_got, width, part):
    block = width // WIDE * LANES
    off = b * 2 * part + parity * part
    if k == 0:
        at = pl.ds(pl.multiple_of(block + off, 32), part)
        return a_send[at, :].astype(F32) + a_got[at, :].astype(F32)
    at = pl.ds(pl.multiple_of((1 - sc[3]) * block + off, 32), part)
    return jnp.where(
        sc[2] == k - 1, b_send[at, :].astype(F32), b_got[at, :].astype(F32)
    )


def late_block(sc, b, parity, send, got, part, quarter):
    pieces = []
    for r in range(2):
        at = b * 2 * part + parity * part + r * (part // 2)
        first, second = at // (2 * quarter), at // quarter % 2
        rel = (second ^ sc[3]) * quarter + at % quarter
        source = pl.ds(pl.multiple_of(rel, 16), part // 2)
        pieces.append(
            jnp.where(
                first == sc[2], send[source, :].astype(F32), got[source, :].astype(F32)
            )
        )
    return jnp.concatenate(pieces, 0)


def pack_kernel(sc, a_send, a_got, b_send, b_got, last_send, last_got, out_ref, own_ref, *, width, part, quarter):
    for which, ref in ((1, out_ref), (0, own_ref)):
        parity = sc[0] if which == 0 else 1 - sc[0]
        at = 0
        for k in range(3):
            for b in range(2):
                ref[at : at + part, :] = up_block(
                    sc, k, b, parity, a_send, a_got, b_send, b_got, width, part
                ).astype(BF)
                at += part
        for b in range(width // WIDE):
            ref[at : at + part, :] = late_block(
                sc, b, parity, last_send, last_got, part, quarter
            ).astype(BF)
            at += part
        few = (last_send.shape[0] - 2 * quarter) // 2
        source = pl.ds(pl.multiple_of(2 * quarter + parity * few, 8), few)
        ref[at : at + few, :] = (
            last_send[source, :].astype(F32) + last_got[source, :].astype(F32)
        ).astype(BF)


def final_kernel(sc, own_ref, got_ref, up_ref, query_ref, proj_ref, kv_ref, norm_ref, *, part, n_pair):
    part_hidden = up_ref.shape[1] // (2 * n_pair)
    half = query_ref.shape[1] // 2
    for which, ref in enumerate((own_ref, got_ref)):
        core = sc[0] if which == 0 else 1 - sc[0]
        at = 0
        for k in range(3):
            for j in range(n_pair):
                lane = (2 * j + core) * part_hidden + k * LANES
                rows = slice((2 * k + j // 2) * part, (2 * k + j // 2 + 1) * part)
                cols = slice(j % 2 * LANES, (j % 2 + 1) * LANES)
                up_ref[:, pl.ds(pl.multiple_of(lane, LANES), LANES)] = ref[rows, cols].astype(F32)
        base = 6 * part
        for n in range(2 * half // LANES):
            rows = slice(base + n // 2 * part, base + (n // 2 + 1) * part)
            value = ref[rows, n % 2 * LANES : (n % 2 + 1) * LANES].astype(F32)
            to, m = (query_ref, n) if n < half // LANES else (proj_ref, n - half // LANES)
            to[:, pl.ds(pl.multiple_of(core * half + m * LANES, LANES), LANES)] = value
    base = 9 * part
    few = own_ref[base:, :].astype(F32) + got_ref[base:, :].astype(F32)
    kv_ref[0 : part // 2, :] = few[0 : part // 2, 0:LANES]
    kv_ref[part // 2 : part, :] = few[0 : part // 2, LANES:WIDE]
    norm_ref[...] = few[part // 2 : part // 2 + 8, :]


class Links:
    def __init__(self, n_grp, n_ctx):
        self.n_grp, self.n_ctx, self.n_pair = n_grp, n_ctx, n_ctx // 2
        self.small = (n_grp, n_ctx) == (4, 8)
        self.ctx = lax.axis_index("ctx")
        self.grp = lax.axis_index("grp")
        self.core = self.ctx % 2
        self.chip = self.ctx // 2
        self.groups = [[2 * z + c for z in range(self.n_pair)] for c in range(2)]

    def swap(self, value):
        return lax.ppermute(value, "ctx", [(i, i ^ 1) for i in range(self.n_ctx)])

    def permute(self, value, target):
        pairs = []
        for g in range(self.n_grp):
            for i in range(self.n_ctx):
                y, x, z, c = target(g // 2, g % 2, i // 2, i % 2)
                pairs.append((g * self.n_ctx + i, (2 * y + x) * self.n_ctx + 2 * z + c))
        return lax.ppermute(value, ("grp", "ctx"), pairs)

    def cross(self, value, stage):
        return self.permute(
            value, lambda y, x, z, c: (y, 1 - x, z, c) if c == stage else (1 - y, x, z, c)
        )

    def bit(self, stage):
        y, x = self.grp // 2, self.grp % 2
        return jnp.where(self.core == stage, x, y)

    def flip(self, value, bit):
        return self.permute(value, lambda y, x, z, c: (y, x, z ^ bit, c))

    def reduce(self, parts):
        moved = lax.all_to_all(parts, "ctx", 0, 0, axis_index_groups=self.groups)
        return lax.psum(jnp.sum(moved.astype(F32), 0).astype(BF), "grp")


def add(*values):
    return sum(value.astype(F32) for value in values).astype(BF)


def low(value):
    return value.astype(BF)


def shards_small(
    layer_input, block_table, ln1_gain, ln1_bias, ln2_gain, ln2_bias,
    w_query, w_keyval, w_out, w_up, w_down, cotangent, *, n_grp, n_ctx,
):
    links = Links(n_grp, n_ctx)
    core, chip, n_pair = links.core, links.chip, links.n_pair
    rows, width = layer_input.shape
    lanes = w_keyval.shape[1]
    size = lanes // 2
    hidden = w_up.shape[1]
    group_len = block_table.shape[1] * BLK
    part, part_hidden = width // n_ctx, hidden // n_ctx
    half = width // 2
    per_chip = 2 * rows // BLK
    table = block_table[0]
    count = rows // BLK
    mine = lax.dynamic_slice_in_dim(table, chip * per_chip, per_chip)
    rank = jnp.sum((mine[None, :] < mine[:, None]).astype(jnp.int32), 1)
    ends = [n // 2 if n % 2 else per_chip - 1 - n // 2 for n in range(per_chip)]
    order = jnp.stack(
        [jnp.sum(jnp.where(rank == n, jnp.arange(per_chip, dtype=jnp.int32), 0)) for n in ends]
    )
    place = jnp.stack([chip * per_chip, core * count, chip, 0 * chip]).astype(jnp.int32)
    place = jnp.concatenate([place, order])
    sc = jnp.stack([core, chip, links.bit(0), links.bit(1)]).astype(jnp.int32)
    sc = jnp.concatenate([sc, lax.rem(order + per_chip - core * count, per_chip)])
    gains = jnp.concatenate([ln1_gain, ln1_bias, ln2_gain, ln2_bias]).reshape(4, width)

    x_other, g_other = links.swap(layer_input), links.swap(cotangent)
    own_slots = lax.dynamic_slice_in_dim(table, chip * per_chip, per_chip).reshape(2, -1)
    slots = jnp.concatenate([own_slots[core], own_slots[1 - core]])
    canon = (slots[:, None] * BLK + jnp.arange(BLK, dtype=jnp.int32)[None, :]).reshape(2 * rows)
    prompt_len = group_len // 2
    cont_span = min(CONT, prompt_len)
    position = jnp.where(
        canon < prompt_len, canon, prompt_len + (canon - prompt_len) % cont_span
    )
    cosine, sine = rope_tables(position)

    h_one, h_two, g_two, kv_low = call(
        prologue_kernel,
        "prologue",
        [shape((2 * rows, width), BF)] * 3 + [shape((2 * rows, lanes), BF)],
        [HBM] * 4 + [VM, HBM, VM, VM],
        [VM] * 4,
        [
            pltpu.VMEM((rows, width), BF),
            pltpu.VMEM((rows, width), BF),
            pltpu.VMEM((width, lanes), BF),
            pltpu.SemaphoreType.DMA((5,)),
        ],
        56,
    )(sc, layer_input, x_other, cotangent, g_other, gains, w_keyval, cosine, sine)

    kv_got = links.flip(kv_low, 1)
    ffn = functools.partial(
        ffn_gradients, sc, w_up=w_up, w_down=w_down, part=part_hidden, n_pair=n_pair
    )
    act_1, dup_1, b_send = ffn(h_two, g_two, n=1)
    b_send, kv_got = meet(b_send, kv_got)
    kv_near = jnp.concatenate([kv_low, kv_got], 0)
    kv_far = links.flip(kv_near, 2)
    b_got = links.cross(b_send, 0)
    act_2, dup_2, b_keep = ffn(tie(h_two, b_send, kv_near), g_two, n=2)
    act_0, dup_0, a_send, a_keep = ffn(tie(h_two, b_keep), g_two, n=0)
    a_send, kv_far = meet(a_send, kv_far)
    a_got = links.flip(a_send, 1)

    q_t, do_t = call(
        functools.partial(project_kernel, size=size),
        "project",
        [shape((half, 2 * rows), BF), shape((half, 2 * rows), F32)],
        [VM] * 4 + [HBM] * 2,
        [VM] * 2,
        [
            pltpu.VMEM((width, half), BF),
            pltpu.VMEM((half, width), BF),
            pltpu.SemaphoreType.DMA((2,)),
        ],
        16,
    )(sc, tie(h_one, a_send), g_two, cosine, sine, w_query, w_out)
    q_t, b_got = meet(q_t, b_got)
    b_send = add(b_keep[1], b_got[1])
    b_got_2 = links.cross(b_send, 1)

    attend = functools.partial(
        attention, table, place, do_t=do_t, cosine=cosine, sine=sine, kvs=(kv_near, kv_far),
        count=count, per_chip=per_chip, split=True,
    )
    mix_0, dq_0, carried = attend(
        q_t=tie(q_t, b_send), carried=None, start=0, last_call=False
    )
    carried, a_got, b_got_2 = meet(carried, a_got, b_got_2)
    b_send = add(b_keep[0, 1], b_got[0, 1], b_got_2[1])
    b_got_3 = links.flip(b_send, 1)
    a_send = add(a_keep[1], tie(a_got, b_send)[1])
    a_got_2 = links.flip(a_send, 2)
    mix_1, dq_1, dkv_send, dkv_keep = attend(
        q_t=tie(q_t, a_send, b_send, carried), carried=carried, start=count, last_call=True
    )
    mix_0, mix_1, dkv_send, a_got_2, b_got_3 = meet(mix_0, mix_1, dkv_send, a_got_2, b_got_3)
    dkv_got = links.swap(dkv_send)
    mix_0_got, mix_1_got = links.swap(mix_0), links.swap(mix_1)
    dkv_got, mix_0_got, mix_1_got = meet(dkv_got, mix_0_got, mix_1_got)
    dkv_sends = [add(dkv_keep[at], dkv_got[at]) for at in ((1, 0), (0, 1), (1, 1))]
    dkv_gots = [links.flip(value, n + 1) for n, value in enumerate(dkv_sends)]
    late_send, late_keep, mix_own, dq_own = late_gradients(
        sc, tie(h_one, *dkv_sends), (dq_0, dq_1), (mix_0, mix_1), (mix_0_got, mix_1_got), g_two, n_pair
    )
    late_got = links.cross(late_send, 0)

    w_specs = [HBM] * 2
    hat_own, hat_send, sums = call(
        functools.partial(hat_kernel, part=part_hidden, n_pair=n_pair),
        "norms",
        [shape((rows, width), F32), shape((rows, width), BF), shape((8, width), F32)],
        [VM] * 7 + w_specs,
        [VM] * 3,
        [
            pltpu.VMEM((3, width, n_pair * LANES), BF),
            pltpu.VMEM((width, half), BF),
            pltpu.SemaphoreType.DMA((2,)),
        ],
        56,
    )(
        sc, dup_0, dup_1, tie(dup_2, late_send), dq_own, layer_input, x_other, gains,
        w_up, w_query,
    )
    hat_send, late_got, *dkv_gots = meet(hat_send, late_got, *dkv_gots)
    hat_got = links.swap(hat_send)
    late_send = add(late_keep[1], late_got[1])
    late_got_2 = links.cross(late_send, 1)
    b_send = add(b_keep[0, 0, 1], b_got[0, 0, 1], b_got_2[0, 1], tie(b_got_3, late_send)[1])
    b_got_4 = links.flip(b_send, 2)
    dkv_own = add(dkv_keep[0, 0], dkv_got[0, 0])
    late_send, hat_got = meet(late_send, hat_got)

    few = part // 2 + 8
    in_grad, few_send, few_keep = call(
        functools.partial(last_kernel, n_pair=n_pair),
        "last",
        [shape((rows, width), F32)] + [shape((2, 2 * few, 2 * lanes), BF)] * 2,
        [VM] * 14,
        [VM] * 3,
        [],
        16,
    )(
        sc, dkv_own, *dkv_gots, tie(cosine, late_send, b_send), sine, w_keyval, h_one,
        layer_input, gains, hat_own, hat_got, sums, cotangent,
    )
    few_send, late_got_2 = meet(few_send, late_got_2)
    quarter = late_keep.shape[3]
    last_send = jnp.concatenate(
        [add(late_keep[0, 1], late_got[0, 1], late_got_2[1]), few_send], 1
    )
    last_got = links.flip(last_send, 1)
    a_sum = add(a_keep[0], a_got[0], a_got_2)
    a_got = links.cross(a_sum, 1)

    out_own, out_send = call(
        functools.partial(out_kernel, part=part_hidden, n_pair=n_pair),
        "outputs",
        [shape((rows, width), F32), shape((rows, width), BF)],
        [VM] * 5 + w_specs,
        [VM] * 2,
        [
            pltpu.VMEM((3, n_pair * LANES, width), BF),
            pltpu.VMEM((half, width), BF),
            pltpu.SemaphoreType.DMA((2,)),
        ],
        56,
    )(
        sc, act_0, act_1, tie(act_2, last_send, a_sum), mix_own, layer_input, w_down, w_out,
    )
    out_send, last_got, a_got = meet(out_send, last_got, a_got)
    out_got = links.swap(out_send)
    last_keep = jnp.concatenate(
        [add(late_keep[0, 0], late_got[0, 0], late_got_2[0]), few_keep], 1
    )
    last_send = add(last_keep[1], last_got[1])
    last_got_2 = links.flip(last_send, 2)
    a_sum = add(a_sum, a_got)
    a_got = links.cross(a_sum, 0)
    out_got, b_got_4 = meet(out_got, b_got_4, a_sum, last_send)[:2]
    layer_output = low(out_own + out_got.astype(F32))
    b_sum = add(b_keep[0, 0, 0], b_got[0, 0, 0], b_got_2[0, 0], b_got_3[0], b_got_4)
    b_got = links.cross(b_sum, 1)
    last_keep = add(last_keep[0], last_got[0])
    b_got, layer_output, a_got = meet(b_got, layer_output, a_got)
    b_sum = jnp.concatenate([b_sum, b_got], 0)
    b_got = links.cross(b_sum, 0)
    last_got_2 = meet(last_got_2, b_sum)[0]
    last = add(last_keep, last_got_2)
    last_got = links.cross(last, 1)
    last_got, b_got = meet(last_got, b_got)
    last = jnp.concatenate(
        [last[:quarter], last_got[:quarter], add(last[quarter:], last_got[quarter:])], 0
    )
    last_got = links.cross(last, 0)
    total_down = call(
        functools.partial(down_kernel, width=width),
        "down", shape((part_hidden, width), F32), [VM] * 4, VM, [], 8,
    )(sc, tie(a_sum, last), a_got, b_sum, b_got)
    total_down, last_got = meet(total_down, last_got)
    size_out = 9 * part + few
    other, own = call(
        functools.partial(pack_kernel, width=width, part=part, quarter=quarter),
        "pack", [shape((size_out, WIDE), BF)] * 2, [VM] * 6, [VM] * 2, [], 8,
    )(sc, a_sum, a_got, b_sum, b_got, last, last_got)
    got = links.swap(other)
    total_up, total_query, total_out, total_kv, norm = call(
        functools.partial(final_kernel, part=part, n_pair=n_pair),
        "final",
        [
            shape((part, hidden), F32),
            shape((part, width), F32),
            shape((part, width), F32),
            shape((part, lanes), F32),
            shape((8, WIDE), F32),
        ],
        [VM] * 2,
        [VM] * 5,
        [],
        8,
    )(sc, own, got)
    norms = [norm[n, :part] for n in range(4)]
    return (layer_output, in_grad, *norms, total_query, total_kv, total_out, total_up, total_down)


def rotate_rows(values, cosine, sine):
    return turn(values.T, cosine, sine).T


def shards(
    layer_input, block_table, ln1_gain, ln1_bias, ln2_gain, ln2_bias,
    w_query, w_keyval, w_out, w_up, w_down, cotangent, *, n_grp, n_ctx,
):
    links = Links(n_grp, n_ctx)
    core, chip, n_pair = links.core, links.chip, links.n_pair
    rows, width = layer_input.shape
    size = w_keyval.shape[1] // 2
    hidden = w_up.shape[1]
    group_len = block_table.shape[1] * BLK
    part_rows, part_hidden = width // n_ctx, hidden // n_ctx
    half_width, half_hidden = width // 2, hidden // 2
    per_chip = 2 * rows // BLK
    table = block_table[0]

    def both(own, other):
        return jnp.concatenate(
            [jnp.where(core == 0, own, other), jnp.where(core == 0, other, own)], 0
        )

    def mine(value, own_core):
        return lax.dynamic_slice_in_dim(value, own_core * rows, rows, 0)

    x_two = both(layer_input, links.swap(layer_input))
    g_two = both(cotangent, links.swap(cotangent))
    canon = (
        lax.dynamic_slice_in_dim(table, chip * per_chip, per_chip)[:, None] * BLK
        + jnp.arange(BLK, dtype=jnp.int32)[None, :]
    ).reshape(2 * rows)
    prompt_len = group_len // 2
    cont_span = min(CONT, prompt_len)
    position = jnp.where(
        canon < prompt_len, canon, prompt_len + (canon - prompt_len) % cont_span
    )
    cosine, sine = rope_tables(position)
    gain_one, gain_two = ln1_gain.astype(F32), ln2_gain.astype(F32)
    hat, scale = normed(x_two.astype(F32))
    h_one = low(hat * gain_one + ln1_bias.astype(F32))
    h_two = low(hat * gain_two + ln2_bias.astype(F32))
    kv_raw = dot(h_one, w_keyval)
    kv_low = low(
        jnp.concatenate([rotate_rows(kv_raw[:, :size], cosine, sine), kv_raw[:, size:]], -1)
    )
    kv_all = lax.all_gather(kv_low, "ctx", axis=0, axis_index_groups=links.groups, tiled=True)

    up_half = lax.dynamic_index_in_dim(
        w_up.reshape(width, n_pair, 2, part_hidden), core, 2, False
    ).reshape(width, half_hidden)
    down_half = lax.dynamic_index_in_dim(
        w_down.reshape(n_pair, 2, part_hidden, width), core, 1, False
    ).reshape(half_hidden, width)
    act, slope = gelu_parts(dot(h_two, up_half))
    act = low(act)
    grad_down = low(dot(act, g_two, ((0,), (0,))))
    total_down = links.reduce(grad_down.reshape(n_pair, part_hidden, width))
    grad_up = low(dot(g_two, down_half, ((1,), (1,))) * slope)
    grad_up_w = low(dot(h_two, grad_up, ((0,), (0,))))
    total_up = links.reduce(grad_up_w.reshape(n_pair, 2 * part_rows, half_hidden))

    query_half = lax.dynamic_slice_in_dim(w_query, core * half_width, half_width, 1)
    out_half = lax.dynamic_slice_in_dim(w_out, core * half_width, half_width, 0)
    q_raw = dot(query_half, h_one, ((0,), (1,))) * (0.125 * LOG2E)
    q_t = low(
        jax.vmap(turn, (0, None, None))(q_raw.reshape(-1, size, 2 * rows), cosine, sine)
    ).reshape(half_width, 2 * rows)
    do_t = dot(out_half, g_two, ((1,), (1,)))
    place = jnp.stack([chip * per_chip] + [0 * chip] * 3 + [n + 0 * chip for n in range(per_chip)])
    place = place.astype(jnp.int32)
    mix_t, dq_t, dkv_part = attention(
        table, place, q_t, do_t, cosine, sine, (kv_all,), None, 0, per_chip, per_chip, True, False
    )

    dkv_part = dkv_part.reshape(n_pair, 2, rows, 2 * size)
    dkv_own = lax.dynamic_index_in_dim(dkv_part, core, 1, False)
    dkv_got = links.swap(lax.dynamic_index_in_dim(dkv_part, 1 - core, 1, False))
    moved = lax.all_to_all(
        add(dkv_own, dkv_got), "ctx", 0, 0, axis_index_groups=links.groups
    )
    dkv = jnp.sum(moved.astype(F32), 0)
    cos_own = lax.dynamic_slice_in_dim(cosine, core * rows, rows, 1)
    sin_own = lax.dynamic_slice_in_dim(sine, core * rows, rows, 1)
    dkv_low = low(
        jnp.concatenate([rotate_rows(dkv[:, :size], cos_own, -sin_own), dkv[:, size:]], -1)
    )

    mix_got = links.swap(mix_t)
    mix_all = jnp.concatenate(
        [jnp.where(core == 0, mix_t, mix_got), jnp.where(core == 0, mix_got, mix_t)], 0
    )
    g_half = lax.dynamic_slice_in_dim(g_two, core * half_width, half_width, 1)
    grad_q_w = low(dot(h_one, dq_t, ((0,), (1,))))
    grad_out_w = low(dot(mix_all, g_half))
    late = jnp.concatenate([grad_q_w, grad_out_w], 1).reshape(n_pair, 2 * part_rows, width)
    total_late = links.reduce(late)

    out_part = dot(act, down_half) + dot(mix_t, out_half, ((0,), (0,)))
    out_got = links.swap(low(mine(out_part, 1 - core)))
    layer_output = low(layer_input.astype(F32) + mine(out_part, core) + out_got.astype(F32))

    d_two = dot(grad_up, up_half, ((1,), (1,)))
    d_one = dot(dq_t, query_half, ((0,), (1,)))
    d_kv = dot(dkv_low, w_keyval, ((1,), (1,)))
    row_core = lax.broadcasted_iota(jnp.int32, (2 * rows, 1), 0) // rows
    d_one = d_one + jnp.where(row_core == core, jnp.concatenate([d_kv, d_kv], 0), 0.0)
    sums = jnp.stack([jnp.sum(v, 0) for v in (d_one * hat, d_one, d_two * hat, d_two)])
    d_hat = d_one * gain_one + d_two * gain_two
    hat_got = links.swap(low(mine(d_hat, 1 - core)))
    d_hat = mine(d_hat, core) + hat_got.astype(F32)
    hat_own = mine(hat, core)
    in_grad = cotangent.astype(F32) + mine(scale, core) * (
        d_hat
        - jnp.mean(d_hat, -1, keepdims=True)
        - hat_own * jnp.mean(d_hat * hat_own, -1, keepdims=True)
    )

    grad_kv_w = dot(mine(h_one, core), dkv_low, ((0,), (0,)))
    sum_rows = sums.reshape(4, n_pair, 2, part_rows).transpose(1, 2, 0, 3)
    sum_rows = jnp.pad(sum_rows, ((0, 0), (0, 0), (0, 0), (0, 2 * size - part_rows)))
    few = jnp.concatenate([grad_kv_w.reshape(n_pair, 2, part_rows, 2 * size), sum_rows], 2)
    few = links.reduce(low(few).reshape(n_pair, 2 * (part_rows + 4), 2 * size))
    few = few.reshape(2, part_rows + 4, 2 * size)
    few_got = links.swap(lax.dynamic_index_in_dim(few, 1 - core, 0, False))
    few = lax.dynamic_index_in_dim(few, core, 0, False).astype(F32) + few_got.astype(F32)

    halves = jnp.concatenate(
        [total_up.reshape(2, part_rows, half_hidden), total_late.reshape(2, part_rows, width)], -1
    )
    own = lax.dynamic_index_in_dim(halves, core, 0, False)
    got = links.swap(lax.dynamic_index_in_dim(halves, 1 - core, 0, False))
    sides = jnp.stack([jnp.where(core == 0, own, got), jnp.where(core == 0, got, own)]).astype(F32)
    ups = sides[:, :, :half_hidden].reshape(2, part_rows, n_pair, part_hidden)
    total_up = ups.transpose(1, 2, 0, 3).reshape(part_rows, hidden)
    lates = sides[:, :, half_hidden:]
    total_query = lates[:, :, :half_width].transpose(1, 0, 2).reshape(part_rows, width)
    total_out = lates[:, :, half_width:].transpose(1, 0, 2).reshape(part_rows, width)
    norms = [few[part_rows + n, :part_rows] for n in range(4)]
    total_kv = few[:part_rows]
    total_down = total_down.astype(F32)
    return (layer_output, in_grad, *norms, total_query, total_kv, total_out, total_up, total_down)


def solution(mesh):
    n_grp, n_ctx = mesh.shape["grp"], mesh.shape["ctx"]
    body = shards_small if (n_grp, n_ctx) == (4, 8) else shards
    return jax.shard_map(
        functools.partial(body, n_grp=n_grp, n_ctx=n_ctx),
        mesh=mesh,
        in_specs=(P(("grp", "ctx"), None), P("grp", None))
        + (P(),) * 9
        + (P(("grp", "ctx"), None),),
        out_specs=(P(("grp", "ctx"), None),) * 2 + (P("ctx"),) * 4 + (P("ctx", None),) * 5,
        check_vma=False,
    )
```

```python
import functools

import jax
import jax.numpy as jnp
import numpy as np
from jax import lax
from jax.experimental import pallas as pl
from jax.experimental.pallas import tpu as pltpu
from jax.sharding import PartitionSpec as P

ROT = 16
HALF = ROT // 2
BLK = 128
CONT = 1024
TILE = 256
LANES = 128
WIDE = 256
EPS = 1e-05
LOG2E = 1.4426950408889634
LN2 = 0.6931471805599453
BF = jnp.bfloat16
F32 = jnp.float32
MIB = 1024 * 1024
VM = pl.BlockSpec(memory_space=pltpu.VMEM)
HBM = pl.BlockSpec(memory_space=pltpu.HBM)


def dot(left, right, dims=((1,), (0,))):
    return lax.dot_general(left, right, (dims, ((), ())), preferred_element_type=F32)


def shape(dims, dtype):
    return jax.ShapeDtypeStruct(dims, dtype)


def tie(value, *others):
    return lax.optimization_barrier((value,) + others)[0]


def meet(*values):
    return lax.optimization_barrier(values)


def rope_tables(position):
    inverse = jnp.asarray(10000.0 ** (-2.0 * np.arange(HALF) / ROT), F32)
    angles = inverse[:, None] * position.astype(F32)[None, :]
    return (jnp.cos(angles), jnp.sin(angles))


def turn(values, cosine, sine):
    first, second = values[:HALF], values[HALF:ROT]
    return jnp.concatenate(
        [first * cosine - second * sine, second * cosine + first * sine, values[ROT:]], 0
    )


def normed(values):
    shifted = values - jnp.mean(values, -1, keepdims=True)
    scale = lax.rsqrt(jnp.mean(shifted * shifted, -1, keepdims=True) + EPS)
    return (shifted * scale, scale)


def gelu_parts(value):
    cdf = 0.5 * (1.0 + lax.erf(value * 0.7071067811865476))
    pdf = jnp.exp(-0.5 * value * value) * 0.3989422804014327
    return value * cdf, cdf + value * pdf


def call(kernel, name, outs, specs, out_specs, scratch, limit, flops=1000):
    def body(table, *refs):
        kernel(scalars(table), *refs)

    made = pl.pallas_call(
        body,
        out_shape=outs,
        grid_spec=pltpu.PrefetchScalarGridSpec(
            num_scalar_prefetch=1, in_specs=specs, out_specs=out_specs, scratch_shapes=scratch
        ),
        compiler_params=pltpu.CompilerParams(vmem_limit_bytes=limit * MIB),
        cost_estimate=pl.CostEstimate(flops=flops, bytes_accessed=flops, transcendentals=0),
        name=name,
    )

    def placed(table, *values):
        return made(
            table,
            *(
                pltpu.with_memory_space_constraint(v, pltpu.HBM) if spec is HBM else v
                for v, spec in zip(values, specs)
            ),
        )

    return placed


def scalars(table):
    ctx, grp = lax.axis_index("ctx"), lax.axis_index("grp")
    per_chip = 2 * table.shape[0] // lax.axis_size("ctx")
    core, chip = lax.rem(ctx, 2), lax.div(ctx, 2)
    y, x = lax.div(grp, 2), lax.rem(grp, 2)
    blocks = [table[chip * per_chip + n] for n in range(per_chip)]
    ranks = [sum((b < a).astype(jnp.int32) for b in blocks if b is not a) for a in blocks]
    order = []
    for k in range(per_chip):
        want = k // 2 if k % 2 else per_chip - 1 - k // 2
        at = sum(jnp.where(rank == want, n, 0) for n, rank in enumerate(ranks))
        order.append(lax.rem(at + per_chip - core * (per_chip // 2), per_chip))
    return [core, chip, jnp.where(core == 0, x, y), jnp.where(core == 1, x, y)] + order


def attn_kernel(
    table, *refs, blocks, heads, size, n_kv, per_chip, start, split, last_call, first_call
):
    q_ref, do_ref, cos_ref, sin_ref = refs[:4]
    kv_refs = refs[4 : 4 + n_kv]
    refs = refs[4 + n_kv :]
    if not first_call:
        sum_ref, refs = refs[0], refs[1:]
    mix_ref, dq_ref = refs[:2]
    outs = refs[2:-11]
    kv_c, kv_t, s_scr, p_scr, rq, rd, rqt, rdt, o_acc, dq_acc, dkv_acc = refs[-11:]
    step, group = pl.program_id(0), pl.program_id(1)
    core, chip, _, _, *order = scalars(table)
    if split:
        column = sum(
            jnp.where(step == n, order[start + n], 0) for n in range(per_chip // 2)
        )
        position = lax.rem(column + core * (per_chip // 2), per_chip)
    else:
        column = position = step
    lanes = heads * BLK
    prompt_blocks = blocks // 2
    prompt_tiles = prompt_blocks * BLK // TILE
    cont_blocks = min(CONT, prompt_blocks * BLK) // BLK

    def block_rows(block):
        return pl.ds(pl.multiple_of(block * BLK, BLK), BLK)

    @pl.when((step == 0) & (group == 0))
    def _():
        ones = jnp.ones((16, BLK), BF)
        share = blocks // n_kv

        for n, kv_ref in enumerate(kv_refs):

            def place_block(at, carry, n=n, kv_ref=kv_ref):
                spot = n * share + at
                owner = (spot // per_chip) ^ chip if split else spot // per_chip
                block = table[owner * per_chip + spot % per_chip]
                rows = kv_ref[block_rows(at), :]
                kv_c[block_rows(block), :] = rows
                turned = jnp.concatenate([rows.T, ones], 0)

                @pl.when(block % 2 == 0)
                def _():
                    kv_t[block // 2, :, 0:BLK] = turned

                @pl.when(block % 2 == 1)
                def _():
                    kv_t[block // 2, :, BLK:TILE] = turned

                return carry

            lax.fori_loop(0, share, place_block, 0)
        dkv_acc[...] = jnp.zeros_like(dkv_acc) if first_call else sum_ref[...]

    block = table[chip * per_chip + position]
    columns = pl.ds(pl.multiple_of(column * BLK, BLK), BLK)
    last = block // 2
    in_prompt = block < prompt_blocks
    seg_tile = (prompt_blocks + (block - prompt_blocks) // cont_blocks * cont_blocks) // 2
    full = jnp.where(in_prompt, last, prompt_tiles + last - seg_tile)

    def tile_of(i):
        return jnp.where(i < prompt_tiles, jnp.minimum(i, last), i - prompt_tiles + seg_tile)

    def key_rows(tile):
        return pl.ds(pl.multiple_of(tile * TILE, TILE), TILE)

    for h in range(heads):
        rq[0:size, h * BLK : (h + 1) * BLK] = q_ref[h * size : (h + 1) * size, columns]
    rq[size : 2 * size, :] = jnp.zeros((size, lanes), BF)

    def scores(tile):
        return dot(kv_c[key_rows(tile), :], rq[...])

    def fold(values):
        return jnp.max(values.reshape(TILE // 8, 8, lanes), 0)

    def first_pass(i, top):
        part = scores(tile_of(i))
        s_scr[i] = part
        return jnp.maximum(top, fold(part))

    top = lax.fori_loop(0, full, first_pass, jnp.full((8, lanes), -1e30, F32))
    part = scores(last)
    key_at = last * TILE + lax.broadcasted_iota(jnp.int32, (TILE, lanes), 0)
    row_at = block * BLK + lax.rem(lax.broadcasted_iota(jnp.int32, (TILE, lanes), 1), BLK)
    part = jnp.where(key_at <= row_at, part, -1e30)
    s_scr[full] = part
    top = jnp.max(jnp.maximum(top, fold(part)), 0, keepdims=True)

    o_acc[...] = jnp.zeros_like(o_acc)

    def second_pass(i, carry):
        p = jnp.exp2(s_scr[i] - top).astype(BF)
        p_scr[i] = p
        o_acc[...] += dot(kv_t[jnp.where(i == full, last, tile_of(i)), size : 2 * size + 16, :], p)
        return carry

    lax.fori_loop(0, full + 1, second_pass, 0)

    inverse = 1.0 / o_acc[size : size + 1, :]
    mixed = o_acc[0:size, :] * inverse
    grads = []
    for h in range(heads):
        at = slice(h * BLK, (h + 1) * BLK)
        mix_ref[h * size : (h + 1) * size, :] = mixed[:, at].astype(BF)
        grads.append(do_ref[h * size : (h + 1) * size, columns])
    scaled = (jnp.concatenate(grads, 1) * inverse).astype(BF)
    delta = jnp.sum(mixed * scaled.astype(F32), 0, keepdims=True)
    rd[0:size, :] = jnp.zeros((size, lanes), BF)
    rd[size : 2 * size, :] = scaled
    rqt[...] = rq[...].T
    rdt[...] = rd[...].T
    dq_acc[...] = jnp.zeros_like(dq_acc)

    def third_pass(i, carry):
        tile = jnp.where(i == full, last, tile_of(i))
        p = p_scr[i]
        d_probs = dot(kv_c[key_rows(tile), :], rd[...])
        ds = (p.astype(F32) * (d_probs - delta)).astype(BF)
        dq_acc[...] += dot(kv_t[tile, 0:size, :], ds)
        dkv_acc[key_rows(tile), :] += dot(p, rdt[...]) + dot(ds, rqt[...])
        return carry

    lax.fori_loop(0, full + 1, third_pass, 0)

    cosine, sine = cos_ref[:, columns], sin_ref[:, columns]
    for h in range(heads):
        part = dq_acc[:, h * BLK : (h + 1) * BLK] * 0.125
        dq_ref[h * size : (h + 1) * size, :] = turn(part, cosine, -sine).astype(BF)

    @pl.when((step == pl.num_programs(0) - 1) & (group == pl.num_programs(1) - 1))
    def _():
        if not last_call:
            outs[0][...] = dkv_acc[...]
            return
        scale = jnp.where(
            lax.broadcasted_iota(jnp.int32, (BLK, 2 * size), 1) < size, F32(LN2), F32(1.0)
        )

        def rows_of(slot):
            return (dkv_acc[block_rows(table[slot]), :] * scale).astype(BF)

        if len(outs) == 1:

            def give_block(slot, carry):
                outs[0][block_rows(slot), :] = rows_of(slot)
                return carry

            lax.fori_loop(0, blocks, give_block, 0)
            return
        per_core = per_chip // 2
        for low in range(2):
            for high in range(2):
                owner = chip ^ (low + 2 * high)
                for n in range(per_core):
                    here = slice(n * BLK, (n + 1) * BLK)
                    base = owner * per_chip + n
                    outs[0][low, high, here, :] = rows_of(base + per_core * (1 - core))
                    outs[1][low, high, here, :] = rows_of(base + per_core * core)


def attention(
    table, q_t, do_t, cosine, sine, kvs, carried, start, count, per_chip, last_call, split
):
    width = q_t.shape[0]
    rows = count * BLK
    first_call = carried is None
    size = kvs[0].shape[1] // 2
    keys = sum(kv.shape[0] for kv in kvs)
    all_heads = width // size
    blocks = keys // BLK
    heads = all_heads if keys <= 4096 else 2
    lanes = heads * BLK
    cont = min(CONT, keys // 2)
    most = (keys // 2 + cont) // TILE
    tiles = keys // TILE

    def whole(dims):
        return pl.BlockSpec(dims, lambda i, j, *_: (0,) * len(dims))

    if not last_call:
        dkv_shapes = [shape((keys, 2 * size), F32)]
    elif split:
        dkv_shapes = [shape((2, 2, keys // 8, 2 * size), BF)] * 2
    else:
        dkv_shapes = [shape((keys, 2 * size), BF)]
    extra = [] if first_call else [carried]
    column = pl.BlockSpec((heads * size, q_t.shape[1]), lambda i, j, *_: (j, 0))
    out_column = pl.BlockSpec((heads * size, BLK), lambda i, j, *_: (j, i))
    return pl.pallas_call(
        functools.partial(
            attn_kernel,
            blocks=blocks,
            heads=heads,
            size=size,
            n_kv=len(kvs),
            per_chip=per_chip,
            start=start,
            split=split,
            last_call=last_call,
            first_call=first_call,
        ),
        out_shape=[shape((width, rows), BF)] * 2 + dkv_shapes,
        grid_spec=pltpu.PrefetchScalarGridSpec(
            num_scalar_prefetch=1,
            grid=(count, all_heads // heads),
            in_specs=[column, column, whole(cosine.shape), whole(cosine.shape)]
            + [whole(kv.shape) for kv in kvs]
            + [whole(e.shape) for e in extra],
            out_specs=[out_column, out_column] + [whole(s.shape) for s in dkv_shapes],
            scratch_shapes=[
                pltpu.VMEM((keys, 2 * size), BF),
                pltpu.VMEM((tiles, 2 * size + 16, TILE), BF),
                pltpu.VMEM((most, TILE, lanes), F32),
                pltpu.VMEM((most, TILE, lanes), BF),
                pltpu.VMEM((2 * size, lanes), BF),
                pltpu.VMEM((2 * size, lanes), BF),
                pltpu.VMEM((lanes, 2 * size), BF),
                pltpu.VMEM((lanes, 2 * size), BF),
                pltpu.VMEM((size + 16, lanes), F32),
                pltpu.VMEM((size, lanes), F32),
                pltpu.VMEM((keys, 2 * size), F32),
            ],
        ),
        compiler_params=pltpu.CompilerParams(
            vmem_limit_bytes=(24 if keys <= 4096 else 60) * MIB
        ),
        cost_estimate=pl.CostEstimate(
            flops=1000, bytes_accessed=1000, transcendentals=0
        ),
        name="attention",
    )(table, q_t, do_t, cosine, sine, *kvs, *extra)


def prologue_kernel(
    sc, x_hbm, xt_hbm, g_hbm, gt_hbm, gains, w_hbm, cos_ref, sin_ref, h1_ref, h2_ref, gg_ref, kv_ref, xo, xt, w_kv, sem
):
    rows = xt.shape[0]
    copies = [
        pltpu.make_async_copy(x_hbm, xo, sem.at[0]),
        pltpu.make_async_copy(xt_hbm, xt, sem.at[1]),
        pltpu.make_async_copy(w_hbm, w_kv, sem.at[2]),
        pltpu.make_async_copy(g_hbm, gg_ref.at[0:rows, :], sem.at[3]),
        pltpu.make_async_copy(gt_hbm, gg_ref.at[rows : 2 * rows, :], sem.at[4]),
    ]
    for copy in copies:
        copy.start()
    gain_one, bias_one = gains[0:1, :].astype(F32), gains[1:2, :].astype(F32)
    gain_two, bias_two = gains[2:3, :].astype(F32), gains[3:4, :].astype(F32)
    for n, x in enumerate((xo, xt)):
        copies[n].wait()
        for t in range(rows // 128):
            here = slice(n * rows + t * 128, n * rows + (t + 1) * 128)
            hat, unused = normed(x[t * 128 : (t + 1) * 128, :].astype(F32))
            h1_ref[here, :] = (hat * gain_one + bias_one).astype(BF)
            h2_ref[here, :] = (hat * gain_two + bias_two).astype(BF)
    copies[2].wait()
    raw = dot(h1_ref[...], w_kv[...])
    kv = turn(raw.T, cos_ref[...], sin_ref[...]).T.astype(BF)
    kv_ref[pl.ds(pl.multiple_of(sc[0] * rows, rows), rows), :] = kv[:rows]
    kv_ref[pl.ds(pl.multiple_of((1 - sc[0]) * rows, rows), rows), :] = kv[rows:]
    copies[3].wait()
    copies[4].wait()


def half_copies(sc, w_query, w_out, query_s, out_s, sem):
    half = out_s.shape[0]
    at = pl.ds(pl.multiple_of(sc[0] * half, 128), half)
    return [
        pltpu.make_async_copy(w_query.at[:, at], query_s, sem.at[0]),
        pltpu.make_async_copy(w_out.at[at, :], out_s, sem.at[1]),
    ]


def project_kernel(
    sc, h_ref, g_ref, cos_ref, sin_ref, w_query, w_out, q_ref, do_ref, query_s, out_s, sem, *, size
):
    copies = half_copies(sc, w_query, w_out, query_s, out_s, sem)
    for copy in copies:
        copy.start()
    cosine, sine = cos_ref[...], sin_ref[...]
    copies[0].wait()
    raw = (dot(h_ref[...], query_s[...]) * (0.125 * LOG2E)).T
    for h in range(raw.shape[0] // size):
        at = slice(h * size, (h + 1) * size)
        q_ref[at, :] = turn(raw[at], cosine, sine).astype(BF)
    copies[1].wait()
    do_ref[...] = dot(out_s[...], g_ref[...], ((1,), (1,)))


def hidden_copies(sc, piece, w_up, w_down, up_s, down_s, sems, part, n_pair):
    copies = []
    for j in range(n_pair):
        source = pl.ds(pl.multiple_of((2 * j + sc[0]) * part + piece * LANES, LANES), LANES)
        at = slice(j * LANES, (j + 1) * LANES)
        if w_up is not None:
            copies.append(
                pltpu.make_async_copy(w_up.at[:, source], up_s.at[:, at], sems.at[0])
            )
        if w_down is not None:
            copies.append(
                pltpu.make_async_copy(w_down.at[source, :], down_s.at[at, :], sems.at[1])
            )
    return copies


def piece_of(sc, n):
    return 0 if n == 0 else (2 - sc[2] if n == 1 else 1 + sc[2])


def ffn_kernel(
    sc, h_ref, g_ref, w_up, w_down, act_ref, dup_ref, *refs, n, part, n_pair
):
    up_s, down_s, grad_s, sems = refs[-4:]
    outs = refs[:-4]
    rows, width = h_ref.shape
    copies = hidden_copies(sc, piece_of(sc, n), w_up, w_down, up_s, down_s, sems, part, n_pair)
    for copy in copies[0::2] + copies[1::2]:
        copy.start()
    for copy in copies[0::2] + copies[1::2]:
        copy.wait()

    def row_tile(r, carry):
        tile = pl.ds(pl.multiple_of(r * 128, 128), 128)
        act, slope = gelu_parts(dot(h_ref[tile, :], up_s[...]))
        act_ref[tile, :] = act.astype(BF)
        d_act = dot(g_ref[tile, :], down_s[...], ((1,), (1,)))
        dup_ref[tile, :] = (d_act * slope).astype(BF)
        return carry

    lax.fori_loop(0, rows // 128, row_tile, 0, unroll=2)
    up_rows = width // n_pair
    block_rows = width // WIDE * LANES

    def give(low, high, kind, first, value):
        here = slice(first, first + value.shape[0])
        if n == 0:
            outs[1 - low][high, kind * block_rows + first : kind * block_rows + here.stop, :] = value
        else:
            outs[0][kind ^ sc[3], low, high, here, :] = value

    grad_s[0 : n_pair * LANES, :] = dot(act_ref[...], g_ref[...], ((0,), (0,))).astype(BF)
    for low in range(2):
        for high in range(2):
            chip = sc[1] ^ (low + 2 * high)
            rows_at = pl.ds(pl.multiple_of(chip * LANES, LANES), LANES)
            for b in range(width // WIDE):
                give(low, high, 0, b * LANES, grad_s[rows_at, b * WIDE : (b + 1) * WIDE])
    span = n_pair * LANES
    grad_s[:, 0:span] = dot(h_ref[...], dup_ref[...], ((0,), (0,))).astype(BF)
    for low in range(2):
        for high in range(2):
            chip = sc[1] ^ (low + 2 * high)
            rows_at = pl.ds(pl.multiple_of(chip * up_rows, 64), up_rows)
            for b in range(span // WIDE):
                give(low, high, 1, b * up_rows, grad_s[rows_at, b * WIDE : (b + 1) * WIDE])


def ffn_gradients(table, h_two, g_two, w_up, w_down, n, part, n_pair):
    rows, width = h_two.shape
    span = n_pair * LANES
    block = width // WIDE * LANES
    if n == 0:
        outs = [shape((2, 2 * block, WIDE), BF)] * 2
    else:
        outs = [shape((2, 2, 2, block, WIDE), BF)]
    return call(
        functools.partial(ffn_kernel, n=n, part=part, n_pair=n_pair),
        "ffn_gradients",
        [shape((rows, span), BF)] * 2 + outs,
        [VM, VM, HBM, HBM],
        [VM] * (2 + len(outs)),
        [
            pltpu.VMEM((width, span), BF),
            pltpu.VMEM((span, width), BF),
            pltpu.VMEM((width, width), BF),
            pltpu.SemaphoreType.DMA((2,)),
        ],
        56,
    )(table, h_two, g_two, w_up, w_down)


def late_kernel(
    sc, h_ref, dq0, dq1, mix0, mix1, got0, got1, g_ref, send_ref, keep_ref, mix_ref, dq_s, mix_s, both_s,
    *, n_pair
):
    half = mix0.shape[0]
    rows = mix0.shape[1]
    width = 2 * half
    count = rows // BLK
    own = pl.multiple_of(sc[0] * half, 128)
    other = pl.multiple_of((1 - sc[0]) * half, 128)
    for n, (mix, got, dq) in enumerate(((mix0, got0, dq0), (mix1, got1, dq1))):
        for k in range(count):
            source = slice(k * BLK, (k + 1) * BLK)
            at = pl.ds(pl.multiple_of(sc[4 + n * count + k] * BLK, BLK), BLK)
            mix_ref[:, at] = mix[:, source]
            mix_s[pl.ds(own, half), at] = mix[:, source]
            mix_s[pl.ds(other, half), at] = got[:, source]
            dq_s[:, at] = dq[:, source]
    both_s[:, 0:half] = dot(h_ref[...], dq_s[...], ((0,), (1,))).astype(BF)
    both_s[:, half:width] = dot(mix_s[...], g_ref[:, pl.ds(own, half)]).astype(BF)
    block = width // n_pair
    quarter = keep_ref.shape[3]
    unit = 48
    for low in range(2):
        for high in range(2):
            chip = sc[1] ^ (low + 2 * high)
            for first in range(2):
                ref = send_ref if first else keep_ref
                for second in range(2):
                    part = 2 * (first ^ sc[2]) + (second ^ sc[3])
                    for r in range(quarter // unit):
                        at = part * quarter + r * unit
                        col, row = at // block, at % block
                        source = pl.ds(pl.multiple_of(chip * block + row, 16), unit)
                        lane = pl.ds(pl.multiple_of(col * WIDE, WIDE), WIDE)
                        ref[second, low, high, r * unit : (r + 1) * unit, :] = both_s[source, lane]


def late_gradients(table, h_one, dqs, mixes, gots, g_two, n_pair):
    half = dqs[0].shape[0]
    width = 2 * half
    rows = h_one.shape[0]
    quarter = width // n_pair * (width // WIDE) // 4
    return call(
        functools.partial(late_kernel, n_pair=n_pair),
        "late_gradients",
        [shape((2, 2, 2, quarter, WIDE), BF)] * 2 + [shape((half, rows), BF)] * 2,
        [VM] * 8,
        [VM] * 4,
        [
            pltpu.VMEM((width, rows), BF),
            pltpu.VMEM((width, width), BF),
        ],
        16,
    )(table, h_one, *dqs, *mixes, *gots, g_two)


def out_kernel(sc, a0, a1, a2, mix_ref, x_ref, w_down, w_out, own_ref, send_ref, down_s, out_s, sems, *, part, n_pair):
    half = out_s.shape[0]
    rows = x_ref.shape[0]
    span = n_pair * LANES
    copies = [
        pltpu.make_async_copy(
            w_out.at[pl.ds(pl.multiple_of(sc[0] * half, 128), half), :], out_s, sems.at[0]
        )
    ]
    for n in range(3):
        copies += hidden_copies(
            sc, piece_of(sc, n), None, w_down, None, down_s.at[n], sems, part, n_pair
        )
    for copy in copies:
        copy.start()
    for copy in copies:
        copy.wait()
    for n in range(2):
        here = slice(n * rows, (n + 1) * rows)
        total = dot(mix_ref[:, here], out_s[...], ((0,), (0,)))
        for k, act in enumerate((a0, a1, a2)):
            total = total + dot(act[here, :], down_s[k])
        if n == 0:
            own_ref[...] = total + x_ref[...].astype(F32)
        else:
            send_ref[...] = total.astype(BF)


def hat_kernel(sc, d0, d1, d2, dq_ref, xo, xt, gains, w_up, w_query, own_ref, send_ref, sum_ref, up_s, query_s, sems, *, part, n_pair):
    half = query_s.shape[1]
    rows, width = xo.shape
    copies = [
        pltpu.make_async_copy(
            w_query.at[:, pl.ds(pl.multiple_of(sc[0] * half, 128), half)], query_s, sems.at[1]
        )
    ]
    for n in range(3):
        copies += hidden_copies(
            sc, piece_of(sc, n), w_up, None, up_s.at[n], None, sems, part, n_pair
        )
    for copy in copies:
        copy.start()
    for copy in copies:
        copy.wait()
    gain_one, gain_two = gains[0:1, :].astype(F32), gains[2:3, :].astype(F32)
    sums = [jnp.zeros((1, width), F32)] * 4
    for n, x in enumerate((xo, xt)):
        here = slice(n * rows, (n + 1) * rows)
        two = dot(d0[here, :], up_s[0], ((1,), (1,)))
        two = two + dot(d1[here, :], up_s[1], ((1,), (1,)))
        two = two + dot(d2[here, :], up_s[2], ((1,), (1,)))
        one = dot(dq_ref[:, here], query_s[...], ((0,), (1,)))
        hat, unused = normed(x[...].astype(F32))
        for k, value in enumerate((one * hat, one, two * hat, two)):
            sums[k] = sums[k] + jnp.sum(value, 0, keepdims=True)
        total = one * gain_one + two * gain_two
        if n == 0:
            own_ref[...] = total
        else:
            send_ref[...] = total.astype(BF)
    sum_ref[...] = jnp.concatenate(sums + [jnp.zeros((4, width), F32)], 0)


def last_kernel(sc, dkv_a, dkv_b, dkv_c, dkv_d, cos_ref, sin_ref, w_kv, h_ref, x_ref, gains, hat_own, hat_got, sum_ref, g_ref, grad_ref, send_ref, keep_ref, *, n_pair):
    rows, width = x_ref.shape
    dkv = sum(ref[...].astype(F32) for ref in (dkv_a, dkv_b, dkv_c, dkv_d)).T
    low_t = turn(dkv, cos_ref[:, 0:rows], -sin_ref[:, 0:rows]).astype(BF)
    low = low_t.T
    weight = dot(low_t, h_ref[0:rows, :]).T.astype(BF)
    d_kv = dot(low, w_kv[...], ((1,), (1,)))
    hat, scale = normed(x_ref[...].astype(F32))
    gain = gains[0:1, :].astype(F32)
    total = hat_own[...] + hat_got[...].astype(F32) + d_kv * gain
    grad_ref[...] = g_ref[...].astype(F32) + scale * (
        total
        - jnp.mean(total, -1, keepdims=True)
        - hat * jnp.mean(total * hat, -1, keepdims=True)
    )
    sums = jnp.concatenate(
        [
            sum_ref[0:1, :] + jnp.sum(d_kv * hat, 0, keepdims=True),
            sum_ref[1:2, :] + jnp.sum(d_kv, 0, keepdims=True),
            sum_ref[2:4, :],
            jnp.zeros((4, width), F32),
        ],
        0,
    ).astype(BF)
    part = width // (2 * n_pair)
    lanes = weight.shape[1]
    for chip in range(n_pair):
        rel = chip ^ sc[1]
        low_bit, high_bit = rel % 2, rel // 2
        blocks = []
        for core in range(2):
            at = (2 * chip + core) * part
            piece = weight[at : at + part, :]
            blocks.append(jnp.concatenate([piece[: part // 2], piece[part // 2 :]], 1))
            row = sums[:, at : at + part]
            blocks.append(jnp.concatenate([row, jnp.zeros((8, 2 * lanes - part), BF)], 1))
        block = jnp.concatenate(blocks, 0)

        @pl.when(low_bit == 1)
        def _():
            send_ref[high_bit] = block

        @pl.when(low_bit == 0)
        def _():
            keep_ref[high_bit] = block


def down_kernel(sc, a_send, a_got, send_ref, got_ref, out_ref, *, width):
    block = width // WIDE * LANES
    for k in range(3):
        for b in range(width // WIDE):
            here = slice(b * LANES, (b + 1) * LANES)
            if k == 0:
                value = a_send[here, :].astype(F32) + a_got[here, :].astype(F32)
            else:
                at = pl.ds(pl.multiple_of(sc[3] * block + b * LANES, LANES), LANES)
                mine = send_ref[at, :].astype(F32)
                value = jnp.where(sc[2] == k - 1, mine, got_ref[at, :].astype(F32))
            out_ref[k * LANES : (k + 1) * LANES, b * WIDE : (b + 1) * WIDE] = value


def up_block(sc, k, b, parity, a_send, a_got, b_send, b_got, width, part):
    block = width // WIDE * LANES
    off = b * 2 * part + parity * part
    if k == 0:
        at = pl.ds(pl.multiple_of(block + off, 32), part)
        return a_send[at, :].astype(F32) + a_got[at, :].astype(F32)
    at = pl.ds(pl.multiple_of((1 - sc[3]) * block + off, 32), part)
    return jnp.where(
        sc[2] == k - 1, b_send[at, :].astype(F32), b_got[at, :].astype(F32)
    )


def late_block(sc, b, parity, send, got, part, quarter):
    pieces = []
    for r in range(2):
        at = b * 2 * part + parity * part + r * (part // 2)
        first, second = at // (2 * quarter), at // quarter % 2
        rel = (second ^ sc[3]) * quarter + at % quarter
        source = pl.ds(pl.multiple_of(rel, 16), part // 2)
        pieces.append(
            jnp.where(
                first == sc[2], send[source, :].astype(F32), got[source, :].astype(F32)
            )
        )
    return jnp.concatenate(pieces, 0)


def pack_kernel(sc, a_send, a_got, b_send, b_got, last_send, last_got, out_ref, own_ref, *, width, part, quarter):
    for which, ref in ((1, out_ref), (0, own_ref)):
        parity = sc[0] if which == 0 else 1 - sc[0]
        at = 0
        for k in range(3):
            for b in range(2):
                ref[at : at + part, :] = up_block(
                    sc, k, b, parity, a_send, a_got, b_send, b_got, width, part
                ).astype(BF)
                at += part
        for b in range(width // WIDE):
            ref[at : at + part, :] = late_block(
                sc, b, parity, last_send, last_got, part, quarter
            ).astype(BF)
            at += part
        few = (last_send.shape[0] - 2 * quarter) // 2
        source = pl.ds(pl.multiple_of(2 * quarter + parity * few, 8), few)
        ref[at : at + few, :] = (
            last_send[source, :].astype(F32) + last_got[source, :].astype(F32)
        ).astype(BF)


def final_kernel(sc, own_ref, got_ref, up_ref, query_ref, proj_ref, kv_ref, norm_ref, *, part, n_pair):
    part_hidden = up_ref.shape[1] // (2 * n_pair)
    half = query_ref.shape[1] // 2
    for which, ref in enumerate((own_ref, got_ref)):
        core = sc[0] if which == 0 else 1 - sc[0]
        at = 0
        for k in range(3):
            for j in range(n_pair):
                lane = (2 * j + core) * part_hidden + k * LANES
                rows = slice((2 * k + j // 2) * part, (2 * k + j // 2 + 1) * part)
                cols = slice(j % 2 * LANES, (j % 2 + 1) * LANES)
                up_ref[:, pl.ds(pl.multiple_of(lane, LANES), LANES)] = ref[rows, cols].astype(F32)
        base = 6 * part
        for n in range(2 * half // LANES):
            rows = slice(base + n // 2 * part, base + (n // 2 + 1) * part)
            value = ref[rows, n % 2 * LANES : (n % 2 + 1) * LANES].astype(F32)
            to, m = (query_ref, n) if n < half // LANES else (proj_ref, n - half // LANES)
            to[:, pl.ds(pl.multiple_of(core * half + m * LANES, LANES), LANES)] = value
    base = 9 * part
    few = own_ref[base:, :].astype(F32) + got_ref[base:, :].astype(F32)
    kv_ref[0 : part // 2, :] = few[0 : part // 2, 0:LANES]
    kv_ref[part // 2 : part, :] = few[0 : part // 2, LANES:WIDE]
    norm_ref[...] = few[part // 2 : part // 2 + 8, :]


class Links:
    def __init__(self, n_grp, n_ctx):
        self.n_grp, self.n_ctx, self.n_pair = n_grp, n_ctx, n_ctx // 2
        self.small = (n_grp, n_ctx) == (4, 8)
        self.ctx = lax.axis_index("ctx")
        self.grp = lax.axis_index("grp")
        self.core = self.ctx % 2
        self.chip = self.ctx // 2
        self.groups = [[2 * z + c for z in range(self.n_pair)] for c in range(2)]

    def swap(self, value):
        return lax.ppermute(value, "ctx", [(i, i ^ 1) for i in range(self.n_ctx)])

    def permute(self, value, target):
        pairs = []
        for g in range(self.n_grp):
            for i in range(self.n_ctx):
                y, x, z, c = target(g // 2, g % 2, i // 2, i % 2)
                pairs.append((g * self.n_ctx + i, (2 * y + x) * self.n_ctx + 2 * z + c))
        return lax.ppermute(value, ("grp", "ctx"), pairs)

    def cross(self, value, stage):
        return self.permute(
            value, lambda y, x, z, c: (y, 1 - x, z, c) if c == stage else (1 - y, x, z, c)
        )

    def bit(self, stage):
        y, x = self.grp // 2, self.grp % 2
        return jnp.where(self.core == stage, x, y)

    def flip(self, value, bit):
        return self.permute(value, lambda y, x, z, c: (y, x, z ^ bit, c))

    def reduce(self, parts):
        moved = lax.all_to_all(parts, "ctx", 0, 0, axis_index_groups=self.groups)
        return lax.psum(jnp.sum(moved.astype(F32), 0).astype(BF), "grp")


def add(*values):
    return sum(value.astype(F32) for value in values).astype(BF)


def low(value):
    return value.astype(BF)


def shards_small(
    layer_input, block_table, ln1_gain, ln1_bias, ln2_gain, ln2_bias,
    w_query, w_keyval, w_out, w_up, w_down, cotangent, *, n_grp, n_ctx,
):
    links = Links(n_grp, n_ctx)
    core, chip, n_pair = links.core, links.chip, links.n_pair
    rows, width = layer_input.shape
    lanes = w_keyval.shape[1]
    size = lanes // 2
    hidden = w_up.shape[1]
    group_len = block_table.shape[1] * BLK
    part, part_hidden = width // n_ctx, hidden // n_ctx
    half = width // 2
    per_chip = 2 * rows // BLK
    table = block_table[0]
    count = rows // BLK
    gains = jnp.concatenate([ln1_gain, ln1_bias, ln2_gain, ln2_bias]).reshape(4, width)

    x_other, g_other = links.swap(layer_input), links.swap(cotangent)
    column = jnp.arange(2 * rows, dtype=jnp.int32)
    slot = chip * per_chip + lax.rem(column // BLK + core * count, per_chip)
    slots = jnp.arange(table.shape[0], dtype=jnp.int32)
    canon = jnp.sum(jnp.where(slots[:, None] == slot[None, :], table[:, None], 0), 0)
    canon = canon * BLK + column % BLK
    prompt_len = group_len // 2
    cont_span = min(CONT, prompt_len)
    position = jnp.where(
        canon < prompt_len, canon, prompt_len + (canon - prompt_len) % cont_span
    )
    cosine, sine = rope_tables(position)

    h_one, h_two, g_two, kv_low = call(
        prologue_kernel,
        "prologue",
        [shape((2 * rows, width), BF)] * 3 + [shape((2 * rows, lanes), BF)],
        [HBM] * 4 + [VM, HBM, VM, VM],
        [VM] * 4,
        [
            pltpu.VMEM((rows, width), BF),
            pltpu.VMEM((rows, width), BF),
            pltpu.VMEM((width, lanes), BF),
            pltpu.SemaphoreType.DMA((5,)),
        ],
        56,
    )(table, layer_input, x_other, cotangent, g_other, gains, w_keyval, cosine, sine)

    kv_got = links.flip(kv_low, 1)
    ffn = functools.partial(
        ffn_gradients, table, w_up=w_up, w_down=w_down, part=part_hidden, n_pair=n_pair
    )
    act_1, dup_1, b_send = ffn(h_two, g_two, n=1)
    b_send, kv_got = meet(b_send, kv_got)
    kv_near = jnp.concatenate([kv_low, kv_got], 0)
    kv_far = links.flip(kv_near, 2)
    b_got = links.cross(b_send, 0)
    act_2, dup_2, b_keep = ffn(tie(h_two, b_send, kv_near), g_two, n=2)
    act_0, dup_0, a_send, a_keep = ffn(tie(h_two, b_keep), g_two, n=0)
    a_send, kv_far = meet(a_send, kv_far)
    a_got = links.flip(a_send, 1)

    q_t, do_t = call(
        functools.partial(project_kernel, size=size),
        "project",
        [shape((half, 2 * rows), BF), shape((half, 2 * rows), F32)],
        [VM] * 4 + [HBM] * 2,
        [VM] * 2,
        [
            pltpu.VMEM((width, half), BF),
            pltpu.VMEM((half, width), BF),
            pltpu.SemaphoreType.DMA((2,)),
        ],
        16,
    )(table, tie(h_one, a_send), g_two, cosine, sine, w_query, w_out)
    q_t, b_got = meet(q_t, b_got)
    b_send = add(b_keep[1], b_got[1])
    b_got_2 = links.cross(b_send, 1)

    attend = functools.partial(
        attention, table, do_t=do_t, cosine=cosine, sine=sine, kvs=(kv_near, kv_far),
        count=count, per_chip=per_chip, split=True,
    )
    mix_0, dq_0, carried = attend(
        q_t=tie(q_t, b_send), carried=None, start=0, last_call=False
    )
    carried, a_got, b_got_2 = meet(carried, a_got, b_got_2)
    b_send = add(b_keep[0, 1], b_got[0, 1], b_got_2[1])
    b_got_3 = links.flip(b_send, 1)
    a_send = add(a_keep[1], tie(a_got, b_send)[1])
    a_got_2 = links.flip(a_send, 2)
    mix_1, dq_1, dkv_send, dkv_keep = attend(
        q_t=tie(q_t, a_send, b_send, carried), carried=carried, start=count, last_call=True
    )
    mix_0, mix_1, dkv_send, a_got_2, b_got_3 = meet(mix_0, mix_1, dkv_send, a_got_2, b_got_3)
    dkv_got = links.swap(dkv_send)
    mix_0_got, mix_1_got = links.swap(mix_0), links.swap(mix_1)
    dkv_got, mix_0_got, mix_1_got = meet(dkv_got, mix_0_got, mix_1_got)
    dkv_sends = [add(dkv_keep[at], dkv_got[at]) for at in ((1, 0), (0, 1), (1, 1))]
    dkv_gots = [links.flip(value, n + 1) for n, value in enumerate(dkv_sends)]
    late_send, late_keep, mix_own, dq_own = late_gradients(
        table, tie(h_one, *dkv_sends), (dq_0, dq_1), (mix_0, mix_1), (mix_0_got, mix_1_got), g_two, n_pair
    )
    late_got = links.cross(late_send, 0)

    w_specs = [HBM] * 2
    hat_own, hat_send, sums = call(
        functools.partial(hat_kernel, part=part_hidden, n_pair=n_pair),
        "norms",
        [shape((rows, width), F32), shape((rows, width), BF), shape((8, width), F32)],
        [VM] * 7 + w_specs,
        [VM] * 3,
        [
            pltpu.VMEM((3, width, n_pair * LANES), BF),
            pltpu.VMEM((width, half), BF),
            pltpu.SemaphoreType.DMA((2,)),
        ],
        24,
    )(
        table, dup_0, dup_1, tie(dup_2, late_send), dq_own, layer_input, x_other, gains,
        w_up, w_query,
    )
    hat_send, late_got, *dkv_gots = meet(hat_send, late_got, *dkv_gots)
    hat_got = links.swap(hat_send)
    late_send = add(late_keep[1], late_got[1])
    late_got_2 = links.cross(late_send, 1)
    b_send = add(b_keep[0, 0, 1], b_got[0, 0, 1], b_got_2[0, 1], tie(b_got_3, late_send)[1])
    b_got_4 = links.flip(b_send, 2)
    dkv_own = add(dkv_keep[0, 0], dkv_got[0, 0])
    late_send, hat_got = meet(late_send, hat_got)

    few = part // 2 + 8
    in_grad, few_send, few_keep = call(
        functools.partial(last_kernel, n_pair=n_pair),
        "last",
        [shape((rows, width), F32)] + [shape((2, 2 * few, 2 * lanes), BF)] * 2,
        [VM] * 14,
        [VM] * 3,
        [],
        16,
    )(
        table, dkv_own, *dkv_gots, tie(cosine, late_send, b_send), sine, w_keyval, h_one,
        layer_input, gains, hat_own, hat_got, sums, cotangent,
    )
    few_send, late_got_2 = meet(few_send, late_got_2)
    quarter = late_keep.shape[3]
    last_send = jnp.concatenate(
        [add(late_keep[0, 1], late_got[0, 1], late_got_2[1]), few_send], 1
    )
    last_got = links.flip(last_send, 1)
    a_sum = add(a_keep[0], a_got[0], a_got_2)
    a_got = links.cross(a_sum, 1)

    out_own, out_send = call(
        functools.partial(out_kernel, part=part_hidden, n_pair=n_pair),
        "outputs",
        [shape((rows, width), F32), shape((rows, width), BF)],
        [VM] * 5 + w_specs,
        [VM] * 2,
        [
            pltpu.VMEM((3, n_pair * LANES, width), BF),
            pltpu.VMEM((half, width), BF),
            pltpu.SemaphoreType.DMA((2,)),
        ],
        24,
    )(
        table, act_0, act_1, tie(act_2, last_send, a_sum), mix_own, layer_input, w_down, w_out,
    )
    out_send, last_got, a_got = meet(out_send, last_got, a_got)
    out_got = links.swap(out_send)
    last_keep = jnp.concatenate(
        [add(late_keep[0, 0], late_got[0, 0], late_got_2[0]), few_keep], 1
    )
    last_send = add(last_keep[1], last_got[1])
    last_got_2 = links.flip(last_send, 2)
    a_sum = add(a_sum, a_got)
    a_got = links.cross(a_sum, 0)
    out_got, b_got_4 = meet(out_got, b_got_4, a_sum, last_send)[:2]
    layer_output = low(out_own + out_got.astype(F32))
    b_sum = add(b_keep[0, 0, 0], b_got[0, 0, 0], b_got_2[0, 0], b_got_3[0], b_got_4)
    b_got = links.cross(b_sum, 1)
    last_keep = add(last_keep[0], last_got[0])
    b_got, layer_output, a_got = meet(b_got, layer_output, a_got)
    b_sum = jnp.concatenate([b_sum, b_got], 0)
    b_got = links.cross(b_sum, 0)
    last_got_2 = meet(last_got_2, b_sum)[0]
    last = add(last_keep, last_got_2)
    last_got = links.cross(last, 1)
    last_got, b_got = meet(last_got, b_got)
    last = jnp.concatenate(
        [last[:quarter], last_got[:quarter], add(last[quarter:], last_got[quarter:])], 0
    )
    last_got = links.cross(last, 0)
    total_down = call(
        functools.partial(down_kernel, width=width),
        "down", shape((part_hidden, width), F32), [VM] * 4, VM, [], 8,
    )(table, tie(a_sum, last), a_got, b_sum, b_got)
    total_down, last_got = meet(total_down, last_got)
    size_out = 9 * part + few
    other, own = call(
        functools.partial(pack_kernel, width=width, part=part, quarter=quarter),
        "pack", [shape((size_out, WIDE), BF)] * 2, [VM] * 6, [VM] * 2, [], 8,
    )(table, a_sum, a_got, b_sum, b_got, last, last_got)
    got = links.swap(other)
    total_up, total_query, total_out, total_kv, norm = call(
        functools.partial(final_kernel, part=part, n_pair=n_pair),
        "final",
        [
            shape((part, hidden), F32),
            shape((part, width), F32),
            shape((part, width), F32),
            shape((part, lanes), F32),
            shape((8, WIDE), F32),
        ],
        [VM] * 2,
        [VM] * 5,
        [],
        8,
    )(table, own, got)
    norms = [norm[n, :part] for n in range(4)]
    return (layer_output, in_grad, *norms, total_query, total_kv, total_out, total_up, total_down)


def rotate_rows(values, cosine, sine):
    return turn(values.T, cosine, sine).T


def shards(
    layer_input, block_table, ln1_gain, ln1_bias, ln2_gain, ln2_bias,
    w_query, w_keyval, w_out, w_up, w_down, cotangent, *, n_grp, n_ctx,
):
    links = Links(n_grp, n_ctx)
    core, chip, n_pair = links.core, links.chip, links.n_pair
    rows, width = layer_input.shape
    size = w_keyval.shape[1] // 2
    hidden = w_up.shape[1]
    group_len = block_table.shape[1] * BLK
    part_rows, part_hidden = width // n_ctx, hidden // n_ctx
    half_width, half_hidden = width // 2, hidden // 2
    per_chip = 2 * rows // BLK
    table = block_table[0]

    def both(own, other):
        return jnp.concatenate(
            [jnp.where(core == 0, own, other), jnp.where(core == 0, other, own)], 0
        )

    def mine(value, own_core):
        return lax.dynamic_slice_in_dim(value, own_core * rows, rows, 0)

    x_two = both(layer_input, links.swap(layer_input))
    g_two = both(cotangent, links.swap(cotangent))
    canon = (
        lax.dynamic_slice_in_dim(table, chip * per_chip, per_chip)[:, None] * BLK
        + jnp.arange(BLK, dtype=jnp.int32)[None, :]
    ).reshape(2 * rows)
    prompt_len = group_len // 2
    cont_span = min(CONT, prompt_len)
    position = jnp.where(
        canon < prompt_len, canon, prompt_len + (canon - prompt_len) % cont_span
    )
    cosine, sine = rope_tables(position)
    gain_one, gain_two = ln1_gain.astype(F32), ln2_gain.astype(F32)
    hat, scale = normed(x_two.astype(F32))
    h_one = low(hat * gain_one + ln1_bias.astype(F32))
    h_two = low(hat * gain_two + ln2_bias.astype(F32))
    kv_raw = dot(h_one, w_keyval)
    kv_low = low(
        jnp.concatenate([rotate_rows(kv_raw[:, :size], cosine, sine), kv_raw[:, size:]], -1)
    )
    kv_all = lax.all_gather(kv_low, "ctx", axis=0, axis_index_groups=links.groups, tiled=True)

    up_half = lax.dynamic_index_in_dim(
        w_up.reshape(width, n_pair, 2, part_hidden), core, 2, False
    ).reshape(width, half_hidden)
    down_half = lax.dynamic_index_in_dim(
        w_down.reshape(n_pair, 2, part_hidden, width), core, 1, False
    ).reshape(half_hidden, width)
    act, slope = gelu_parts(dot(h_two, up_half))
    act = low(act)
    grad_down = low(dot(act, g_two, ((0,), (0,))))
    total_down = links.reduce(grad_down.reshape(n_pair, part_hidden, width))
    grad_up = low(dot(g_two, down_half, ((1,), (1,))) * slope)
    grad_up_w = low(dot(h_two, grad_up, ((0,), (0,))))
    total_up = links.reduce(grad_up_w.reshape(n_pair, 2 * part_rows, half_hidden))

    query_half = lax.dynamic_slice_in_dim(w_query, core * half_width, half_width, 1)
    out_half = lax.dynamic_slice_in_dim(w_out, core * half_width, half_width, 0)
    q_raw = dot(query_half, h_one, ((0,), (1,))) * (0.125 * LOG2E)
    q_t = low(
        jax.vmap(turn, (0, None, None))(q_raw.reshape(-1, size, 2 * rows), cosine, sine)
    ).reshape(half_width, 2 * rows)
    do_t = dot(out_half, g_two, ((1,), (1,)))
    mix_t, dq_t, dkv_part = attention(
        table, q_t, do_t, cosine, sine, (kv_all,), None, 0, per_chip, per_chip, True, False
    )

    dkv_part = dkv_part.reshape(n_pair, 2, rows, 2 * size)
    dkv_own = lax.dynamic_index_in_dim(dkv_part, core, 1, False)
    dkv_got = links.swap(lax.dynamic_index_in_dim(dkv_part, 1 - core, 1, False))
    moved = lax.all_to_all(
        add(dkv_own, dkv_got), "ctx", 0, 0, axis_index_groups=links.groups
    )
    dkv = jnp.sum(moved.astype(F32), 0)
    cos_own = lax.dynamic_slice_in_dim(cosine, core * rows, rows, 1)
    sin_own = lax.dynamic_slice_in_dim(sine, core * rows, rows, 1)
    dkv_low = low(
        jnp.concatenate([rotate_rows(dkv[:, :size], cos_own, -sin_own), dkv[:, size:]], -1)
    )

    mix_got = links.swap(mix_t)
    mix_all = jnp.concatenate(
        [jnp.where(core == 0, mix_t, mix_got), jnp.where(core == 0, mix_got, mix_t)], 0
    )
    g_half = lax.dynamic_slice_in_dim(g_two, core * half_width, half_width, 1)
    grad_q_w = low(dot(h_one, dq_t, ((0,), (1,))))
    grad_out_w = low(dot(mix_all, g_half))
    late = jnp.concatenate([grad_q_w, grad_out_w], 1).reshape(n_pair, 2 * part_rows, width)
    total_late = links.reduce(late)

    out_part = dot(act, down_half) + dot(mix_t, out_half, ((0,), (0,)))
    out_got = links.swap(low(mine(out_part, 1 - core)))
    layer_output = low(layer_input.astype(F32) + mine(out_part, core) + out_got.astype(F32))

    d_two = dot(grad_up, up_half, ((1,), (1,)))
    d_one = dot(dq_t, query_half, ((0,), (1,)))
    d_kv = dot(dkv_low, w_keyval, ((1,), (1,)))
    row_core = lax.broadcasted_iota(jnp.int32, (2 * rows, 1), 0) // rows
    d_one = d_one + jnp.where(row_core == core, jnp.concatenate([d_kv, d_kv], 0), 0.0)
    sums = jnp.stack([jnp.sum(v, 0) for v in (d_one * hat, d_one, d_two * hat, d_two)])
    d_hat = d_one * gain_one + d_two * gain_two
    hat_got = links.swap(low(mine(d_hat, 1 - core)))
    d_hat = mine(d_hat, core) + hat_got.astype(F32)
    hat_own = mine(hat, core)
    in_grad = cotangent.astype(F32) + mine(scale, core) * (
        d_hat
        - jnp.mean(d_hat, -1, keepdims=True)
        - hat_own * jnp.mean(d_hat * hat_own, -1, keepdims=True)
    )

    grad_kv_w = dot(mine(h_one, core), dkv_low, ((0,), (0,)))
    sum_rows = sums.reshape(4, n_pair, 2, part_rows).transpose(1, 2, 0, 3)
    sum_rows = jnp.pad(sum_rows, ((0, 0), (0, 0), (0, 0), (0, 2 * size - part_rows)))
    few = jnp.concatenate([grad_kv_w.reshape(n_pair, 2, part_rows, 2 * size), sum_rows], 2)
    few = links.reduce(low(few).reshape(n_pair, 2 * (part_rows + 4), 2 * size))
    few = few.reshape(2, part_rows + 4, 2 * size)
    few_got = links.swap(lax.dynamic_index_in_dim(few, 1 - core, 0, False))
    few = lax.dynamic_index_in_dim(few, core, 0, False).astype(F32) + few_got.astype(F32)

    halves = jnp.concatenate(
        [total_up.reshape(2, part_rows, half_hidden), total_late.reshape(2, part_rows, width)], -1
    )
    own = lax.dynamic_index_in_dim(halves, core, 0, False)
    got = links.swap(lax.dynamic_index_in_dim(halves, 1 - core, 0, False))
    sides = jnp.stack([jnp.where(core == 0, own, got), jnp.where(core == 0, got, own)]).astype(F32)
    ups = sides[:, :, :half_hidden].reshape(2, part_rows, n_pair, part_hidden)
    total_up = ups.transpose(1, 2, 0, 3).reshape(part_rows, hidden)
    lates = sides[:, :, half_hidden:]
    total_query = lates[:, :, :half_width].transpose(1, 0, 2).reshape(part_rows, width)
    total_out = lates[:, :, half_width:].transpose(1, 0, 2).reshape(part_rows, width)
    norms = [few[part_rows + n, :part_rows] for n in range(4)]
    total_kv = few[:part_rows]
    total_down = total_down.astype(F32)
    return (layer_output, in_grad, *norms, total_query, total_kv, total_out, total_up, total_down)


def solution(mesh):
    n_grp, n_ctx = mesh.shape["grp"], mesh.shape["ctx"]
    body = shards_small if (n_grp, n_ctx) == (4, 8) else shards
    return jax.shard_map(
        functools.partial(body, n_grp=n_grp, n_ctx=n_ctx),
        mesh=mesh,
        in_specs=(P(("grp", "ctx"), None), P("grp", None))
        + (P(),) * 9
        + (P(("grp", "ctx"), None),),
        out_specs=(P(("grp", "ctx"), None),) * 2 + (P("ctx"),) * 4 + (P("ctx", None),) * 5,
        check_vma=False,
    )
```

```python
import functools

import jax
import jax.numpy as jnp
import numpy as np
from jax import lax
from jax.experimental import pallas as pl
from jax.experimental.pallas import tpu as pltpu
from jax.sharding import PartitionSpec as P

ROT = 16
HALF = ROT // 2
BLK = 128
CONT = 1024
TILE = 256
LANES = 128
WIDE = 256
EPS = 1e-05
LOG2E = 1.4426950408889634
LN2 = 0.6931471805599453
BF = jnp.bfloat16
F32 = jnp.float32
MIB = 1024 * 1024
VM = pl.BlockSpec(memory_space=pltpu.VMEM)
HBM = pl.BlockSpec(memory_space=pltpu.HBM)


def dot(left, right, dims=((1,), (0,))):
    return lax.dot_general(left, right, (dims, ((), ())), preferred_element_type=F32)


def shape(dims, dtype):
    return jax.ShapeDtypeStruct(dims, dtype)


def tie(value, *others):
    return lax.optimization_barrier((value,) + others)[0]


def meet(*values):
    return lax.optimization_barrier(values)


def rope_tables(position):
    inverse = jnp.asarray(10000.0 ** (-2.0 * np.arange(HALF) / ROT), F32)
    angles = inverse[:, None] * position.astype(F32)[None, :]
    return (jnp.cos(angles), jnp.sin(angles))


def turn(values, cosine, sine):
    first, second = values[:HALF], values[HALF:ROT]
    return jnp.concatenate(
        [first * cosine - second * sine, second * cosine + first * sine, values[ROT:]], 0
    )


def normed(values):
    shifted = values - jnp.mean(values, -1, keepdims=True)
    scale = lax.rsqrt(jnp.mean(shifted * shifted, -1, keepdims=True) + EPS)
    return (shifted * scale, scale)


def gelu_parts(value):
    cdf = 0.5 * (1.0 + lax.erf(value * 0.7071067811865476))
    pdf = jnp.exp(-0.5 * value * value) * 0.3989422804014327
    return value * cdf, cdf + value * pdf


def call(kernel, name, outs, specs, out_specs, scratch, limit, flops=1000):
    def body(table, *refs):
        kernel(scalars(table), *refs)

    made = pl.pallas_call(
        body,
        out_shape=outs,
        grid_spec=pltpu.PrefetchScalarGridSpec(
            num_scalar_prefetch=1, in_specs=specs, out_specs=out_specs, scratch_shapes=scratch
        ),
        compiler_params=pltpu.CompilerParams(vmem_limit_bytes=limit * MIB),
        cost_estimate=pl.CostEstimate(flops=flops, bytes_accessed=flops, transcendentals=0),
        name=name,
    )

    def placed(table, *values):
        return made(
            table,
            *(
                pltpu.with_memory_space_constraint(v, pltpu.HBM) if spec is HBM else v
                for v, spec in zip(values, specs)
            ),
        )

    return placed


def scalars(table):
    ctx, grp = lax.axis_index("ctx"), lax.axis_index("grp")
    per_chip = 2 * table.shape[0] // lax.axis_size("ctx")
    core, chip = lax.rem(ctx, 2), lax.div(ctx, 2)
    y, x = lax.div(grp, 2), lax.rem(grp, 2)
    blocks = [table[chip * per_chip + n] for n in range(per_chip)]
    ranks = [sum((b < a).astype(jnp.int32) for b in blocks if b is not a) for a in blocks]
    order = []
    for k in range(per_chip):
        want = k // 2 if k % 2 else per_chip - 1 - k // 2
        at = sum(jnp.where(rank == want, n, 0) for n, rank in enumerate(ranks))
        order.append(lax.rem(at + per_chip - core * (per_chip // 2), per_chip))
    return [core, chip, jnp.where(core == 0, x, y), jnp.where(core == 1, x, y)] + order


def attn_kernel(
    table, *refs, blocks, heads, size, n_kv, per_chip, start, split, last_call, first_call
):
    q_ref, do_ref, cos_ref, sin_ref = refs[:4]
    kv_refs = refs[4 : 4 + n_kv]
    refs = refs[4 + n_kv :]
    if not first_call:
        sum_ref, refs = refs[0], refs[1:]
    mix_ref, dq_ref = refs[:2]
    outs = refs[2:-11]
    kv_c, kv_t, s_scr, p_scr, rq, rd, rqt, rdt, o_acc, dq_acc, dkv_acc = refs[-11:]
    step, group = pl.program_id(0), pl.program_id(1)
    core, chip, _, _, *order = scalars(table)
    if split:
        column = sum(
            jnp.where(step == n, order[start + n], 0) for n in range(per_chip // 2)
        )
        position = lax.rem(column + core * (per_chip // 2), per_chip)
    else:
        column = position = step
    lanes = heads * BLK
    prompt_blocks = blocks // 2
    prompt_tiles = prompt_blocks * BLK // TILE
    cont_blocks = min(CONT, prompt_blocks * BLK) // BLK

    def block_rows(block):
        return pl.ds(pl.multiple_of(block * BLK, BLK), BLK)

    @pl.when((step == 0) & (group == 0))
    def _():
        ones = jnp.ones((16, BLK), BF)
        share = blocks // n_kv

        for n, kv_ref in enumerate(kv_refs):

            def place_block(at, carry, n=n, kv_ref=kv_ref):
                spot = n * share + at
                owner = (spot // per_chip) ^ chip if split else spot // per_chip
                block = table[owner * per_chip + spot % per_chip]
                rows = kv_ref[block_rows(at), :]
                kv_c[block_rows(block), :] = rows
                turned = jnp.concatenate([rows.T, ones], 0)

                @pl.when(block % 2 == 0)
                def _():
                    kv_t[block // 2, :, 0:BLK] = turned

                @pl.when(block % 2 == 1)
                def _():
                    kv_t[block // 2, :, BLK:TILE] = turned

                return carry

            lax.fori_loop(0, share, place_block, 0)
        dkv_acc[...] = jnp.zeros_like(dkv_acc) if first_call else sum_ref[...]

    block = table[chip * per_chip + position]
    columns = pl.ds(pl.multiple_of(column * BLK, BLK), BLK)
    last = block // 2
    in_prompt = block < prompt_blocks
    seg_tile = (prompt_blocks + (block - prompt_blocks) // cont_blocks * cont_blocks) // 2
    full = jnp.where(in_prompt, last, prompt_tiles + last - seg_tile)

    def tile_of(i):
        return jnp.where(i < prompt_tiles, jnp.minimum(i, last), i - prompt_tiles + seg_tile)

    def key_rows(tile):
        return pl.ds(pl.multiple_of(tile * TILE, TILE), TILE)

    for h in range(heads):
        rq[0:size, h * BLK : (h + 1) * BLK] = q_ref[h * size : (h + 1) * size, columns]
    rq[size : 2 * size, :] = jnp.zeros((size, lanes), BF)

    def scores(tile):
        return dot(kv_c[key_rows(tile), :], rq[...])

    def fold(values):
        return jnp.max(values.reshape(TILE // 8, 8, lanes), 0)

    def first_pass(i, top):
        part = scores(tile_of(i))
        s_scr[i] = part
        return jnp.maximum(top, fold(part))

    top = lax.fori_loop(0, full, first_pass, jnp.full((8, lanes), -1e30, F32))
    part = scores(last)
    key_at = last * TILE + lax.broadcasted_iota(jnp.int32, (TILE, lanes), 0)
    row_at = block * BLK + lax.rem(lax.broadcasted_iota(jnp.int32, (TILE, lanes), 1), BLK)
    part = jnp.where(key_at <= row_at, part, -1e30)
    s_scr[full] = part
    top = jnp.max(jnp.maximum(top, fold(part)), 0, keepdims=True)

    o_acc[...] = jnp.zeros_like(o_acc)

    def second_pass(i, carry):
        p = jnp.exp2(s_scr[i] - top).astype(BF)
        p_scr[i] = p
        o_acc[...] += dot(kv_t[jnp.where(i == full, last, tile_of(i)), size : 2 * size + 16, :], p)
        return carry

    lax.fori_loop(0, full + 1, second_pass, 0)

    inverse = 1.0 / o_acc[size : size + 1, :]
    mixed = o_acc[0:size, :] * inverse
    grads = []
    for h in range(heads):
        at = slice(h * BLK, (h + 1) * BLK)
        mix_ref[h * size : (h + 1) * size, :] = mixed[:, at].astype(BF)
        grads.append(do_ref[h * size : (h + 1) * size, columns])
    scaled = (jnp.concatenate(grads, 1) * inverse).astype(BF)
    delta = jnp.sum(mixed * scaled.astype(F32), 0, keepdims=True)
    rd[0:size, :] = jnp.zeros((size, lanes), BF)
    rd[size : 2 * size, :] = scaled
    rqt[...] = rq[...].T
    rdt[...] = rd[...].T
    dq_acc[...] = jnp.zeros_like(dq_acc)

    def third_pass(i, carry):
        tile = jnp.where(i == full, last, tile_of(i))
        p = p_scr[i]
        d_probs = dot(kv_c[key_rows(tile), :], rd[...])
        ds = (p.astype(F32) * (d_probs - delta)).astype(BF)
        dq_acc[...] += dot(kv_t[tile, 0:size, :], ds)
        dkv_acc[key_rows(tile), :] += dot(p, rdt[...]) + dot(ds, rqt[...])
        return carry

    lax.fori_loop(0, full + 1, third_pass, 0)

    cosine, sine = cos_ref[:, columns], sin_ref[:, columns]
    for h in range(heads):
        part = dq_acc[:, h * BLK : (h + 1) * BLK] * 0.125
        dq_ref[h * size : (h + 1) * size, :] = turn(part, cosine, -sine).astype(BF)

    @pl.when((step == pl.num_programs(0) - 1) & (group == pl.num_programs(1) - 1))
    def _():
        if not last_call:
            outs[0][...] = dkv_acc[...]
            return
        scale = jnp.where(
            lax.broadcasted_iota(jnp.int32, (BLK, 2 * size), 1) < size, F32(LN2), F32(1.0)
        )

        def rows_of(slot):
            return (dkv_acc[block_rows(table[slot]), :] * scale).astype(BF)

        if len(outs) == 1:

            def give_block(slot, carry):
                outs[0][block_rows(slot), :] = rows_of(slot)
                return carry

            lax.fori_loop(0, blocks, give_block, 0)
            return
        per_core = per_chip // 2
        for low in range(2):
            for high in range(2):
                owner = chip ^ (low + 2 * high)
                for n in range(per_core):
                    here = slice(n * BLK, (n + 1) * BLK)
                    base = owner * per_chip + n
                    outs[0][low, high, here, :] = rows_of(base + per_core * (1 - core))
                    outs[1][low, high, here, :] = rows_of(base + per_core * core)


def attention(
    table, q_t, do_t, cosine, sine, kvs, carried, start, count, per_chip, last_call, split
):
    width = q_t.shape[0]
    rows = count * BLK
    first_call = carried is None
    size = kvs[0].shape[1] // 2
    keys = sum(kv.shape[0] for kv in kvs)
    all_heads = width // size
    blocks = keys // BLK
    heads = all_heads if keys <= 4096 else 2
    lanes = heads * BLK
    cont = min(CONT, keys // 2)
    most = (keys // 2 + cont) // TILE
    tiles = keys // TILE

    def whole(dims):
        return pl.BlockSpec(dims, lambda i, j, *_: (0,) * len(dims))

    if not last_call:
        dkv_shapes = [shape((keys, 2 * size), F32)]
    elif split:
        dkv_shapes = [shape((2, 2, keys // 8, 2 * size), BF)] * 2
    else:
        dkv_shapes = [shape((keys, 2 * size), BF)]
    extra = [] if first_call else [carried]
    column = pl.BlockSpec((heads * size, q_t.shape[1]), lambda i, j, *_: (j, 0))
    out_column = pl.BlockSpec((heads * size, BLK), lambda i, j, *_: (j, i))
    return pl.pallas_call(
        functools.partial(
            attn_kernel,
            blocks=blocks,
            heads=heads,
            size=size,
            n_kv=len(kvs),
            per_chip=per_chip,
            start=start,
            split=split,
            last_call=last_call,
            first_call=first_call,
        ),
        out_shape=[shape((width, rows), BF)] * 2 + dkv_shapes,
        grid_spec=pltpu.PrefetchScalarGridSpec(
            num_scalar_prefetch=1,
            grid=(count, all_heads // heads),
            in_specs=[column, column, whole(cosine.shape), whole(cosine.shape)]
            + [whole(kv.shape) for kv in kvs]
            + [whole(e.shape) for e in extra],
            out_specs=[out_column, out_column] + [whole(s.shape) for s in dkv_shapes],
            scratch_shapes=[
                pltpu.VMEM((keys, 2 * size), BF),
                pltpu.VMEM((tiles, 2 * size + 16, TILE), BF),
                pltpu.VMEM((most, TILE, lanes), F32),
                pltpu.VMEM((most, TILE, lanes), BF),
                pltpu.VMEM((2 * size, lanes), BF),
                pltpu.VMEM((2 * size, lanes), BF),
                pltpu.VMEM((lanes, 2 * size), BF),
                pltpu.VMEM((lanes, 2 * size), BF),
                pltpu.VMEM((size + 16, lanes), F32),
                pltpu.VMEM((size, lanes), F32),
                pltpu.VMEM((keys, 2 * size), F32),
            ],
        ),
        compiler_params=pltpu.CompilerParams(
            vmem_limit_bytes=(24 if keys <= 4096 else 60) * MIB
        ),
        cost_estimate=pl.CostEstimate(
            flops=1000, bytes_accessed=1000, transcendentals=0
        ),
        name="attention",
    )(table, q_t, do_t, cosine, sine, *kvs, *extra)


def prologue_kernel(
    sc, x_hbm, xt, g_hbm, gt, gains, w_hbm, cos_ref, sin_ref, h1_ref, h2_ref, gg_ref, kv_ref, xo, w_kv, sem
):
    rows = xt.shape[0]
    copies = [
        pltpu.make_async_copy(x_hbm, xo, sem.at[0]),
        pltpu.make_async_copy(w_hbm, w_kv, sem.at[1]),
        pltpu.make_async_copy(g_hbm, gg_ref.at[0:rows, :], sem.at[2]),
    ]
    for copy in copies:
        copy.start()
    gg_ref[rows : 2 * rows, :] = gt[...]
    gain_one, bias_one = gains[0:1, :].astype(F32), gains[1:2, :].astype(F32)
    gain_two, bias_two = gains[2:3, :].astype(F32), gains[3:4, :].astype(F32)
    for n, x in ((1, xt), (0, xo)):
        if n == 0:
            copies[0].wait()
        for t in range(rows // 128):
            here = slice(n * rows + t * 128, n * rows + (t + 1) * 128)
            hat, unused = normed(x[t * 128 : (t + 1) * 128, :].astype(F32))
            h1_ref[here, :] = (hat * gain_one + bias_one).astype(BF)
            h2_ref[here, :] = (hat * gain_two + bias_two).astype(BF)
    copies[1].wait()
    raw = dot(h1_ref[...], w_kv[...])
    kv = turn(raw.T, cos_ref[...], sin_ref[...]).T.astype(BF)
    kv_ref[pl.ds(pl.multiple_of(sc[0] * rows, rows), rows), :] = kv[:rows]
    kv_ref[pl.ds(pl.multiple_of((1 - sc[0]) * rows, rows), rows), :] = kv[rows:]
    copies[2].wait()


def half_copies(sc, w_query, w_out, query_s, out_s, sem):
    half = out_s.shape[0]
    at = pl.ds(pl.multiple_of(sc[0] * half, 128), half)
    return [
        pltpu.make_async_copy(w_query.at[:, at], query_s, sem.at[0]),
        pltpu.make_async_copy(w_out.at[at, :], out_s, sem.at[1]),
    ]


def project_kernel(
    sc, h_ref, g_ref, cos_ref, sin_ref, w_query, w_out, q_ref, do_ref, query_s, out_s, sem, *, size
):
    copies = half_copies(sc, w_query, w_out, query_s, out_s, sem)
    for copy in copies:
        copy.start()
    cosine, sine = cos_ref[...], sin_ref[...]
    copies[0].wait()
    raw = (dot(h_ref[...], query_s[...]) * (0.125 * LOG2E)).T
    for h in range(raw.shape[0] // size):
        at = slice(h * size, (h + 1) * size)
        q_ref[at, :] = turn(raw[at], cosine, sine).astype(BF)
    copies[1].wait()
    do_ref[...] = dot(out_s[...], g_ref[...], ((1,), (1,)))


def hidden_copies(sc, piece, w_up, w_down, up_s, down_s, sems, part, n_pair):
    copies = []
    for j in range(n_pair):
        source = pl.ds(pl.multiple_of((2 * j + sc[0]) * part + piece * LANES, LANES), LANES)
        at = slice(j * LANES, (j + 1) * LANES)
        if w_up is not None:
            copies.append(
                pltpu.make_async_copy(w_up.at[:, source], up_s.at[:, at], sems.at[0])
            )
        if w_down is not None:
            copies.append(
                pltpu.make_async_copy(w_down.at[source, :], down_s.at[at, :], sems.at[1])
            )
    return copies


def piece_of(sc, n):
    return 0 if n == 0 else (2 - sc[2] if n == 1 else 1 + sc[2])


def ffn_kernel(
    sc, h_ref, g_ref, w_up, w_down, act_ref, dup_ref, *refs, n, part, n_pair
):
    up_s, down_s, grad_s, sems = refs[-4:]
    outs = refs[:-4]
    rows, width = h_ref.shape
    copies = hidden_copies(sc, piece_of(sc, n), w_up, w_down, up_s, down_s, sems, part, n_pair)
    for copy in copies[0::2] + copies[1::2]:
        copy.start()
    for copy in copies[0::2] + copies[1::2]:
        copy.wait()

    def row_tile(r, carry):
        tile = pl.ds(pl.multiple_of(r * 128, 128), 128)
        act, slope = gelu_parts(dot(h_ref[tile, :], up_s[...]))
        act_ref[tile, :] = act.astype(BF)
        d_act = dot(g_ref[tile, :], down_s[...], ((1,), (1,)))
        dup_ref[tile, :] = (d_act * slope).astype(BF)
        return carry

    lax.fori_loop(0, rows // 128, row_tile, 0, unroll=2)
    up_rows = width // n_pair
    block_rows = width // WIDE * LANES

    def give(low, high, kind, first, value):
        here = slice(first, first + value.shape[0])
        if n == 0:
            outs[1 - low][high, kind * block_rows + first : kind * block_rows + here.stop, :] = value
        else:
            outs[0][kind ^ sc[3], low, high, here, :] = value

    grad_s[0 : n_pair * LANES, :] = dot(act_ref[...], g_ref[...], ((0,), (0,))).astype(BF)
    for low in range(2):
        for high in range(2):
            chip = sc[1] ^ (low + 2 * high)
            rows_at = pl.ds(pl.multiple_of(chip * LANES, LANES), LANES)
            for b in range(width // WIDE):
                give(low, high, 0, b * LANES, grad_s[rows_at, b * WIDE : (b + 1) * WIDE])
    span = n_pair * LANES
    grad_s[:, 0:span] = dot(h_ref[...], dup_ref[...], ((0,), (0,))).astype(BF)
    for low in range(2):
        for high in range(2):
            chip = sc[1] ^ (low + 2 * high)
            rows_at = pl.ds(pl.multiple_of(chip * up_rows, 64), up_rows)
            for b in range(span // WIDE):
                give(low, high, 1, b * up_rows, grad_s[rows_at, b * WIDE : (b + 1) * WIDE])


def ffn_gradients(table, h_two, g_two, w_up, w_down, n, part, n_pair):
    rows, width = h_two.shape
    span = n_pair * LANES
    block = width // WIDE * LANES
    if n == 0:
        outs = [shape((2, 2 * block, WIDE), BF)] * 2
    else:
        outs = [shape((2, 2, 2, block, WIDE), BF)]
    return call(
        functools.partial(ffn_kernel, n=n, part=part, n_pair=n_pair),
        "ffn_gradients",
        [shape((rows, span), BF)] * 2 + outs,
        [VM, VM, HBM, HBM],
        [VM] * (2 + len(outs)),
        [
            pltpu.VMEM((width, span), BF),
            pltpu.VMEM((span, width), BF),
            pltpu.VMEM((width, width), BF),
            pltpu.SemaphoreType.DMA((2,)),
        ],
        24,
    )(table, h_two, g_two, w_up, w_down)


def late_kernel(
    sc, h_ref, dq0, dq1, mix0, mix1, got0, got1, g_ref, send_ref, keep_ref, mix_ref, dq_s, mix_s, both_s,
    *, n_pair
):
    half = mix0.shape[0]
    rows = mix0.shape[1]
    width = 2 * half
    count = rows // BLK
    own = pl.multiple_of(sc[0] * half, 128)
    other = pl.multiple_of((1 - sc[0]) * half, 128)
    for n, (mix, got, dq) in enumerate(((mix0, got0, dq0), (mix1, got1, dq1))):
        for k in range(count):
            source = slice(k * BLK, (k + 1) * BLK)
            at = pl.ds(pl.multiple_of(sc[4 + n * count + k] * BLK, BLK), BLK)
            mix_ref[:, at] = mix[:, source]
            mix_s[pl.ds(own, half), at] = mix[:, source]
            mix_s[pl.ds(other, half), at] = got[:, source]
            dq_s[:, at] = dq[:, source]
    both_s[:, 0:half] = dot(h_ref[...], dq_s[...], ((0,), (1,))).astype(BF)
    both_s[:, half:width] = dot(mix_s[...], g_ref[:, pl.ds(own, half)]).astype(BF)
    block = width // n_pair
    quarter = keep_ref.shape[3]
    unit = 48
    for low in range(2):
        for high in range(2):
            chip = sc[1] ^ (low + 2 * high)
            for first in range(2):
                ref = send_ref if first else keep_ref
                for second in range(2):
                    part = 2 * (first ^ sc[2]) + (second ^ sc[3])
                    for r in range(quarter // unit):
                        at = part * quarter + r * unit
                        col, row = at // block, at % block
                        source = pl.ds(pl.multiple_of(chip * block + row, 16), unit)
                        lane = pl.ds(pl.multiple_of(col * WIDE, WIDE), WIDE)
                        ref[second, low, high, r * unit : (r + 1) * unit, :] = both_s[source, lane]


def late_gradients(table, h_one, dqs, mixes, gots, g_two, n_pair):
    half = dqs[0].shape[0]
    width = 2 * half
    rows = h_one.shape[0]
    quarter = width // n_pair * (width // WIDE) // 4
    return call(
        functools.partial(late_kernel, n_pair=n_pair),
        "late_gradients",
        [shape((2, 2, 2, quarter, WIDE), BF)] * 2 + [shape((half, rows), BF)] * 2,
        [VM] * 8,
        [VM] * 4,
        [
            pltpu.VMEM((width, rows), BF),
            pltpu.VMEM((width, width), BF),
        ],
        16,
    )(table, h_one, *dqs, *mixes, *gots, g_two)


def out_kernel(sc, a0, a1, a2, mix_ref, x_ref, w_down, w_out, own_ref, send_ref, down_s, out_s, sems, *, part, n_pair):
    half = out_s.shape[0]
    rows = x_ref.shape[0]
    span = n_pair * LANES
    copies = [
        pltpu.make_async_copy(
            w_out.at[pl.ds(pl.multiple_of(sc[0] * half, 128), half), :], out_s, sems.at[0]
        )
    ]
    for n in range(3):
        copies += hidden_copies(
            sc, piece_of(sc, n), None, w_down, None, down_s.at[n], sems, part, n_pair
        )
    for copy in copies:
        copy.start()
    for copy in copies:
        copy.wait()
    for n in range(2):
        here = slice(n * rows, (n + 1) * rows)
        total = dot(mix_ref[:, here], out_s[...], ((0,), (0,)))
        for k, act in enumerate((a0, a1, a2)):
            total = total + dot(act[here, :], down_s[k])
        if n == 0:
            own_ref[...] = total + x_ref[...].astype(F32)
        else:
            send_ref[...] = total.astype(BF)


def hat_kernel(sc, d0, d1, d2, dq_ref, xo, xt, gains, w_up, w_query, own_ref, send_ref, sum_ref, up_s, query_s, sems, *, part, n_pair):
    half = query_s.shape[1]
    rows, width = xo.shape
    copies = [
        pltpu.make_async_copy(
            w_query.at[:, pl.ds(pl.multiple_of(sc[0] * half, 128), half)], query_s, sems.at[1]
        )
    ]
    for n in range(3):
        copies += hidden_copies(
            sc, piece_of(sc, n), w_up, None, up_s.at[n], None, sems, part, n_pair
        )
    for copy in copies:
        copy.start()
    for copy in copies:
        copy.wait()
    gain_one, gain_two = gains[0:1, :].astype(F32), gains[2:3, :].astype(F32)
    sums = [jnp.zeros((1, width), F32)] * 4
    for n, x in enumerate((xo, xt)):
        here = slice(n * rows, (n + 1) * rows)
        two = dot(d0[here, :], up_s[0], ((1,), (1,)))
        two = two + dot(d1[here, :], up_s[1], ((1,), (1,)))
        two = two + dot(d2[here, :], up_s[2], ((1,), (1,)))
        one = dot(dq_ref[:, here], query_s[...], ((0,), (1,)))
        hat, unused = normed(x[...].astype(F32))
        for k, value in enumerate((one * hat, one, two * hat, two)):
            sums[k] = sums[k] + jnp.sum(value, 0, keepdims=True)
        total = one * gain_one + two * gain_two
        if n == 0:
            own_ref[...] = total
        else:
            send_ref[...] = total.astype(BF)
    sum_ref[...] = jnp.concatenate(sums + [jnp.zeros((4, width), F32)], 0)


def last_kernel(sc, dkv_a, dkv_b, dkv_c, dkv_d, cos_ref, sin_ref, w_kv, h_ref, x_ref, gains, hat_own, hat_got, sum_ref, g_ref, grad_ref, send_ref, keep_ref, *, n_pair):
    rows, width = x_ref.shape
    dkv = sum(ref[...].astype(F32) for ref in (dkv_a, dkv_b, dkv_c, dkv_d)).T
    low_t = turn(dkv, cos_ref[:, 0:rows], -sin_ref[:, 0:rows]).astype(BF)
    low = low_t.T
    weight = dot(low_t, h_ref[0:rows, :]).T.astype(BF)
    d_kv = dot(low, w_kv[...], ((1,), (1,)))
    hat, scale = normed(x_ref[...].astype(F32))
    gain = gains[0:1, :].astype(F32)
    total = hat_own[...] + hat_got[...].astype(F32) + d_kv * gain
    grad_ref[...] = g_ref[...].astype(F32) + scale * (
        total
        - jnp.mean(total, -1, keepdims=True)
        - hat * jnp.mean(total * hat, -1, keepdims=True)
    )
    sums = jnp.concatenate(
        [
            sum_ref[0:1, :] + jnp.sum(d_kv * hat, 0, keepdims=True),
            sum_ref[1:2, :] + jnp.sum(d_kv, 0, keepdims=True),
            sum_ref[2:4, :],
            jnp.zeros((4, width), F32),
        ],
        0,
    ).astype(BF)
    part = width // (2 * n_pair)
    lanes = weight.shape[1]
    for chip in range(n_pair):
        rel = chip ^ sc[1]
        low_bit, high_bit = rel % 2, rel // 2
        blocks = []
        for core in range(2):
            at = (2 * chip + core) * part
            piece = weight[at : at + part, :]
            blocks.append(jnp.concatenate([piece[: part // 2], piece[part // 2 :]], 1))
            row = sums[:, at : at + part]
            blocks.append(jnp.concatenate([row, jnp.zeros((8, 2 * lanes - part), BF)], 1))
        block = jnp.concatenate(blocks, 0)

        @pl.when(low_bit == 1)
        def _():
            send_ref[high_bit] = block

        @pl.when(low_bit == 0)
        def _():
            keep_ref[high_bit] = block


def down_kernel(sc, a_send, a_got, send_ref, got_ref, out_ref, *, width):
    block = width // WIDE * LANES
    for k in range(3):
        for b in range(width // WIDE):
            here = slice(b * LANES, (b + 1) * LANES)
            if k == 0:
                value = a_send[here, :].astype(F32) + a_got[here, :].astype(F32)
            else:
                at = pl.ds(pl.multiple_of(sc[3] * block + b * LANES, LANES), LANES)
                mine = send_ref[at, :].astype(F32)
                value = jnp.where(sc[2] == k - 1, mine, got_ref[at, :].astype(F32))
            out_ref[k * LANES : (k + 1) * LANES, b * WIDE : (b + 1) * WIDE] = value


def up_block(sc, k, b, parity, a_send, a_got, b_send, b_got, width, part):
    block = width // WIDE * LANES
    off = b * 2 * part + parity * part
    if k == 0:
        at = pl.ds(pl.multiple_of(block + off, 32), part)
        return a_send[at, :].astype(F32) + a_got[at, :].astype(F32)
    at = pl.ds(pl.multiple_of((1 - sc[3]) * block + off, 32), part)
    return jnp.where(
        sc[2] == k - 1, b_send[at, :].astype(F32), b_got[at, :].astype(F32)
    )


def late_block(sc, b, parity, send, got, part, quarter):
    pieces = []
    for r in range(2):
        at = b * 2 * part + parity * part + r * (part // 2)
        first, second = at // (2 * quarter), at // quarter % 2
        rel = (second ^ sc[3]) * quarter + at % quarter
        source = pl.ds(pl.multiple_of(rel, 16), part // 2)
        pieces.append(
            jnp.where(
                first == sc[2], send[source, :].astype(F32), got[source, :].astype(F32)
            )
        )
    return jnp.concatenate(pieces, 0)


def pack_kernel(sc, a_send, a_got, b_send, b_got, last_send, last_got, out_ref, own_ref, *, width, part, quarter):
    for which, ref in ((1, out_ref), (0, own_ref)):
        parity = sc[0] if which == 0 else 1 - sc[0]
        at = 0
        for k in range(3):
            for b in range(2):
                ref[at : at + part, :] = up_block(
                    sc, k, b, parity, a_send, a_got, b_send, b_got, width, part
                ).astype(BF)
                at += part
        for b in range(width // WIDE):
            ref[at : at + part, :] = late_block(
                sc, b, parity, last_send, last_got, part, quarter
            ).astype(BF)
            at += part
        few = (last_send.shape[0] - 2 * quarter) // 2
        source = pl.ds(pl.multiple_of(2 * quarter + parity * few, 8), few)
        ref[at : at + few, :] = (
            last_send[source, :].astype(F32) + last_got[source, :].astype(F32)
        ).astype(BF)


def final_kernel(sc, own_ref, got_ref, up_ref, query_ref, proj_ref, kv_ref, norm_ref, *, part, n_pair):
    part_hidden = up_ref.shape[1] // (2 * n_pair)
    half = query_ref.shape[1] // 2
    for which, ref in enumerate((own_ref, got_ref)):
        core = sc[0] if which == 0 else 1 - sc[0]
        at = 0
        for k in range(3):
            for j in range(n_pair):
                lane = (2 * j + core) * part_hidden + k * LANES
                rows = slice((2 * k + j // 2) * part, (2 * k + j // 2 + 1) * part)
                cols = slice(j % 2 * LANES, (j % 2 + 1) * LANES)
                up_ref[:, pl.ds(pl.multiple_of(lane, LANES), LANES)] = ref[rows, cols].astype(F32)
        base = 6 * part
        for n in range(2 * half // LANES):
            rows = slice(base + n // 2 * part, base + (n // 2 + 1) * part)
            value = ref[rows, n % 2 * LANES : (n % 2 + 1) * LANES].astype(F32)
            to, m = (query_ref, n) if n < half // LANES else (proj_ref, n - half // LANES)
            to[:, pl.ds(pl.multiple_of(core * half + m * LANES, LANES), LANES)] = value
    base = 9 * part
    few = own_ref[base:, :].astype(F32) + got_ref[base:, :].astype(F32)
    kv_ref[0 : part // 2, :] = few[0 : part // 2, 0:LANES]
    kv_ref[part // 2 : part, :] = few[0 : part // 2, LANES:WIDE]
    norm_ref[...] = few[part // 2 : part // 2 + 8, :]


class Links:
    def __init__(self, n_grp, n_ctx):
        self.n_grp, self.n_ctx, self.n_pair = n_grp, n_ctx, n_ctx // 2
        self.small = (n_grp, n_ctx) == (4, 8)
        self.ctx = lax.axis_index("ctx")
        self.grp = lax.axis_index("grp")
        self.core = self.ctx % 2
        self.chip = self.ctx // 2
        self.groups = [[2 * z + c for z in range(self.n_pair)] for c in range(2)]

    def swap(self, value):
        return lax.ppermute(value, "ctx", [(i, i ^ 1) for i in range(self.n_ctx)])

    def permute(self, value, target):
        pairs = []
        for g in range(self.n_grp):
            for i in range(self.n_ctx):
                y, x, z, c = target(g // 2, g % 2, i // 2, i % 2)
                pairs.append((g * self.n_ctx + i, (2 * y + x) * self.n_ctx + 2 * z + c))
        return lax.ppermute(value, ("grp", "ctx"), pairs)

    def cross(self, value, stage):
        return self.permute(
            value, lambda y, x, z, c: (y, 1 - x, z, c) if c == stage else (1 - y, x, z, c)
        )

    def bit(self, stage):
        y, x = self.grp // 2, self.grp % 2
        return jnp.where(self.core == stage, x, y)

    def flip(self, value, bit):
        return self.permute(value, lambda y, x, z, c: (y, x, z ^ bit, c))

    def reduce(self, parts):
        moved = lax.all_to_all(parts, "ctx", 0, 0, axis_index_groups=self.groups)
        return lax.psum(jnp.sum(moved.astype(F32), 0).astype(BF), "grp")


def add(*values):
    return sum(value.astype(F32) for value in values).astype(BF)


def low(value):
    return value.astype(BF)


def shards_small(
    layer_input, block_table, ln1_gain, ln1_bias, ln2_gain, ln2_bias,
    w_query, w_keyval, w_out, w_up, w_down, cotangent, *, n_grp, n_ctx,
):
    links = Links(n_grp, n_ctx)
    core, chip, n_pair = links.core, links.chip, links.n_pair
    rows, width = layer_input.shape
    lanes = w_keyval.shape[1]
    size = lanes // 2
    hidden = w_up.shape[1]
    group_len = block_table.shape[1] * BLK
    part, part_hidden = width // n_ctx, hidden // n_ctx
    half = width // 2
    per_chip = 2 * rows // BLK
    table = block_table[0]
    count = rows // BLK
    gains = jnp.concatenate([ln1_gain, ln1_bias, ln2_gain, ln2_bias]).reshape(4, width)

    x_other, g_other = links.swap(layer_input), links.swap(cotangent)
    column = jnp.arange(2 * rows, dtype=jnp.int32)
    slot = chip * per_chip + lax.rem(column // BLK + core * count, per_chip)
    slots = jnp.arange(table.shape[0], dtype=jnp.int32)
    canon = jnp.sum(jnp.where(slots[:, None] == slot[None, :], table[:, None], 0), 0)
    canon = canon * BLK + column % BLK
    prompt_len = group_len // 2
    cont_span = min(CONT, prompt_len)
    position = jnp.where(
        canon < prompt_len, canon, prompt_len + (canon - prompt_len) % cont_span
    )
    cosine, sine = rope_tables(position)

    h_one, h_two, g_two, kv_low = call(
        prologue_kernel,
        "prologue",
        [shape((2 * rows, width), BF)] * 3 + [shape((2 * rows, lanes), BF)],
        [HBM, VM, HBM, VM, VM, HBM, VM, VM],
        [VM] * 4,
        [
            pltpu.VMEM((rows, width), BF),
            pltpu.VMEM((width, lanes), BF),
            pltpu.SemaphoreType.DMA((3,)),
        ],
        16,
    )(table, layer_input, x_other, cotangent, g_other, gains, w_keyval, cosine, sine)

    kv_got = links.flip(kv_low, 1)
    ffn = functools.partial(
        ffn_gradients, table, w_up=w_up, w_down=w_down, part=part_hidden, n_pair=n_pair
    )
    act_1, dup_1, b_send = ffn(h_two, g_two, n=1)
    b_send, kv_got = meet(b_send, kv_got)
    kv_near = jnp.concatenate([kv_low, kv_got], 0)
    kv_far = links.flip(kv_near, 2)
    b_got = links.cross(b_send, 0)
    act_2, dup_2, b_keep = ffn(tie(h_two, b_send, kv_near), g_two, n=2)
    act_0, dup_0, a_send, a_keep = ffn(tie(h_two, b_keep), g_two, n=0)
    a_send, kv_far = meet(a_send, kv_far)
    a_got = links.flip(a_send, 1)

    q_t, do_t = call(
        functools.partial(project_kernel, size=size),
        "project",
        [shape((half, 2 * rows), BF), shape((half, 2 * rows), F32)],
        [VM] * 4 + [HBM] * 2,
        [VM] * 2,
        [
            pltpu.VMEM((width, half), BF),
            pltpu.VMEM((half, width), BF),
            pltpu.SemaphoreType.DMA((2,)),
        ],
        16,
    )(table, tie(h_one, a_send), g_two, cosine, sine, w_query, w_out)
    q_t, b_got = meet(q_t, b_got)
    b_send = add(b_keep[1], b_got[1])
    b_got_2 = links.cross(b_send, 1)

    attend = functools.partial(
        attention, table, do_t=do_t, cosine=cosine, sine=sine, kvs=(kv_near, kv_far),
        count=count, per_chip=per_chip, split=True,
    )
    mix_0, dq_0, carried = attend(
        q_t=tie(q_t, b_send), carried=None, start=0, last_call=False
    )
    carried, a_got, b_got_2 = meet(carried, a_got, b_got_2)
    b_send = add(b_keep[0, 1], b_got[0, 1], b_got_2[1])
    b_got_3 = links.flip(b_send, 1)
    a_send = add(a_keep[1], tie(a_got, b_send)[1])
    a_got_2 = links.flip(a_send, 2)
    mix_1, dq_1, dkv_send, dkv_keep = attend(
        q_t=tie(q_t, a_send, b_send, carried), carried=carried, start=count, last_call=True
    )
    mix_0, mix_1, dkv_send, a_got_2, b_got_3 = meet(mix_0, mix_1, dkv_send, a_got_2, b_got_3)
    dkv_got = links.swap(dkv_send)
    mix_0_got, mix_1_got = links.swap(mix_0), links.swap(mix_1)
    dkv_got, mix_0_got, mix_1_got = meet(dkv_got, mix_0_got, mix_1_got)
    dkv_sends = [add(dkv_keep[at], dkv_got[at]) for at in ((1, 0), (0, 1), (1, 1))]
    dkv_gots = [links.flip(value, n + 1) for n, value in enumerate(dkv_sends)]
    a_sum = add(a_keep[0], a_got[0], tie(a_got_2, *dkv_sends))
    a_got = links.cross(a_sum, 1)
    late_send, late_keep, mix_own, dq_own = late_gradients(
        table, tie(h_one, a_sum, *dkv_sends), (dq_0, dq_1), (mix_0, mix_1), (mix_0_got, mix_1_got), g_two, n_pair
    )
    late_got = links.cross(late_send, 0)
    b_send = add(b_keep[0, 0, 1], b_got[0, 0, 1], b_got_2[0, 1], tie(b_got_3, late_send)[1])
    b_got_4 = links.flip(b_send, 2)

    w_specs = [HBM] * 2
    hat_own, hat_send, sums = call(
        functools.partial(hat_kernel, part=part_hidden, n_pair=n_pair),
        "norms",
        [shape((rows, width), F32), shape((rows, width), BF), shape((8, width), F32)],
        [VM] * 7 + w_specs,
        [VM] * 3,
        [
            pltpu.VMEM((3, width, n_pair * LANES), BF),
            pltpu.VMEM((width, half), BF),
            pltpu.SemaphoreType.DMA((2,)),
        ],
        24,
    )(
        table, dup_0, dup_1, tie(dup_2, b_send), dq_own, layer_input, x_other, gains,
        w_up, w_query,
    )
    hat_send, late_got, a_got, *dkv_gots = meet(hat_send, late_got, a_got, *dkv_gots)
    hat_got = links.swap(hat_send)
    late_send = add(late_keep[1], late_got[1])
    late_got_2 = links.cross(late_send, 1)
    a_sum = add(a_sum, tie(a_got, late_send))
    a_got = links.cross(a_sum, 0)
    dkv_own = add(dkv_keep[0, 0], dkv_got[0, 0])
    a_sum, hat_got = meet(a_sum, hat_got)

    few = part // 2 + 8
    in_grad, few_send, few_keep = call(
        functools.partial(last_kernel, n_pair=n_pair),
        "last",
        [shape((rows, width), F32)] + [shape((2, 2 * few, 2 * lanes), BF)] * 2,
        [VM] * 14,
        [VM] * 3,
        [],
        16,
    )(
        table, dkv_own, *dkv_gots, tie(cosine, a_sum), sine, w_keyval, h_one,
        layer_input, gains, hat_own, hat_got, sums, cotangent,
    )
    few_send, late_got_2, b_got_4 = meet(few_send, late_got_2, b_got_4)
    quarter = late_keep.shape[3]
    last_send = jnp.concatenate(
        [add(late_keep[0, 1], late_got[0, 1], late_got_2[1]), few_send], 1
    )
    last_got = links.flip(last_send, 1)
    b_sum = add(
        b_keep[0, 0, 0], b_got[0, 0, 0], b_got_2[0, 0], b_got_3[0], tie(b_got_4, last_send)
    )
    b_got = links.cross(b_sum, 1)

    out_own, out_send = call(
        functools.partial(out_kernel, part=part_hidden, n_pair=n_pair),
        "outputs",
        [shape((rows, width), F32), shape((rows, width), BF)],
        [VM] * 5 + w_specs,
        [VM] * 2,
        [
            pltpu.VMEM((3, n_pair * LANES, width), BF),
            pltpu.VMEM((half, width), BF),
            pltpu.SemaphoreType.DMA((2,)),
        ],
        24,
    )(
        table, act_0, act_1, tie(act_2, b_sum), mix_own, layer_input, w_down, w_out,
    )
    out_send, last_got, a_got, b_got = meet(out_send, last_got, a_got, b_got)
    out_got = links.swap(out_send)
    last_keep = jnp.concatenate(
        [add(late_keep[0, 0], late_got[0, 0], late_got_2[0]), few_keep], 1
    )
    last_send = add(last_keep[1], last_got[1])
    last_got_2 = links.flip(last_send, 2)
    b_sum = jnp.concatenate([b_sum, b_got], 0)
    b_got = links.cross(tie(b_sum, last_send), 0)
    out_got = tie(out_got, b_sum, last_send)
    layer_output = low(out_own + out_got.astype(F32))
    last_got_2, b_got, layer_output = meet(last_got_2, b_got, layer_output)
    last = add(last_keep[0], last_got[0], last_got_2)
    last_got = links.cross(last, 1)
    total_down = call(
        functools.partial(down_kernel, width=width),
        "down", shape((part_hidden, width), F32), [VM] * 4, VM, [], 8,
    )(table, tie(a_sum, last), a_got, b_sum, b_got)
    total_down, last_got = meet(total_down, last_got)
    last = jnp.concatenate(
        [last[:quarter], last_got[:quarter], add(last[quarter:], last_got[quarter:])], 0
    )
    last_got = links.cross(last, 0)
    size_out = 9 * part + few
    other, own = call(
        functools.partial(pack_kernel, width=width, part=part, quarter=quarter),
        "pack", [shape((size_out, WIDE), BF)] * 2, [VM] * 6, [VM] * 2, [], 8,
    )(table, a_sum, a_got, b_sum, b_got, last, last_got)
    got = links.swap(other)
    total_up, total_query, total_out, total_kv, norm = call(
        functools.partial(final_kernel, part=part, n_pair=n_pair),
        "final",
        [
            shape((part, hidden), F32),
            shape((part, width), F32),
            shape((part, width), F32),
            shape((part, lanes), F32),
            shape((8, WIDE), F32),
        ],
        [VM] * 2,
        [VM] * 5,
        [],
        8,
    )(table, own, got)
    norms = [norm[n, :part] for n in range(4)]
    return (layer_output, in_grad, *norms, total_query, total_kv, total_out, total_up, total_down)


def rotate_rows(values, cosine, sine):
    return turn(values.T, cosine, sine).T


def shards(
    layer_input, block_table, ln1_gain, ln1_bias, ln2_gain, ln2_bias,
    w_query, w_keyval, w_out, w_up, w_down, cotangent, *, n_grp, n_ctx,
):
    links = Links(n_grp, n_ctx)
    core, chip, n_pair = links.core, links.chip, links.n_pair
    rows, width = layer_input.shape
    size = w_keyval.shape[1] // 2
    hidden = w_up.shape[1]
    group_len = block_table.shape[1] * BLK
    part_rows, part_hidden = width // n_ctx, hidden // n_ctx
    half_width, half_hidden = width // 2, hidden // 2
    per_chip = 2 * rows // BLK
    table = block_table[0]

    def both(own, other):
        return jnp.concatenate(
            [jnp.where(core == 0, own, other), jnp.where(core == 0, other, own)], 0
        )

    def mine(value, own_core):
        return lax.dynamic_slice_in_dim(value, own_core * rows, rows, 0)

    x_two = both(layer_input, links.swap(layer_input))
    g_two = both(cotangent, links.swap(cotangent))
    canon = (
        lax.dynamic_slice_in_dim(table, chip * per_chip, per_chip)[:, None] * BLK
        + jnp.arange(BLK, dtype=jnp.int32)[None, :]
    ).reshape(2 * rows)
    prompt_len = group_len // 2
    cont_span = min(CONT, prompt_len)
    position = jnp.where(
        canon < prompt_len, canon, prompt_len + (canon - prompt_len) % cont_span
    )
    cosine, sine = rope_tables(position)
    gain_one, gain_two = ln1_gain.astype(F32), ln2_gain.astype(F32)
    hat, scale = normed(x_two.astype(F32))
    h_one = low(hat * gain_one + ln1_bias.astype(F32))
    h_two = low(hat * gain_two + ln2_bias.astype(F32))
    kv_raw = dot(h_one, w_keyval)
    kv_low = low(
        jnp.concatenate([rotate_rows(kv_raw[:, :size], cosine, sine), kv_raw[:, size:]], -1)
    )
    kv_all = lax.all_gather(kv_low, "ctx", axis=0, axis_index_groups=links.groups, tiled=True)

    up_half = lax.dynamic_index_in_dim(
        w_up.reshape(width, n_pair, 2, part_hidden), core, 2, False
    ).reshape(width, half_hidden)
    down_half = lax.dynamic_index_in_dim(
        w_down.reshape(n_pair, 2, part_hidden, width), core, 1, False
    ).reshape(half_hidden, width)
    act, slope = gelu_parts(dot(h_two, up_half))
    act = low(act)
    grad_down = low(dot(act, g_two, ((0,), (0,))))
    total_down = links.reduce(grad_down.reshape(n_pair, part_hidden, width))
    grad_up = low(dot(g_two, down_half, ((1,), (1,))) * slope)
    grad_up_w = low(dot(h_two, grad_up, ((0,), (0,))))
    total_up = links.reduce(grad_up_w.reshape(n_pair, 2 * part_rows, half_hidden))

    query_half = lax.dynamic_slice_in_dim(w_query, core * half_width, half_width, 1)
    out_half = lax.dynamic_slice_in_dim(w_out, core * half_width, half_width, 0)
    q_raw = dot(query_half, h_one, ((0,), (1,))) * (0.125 * LOG2E)
    q_t = low(
        jax.vmap(turn, (0, None, None))(q_raw.reshape(-1, size, 2 * rows), cosine, sine)
    ).reshape(half_width, 2 * rows)
    do_t = dot(out_half, g_two, ((1,), (1,)))
    mix_t, dq_t, dkv_part = attention(
        table, q_t, do_t, cosine, sine, (kv_all,), None, 0, per_chip, per_chip, True, False
    )

    dkv_part = dkv_part.reshape(n_pair, 2, rows, 2 * size)
    dkv_own = lax.dynamic_index_in_dim(dkv_part, core, 1, False)
    dkv_got = links.swap(lax.dynamic_index_in_dim(dkv_part, 1 - core, 1, False))
    moved = lax.all_to_all(
        add(dkv_own, dkv_got), "ctx", 0, 0, axis_index_groups=links.groups
    )
    dkv = jnp.sum(moved.astype(F32), 0)
    cos_own = lax.dynamic_slice_in_dim(cosine, core * rows, rows, 1)
    sin_own = lax.dynamic_slice_in_dim(sine, core * rows, rows, 1)
    dkv_low = low(
        jnp.concatenate([rotate_rows(dkv[:, :size], cos_own, -sin_own), dkv[:, size:]], -1)
    )

    mix_got = links.swap(mix_t)
    mix_all = jnp.concatenate(
        [jnp.where(core == 0, mix_t, mix_got), jnp.where(core == 0, mix_got, mix_t)], 0
    )
    g_half = lax.dynamic_slice_in_dim(g_two, core * half_width, half_width, 1)
    grad_q_w = low(dot(h_one, dq_t, ((0,), (1,))))
    grad_out_w = low(dot(mix_all, g_half))
    late = jnp.concatenate([grad_q_w, grad_out_w], 1).reshape(n_pair, 2 * part_rows, width)
    total_late = links.reduce(late)

    out_part = dot(act, down_half) + dot(mix_t, out_half, ((0,), (0,)))
    out_got = links.swap(low(mine(out_part, 1 - core)))
    layer_output = low(layer_input.astype(F32) + mine(out_part, core) + out_got.astype(F32))

    d_two = dot(grad_up, up_half, ((1,), (1,)))
    d_one = dot(dq_t, query_half, ((0,), (1,)))
    d_kv = dot(dkv_low, w_keyval, ((1,), (1,)))
    row_core = lax.broadcasted_iota(jnp.int32, (2 * rows, 1), 0) // rows
    d_one = d_one + jnp.where(row_core == core, jnp.concatenate([d_kv, d_kv], 0), 0.0)
    sums = jnp.stack([jnp.sum(v, 0) for v in (d_one * hat, d_one, d_two * hat, d_two)])
    d_hat = d_one * gain_one + d_two * gain_two
    hat_got = links.swap(low(mine(d_hat, 1 - core)))
    d_hat = mine(d_hat, core) + hat_got.astype(F32)
    hat_own = mine(hat, core)
    in_grad = cotangent.astype(F32) + mine(scale, core) * (
        d_hat
        - jnp.mean(d_hat, -1, keepdims=True)
        - hat_own * jnp.mean(d_hat * hat_own, -1, keepdims=True)
    )

    grad_kv_w = dot(mine(h_one, core), dkv_low, ((0,), (0,)))
    sum_rows = sums.reshape(4, n_pair, 2, part_rows).transpose(1, 2, 0, 3)
    sum_rows = jnp.pad(sum_rows, ((0, 0), (0, 0), (0, 0), (0, 2 * size - part_rows)))
    few = jnp.concatenate([grad_kv_w.reshape(n_pair, 2, part_rows, 2 * size), sum_rows], 2)
    few = links.reduce(low(few).reshape(n_pair, 2 * (part_rows + 4), 2 * size))
    few = few.reshape(2, part_rows + 4, 2 * size)
    few_got = links.swap(lax.dynamic_index_in_dim(few, 1 - core, 0, False))
    few = lax.dynamic_index_in_dim(few, core, 0, False).astype(F32) + few_got.astype(F32)

    halves = jnp.concatenate(
        [total_up.reshape(2, part_rows, half_hidden), total_late.reshape(2, part_rows, width)], -1
    )
    own = lax.dynamic_index_in_dim(halves, core, 0, False)
    got = links.swap(lax.dynamic_index_in_dim(halves, 1 - core, 0, False))
    sides = jnp.stack([jnp.where(core == 0, own, got), jnp.where(core == 0, got, own)]).astype(F32)
    ups = sides[:, :, :half_hidden].reshape(2, part_rows, n_pair, part_hidden)
    total_up = ups.transpose(1, 2, 0, 3).reshape(part_rows, hidden)
    lates = sides[:, :, half_hidden:]
    total_query = lates[:, :, :half_width].transpose(1, 0, 2).reshape(part_rows, width)
    total_out = lates[:, :, half_width:].transpose(1, 0, 2).reshape(part_rows, width)
    norms = [few[part_rows + n, :part_rows] for n in range(4)]
    total_kv = few[:part_rows]
    total_down = total_down.astype(F32)
    return (layer_output, in_grad, *norms, total_query, total_kv, total_out, total_up, total_down)


def solution(mesh):
    n_grp, n_ctx = mesh.shape["grp"], mesh.shape["ctx"]
    body = shards_small if (n_grp, n_ctx) == (4, 8) else shards
    return jax.shard_map(
        functools.partial(body, n_grp=n_grp, n_ctx=n_ctx),
        mesh=mesh,
        in_specs=(P(("grp", "ctx"), None), P("grp", None))
        + (P(),) * 9
        + (P(("grp", "ctx"), None),),
        out_specs=(P(("grp", "ctx"), None),) * 2 + (P("ctx"),) * 4 + (P("ctx", None),) * 5,
        check_vma=False,
    )
```

```python
import functools

import jax
import jax.numpy as jnp
import numpy as np
from jax import lax
from jax.experimental import pallas as pl
from jax.experimental.pallas import tpu as pltpu
from jax.sharding import PartitionSpec as P

ROT = 16
HALF = ROT // 2
BLK = 128
CONT = 1024
TILE = 256
LANES = 128
WIDE = 256
EPS = 1e-05
LOG2E = 1.4426950408889634
LN2 = 0.6931471805599453
BF = jnp.bfloat16
F32 = jnp.float32
MIB = 1024 * 1024
VM = pl.BlockSpec(memory_space=pltpu.VMEM)
HBM = pl.BlockSpec(memory_space=pltpu.HBM)


def dot(left, right, dims=((1,), (0,))):
    return lax.dot_general(left, right, (dims, ((), ())), preferred_element_type=F32)


def shape(dims, dtype):
    return jax.ShapeDtypeStruct(dims, dtype)


def tie(value, *others):
    return lax.optimization_barrier((value,) + others)[0]


def meet(*values):
    return lax.optimization_barrier(values)


def rope_tables(position):
    inverse = jnp.asarray(10000.0 ** (-2.0 * np.arange(HALF) / ROT), F32)
    angles = inverse[:, None] * position.astype(F32)[None, :]
    return (jnp.cos(angles), jnp.sin(angles))


def turn(values, cosine, sine):
    first, second = values[:HALF], values[HALF:ROT]
    return jnp.concatenate(
        [first * cosine - second * sine, second * cosine + first * sine, values[ROT:]], 0
    )


def normed(values):
    shifted = values - jnp.mean(values, -1, keepdims=True)
    scale = lax.rsqrt(jnp.mean(shifted * shifted, -1, keepdims=True) + EPS)
    return (shifted * scale, scale)


def gelu_parts(value):
    cdf = 0.5 * (1.0 + lax.erf(value * 0.7071067811865476))
    pdf = jnp.exp(-0.5 * value * value) * 0.3989422804014327
    return value * cdf, cdf + value * pdf


def call(kernel, name, outs, specs, out_specs, scratch, limit, flops=1000):
    def body(table, *refs):
        kernel(scalars(table), *refs)

    made = pl.pallas_call(
        body,
        out_shape=outs,
        grid_spec=pltpu.PrefetchScalarGridSpec(
            num_scalar_prefetch=1, in_specs=specs, out_specs=out_specs, scratch_shapes=scratch
        ),
        compiler_params=pltpu.CompilerParams(vmem_limit_bytes=limit * MIB),
        cost_estimate=pl.CostEstimate(flops=flops, bytes_accessed=flops, transcendentals=0),
        name=name,
    )

    def placed(table, *values):
        return made(
            table,
            *(
                pltpu.with_memory_space_constraint(v, pltpu.HBM) if spec is HBM else v
                for v, spec in zip(values, specs)
            ),
        )

    return placed


def scalars(table):
    ctx, grp = lax.axis_index("ctx"), lax.axis_index("grp")
    per_chip = 2 * table.shape[0] // lax.axis_size("ctx")
    core, chip = lax.rem(ctx, 2), lax.div(ctx, 2)
    y, x = lax.div(grp, 2), lax.rem(grp, 2)
    blocks = [table[chip * per_chip + n] for n in range(per_chip)]
    ranks = [sum((b < a).astype(jnp.int32) for b in blocks if b is not a) for a in blocks]
    order = []
    for k in range(per_chip):
        want = k // 2 if k % 2 else per_chip - 1 - k // 2
        at = sum(jnp.where(rank == want, n, 0) for n, rank in enumerate(ranks))
        order.append(lax.rem(at + per_chip - core * (per_chip // 2), per_chip))
    return [core, chip, jnp.where(core == 0, x, y), jnp.where(core == 1, x, y)] + order


def attn_kernel(
    table, *refs, blocks, heads, size, n_kv, per_chip, start, split, last_call, first_call
):
    q_ref, do_ref, cos_ref, sin_ref = refs[:4]
    kv_refs = refs[4 : 4 + n_kv]
    refs = refs[4 + n_kv :]
    if not first_call:
        sum_ref, refs = refs[0], refs[1:]
    mix_ref, dq_ref = refs[:2]
    outs = refs[2:-11]
    kv_c, kv_t, s_scr, p_scr, rq, rd, rqt, rdt, o_acc, dq_acc, dkv_acc = refs[-11:]
    step, group = pl.program_id(0), pl.program_id(1)
    core, chip, _, _, *order = scalars(table)
    if split:
        column = sum(
            jnp.where(step == n, order[start + n], 0) for n in range(per_chip // 2)
        )
        position = lax.rem(column + core * (per_chip // 2), per_chip)
    else:
        column = position = step
    lanes = heads * BLK
    prompt_blocks = blocks // 2
    prompt_tiles = prompt_blocks * BLK // TILE
    cont_blocks = min(CONT, prompt_blocks * BLK) // BLK

    def block_rows(block):
        return pl.ds(pl.multiple_of(block * BLK, BLK), BLK)

    @pl.when((step == 0) & (group == 0))
    def _():
        ones = jnp.ones((16, BLK), BF)
        share = blocks // n_kv

        for n, kv_ref in enumerate(kv_refs):

            def place_block(at, carry, n=n, kv_ref=kv_ref):
                spot = n * share + at
                owner = (spot // per_chip) ^ chip if split else spot // per_chip
                block = table[owner * per_chip + spot % per_chip]
                rows = kv_ref[block_rows(at), :]
                kv_c[block_rows(block), :] = rows
                turned = jnp.concatenate([rows.T, ones], 0)

                @pl.when(block % 2 == 0)
                def _():
                    kv_t[block // 2, :, 0:BLK] = turned

                @pl.when(block % 2 == 1)
                def _():
                    kv_t[block // 2, :, BLK:TILE] = turned

                return carry

            lax.fori_loop(0, share, place_block, 0)
        dkv_acc[...] = jnp.zeros_like(dkv_acc) if first_call else sum_ref[...]

    block = table[chip * per_chip + position]
    columns = pl.ds(pl.multiple_of(column * BLK, BLK), BLK)
    last = block // 2
    in_prompt = block < prompt_blocks
    seg_tile = (prompt_blocks + (block - prompt_blocks) // cont_blocks * cont_blocks) // 2
    full = jnp.where(in_prompt, last, prompt_tiles + last - seg_tile)

    def tile_of(i):
        return jnp.where(i < prompt_tiles, jnp.minimum(i, last), i - prompt_tiles + seg_tile)

    def key_rows(tile):
        return pl.ds(pl.multiple_of(tile * TILE, TILE), TILE)

    for h in range(heads):
        rq[0:size, h * BLK : (h + 1) * BLK] = q_ref[h * size : (h + 1) * size, columns]
    rq[size : 2 * size, :] = jnp.zeros((size, lanes), BF)

    def scores(tile):
        return dot(kv_c[key_rows(tile), :], rq[...])

    def fold(values):
        return jnp.max(values.reshape(TILE // 8, 8, lanes), 0)

    def first_pass(i, top):
        part = scores(tile_of(i))
        s_scr[i] = part
        return jnp.maximum(top, fold(part))

    top = lax.fori_loop(0, full, first_pass, jnp.full((8, lanes), -1e30, F32))
    part = scores(last)
    key_at = last * TILE + lax.broadcasted_iota(jnp.int32, (TILE, lanes), 0)
    row_at = block * BLK + lax.rem(lax.broadcasted_iota(jnp.int32, (TILE, lanes), 1), BLK)
    part = jnp.where(key_at <= row_at, part, -1e30)
    s_scr[full] = part
    top = jnp.max(jnp.maximum(top, fold(part)), 0, keepdims=True)

    o_acc[...] = jnp.zeros_like(o_acc)

    def second_pass(i, carry):
        p = jnp.exp2(s_scr[i] - top).astype(BF)
        p_scr[i] = p
        o_acc[...] += dot(kv_t[jnp.where(i == full, last, tile_of(i)), size : 2 * size + 16, :], p)
        return carry

    lax.fori_loop(0, full + 1, second_pass, 0)

    inverse = 1.0 / o_acc[size : size + 1, :]
    mixed = o_acc[0:size, :] * inverse
    grads = []
    for h in range(heads):
        at = slice(h * BLK, (h + 1) * BLK)
        mix_ref[h * size : (h + 1) * size, :] = mixed[:, at].astype(BF)
        grads.append(do_ref[h * size : (h + 1) * size, columns])
    scaled = (jnp.concatenate(grads, 1) * inverse).astype(BF)
    delta = jnp.sum(mixed * scaled.astype(F32), 0, keepdims=True)
    rd[0:size, :] = jnp.zeros((size, lanes), BF)
    rd[size : 2 * size, :] = scaled
    rqt[...] = rq[...].T
    rdt[...] = rd[...].T
    dq_acc[...] = jnp.zeros_like(dq_acc)

    def third_pass(i, carry):
        tile = jnp.where(i == full, last, tile_of(i))
        p = p_scr[i]
        d_probs = dot(kv_c[key_rows(tile), :], rd[...])
        ds = (p.astype(F32) * (d_probs - delta)).astype(BF)
        dq_acc[...] += dot(kv_t[tile, 0:size, :], ds)
        dkv_acc[key_rows(tile), :] += dot(p, rdt[...]) + dot(ds, rqt[...])
        return carry

    lax.fori_loop(0, full + 1, third_pass, 0)

    cosine, sine = cos_ref[:, columns], sin_ref[:, columns]
    for h in range(heads):
        part = dq_acc[:, h * BLK : (h + 1) * BLK] * 0.125
        dq_ref[h * size : (h + 1) * size, :] = turn(part, cosine, -sine).astype(BF)

    @pl.when((step == pl.num_programs(0) - 1) & (group == pl.num_programs(1) - 1))
    def _():
        if not last_call:
            outs[0][...] = dkv_acc[...]
            return
        scale = jnp.where(
            lax.broadcasted_iota(jnp.int32, (BLK, 2 * size), 1) < size, F32(LN2), F32(1.0)
        )

        def rows_of(slot):
            return (dkv_acc[block_rows(table[slot]), :] * scale).astype(BF)

        if len(outs) == 1:

            def give_block(slot, carry):
                outs[0][block_rows(slot), :] = rows_of(slot)
                return carry

            lax.fori_loop(0, blocks, give_block, 0)
            return
        per_core = per_chip // 2
        for low in range(2):
            for high in range(2):
                owner = chip ^ (low + 2 * high)
                for n in range(per_core):
                    here = slice(n * BLK, (n + 1) * BLK)
                    base = owner * per_chip + n
                    outs[0][low, high, here, :] = rows_of(base + per_core * (1 - core))
                    outs[1][low, high, here, :] = rows_of(base + per_core * core)


def attention(
    table, q_t, do_t, cosine, sine, kvs, carried, start, count, per_chip, last_call, split
):
    width = q_t.shape[0]
    rows = count * BLK
    first_call = carried is None
    size = kvs[0].shape[1] // 2
    keys = sum(kv.shape[0] for kv in kvs)
    all_heads = width // size
    blocks = keys // BLK
    heads = all_heads if keys <= 4096 else 2
    lanes = heads * BLK
    cont = min(CONT, keys // 2)
    most = (keys // 2 + cont) // TILE
    tiles = keys // TILE

    def whole(dims):
        return pl.BlockSpec(dims, lambda i, j, *_: (0,) * len(dims))

    if not last_call:
        dkv_shapes = [shape((keys, 2 * size), F32)]
    elif split:
        dkv_shapes = [shape((2, 2, keys // 8, 2 * size), BF)] * 2
    else:
        dkv_shapes = [shape((keys, 2 * size), BF)]
    extra = [] if first_call else [carried]
    column = pl.BlockSpec((heads * size, q_t.shape[1]), lambda i, j, *_: (j, 0))
    out_column = pl.BlockSpec((heads * size, BLK), lambda i, j, *_: (j, i))
    return pl.pallas_call(
        functools.partial(
            attn_kernel,
            blocks=blocks,
            heads=heads,
            size=size,
            n_kv=len(kvs),
            per_chip=per_chip,
            start=start,
            split=split,
            last_call=last_call,
            first_call=first_call,
        ),
        out_shape=[shape((width, rows), BF)] * 2 + dkv_shapes,
        grid_spec=pltpu.PrefetchScalarGridSpec(
            num_scalar_prefetch=1,
            grid=(count, all_heads // heads),
            in_specs=[column, column, whole(cosine.shape), whole(cosine.shape)]
            + [whole(kv.shape) for kv in kvs]
            + [whole(e.shape) for e in extra],
            out_specs=[out_column, out_column] + [whole(s.shape) for s in dkv_shapes],
            scratch_shapes=[
                pltpu.VMEM((keys, 2 * size), BF),
                pltpu.VMEM((tiles, 2 * size + 16, TILE), BF),
                pltpu.VMEM((most, TILE, lanes), F32),
                pltpu.VMEM((most, TILE, lanes), BF),
                pltpu.VMEM((2 * size, lanes), BF),
                pltpu.VMEM((2 * size, lanes), BF),
                pltpu.VMEM((lanes, 2 * size), BF),
                pltpu.VMEM((lanes, 2 * size), BF),
                pltpu.VMEM((size + 16, lanes), F32),
                pltpu.VMEM((size, lanes), F32),
                pltpu.VMEM((keys, 2 * size), F32),
            ],
        ),
        compiler_params=pltpu.CompilerParams(
            vmem_limit_bytes=(24 if keys <= 4096 else 60) * MIB
        ),
        cost_estimate=pl.CostEstimate(
            flops=1000, bytes_accessed=1000, transcendentals=0
        ),
        name="attention",
    )(table, q_t, do_t, cosine, sine, *kvs, *extra)


def prologue_kernel(
    sc, x_hbm, xt, g_hbm, gt, gains, w_hbm, cos_ref, sin_ref, h1_ref, h2_ref, gg_ref, kv_ref, xo, w_kv, sem
):
    rows = xt.shape[0]
    copies = [
        pltpu.make_async_copy(x_hbm, xo, sem.at[0]),
        pltpu.make_async_copy(w_hbm, w_kv, sem.at[1]),
        pltpu.make_async_copy(g_hbm, gg_ref.at[0:rows, :], sem.at[2]),
    ]
    for copy in copies:
        copy.start()
    gg_ref[rows : 2 * rows, :] = gt[...]
    gain_one, bias_one = gains[0:1, :].astype(F32), gains[1:2, :].astype(F32)
    gain_two, bias_two = gains[2:3, :].astype(F32), gains[3:4, :].astype(F32)
    for n, x in ((1, xt), (0, xo)):
        if n == 0:
            copies[0].wait()
        for t in range(rows // 128):
            here = slice(n * rows + t * 128, n * rows + (t + 1) * 128)
            hat, unused = normed(x[t * 128 : (t + 1) * 128, :].astype(F32))
            h1_ref[here, :] = (hat * gain_one + bias_one).astype(BF)
            h2_ref[here, :] = (hat * gain_two + bias_two).astype(BF)
    copies[1].wait()
    raw = dot(h1_ref[...], w_kv[...])
    kv = turn(raw.T, cos_ref[...], sin_ref[...]).T.astype(BF)
    kv_ref[pl.ds(pl.multiple_of(sc[0] * rows, rows), rows), :] = kv[:rows]
    kv_ref[pl.ds(pl.multiple_of((1 - sc[0]) * rows, rows), rows), :] = kv[rows:]
    copies[2].wait()


def half_copies(sc, w_query, w_out, query_s, out_s, sem):
    half = out_s.shape[0]
    at = pl.ds(pl.multiple_of(sc[0] * half, 128), half)
    return [
        pltpu.make_async_copy(w_query.at[:, at], query_s, sem.at[0]),
        pltpu.make_async_copy(w_out.at[at, :], out_s, sem.at[1]),
    ]


def project_kernel(
    sc, h_ref, g_ref, cos_ref, sin_ref, w_query, w_out, q_ref, do_ref, query_s, out_s, sem, *, size
):
    copies = half_copies(sc, w_query, w_out, query_s, out_s, sem)
    for copy in copies:
        copy.start()
    cosine, sine = cos_ref[...], sin_ref[...]
    copies[0].wait()
    raw = (dot(h_ref[...], query_s[...]) * (0.125 * LOG2E)).T
    for h in range(raw.shape[0] // size):
        at = slice(h * size, (h + 1) * size)
        q_ref[at, :] = turn(raw[at], cosine, sine).astype(BF)
    copies[1].wait()
    do_ref[...] = dot(out_s[...], g_ref[...], ((1,), (1,)))


def hidden_copies(sc, piece, w_up, w_down, up_s, down_s, sems, part, n_pair):
    copies = []
    for j in range(n_pair):
        source = pl.ds(pl.multiple_of((2 * j + sc[0]) * part + piece * LANES, LANES), LANES)
        at = slice(j * LANES, (j + 1) * LANES)
        if w_up is not None:
            copies.append(
                pltpu.make_async_copy(w_up.at[:, source], up_s.at[:, at], sems.at[0])
            )
        if w_down is not None:
            copies.append(
                pltpu.make_async_copy(w_down.at[source, :], down_s.at[at, :], sems.at[1])
            )
    return copies


def piece_of(sc, n):
    return 0 if n == 0 else (2 - sc[2] if n == 1 else 1 + sc[2])


def ffn_kernel(
    sc, h_ref, g_ref, w_up, w_down, act_ref, dup_ref, *refs, n, part, n_pair
):
    up_s, down_s, grad_s, sems = refs[-4:]
    outs = refs[:-4]
    rows, width = h_ref.shape
    copies = hidden_copies(sc, piece_of(sc, n), w_up, w_down, up_s, down_s, sems, part, n_pair)
    for copy in copies[0::2] + copies[1::2]:
        copy.start()
    for copy in copies[0::2] + copies[1::2]:
        copy.wait()

    def row_tile(r, carry):
        tile = pl.ds(pl.multiple_of(r * 128, 128), 128)
        act, slope = gelu_parts(dot(h_ref[tile, :], up_s[...]))
        act_ref[tile, :] = act.astype(BF)
        d_act = dot(g_ref[tile, :], down_s[...], ((1,), (1,)))
        dup_ref[tile, :] = (d_act * slope).astype(BF)
        return carry

    lax.fori_loop(0, rows // 128, row_tile, 0, unroll=2)
    up_rows = width // n_pair
    block_rows = width // WIDE * LANES

    def give(low, high, kind, first, value):
        here = slice(first, first + value.shape[0])
        if n == 0:
            outs[1 - low][high, kind * block_rows + first : kind * block_rows + here.stop, :] = value
        else:
            outs[0][kind ^ sc[3], low, high, here, :] = value

    grad_s[0 : n_pair * LANES, :] = dot(act_ref[...], g_ref[...], ((0,), (0,))).astype(BF)
    for low in range(2):
        for high in range(2):
            chip = sc[1] ^ (low + 2 * high)
            rows_at = pl.ds(pl.multiple_of(chip * LANES, LANES), LANES)
            for b in range(width // WIDE):
                give(low, high, 0, b * LANES, grad_s[rows_at, b * WIDE : (b + 1) * WIDE])
    span = n_pair * LANES
    grad_s[:, 0:span] = dot(h_ref[...], dup_ref[...], ((0,), (0,))).astype(BF)
    for low in range(2):
        for high in range(2):
            chip = sc[1] ^ (low + 2 * high)
            rows_at = pl.ds(pl.multiple_of(chip * up_rows, 64), up_rows)
            for b in range(span // WIDE):
                give(low, high, 1, b * up_rows, grad_s[rows_at, b * WIDE : (b + 1) * WIDE])


def ffn_gradients(table, h_two, g_two, w_up, w_down, n, part, n_pair):
    rows, width = h_two.shape
    span = n_pair * LANES
    block = width // WIDE * LANES
    if n == 0:
        outs = [shape((2, 2 * block, WIDE), BF)] * 2
    else:
        outs = [shape((2, 2, 2, block, WIDE), BF)]
    return call(
        functools.partial(ffn_kernel, n=n, part=part, n_pair=n_pair),
        "ffn_gradients",
        [shape((rows, span), BF)] * 2 + outs,
        [VM, VM, HBM, HBM],
        [VM] * (2 + len(outs)),
        [
            pltpu.VMEM((width, span), BF),
            pltpu.VMEM((span, width), BF),
            pltpu.VMEM((width, width), BF),
            pltpu.SemaphoreType.DMA((2,)),
        ],
        24,
    )(table, h_two, g_two, w_up, w_down)


def late_kernel(
    sc, h_ref, dq0, dq1, mix0, mix1, got0, got1, g_ref, send_ref, keep_ref, mix_ref, dq_s, mix_s, both_s,
    *, n_pair
):
    half = mix0.shape[0]
    rows = mix0.shape[1]
    width = 2 * half
    count = rows // BLK
    own = pl.multiple_of(sc[0] * half, 128)
    other = pl.multiple_of((1 - sc[0]) * half, 128)
    for n, (mix, got, dq) in enumerate(((mix0, got0, dq0), (mix1, got1, dq1))):
        for k in range(count):
            source = slice(k * BLK, (k + 1) * BLK)
            at = pl.ds(pl.multiple_of(sc[4 + n * count + k] * BLK, BLK), BLK)
            mix_ref[:, at] = mix[:, source]
            mix_s[pl.ds(own, half), at] = mix[:, source]
            mix_s[pl.ds(other, half), at] = got[:, source]
            dq_s[:, at] = dq[:, source]
    both_s[:, 0:half] = dot(h_ref[...], dq_s[...], ((0,), (1,))).astype(BF)
    both_s[:, half:width] = dot(mix_s[...], g_ref[:, pl.ds(own, half)]).astype(BF)
    block = width // n_pair
    quarter = keep_ref.shape[3]
    unit = 48
    for low in range(2):
        for high in range(2):
            chip = sc[1] ^ (low + 2 * high)
            for first in range(2):
                ref = send_ref if first else keep_ref
                for second in range(2):
                    part = 2 * (first ^ sc[2]) + (second ^ sc[3])
                    for r in range(quarter // unit):
                        at = part * quarter + r * unit
                        col, row = at // block, at % block
                        source = pl.ds(pl.multiple_of(chip * block + row, 16), unit)
                        lane = pl.ds(pl.multiple_of(col * WIDE, WIDE), WIDE)
                        ref[second, low, high, r * unit : (r + 1) * unit, :] = both_s[source, lane]


def late_gradients(table, h_one, dqs, mixes, gots, g_two, n_pair):
    half = dqs[0].shape[0]
    width = 2 * half
    rows = h_one.shape[0]
    quarter = width // n_pair * (width // WIDE) // 4
    return call(
        functools.partial(late_kernel, n_pair=n_pair),
        "late_gradients",
        [shape((2, 2, 2, quarter, WIDE), BF)] * 2 + [shape((half, rows), BF)] * 2,
        [VM] * 8,
        [VM] * 4,
        [
            pltpu.VMEM((width, rows), BF),
            pltpu.VMEM((width, width), BF),
        ],
        16,
    )(table, h_one, *dqs, *mixes, *gots, g_two)


def out_kernel(sc, a0, a1, a2, mix_ref, x_ref, w_down, w_out, own_ref, send_ref, down_s, out_s, sems, *, part, n_pair):
    half = out_s.shape[0]
    rows = x_ref.shape[0]
    span = n_pair * LANES
    copies = [
        pltpu.make_async_copy(
            w_out.at[pl.ds(pl.multiple_of(sc[0] * half, 128), half), :], out_s, sems.at[0]
        )
    ]
    for n in range(3):
        copies += hidden_copies(
            sc, piece_of(sc, n), None, w_down, None, down_s.at[n], sems, part, n_pair
        )
    for copy in copies:
        copy.start()
    for copy in copies:
        copy.wait()
    for n in range(2):
        here = slice(n * rows, (n + 1) * rows)
        total = dot(mix_ref[:, here], out_s[...], ((0,), (0,)))
        for k, act in enumerate((a0, a1, a2)):
            total = total + dot(act[here, :], down_s[k])
        if n == 0:
            own_ref[...] = total + x_ref[...].astype(F32)
        else:
            send_ref[...] = total.astype(BF)


def hat_kernel(sc, d0, d1, d2, dq_ref, xo, xt, gains, w_up, w_query, own_ref, send_ref, sum_ref, up_s, query_s, sems, *, part, n_pair):
    half = query_s.shape[1]
    rows, width = xo.shape
    copies = [
        pltpu.make_async_copy(
            w_query.at[:, pl.ds(pl.multiple_of(sc[0] * half, 128), half)], query_s, sems.at[1]
        )
    ]
    for n in range(3):
        copies += hidden_copies(
            sc, piece_of(sc, n), w_up, None, up_s.at[n], None, sems, part, n_pair
        )
    for copy in copies:
        copy.start()
    for copy in copies:
        copy.wait()
    gain_one, gain_two = gains[0:1, :].astype(F32), gains[2:3, :].astype(F32)
    sums = [jnp.zeros((1, width), F32)] * 4
    for n, x in enumerate((xo, xt)):
        here = slice(n * rows, (n + 1) * rows)
        two = dot(d0[here, :], up_s[0], ((1,), (1,)))
        two = two + dot(d1[here, :], up_s[1], ((1,), (1,)))
        two = two + dot(d2[here, :], up_s[2], ((1,), (1,)))
        one = dot(dq_ref[:, here], query_s[...], ((0,), (1,)))
        hat, unused = normed(x[...].astype(F32))
        for k, value in enumerate((one * hat, one, two * hat, two)):
            sums[k] = sums[k] + jnp.sum(value, 0, keepdims=True)
        total = one * gain_one + two * gain_two
        if n == 0:
            own_ref[...] = total
        else:
            send_ref[...] = total.astype(BF)
    sum_ref[...] = jnp.concatenate(sums + [jnp.zeros((4, width), F32)], 0)


def last_kernel(sc, dkv_a, dkv_b, dkv_c, dkv_d, cos_ref, sin_ref, w_kv, h_ref, x_ref, gains, hat_own, hat_got, sum_ref, g_ref, grad_ref, send_ref, keep_ref, *, n_pair):
    rows, width = x_ref.shape
    dkv = sum(ref[...].astype(F32) for ref in (dkv_a, dkv_b, dkv_c, dkv_d)).T
    low_t = turn(dkv, cos_ref[:, 0:rows], -sin_ref[:, 0:rows]).astype(BF)
    low = low_t.T
    weight = dot(low_t, h_ref[0:rows, :]).T.astype(BF)
    d_kv = dot(low, w_kv[...], ((1,), (1,)))
    hat, scale = normed(x_ref[...].astype(F32))
    gain = gains[0:1, :].astype(F32)
    total = hat_own[...] + hat_got[...].astype(F32) + d_kv * gain
    grad_ref[...] = g_ref[...].astype(F32) + scale * (
        total
        - jnp.mean(total, -1, keepdims=True)
        - hat * jnp.mean(total * hat, -1, keepdims=True)
    )
    sums = jnp.concatenate(
        [
            sum_ref[0:1, :] + jnp.sum(d_kv * hat, 0, keepdims=True),
            sum_ref[1:2, :] + jnp.sum(d_kv, 0, keepdims=True),
            sum_ref[2:4, :],
            jnp.zeros((4, width), F32),
        ],
        0,
    ).astype(BF)
    part = width // (2 * n_pair)
    lanes = weight.shape[1]
    for chip in range(n_pair):
        rel = chip ^ sc[1]
        low_bit, high_bit = rel % 2, rel // 2
        blocks = []
        for core in range(2):
            at = (2 * chip + core) * part
            piece = weight[at : at + part, :]
            blocks.append(jnp.concatenate([piece[: part // 2], piece[part // 2 :]], 1))
            row = sums[:, at : at + part]
            blocks.append(jnp.concatenate([row, jnp.zeros((8, 2 * lanes - part), BF)], 1))
        block = jnp.concatenate(blocks, 0)

        @pl.when(low_bit == 1)
        def _():
            send_ref[high_bit] = block

        @pl.when(low_bit == 0)
        def _():
            keep_ref[high_bit] = block


def down_kernel(sc, a_send, a_got, send_ref, got_ref, out_ref, *, width):
    block = width // WIDE * LANES
    for k in range(3):
        for b in range(width // WIDE):
            here = slice(b * LANES, (b + 1) * LANES)
            if k == 0:
                value = a_send[here, :].astype(F32) + a_got[here, :].astype(F32)
            else:
                at = pl.ds(pl.multiple_of(sc[3] * block + b * LANES, LANES), LANES)
                mine = send_ref[at, :].astype(F32)
                value = jnp.where(sc[2] == k - 1, mine, got_ref[at, :].astype(F32))
            out_ref[k * LANES : (k + 1) * LANES, b * WIDE : (b + 1) * WIDE] = value


def up_block(sc, k, b, parity, a_send, a_got, b_send, b_got, width, part):
    block = width // WIDE * LANES
    off = b * 2 * part + parity * part
    if k == 0:
        at = pl.ds(pl.multiple_of(block + off, 32), part)
        return a_send[at, :].astype(F32) + a_got[at, :].astype(F32)
    at = pl.ds(pl.multiple_of((1 - sc[3]) * block + off, 32), part)
    return jnp.where(
        sc[2] == k - 1, b_send[at, :].astype(F32), b_got[at, :].astype(F32)
    )


def late_block(sc, b, parity, send, got, part, quarter):
    pieces = []
    for r in range(2):
        at = b * 2 * part + parity * part + r * (part // 2)
        first, second = at // (2 * quarter), at // quarter % 2
        rel = (second ^ sc[3]) * quarter + at % quarter
        source = pl.ds(pl.multiple_of(rel, 16), part // 2)
        pieces.append(
            jnp.where(
                first == sc[2], send[source, :].astype(F32), got[source, :].astype(F32)
            )
        )
    return jnp.concatenate(pieces, 0)


def pack_up_kernel(sc, a_send, a_got, b_send, b_got, out_ref, own_ref, *, width, part):
    for which, ref in ((1, out_ref), (0, own_ref)):
        parity = sc[0] if which == 0 else 1 - sc[0]
        at = 0
        for k in range(3):
            for b in range(2):
                ref[at : at + part, :] = up_block(
                    sc, k, b, parity, a_send, a_got, b_send, b_got, width, part
                ).astype(BF)
                at += part


def pack_late_kernel(sc, last_send, last_got, out_ref, own_ref, *, width, part, quarter):
    for which, ref in ((1, out_ref), (0, own_ref)):
        parity = sc[0] if which == 0 else 1 - sc[0]
        at = 0
        for b in range(width // WIDE):
            ref[at : at + part, :] = late_block(
                sc, b, parity, last_send, last_got, part, quarter
            ).astype(BF)
            at += part
        few = (last_send.shape[0] - 2 * quarter) // 2
        source = pl.ds(pl.multiple_of(2 * quarter + parity * few, 8), few)
        ref[at : at + few, :] = (
            last_send[source, :].astype(F32) + last_got[source, :].astype(F32)
        ).astype(BF)


def final_up_kernel(sc, own_ref, got_ref, up_ref, *, part, n_pair):
    part_hidden = up_ref.shape[1] // (2 * n_pair)
    for which, ref in enumerate((own_ref, got_ref)):
        core = sc[0] if which == 0 else 1 - sc[0]
        for k in range(3):
            for j in range(n_pair):
                lane = (2 * j + core) * part_hidden + k * LANES
                rows = slice((2 * k + j // 2) * part, (2 * k + j // 2 + 1) * part)
                cols = slice(j % 2 * LANES, (j % 2 + 1) * LANES)
                up_ref[:, pl.ds(pl.multiple_of(lane, LANES), LANES)] = ref[rows, cols].astype(F32)


def final_late_kernel(sc, own_ref, got_ref, query_ref, proj_ref, kv_ref, norm_ref, *, part):
    half = query_ref.shape[1] // 2
    for which, ref in enumerate((own_ref, got_ref)):
        core = sc[0] if which == 0 else 1 - sc[0]
        for n in range(2 * half // LANES):
            rows = slice(n // 2 * part, (n // 2 + 1) * part)
            value = ref[rows, n % 2 * LANES : (n % 2 + 1) * LANES].astype(F32)
            to, m = (query_ref, n) if n < half // LANES else (proj_ref, n - half // LANES)
            to[:, pl.ds(pl.multiple_of(core * half + m * LANES, LANES), LANES)] = value
    base = 2 * half // WIDE * part
    few = own_ref[base:, :].astype(F32) + got_ref[base:, :].astype(F32)
    kv_ref[0 : part // 2, :] = few[0 : part // 2, 0:LANES]
    kv_ref[part // 2 : part, :] = few[0 : part // 2, LANES:WIDE]
    norm_ref[...] = few[part // 2 : part // 2 + 8, :]


class Links:
    def __init__(self, n_grp, n_ctx):
        self.n_grp, self.n_ctx, self.n_pair = n_grp, n_ctx, n_ctx // 2
        self.small = (n_grp, n_ctx) == (4, 8)
        self.ctx = lax.axis_index("ctx")
        self.grp = lax.axis_index("grp")
        self.core = self.ctx % 2
        self.chip = self.ctx // 2
        self.groups = [[2 * z + c for z in range(self.n_pair)] for c in range(2)]

    def swap(self, value):
        return lax.ppermute(value, "ctx", [(i, i ^ 1) for i in range(self.n_ctx)])

    def permute(self, value, target):
        pairs = []
        for g in range(self.n_grp):
            for i in range(self.n_ctx):
                y, x, z, c = target(g // 2, g % 2, i // 2, i % 2)
                pairs.append((g * self.n_ctx + i, (2 * y + x) * self.n_ctx + 2 * z + c))
        return lax.ppermute(value, ("grp", "ctx"), pairs)

    def cross(self, value, stage):
        return self.permute(
            value, lambda y, x, z, c: (y, 1 - x, z, c) if c == stage else (1 - y, x, z, c)
        )

    def bit(self, stage):
        y, x = self.grp // 2, self.grp % 2
        return jnp.where(self.core == stage, x, y)

    def flip(self, value, bit):
        return self.permute(value, lambda y, x, z, c: (y, x, z ^ bit, c))

    def reduce(self, parts):
        moved = lax.all_to_all(parts, "ctx", 0, 0, axis_index_groups=self.groups)
        return lax.psum(jnp.sum(moved.astype(F32), 0).astype(BF), "grp")


def add(*values):
    return sum(value.astype(F32) for value in values).astype(BF)


def low(value):
    return value.astype(BF)


def shards_small(
    layer_input, block_table, ln1_gain, ln1_bias, ln2_gain, ln2_bias,
    w_query, w_keyval, w_out, w_up, w_down, cotangent, *, n_grp, n_ctx,
):
    links = Links(n_grp, n_ctx)
    core, chip, n_pair = links.core, links.chip, links.n_pair
    rows, width = layer_input.shape
    lanes = w_keyval.shape[1]
    size = lanes // 2
    hidden = w_up.shape[1]
    group_len = block_table.shape[1] * BLK
    part, part_hidden = width // n_ctx, hidden // n_ctx
    half = width // 2
    per_chip = 2 * rows // BLK
    table = block_table[0]
    count = rows // BLK
    gains = jnp.concatenate([ln1_gain, ln1_bias, ln2_gain, ln2_bias]).reshape(4, width)

    x_other, g_other = links.swap(layer_input), links.swap(cotangent)
    column = jnp.arange(2 * rows, dtype=jnp.int32)
    slot = chip * per_chip + lax.rem(column // BLK + core * count, per_chip)
    slots = jnp.arange(table.shape[0], dtype=jnp.int32)
    canon = jnp.sum(jnp.where(slots[:, None] == slot[None, :], table[:, None], 0), 0)
    canon = canon * BLK + column % BLK
    prompt_len = group_len // 2
    cont_span = min(CONT, prompt_len)
    position = jnp.where(
        canon < prompt_len, canon, prompt_len + (canon - prompt_len) % cont_span
    )
    cosine, sine = rope_tables(position)

    h_one, h_two, g_two, kv_low = call(
        prologue_kernel,
        "prologue",
        [shape((2 * rows, width), BF)] * 3 + [shape((2 * rows, lanes), BF)],
        [HBM, VM, HBM, VM, VM, HBM, VM, VM],
        [VM] * 4,
        [
            pltpu.VMEM((rows, width), BF),
            pltpu.VMEM((width, lanes), BF),
            pltpu.SemaphoreType.DMA((3,)),
        ],
        16,
    )(table, layer_input, x_other, cotangent, g_other, gains, w_keyval, cosine, sine)

    kv_got = links.flip(kv_low, 1)
    ffn = functools.partial(
        ffn_gradients, table, w_up=w_up, w_down=w_down, part=part_hidden, n_pair=n_pair
    )
    act_1, dup_1, b_send = ffn(h_two, g_two, n=1)
    b_send, kv_got = meet(b_send, kv_got)
    kv_near = jnp.concatenate([kv_low, kv_got], 0)
    kv_far = links.flip(kv_near, 2)
    b_got = links.cross(b_send, 0)
    act_2, dup_2, b_keep = ffn(tie(h_two, b_send, kv_near), g_two, n=2)
    act_0, dup_0, a_send, a_keep = ffn(tie(h_two, b_keep), g_two, n=0)
    a_send, kv_far = meet(a_send, kv_far)
    a_got = links.flip(a_send, 1)

    q_t, do_t = call(
        functools.partial(project_kernel, size=size),
        "project",
        [shape((half, 2 * rows), BF), shape((half, 2 * rows), F32)],
        [VM] * 4 + [HBM] * 2,
        [VM] * 2,
        [
            pltpu.VMEM((width, half), BF),
            pltpu.VMEM((half, width), BF),
            pltpu.SemaphoreType.DMA((2,)),
        ],
        16,
    )(table, tie(h_one, a_send), g_two, cosine, sine, w_query, w_out)
    q_t, b_got = meet(q_t, b_got)
    b_send = add(b_keep[1], b_got[1])
    b_got_2 = links.cross(b_send, 1)

    attend = functools.partial(
        attention, table, do_t=do_t, cosine=cosine, sine=sine, kvs=(kv_near, kv_far),
        count=count, per_chip=per_chip, split=True,
    )
    mix_0, dq_0, carried = attend(
        q_t=tie(q_t, b_send), carried=None, start=0, last_call=False
    )
    carried, a_got, b_got_2 = meet(carried, a_got, b_got_2)
    b_send = add(b_keep[0, 1], b_got[0, 1], b_got_2[1])
    b_got_3 = links.flip(b_send, 1)
    a_send = add(a_keep[1], tie(a_got, b_send)[1])
    a_got_2 = links.flip(a_send, 2)
    mix_1, dq_1, dkv_send, dkv_keep = attend(
        q_t=tie(q_t, a_send, b_send, carried), carried=carried, start=count, last_call=True
    )
    mix_0, mix_1, dkv_send, a_got_2, b_got_3 = meet(mix_0, mix_1, dkv_send, a_got_2, b_got_3)
    dkv_got = links.swap(dkv_send)
    mix_0_got, mix_1_got = links.swap(mix_0), links.swap(mix_1)
    dkv_got, mix_0_got, mix_1_got = meet(dkv_got, mix_0_got, mix_1_got)
    dkv_sends = [add(dkv_keep[at], dkv_got[at]) for at in ((1, 0), (0, 1), (1, 1))]
    dkv_gots = [links.flip(value, n + 1) for n, value in enumerate(dkv_sends)]
    a_sum = add(a_keep[0], a_got[0], tie(a_got_2, *dkv_sends))
    a_got = links.cross(a_sum, 1)
    late_send, late_keep, mix_own, dq_own = late_gradients(
        table, tie(h_one, a_sum, *dkv_sends), (dq_0, dq_1), (mix_0, mix_1), (mix_0_got, mix_1_got), g_two, n_pair
    )
    late_got = links.cross(late_send, 0)
    b_send = add(b_keep[0, 0, 1], b_got[0, 0, 1], b_got_2[0, 1], tie(b_got_3, late_send)[1])
    b_got_4 = links.flip(b_send, 2)

    w_specs = [HBM] * 2
    hat_own, hat_send, sums = call(
        functools.partial(hat_kernel, part=part_hidden, n_pair=n_pair),
        "norms",
        [shape((rows, width), F32), shape((rows, width), BF), shape((8, width), F32)],
        [VM] * 7 + w_specs,
        [VM] * 3,
        [
            pltpu.VMEM((3, width, n_pair * LANES), BF),
            pltpu.VMEM((width, half), BF),
            pltpu.SemaphoreType.DMA((2,)),
        ],
        24,
    )(
        table, dup_0, dup_1, tie(dup_2, b_send), dq_own, layer_input, x_other, gains,
        w_up, w_query,
    )
    hat_send, late_got, a_got, *dkv_gots = meet(hat_send, late_got, a_got, *dkv_gots)
    hat_got = links.swap(hat_send)
    late_send = add(late_keep[1], late_got[1])
    late_got_2 = links.cross(late_send, 1)
    a_sum = add(a_sum, tie(a_got, late_send))
    a_got = links.cross(a_sum, 0)
    dkv_own = add(dkv_keep[0, 0], dkv_got[0, 0])
    a_sum, hat_got = meet(a_sum, hat_got)

    few = part // 2 + 8
    in_grad, few_send, few_keep = call(
        functools.partial(last_kernel, n_pair=n_pair),
        "last",
        [shape((rows, width), F32)] + [shape((2, 2 * few, 2 * lanes), BF)] * 2,
        [VM] * 14,
        [VM] * 3,
        [],
        16,
    )(
        table, dkv_own, *dkv_gots, tie(cosine, a_sum), sine, w_keyval, h_one,
        layer_input, gains, hat_own, hat_got, sums, cotangent,
    )
    few_send, late_got_2, b_got_4 = meet(few_send, late_got_2, b_got_4)
    quarter = late_keep.shape[3]
    last_send = jnp.concatenate(
        [add(late_keep[0, 1], late_got[0, 1], late_got_2[1]), few_send], 1
    )
    last_got = links.flip(last_send, 1)
    b_sum = add(
        b_keep[0, 0, 0], b_got[0, 0, 0], b_got_2[0, 0], b_got_3[0], tie(b_got_4, last_send)
    )
    b_got = links.cross(b_sum, 1)

    out_own, out_send = call(
        functools.partial(out_kernel, part=part_hidden, n_pair=n_pair),
        "outputs",
        [shape((rows, width), F32), shape((rows, width), BF)],
        [VM] * 5 + w_specs,
        [VM] * 2,
        [
            pltpu.VMEM((3, n_pair * LANES, width), BF),
            pltpu.VMEM((half, width), BF),
            pltpu.SemaphoreType.DMA((2,)),
        ],
        24,
    )(
        table, act_0, act_1, tie(act_2, b_sum), mix_own, layer_input, w_down, w_out,
    )
    out_send, last_got, a_got, b_got = meet(out_send, last_got, a_got, b_got)
    out_got = links.swap(out_send)
    last_keep = jnp.concatenate(
        [add(late_keep[0, 0], late_got[0, 0], late_got_2[0]), few_keep], 1
    )
    last_send = add(last_keep[1], last_got[1])
    last_got_2 = links.flip(last_send, 2)
    b_sum = jnp.concatenate([b_sum, b_got], 0)
    b_got = links.cross(tie(b_sum, last_send), 0)
    out_got = tie(out_got, b_sum, last_send)
    layer_output = low(out_own + out_got.astype(F32))
    b_got, layer_output = meet(b_got, layer_output)
    up_send, up_own = call(
        functools.partial(pack_up_kernel, width=width, part=part),
        "pack_up", [shape((6 * part, WIDE), BF)] * 2, [VM] * 4, [VM] * 2, [], 8,
    )(table, a_sum, a_got, b_sum, b_got)
    up_got = links.swap(up_send)
    last_got_2 = tie(last_got_2, up_send)
    last = add(last_keep[0], last_got[0], last_got_2)
    last_got = links.cross(last, 1)
    total_down = call(
        functools.partial(down_kernel, width=width),
        "down", shape((part_hidden, width), F32), [VM] * 4, VM, [], 8,
    )(table, tie(a_sum, last), a_got, b_sum, b_got)
    total_down, last_got, up_got = meet(total_down, last_got, up_got)
    last = jnp.concatenate(
        [last[:quarter], last_got[:quarter], add(last[quarter:], last_got[quarter:])], 0
    )
    last_got = links.cross(last, 0)
    total_up = call(
        functools.partial(final_up_kernel, part=part, n_pair=n_pair),
        "final_up", shape((part, hidden), F32), [VM] * 2, VM, [], 8,
    )(table, tie(up_own, last), up_got)
    total_up, last_got = meet(total_up, last_got)
    other, own = call(
        functools.partial(pack_late_kernel, width=width, part=part, quarter=quarter),
        "pack_late", [shape((width // WIDE * part + few, WIDE), BF)] * 2, [VM] * 2, [VM] * 2, [], 8,
    )(table, last, last_got)
    got = links.swap(other)
    total_query, total_out, total_kv, norm = call(
        functools.partial(final_late_kernel, part=part),
        "final_late",
        [
            shape((part, width), F32),
            shape((part, width), F32),
            shape((part, lanes), F32),
            shape((8, WIDE), F32),
        ],
        [VM] * 2,
        [VM] * 4,
        [],
        8,
    )(table, own, got)
    norms = [norm[n, :part] for n in range(4)]
    return (layer_output, in_grad, *norms, total_query, total_kv, total_out, total_up, total_down)


def rotate_rows(values, cosine, sine):
    return turn(values.T, cosine, sine).T


def shards(
    layer_input, block_table, ln1_gain, ln1_bias, ln2_gain, ln2_bias,
    w_query, w_keyval, w_out, w_up, w_down, cotangent, *, n_grp, n_ctx,
):
    links = Links(n_grp, n_ctx)
    core, chip, n_pair = links.core, links.chip, links.n_pair
    rows, width = layer_input.shape
    size = w_keyval.shape[1] // 2
    hidden = w_up.shape[1]
    group_len = block_table.shape[1] * BLK
    part_rows, part_hidden = width // n_ctx, hidden // n_ctx
    half_width, half_hidden = width // 2, hidden // 2
    per_chip = 2 * rows // BLK
    table = block_table[0]

    def both(own, other):
        return jnp.concatenate(
            [jnp.where(core == 0, own, other), jnp.where(core == 0, other, own)], 0
        )

    def mine(value, own_core):
        return lax.dynamic_slice_in_dim(value, own_core * rows, rows, 0)

    x_two = both(layer_input, links.swap(layer_input))
    g_two = both(cotangent, links.swap(cotangent))
    canon = (
        lax.dynamic_slice_in_dim(table, chip * per_chip, per_chip)[:, None] * BLK
        + jnp.arange(BLK, dtype=jnp.int32)[None, :]
    ).reshape(2 * rows)
    prompt_len = group_len // 2
    cont_span = min(CONT, prompt_len)
    position = jnp.where(
        canon < prompt_len, canon, prompt_len + (canon - prompt_len) % cont_span
    )
    cosine, sine = rope_tables(position)
    gain_one, gain_two = ln1_gain.astype(F32), ln2_gain.astype(F32)
    hat, scale = normed(x_two.astype(F32))
    h_one = low(hat * gain_one + ln1_bias.astype(F32))
    h_two = low(hat * gain_two + ln2_bias.astype(F32))
    kv_raw = dot(h_one, w_keyval)
    kv_low = low(
        jnp.concatenate([rotate_rows(kv_raw[:, :size], cosine, sine), kv_raw[:, size:]], -1)
    )
    kv_all = lax.all_gather(kv_low, "ctx", axis=0, axis_index_groups=links.groups, tiled=True)

    up_half = lax.dynamic_index_in_dim(
        w_up.reshape(width, n_pair, 2, part_hidden), core, 2, False
    ).reshape(width, half_hidden)
    down_half = lax.dynamic_index_in_dim(
        w_down.reshape(n_pair, 2, part_hidden, width), core, 1, False
    ).reshape(half_hidden, width)
    act, slope = gelu_parts(dot(h_two, up_half))
    act = low(act)
    grad_down = low(dot(act, g_two, ((0,), (0,))))
    total_down = links.reduce(grad_down.reshape(n_pair, part_hidden, width))
    grad_up = low(dot(g_two, down_half, ((1,), (1,))) * slope)
    grad_up_w = low(dot(h_two, grad_up, ((0,), (0,))))
    total_up = links.reduce(grad_up_w.reshape(n_pair, 2 * part_rows, half_hidden))

    query_half = lax.dynamic_slice_in_dim(w_query, core * half_width, half_width, 1)
    out_half = lax.dynamic_slice_in_dim(w_out, core * half_width, half_width, 0)
    q_raw = dot(query_half, h_one, ((0,), (1,))) * (0.125 * LOG2E)
    q_t = low(
        jax.vmap(turn, (0, None, None))(q_raw.reshape(-1, size, 2 * rows), cosine, sine)
    ).reshape(half_width, 2 * rows)
    do_t = dot(out_half, g_two, ((1,), (1,)))
    mix_t, dq_t, dkv_part = attention(
        table, q_t, do_t, cosine, sine, (kv_all,), None, 0, per_chip, per_chip, True, False
    )

    dkv_part = dkv_part.reshape(n_pair, 2, rows, 2 * size)
    dkv_own = lax.dynamic_index_in_dim(dkv_part, core, 1, False)
    dkv_got = links.swap(lax.dynamic_index_in_dim(dkv_part, 1 - core, 1, False))
    moved = lax.all_to_all(
        add(dkv_own, dkv_got), "ctx", 0, 0, axis_index_groups=links.groups
    )
    dkv = jnp.sum(moved.astype(F32), 0)
    cos_own = lax.dynamic_slice_in_dim(cosine, core * rows, rows, 1)
    sin_own = lax.dynamic_slice_in_dim(sine, core * rows, rows, 1)
    dkv_low = low(
        jnp.concatenate([rotate_rows(dkv[:, :size], cos_own, -sin_own), dkv[:, size:]], -1)
    )

    mix_got = links.swap(mix_t)
    mix_all = jnp.concatenate(
        [jnp.where(core == 0, mix_t, mix_got), jnp.where(core == 0, mix_got, mix_t)], 0
    )
    g_half = lax.dynamic_slice_in_dim(g_two, core * half_width, half_width, 1)
    grad_q_w = low(dot(h_one, dq_t, ((0,), (1,))))
    grad_out_w = low(dot(mix_all, g_half))
    late = jnp.concatenate([grad_q_w, grad_out_w], 1).reshape(n_pair, 2 * part_rows, width)
    total_late = links.reduce(late)

    out_part = dot(act, down_half) + dot(mix_t, out_half, ((0,), (0,)))
    out_got = links.swap(low(mine(out_part, 1 - core)))
    layer_output = low(layer_input.astype(F32) + mine(out_part, core) + out_got.astype(F32))

    d_two = dot(grad_up, up_half, ((1,), (1,)))
    d_one = dot(dq_t, query_half, ((0,), (1,)))
    d_kv = dot(dkv_low, w_keyval, ((1,), (1,)))
    row_core = lax.broadcasted_iota(jnp.int32, (2 * rows, 1), 0) // rows
    d_one = d_one + jnp.where(row_core == core, jnp.concatenate([d_kv, d_kv], 0), 0.0)
    sums = jnp.stack([jnp.sum(v, 0) for v in (d_one * hat, d_one, d_two * hat, d_two)])
    d_hat = d_one * gain_one + d_two * gain_two
    hat_got = links.swap(low(mine(d_hat, 1 - core)))
    d_hat = mine(d_hat, core) + hat_got.astype(F32)
    hat_own = mine(hat, core)
    in_grad = cotangent.astype(F32) + mine(scale, core) * (
        d_hat
        - jnp.mean(d_hat, -1, keepdims=True)
        - hat_own * jnp.mean(d_hat * hat_own, -1, keepdims=True)
    )

    grad_kv_w = dot(mine(h_one, core), dkv_low, ((0,), (0,)))
    sum_rows = sums.reshape(4, n_pair, 2, part_rows).transpose(1, 2, 0, 3)
    sum_rows = jnp.pad(sum_rows, ((0, 0), (0, 0), (0, 0), (0, 2 * size - part_rows)))
    few = jnp.concatenate([grad_kv_w.reshape(n_pair, 2, part_rows, 2 * size), sum_rows], 2)
    few = links.reduce(low(few).reshape(n_pair, 2 * (part_rows + 4), 2 * size))
    few = few.reshape(2, part_rows + 4, 2 * size)
    few_got = links.swap(lax.dynamic_index_in_dim(few, 1 - core, 0, False))
    few = lax.dynamic_index_in_dim(few, core, 0, False).astype(F32) + few_got.astype(F32)

    halves = jnp.concatenate(
        [total_up.reshape(2, part_rows, half_hidden), total_late.reshape(2, part_rows, width)], -1
    )
    own = lax.dynamic_index_in_dim(halves, core, 0, False)
    got = links.swap(lax.dynamic_index_in_dim(halves, 1 - core, 0, False))
    sides = jnp.stack([jnp.where(core == 0, own, got), jnp.where(core == 0, got, own)]).astype(F32)
    ups = sides[:, :, :half_hidden].reshape(2, part_rows, n_pair, part_hidden)
    total_up = ups.transpose(1, 2, 0, 3).reshape(part_rows, hidden)
    lates = sides[:, :, half_hidden:]
    total_query = lates[:, :, :half_width].transpose(1, 0, 2).reshape(part_rows, width)
    total_out = lates[:, :, half_width:].transpose(1, 0, 2).reshape(part_rows, width)
    norms = [few[part_rows + n, :part_rows] for n in range(4)]
    total_kv = few[:part_rows]
    total_down = total_down.astype(F32)
    return (layer_output, in_grad, *norms, total_query, total_kv, total_out, total_up, total_down)


def solution(mesh):
    n_grp, n_ctx = mesh.shape["grp"], mesh.shape["ctx"]
    body = shards_small if (n_grp, n_ctx) == (4, 8) else shards
    return jax.shard_map(
        functools.partial(body, n_grp=n_grp, n_ctx=n_ctx),
        mesh=mesh,
        in_specs=(P(("grp", "ctx"), None), P("grp", None))
        + (P(),) * 9
        + (P(("grp", "ctx"), None),),
        out_specs=(P(("grp", "ctx"), None),) * 2 + (P("ctx"),) * 4 + (P("ctx", None),) * 5,
        check_vma=False,
    )
```

```python
import functools

import jax
import jax.numpy as jnp
import numpy as np
from jax import lax
from jax.experimental import pallas as pl
from jax.experimental.pallas import tpu as pltpu
from jax.sharding import PartitionSpec as P

ROT = 16
HALF = ROT // 2
BLK = 128
CONT = 1024
TILE = 256
LANES = 128
WIDE = 256
EPS = 1e-05
LOG2E = 1.4426950408889634
LN2 = 0.6931471805599453
BF = jnp.bfloat16
F32 = jnp.float32
MIB = 1024 * 1024
VM = pl.BlockSpec(memory_space=pltpu.VMEM)
HBM = pl.BlockSpec(memory_space=pltpu.HBM)


def dot(left, right, dims=((1,), (0,))):
    return lax.dot_general(left, right, (dims, ((), ())), preferred_element_type=F32)


def shape(dims, dtype):
    return jax.ShapeDtypeStruct(dims, dtype)


def tie(value, *others):
    return lax.optimization_barrier((value,) + others)[0]


def meet(*values):
    return lax.optimization_barrier(values)


def rope_tables(position):
    inverse = jnp.asarray(10000.0 ** (-2.0 * np.arange(HALF) / ROT), F32)
    angles = inverse[:, None] * position.astype(F32)[None, :]
    return (jnp.cos(angles), jnp.sin(angles))


def turn(values, cosine, sine):
    first, second = values[:HALF], values[HALF:ROT]
    return jnp.concatenate(
        [first * cosine - second * sine, second * cosine + first * sine, values[ROT:]], 0
    )


def normed(values):
    shifted = values - jnp.mean(values, -1, keepdims=True)
    scale = lax.rsqrt(jnp.mean(shifted * shifted, -1, keepdims=True) + EPS)
    return (shifted * scale, scale)


def gelu_parts(value):
    cdf = 0.5 * (1.0 + lax.erf(value * 0.7071067811865476))
    pdf = jnp.exp(-0.5 * value * value) * 0.3989422804014327
    return value * cdf, cdf + value * pdf


def call(kernel, name, outs, specs, out_specs, scratch, limit, flops=1000):
    def body(table, *refs):
        kernel(scalars(table), *refs)

    made = pl.pallas_call(
        body,
        out_shape=outs,
        grid_spec=pltpu.PrefetchScalarGridSpec(
            num_scalar_prefetch=1, in_specs=specs, out_specs=out_specs, scratch_shapes=scratch
        ),
        compiler_params=pltpu.CompilerParams(vmem_limit_bytes=limit * MIB),
        cost_estimate=pl.CostEstimate(flops=flops, bytes_accessed=flops, transcendentals=0),
        name=name,
    )

    def placed(table, *values):
        return made(
            table,
            *(
                pltpu.with_memory_space_constraint(v, pltpu.HBM) if spec is HBM else v
                for v, spec in zip(values, specs)
            ),
        )

    return placed


def scalars(table):
    ctx, grp = lax.axis_index("ctx"), lax.axis_index("grp")
    per_chip = 2 * table.shape[0] // lax.axis_size("ctx")
    core, chip = lax.rem(ctx, 2), lax.div(ctx, 2)
    y, x = lax.div(grp, 2), lax.rem(grp, 2)
    blocks = [table[chip * per_chip + n] for n in range(per_chip)]
    ranks = [sum((b < a).astype(jnp.int32) for b in blocks if b is not a) for a in blocks]
    order = []
    for k in range(per_chip):
        want = k // 2 if k % 2 else per_chip - 1 - k // 2
        at = sum(jnp.where(rank == want, n, 0) for n, rank in enumerate(ranks))
        order.append(lax.rem(at + per_chip - core * (per_chip // 2), per_chip))
    return [core, chip, jnp.where(core == 0, x, y), jnp.where(core == 1, x, y)] + order


def attn_kernel(
    table, *refs, blocks, heads, size, n_kv, per_chip, start, split, last_call, first_call
):
    q_ref, do_ref, cos_ref, sin_ref = refs[:4]
    kv_refs = refs[4 : 4 + n_kv]
    refs = refs[4 + n_kv :]
    if not first_call:
        sum_ref, refs = refs[0], refs[1:]
    mix_ref, dq_ref = refs[:2]
    outs = refs[2:-11]
    kv_c, kv_t, s_scr, p_scr, rq, rd, rqt, rdt, o_acc, dq_acc, dkv_acc = refs[-11:]
    step, group = pl.program_id(0), pl.program_id(1)
    core, chip, _, _, *order = scalars(table)
    if split:
        column = sum(
            jnp.where(step == n, order[start + n], 0) for n in range(per_chip // 2)
        )
        position = lax.rem(column + core * (per_chip // 2), per_chip)
    else:
        column = position = step
    lanes = heads * BLK
    prompt_blocks = blocks // 2
    prompt_tiles = prompt_blocks * BLK // TILE
    cont_blocks = min(CONT, prompt_blocks * BLK) // BLK

    def block_rows(block):
        return pl.ds(pl.multiple_of(block * BLK, BLK), BLK)

    @pl.when((step == 0) & (group == 0))
    def _():
        ones = jnp.ones((16, BLK), BF)
        share = blocks // n_kv

        for n, kv_ref in enumerate(kv_refs):

            def place_block(at, carry, n=n, kv_ref=kv_ref):
                spot = n * share + at
                owner = (spot // per_chip) ^ chip if split else spot // per_chip
                block = table[owner * per_chip + spot % per_chip]
                rows = kv_ref[block_rows(at), :]
                kv_c[block_rows(block), :] = rows
                turned = jnp.concatenate([rows.T, ones], 0)

                @pl.when(block % 2 == 0)
                def _():
                    kv_t[block // 2, :, 0:BLK] = turned

                @pl.when(block % 2 == 1)
                def _():
                    kv_t[block // 2, :, BLK:TILE] = turned

                return carry

            lax.fori_loop(0, share, place_block, 0)
        dkv_acc[...] = jnp.zeros_like(dkv_acc) if first_call else sum_ref[...]

    block = table[chip * per_chip + position]
    columns = pl.ds(pl.multiple_of(column * BLK, BLK), BLK)
    last = block // 2
    in_prompt = block < prompt_blocks
    seg_tile = (prompt_blocks + (block - prompt_blocks) // cont_blocks * cont_blocks) // 2
    full = jnp.where(in_prompt, last, prompt_tiles + last - seg_tile)

    def tile_of(i):
        return jnp.where(i < prompt_tiles, jnp.minimum(i, last), i - prompt_tiles + seg_tile)

    def key_rows(tile):
        return pl.ds(pl.multiple_of(tile * TILE, TILE), TILE)

    for h in range(heads):
        rq[0:size, h * BLK : (h + 1) * BLK] = q_ref[h * size : (h + 1) * size, columns]
    rq[size : 2 * size, :] = jnp.zeros((size, lanes), BF)

    def scores(tile):
        return dot(kv_c[key_rows(tile), :], rq[...])

    def fold(values):
        return jnp.max(values.reshape(TILE // 8, 8, lanes), 0)

    def first_pass(i, top):
        part = scores(tile_of(i))
        s_scr[i] = part
        return jnp.maximum(top, fold(part))

    top = lax.fori_loop(0, full, first_pass, jnp.full((8, lanes), -1e30, F32))
    part = scores(last)
    key_at = last * TILE + lax.broadcasted_iota(jnp.int32, (TILE, lanes), 0)
    row_at = block * BLK + lax.rem(lax.broadcasted_iota(jnp.int32, (TILE, lanes), 1), BLK)
    part = jnp.where(key_at <= row_at, part, -1e30)
    s_scr[full] = part
    top = jnp.max(jnp.maximum(top, fold(part)), 0, keepdims=True)

    o_acc[...] = jnp.zeros_like(o_acc)

    def second_pass(i, carry):
        p = jnp.exp2(s_scr[i] - top).astype(BF)
        p_scr[i] = p
        o_acc[...] += dot(kv_t[jnp.where(i == full, last, tile_of(i)), size : 2 * size + 16, :], p)
        return carry

    lax.fori_loop(0, full + 1, second_pass, 0)

    inverse = 1.0 / o_acc[size : size + 1, :]
    mixed = o_acc[0:size, :] * inverse
    grads = []
    for h in range(heads):
        at = slice(h * BLK, (h + 1) * BLK)
        mix_ref[h * size : (h + 1) * size, :] = mixed[:, at].astype(BF)
        grads.append(do_ref[h * size : (h + 1) * size, columns])
    scaled = (jnp.concatenate(grads, 1) * inverse).astype(BF)
    delta = jnp.sum(mixed * scaled.astype(F32), 0, keepdims=True)
    rd[0:size, :] = jnp.zeros((size, lanes), BF)
    rd[size : 2 * size, :] = scaled
    rqt[...] = rq[...].T
    rdt[...] = rd[...].T
    dq_acc[...] = jnp.zeros_like(dq_acc)

    def third_pass(i, carry):
        tile = jnp.where(i == full, last, tile_of(i))
        p = p_scr[i]
        d_probs = dot(kv_c[key_rows(tile), :], rd[...])
        ds = (p.astype(F32) * (d_probs - delta)).astype(BF)
        dq_acc[...] += dot(kv_t[tile, 0:size, :], ds)
        dkv_acc[key_rows(tile), :] += dot(p, rdt[...]) + dot(ds, rqt[...])
        return carry

    lax.fori_loop(0, full + 1, third_pass, 0)

    cosine, sine = cos_ref[:, columns], sin_ref[:, columns]
    for h in range(heads):
        part = dq_acc[:, h * BLK : (h + 1) * BLK] * 0.125
        dq_ref[h * size : (h + 1) * size, :] = turn(part, cosine, -sine).astype(BF)

    @pl.when((step == pl.num_programs(0) - 1) & (group == pl.num_programs(1) - 1))
    def _():
        if not last_call:
            outs[0][...] = dkv_acc[...]
            return
        scale = jnp.where(
            lax.broadcasted_iota(jnp.int32, (BLK, 2 * size), 1) < size, F32(LN2), F32(1.0)
        )

        def rows_of(slot):
            return (dkv_acc[block_rows(table[slot]), :] * scale).astype(BF)

        if len(outs) == 1:

            def give_block(slot, carry):
                outs[0][block_rows(slot), :] = rows_of(slot)
                return carry

            lax.fori_loop(0, blocks, give_block, 0)
            return
        per_core = per_chip // 2
        for low in range(2):
            for high in range(2):
                owner = chip ^ (low + 2 * high)
                for n in range(per_core):
                    here = slice(n * BLK, (n + 1) * BLK)
                    base = owner * per_chip + n
                    outs[0][low, high, here, :] = rows_of(base + per_core * (1 - core))
                    outs[1][low, high, here, :] = rows_of(base + per_core * core)


def attention(
    table, q_t, do_t, cosine, sine, kvs, carried, start, count, per_chip, last_call, split
):
    width = q_t.shape[0]
    rows = count * BLK
    first_call = carried is None
    size = kvs[0].shape[1] // 2
    keys = sum(kv.shape[0] for kv in kvs)
    all_heads = width // size
    blocks = keys // BLK
    heads = all_heads if keys <= 4096 else 2
    lanes = heads * BLK
    cont = min(CONT, keys // 2)
    most = (keys // 2 + cont) // TILE
    tiles = keys // TILE

    def whole(dims):
        return pl.BlockSpec(dims, lambda i, j, *_: (0,) * len(dims))

    if not last_call:
        dkv_shapes = [shape((keys, 2 * size), F32)]
    elif split:
        dkv_shapes = [shape((2, 2, keys // 8, 2 * size), BF)] * 2
    else:
        dkv_shapes = [shape((keys, 2 * size), BF)]
    extra = [] if first_call else [carried]
    column = pl.BlockSpec((heads * size, q_t.shape[1]), lambda i, j, *_: (j, 0))
    out_column = pl.BlockSpec((heads * size, BLK), lambda i, j, *_: (j, i))
    return pl.pallas_call(
        functools.partial(
            attn_kernel,
            blocks=blocks,
            heads=heads,
            size=size,
            n_kv=len(kvs),
            per_chip=per_chip,
            start=start,
            split=split,
            last_call=last_call,
            first_call=first_call,
        ),
        out_shape=[shape((width, rows), BF)] * 2 + dkv_shapes,
        grid_spec=pltpu.PrefetchScalarGridSpec(
            num_scalar_prefetch=1,
            grid=(count, all_heads // heads),
            in_specs=[column, column, whole(cosine.shape), whole(cosine.shape)]
            + [whole(kv.shape) for kv in kvs]
            + [whole(e.shape) for e in extra],
            out_specs=[out_column, out_column] + [whole(s.shape) for s in dkv_shapes],
            scratch_shapes=[
                pltpu.VMEM((keys, 2 * size), BF),
                pltpu.VMEM((tiles, 2 * size + 16, TILE), BF),
                pltpu.VMEM((most, TILE, lanes), F32),
                pltpu.VMEM((most, TILE, lanes), BF),
                pltpu.VMEM((2 * size, lanes), BF),
                pltpu.VMEM((2 * size, lanes), BF),
                pltpu.VMEM((lanes, 2 * size), BF),
                pltpu.VMEM((lanes, 2 * size), BF),
                pltpu.VMEM((size + 16, lanes), F32),
                pltpu.VMEM((size, lanes), F32),
                pltpu.VMEM((keys, 2 * size), F32),
            ],
        ),
        compiler_params=pltpu.CompilerParams(
            vmem_limit_bytes=(24 if keys <= 4096 else 60) * MIB
        ),
        cost_estimate=pl.CostEstimate(
            flops=1000, bytes_accessed=1000, transcendentals=0
        ),
        name="attention",
    )(table, q_t, do_t, cosine, sine, *kvs, *extra)


def prologue_kernel(
    sc, x_hbm, xt, g_hbm, gt, gains, w_hbm, cos_ref, sin_ref, h1_ref, h2_ref, gg_ref, kv_ref, xo, w_kv, sem
):
    rows = xt.shape[0]
    copies = [
        pltpu.make_async_copy(x_hbm, xo, sem.at[0]),
        pltpu.make_async_copy(w_hbm, w_kv, sem.at[1]),
        pltpu.make_async_copy(g_hbm, gg_ref.at[0:rows, :], sem.at[2]),
    ]
    for copy in copies:
        copy.start()
    gg_ref[rows : 2 * rows, :] = gt[...]
    width = xt.shape[1]
    gain_one, bias_one, gain_two, bias_two = (
        gains[:, n * width : (n + 1) * width] for n in range(4)
    )
    for n, x in ((1, xt), (0, xo)):
        if n == 0:
            copies[0].wait()
        for t in range(rows // 128):
            here = slice(n * rows + t * 128, n * rows + (t + 1) * 128)
            hat, unused = normed(x[t * 128 : (t + 1) * 128, :].astype(F32))
            h1_ref[here, :] = (hat * gain_one + bias_one).astype(BF)
            h2_ref[here, :] = (hat * gain_two + bias_two).astype(BF)
    copies[1].wait()
    raw = dot(h1_ref[...], w_kv[...])
    kv = turn(raw.T, cos_ref[...], sin_ref[...]).T.astype(BF)
    kv_ref[pl.ds(pl.multiple_of(sc[0] * rows, rows), rows), :] = kv[:rows]
    kv_ref[pl.ds(pl.multiple_of((1 - sc[0]) * rows, rows), rows), :] = kv[rows:]
    copies[2].wait()


def half_copies(sc, w_query, w_out, query_s, out_s, sem):
    half = out_s.shape[0]
    at = pl.ds(pl.multiple_of(sc[0] * half, 128), half)
    return [
        pltpu.make_async_copy(w_query.at[:, at], query_s, sem.at[0]),
        pltpu.make_async_copy(w_out.at[at, :], out_s, sem.at[1]),
    ]


def project_kernel(
    sc, h_ref, g_ref, cos_ref, sin_ref, w_query, w_out, q_ref, do_ref, query_s, out_s, sem, *, size
):
    copies = half_copies(sc, w_query, w_out, query_s, out_s, sem)
    for copy in copies:
        copy.start()
    cosine, sine = cos_ref[...], sin_ref[...]
    copies[0].wait()
    raw = (dot(h_ref[...], query_s[...]) * (0.125 * LOG2E)).T
    for h in range(raw.shape[0] // size):
        at = slice(h * size, (h + 1) * size)
        q_ref[at, :] = turn(raw[at], cosine, sine).astype(BF)
    copies[1].wait()
    do_ref[...] = dot(out_s[...], g_ref[...], ((1,), (1,)))


def hidden_copies(sc, piece, w_up, w_down, up_s, down_s, sems, part, n_pair):
    copies = []
    for j in range(n_pair):
        source = pl.ds(pl.multiple_of((2 * j + sc[0]) * part + piece * LANES, LANES), LANES)
        at = slice(j * LANES, (j + 1) * LANES)
        if w_up is not None:
            copies.append(
                pltpu.make_async_copy(w_up.at[:, source], up_s.at[:, at], sems.at[0])
            )
        if w_down is not None:
            copies.append(
                pltpu.make_async_copy(w_down.at[source, :], down_s.at[at, :], sems.at[1])
            )
    return copies


def piece_of(sc, n):
    return 0 if n == 0 else (2 - sc[2] if n == 1 else 1 + sc[2])


def ffn_kernel(
    sc, h_ref, g_ref, w_up, w_down, act_ref, dup_ref, *refs, n, part, n_pair
):
    up_s, down_s, grad_s, sems = refs[-4:]
    outs = refs[:-4]
    rows, width = h_ref.shape
    copies = hidden_copies(sc, piece_of(sc, n), w_up, w_down, up_s, down_s, sems, part, n_pair)
    for copy in copies[0::2] + copies[1::2]:
        copy.start()
    for copy in copies[0::2] + copies[1::2]:
        copy.wait()

    def row_tile(r, carry):
        tile = pl.ds(pl.multiple_of(r * 128, 128), 128)
        act, slope = gelu_parts(dot(h_ref[tile, :], up_s[...]))
        act_ref[tile, :] = act.astype(BF)
        d_act = dot(g_ref[tile, :], down_s[...], ((1,), (1,)))
        dup_ref[tile, :] = (d_act * slope).astype(BF)
        return carry

    lax.fori_loop(0, rows // 128, row_tile, 0, unroll=2)
    up_rows = width // n_pair
    block_rows = width // WIDE * LANES

    def give(low, high, kind, first, value):
        here = slice(first, first + value.shape[0])
        if n == 0:
            outs[1 - low][high, kind * block_rows + first : kind * block_rows + here.stop, :] = value
        else:
            outs[0][kind ^ sc[3], low, high, here, :] = value

    grad_s[0 : n_pair * LANES, :] = dot(act_ref[...], g_ref[...], ((0,), (0,))).astype(BF)
    for low in range(2):
        for high in range(2):
            chip = sc[1] ^ (low + 2 * high)
            rows_at = pl.ds(pl.multiple_of(chip * LANES, LANES), LANES)
            for b in range(width // WIDE):
                give(low, high, 0, b * LANES, grad_s[rows_at, b * WIDE : (b + 1) * WIDE])
    span = n_pair * LANES
    grad_s[:, 0:span] = dot(h_ref[...], dup_ref[...], ((0,), (0,))).astype(BF)
    for low in range(2):
        for high in range(2):
            chip = sc[1] ^ (low + 2 * high)
            rows_at = pl.ds(pl.multiple_of(chip * up_rows, 64), up_rows)
            for b in range(span // WIDE):
                give(low, high, 1, b * up_rows, grad_s[rows_at, b * WIDE : (b + 1) * WIDE])


def ffn_gradients(table, h_two, g_two, w_up, w_down, n, part, n_pair):
    rows, width = h_two.shape
    span = n_pair * LANES
    block = width // WIDE * LANES
    if n == 0:
        outs = [shape((2, 2 * block, WIDE), BF)] * 2
    else:
        outs = [shape((2, 2, 2, block, WIDE), BF)]
    return call(
        functools.partial(ffn_kernel, n=n, part=part, n_pair=n_pair),
        "ffn_gradients",
        [shape((rows, span), BF)] * 2 + outs,
        [VM, VM, HBM, HBM],
        [VM] * (2 + len(outs)),
        [
            pltpu.VMEM((width, span), BF),
            pltpu.VMEM((span, width), BF),
            pltpu.VMEM((width, width), BF),
            pltpu.SemaphoreType.DMA((2,)),
        ],
        24,
    )(table, h_two, g_two, w_up, w_down)


def late_kernel(
    sc, h_ref, dq0, dq1, mix0, mix1, got0, got1, g_ref, send_ref, keep_ref, mix_ref, dq_s, mix_s, both_s,
    *, n_pair
):
    half = mix0.shape[0]
    rows = mix0.shape[1]
    width = 2 * half
    count = rows // BLK
    own = pl.multiple_of(sc[0] * half, 128)
    other = pl.multiple_of((1 - sc[0]) * half, 128)
    for n, (mix, got, dq) in enumerate(((mix0, got0, dq0), (mix1, got1, dq1))):
        for k in range(count):
            source = slice(k * BLK, (k + 1) * BLK)
            at = pl.ds(pl.multiple_of(sc[4 + n * count + k] * BLK, BLK), BLK)
            mix_ref[:, at] = mix[:, source]
            mix_s[pl.ds(own, half), at] = mix[:, source]
            mix_s[pl.ds(other, half), at] = got[:, source]
            dq_s[:, at] = dq[:, source]
    both_s[:, 0:half] = dot(h_ref[...], dq_s[...], ((0,), (1,))).astype(BF)
    both_s[:, half:width] = dot(mix_s[...], g_ref[:, pl.ds(own, half)]).astype(BF)
    block = width // n_pair
    quarter = keep_ref.shape[3]
    unit = 48
    for low in range(2):
        for high in range(2):
            chip = sc[1] ^ (low + 2 * high)
            for first in range(2):
                ref = send_ref if first else keep_ref
                for second in range(2):
                    part = 2 * (first ^ sc[2]) + (second ^ sc[3])
                    for r in range(quarter // unit):
                        at = part * quarter + r * unit
                        col, row = at // block, at % block
                        source = pl.ds(pl.multiple_of(chip * block + row, 16), unit)
                        lane = pl.ds(pl.multiple_of(col * WIDE, WIDE), WIDE)
                        ref[second, low, high, r * unit : (r + 1) * unit, :] = both_s[source, lane]


def late_gradients(table, h_one, dqs, mixes, gots, g_two, n_pair):
    half = dqs[0].shape[0]
    width = 2 * half
    rows = h_one.shape[0]
    quarter = width // n_pair * (width // WIDE) // 4
    return call(
        functools.partial(late_kernel, n_pair=n_pair),
        "late_gradients",
        [shape((2, 2, 2, quarter, WIDE), BF)] * 2 + [shape((half, rows), BF)] * 2,
        [VM] * 8,
        [VM] * 4,
        [
            pltpu.VMEM((width, rows), BF),
            pltpu.VMEM((width, width), BF),
        ],
        16,
    )(table, h_one, *dqs, *mixes, *gots, g_two)


def out_kernel(sc, a0, a1, a2, mix_ref, x_ref, w_down, w_out, own_ref, send_ref, down_s, out_s, sems, *, part, n_pair):
    half = out_s.shape[0]
    rows = x_ref.shape[0]
    span = n_pair * LANES
    copies = [
        pltpu.make_async_copy(
            w_out.at[pl.ds(pl.multiple_of(sc[0] * half, 128), half), :], out_s, sems.at[0]
        )
    ]
    for n in range(3):
        copies += hidden_copies(
            sc, piece_of(sc, n), None, w_down, None, down_s.at[n], sems, part, n_pair
        )
    for copy in copies:
        copy.start()
    for copy in copies:
        copy.wait()
    for n in range(2):
        here = slice(n * rows, (n + 1) * rows)
        total = dot(mix_ref[:, here], out_s[...], ((0,), (0,)))
        for k, act in enumerate((a0, a1, a2)):
            total = total + dot(act[here, :], down_s[k])
        if n == 0:
            own_ref[...] = total + x_ref[...].astype(F32)
        else:
            send_ref[...] = total.astype(BF)


def hat_kernel(sc, d0, d1, d2, dq_ref, xo, xt, gains, w_up, w_query, own_ref, send_ref, sum_ref, up_s, query_s, sems, *, part, n_pair):
    half = query_s.shape[1]
    rows, width = xo.shape
    copies = [
        pltpu.make_async_copy(
            w_query.at[:, pl.ds(pl.multiple_of(sc[0] * half, 128), half)], query_s, sems.at[1]
        )
    ]
    for n in range(3):
        copies += hidden_copies(
            sc, piece_of(sc, n), w_up, None, up_s.at[n], None, sems, part, n_pair
        )
    for copy in copies:
        copy.start()
    for copy in copies:
        copy.wait()
    gain_one, gain_two = gains[:, 0:width], gains[:, 2 * width : 3 * width]
    sums = [jnp.zeros((1, width), F32)] * 4
    for n, x in enumerate((xo, xt)):
        here = slice(n * rows, (n + 1) * rows)
        two = dot(d0[here, :], up_s[0], ((1,), (1,)))
        two = two + dot(d1[here, :], up_s[1], ((1,), (1,)))
        two = two + dot(d2[here, :], up_s[2], ((1,), (1,)))
        one = dot(dq_ref[:, here], query_s[...], ((0,), (1,)))
        hat, unused = normed(x[...].astype(F32))
        for k, value in enumerate((one * hat, one, two * hat, two)):
            sums[k] = sums[k] + jnp.sum(value, 0, keepdims=True)
        total = one * gain_one + two * gain_two
        if n == 0:
            own_ref[...] = total
        else:
            send_ref[...] = total.astype(BF)
    sum_ref[...] = jnp.concatenate(sums + [jnp.zeros((4, width), F32)], 0)


def last_kernel(sc, dkv_a, dkv_b, dkv_c, dkv_d, cos_ref, sin_ref, w_kv, h_ref, x_ref, gains, hat_own, hat_got, sum_ref, g_ref, grad_ref, send_ref, keep_ref, *, n_pair):
    rows, width = x_ref.shape
    dkv = sum(ref[...].astype(F32) for ref in (dkv_a, dkv_b, dkv_c, dkv_d)).T
    low_t = turn(dkv, cos_ref[:, 0:rows], -sin_ref[:, 0:rows]).astype(BF)
    low = low_t.T
    weight = dot(low_t, h_ref[0:rows, :]).T.astype(BF)
    d_kv = dot(low, w_kv[...], ((1,), (1,)))
    hat, scale = normed(x_ref[...].astype(F32))
    gain = gains[:, 0:width]
    total = hat_own[...] + hat_got[...].astype(F32) + d_kv * gain
    grad_ref[...] = g_ref[...].astype(F32) + scale * (
        total
        - jnp.mean(total, -1, keepdims=True)
        - hat * jnp.mean(total * hat, -1, keepdims=True)
    )
    sums = jnp.concatenate(
        [
            sum_ref[0:1, :] + jnp.sum(d_kv * hat, 0, keepdims=True),
            sum_ref[1:2, :] + jnp.sum(d_kv, 0, keepdims=True),
            sum_ref[2:4, :],
            jnp.zeros((4, width), F32),
        ],
        0,
    ).astype(BF)
    part = width // (2 * n_pair)
    lanes = weight.shape[1]
    for chip in range(n_pair):
        rel = chip ^ sc[1]
        low_bit, high_bit = rel % 2, rel // 2
        blocks = []
        for core in range(2):
            at = (2 * chip + core) * part
            piece = weight[at : at + part, :]
            blocks.append(jnp.concatenate([piece[: part // 2], piece[part // 2 :]], 1))
            row = sums[:, at : at + part]
            blocks.append(jnp.concatenate([row, jnp.zeros((8, 2 * lanes - part), BF)], 1))
        block = jnp.concatenate(blocks, 0)

        @pl.when(low_bit == 1)
        def _():
            send_ref[high_bit] = block

        @pl.when(low_bit == 0)
        def _():
            keep_ref[high_bit] = block


def down_kernel(sc, a_send, a_got, send_ref, got_ref, out_ref, *, width):
    block = width // WIDE * LANES
    for k in range(3):
        for b in range(width // WIDE):
            here = slice(b * LANES, (b + 1) * LANES)
            if k == 0:
                value = a_send[here, :].astype(F32) + a_got[here, :].astype(F32)
            else:
                at = pl.ds(pl.multiple_of(sc[3] * block + b * LANES, LANES), LANES)
                mine = send_ref[at, :].astype(F32)
                value = jnp.where(sc[2] == k - 1, mine, got_ref[at, :].astype(F32))
            out_ref[k * LANES : (k + 1) * LANES, b * WIDE : (b + 1) * WIDE] = value


def up_block(sc, k, b, parity, a_send, a_got, b_send, b_got, width, part):
    block = width // WIDE * LANES
    off = b * 2 * part + parity * part
    if k == 0:
        at = pl.ds(pl.multiple_of(block + off, 32), part)
        return a_send[at, :].astype(F32) + a_got[at, :].astype(F32)
    at = pl.ds(pl.multiple_of((1 - sc[3]) * block + off, 32), part)
    return jnp.where(
        sc[2] == k - 1, b_send[at, :].astype(F32), b_got[at, :].astype(F32)
    )


def late_block(sc, b, parity, send, got, part, quarter):
    pieces = []
    for r in range(2):
        at = b * 2 * part + parity * part + r * (part // 2)
        first, second = at // (2 * quarter), at // quarter % 2
        rel = (second ^ sc[3]) * quarter + at % quarter
        source = pl.ds(pl.multiple_of(rel, 16), part // 2)
        pieces.append(
            jnp.where(
                first == sc[2], send[source, :].astype(F32), got[source, :].astype(F32)
            )
        )
    return jnp.concatenate(pieces, 0)


def pack_up_kernel(sc, a_send, a_got, b_send, b_got, out_ref, own_ref, *, width, part):
    for which, ref in ((1, out_ref), (0, own_ref)):
        parity = sc[0] if which == 0 else 1 - sc[0]
        at = 0
        for k in range(3):
            for b in range(2):
                ref[at : at + part, :] = up_block(
                    sc, k, b, parity, a_send, a_got, b_send, b_got, width, part
                ).astype(BF)
                at += part


def pack_late_kernel(sc, last_send, last_got, out_ref, own_ref, *, width, part, quarter):
    for which, ref in ((1, out_ref), (0, own_ref)):
        parity = sc[0] if which == 0 else 1 - sc[0]
        at = 0
        for b in range(width // WIDE):
            ref[at : at + part, :] = late_block(
                sc, b, parity, last_send, last_got, part, quarter
            ).astype(BF)
            at += part
        few = (last_send.shape[0] - 2 * quarter) // 2
        source = pl.ds(pl.multiple_of(2 * quarter + parity * few, 8), few)
        ref[at : at + few, :] = (
            last_send[source, :].astype(F32) + last_got[source, :].astype(F32)
        ).astype(BF)


def final_up_kernel(sc, own_ref, got_ref, up_ref, *, part, n_pair):
    part_hidden = up_ref.shape[1] // (2 * n_pair)
    for which, ref in enumerate((own_ref, got_ref)):
        core = sc[0] if which == 0 else 1 - sc[0]
        for k in range(3):
            for j in range(n_pair):
                lane = (2 * j + core) * part_hidden + k * LANES
                rows = slice((2 * k + j // 2) * part, (2 * k + j // 2 + 1) * part)
                cols = slice(j % 2 * LANES, (j % 2 + 1) * LANES)
                up_ref[:, pl.ds(pl.multiple_of(lane, LANES), LANES)] = ref[rows, cols].astype(F32)


def final_late_kernel(sc, own_ref, got_ref, query_ref, proj_ref, kv_ref, norm_ref, *, part):
    half = query_ref.shape[1] // 2
    for which, ref in enumerate((own_ref, got_ref)):
        core = sc[0] if which == 0 else 1 - sc[0]
        for n in range(2 * half // LANES):
            rows = slice(n // 2 * part, (n // 2 + 1) * part)
            value = ref[rows, n % 2 * LANES : (n % 2 + 1) * LANES].astype(F32)
            to, m = (query_ref, n) if n < half // LANES else (proj_ref, n - half // LANES)
            to[:, pl.ds(pl.multiple_of(core * half + m * LANES, LANES), LANES)] = value
    base = 2 * half // WIDE * part
    few = own_ref[base:, :].astype(F32) + got_ref[base:, :].astype(F32)
    kv_ref[0 : part // 2, :] = few[0 : part // 2, 0:LANES]
    kv_ref[part // 2 : part, :] = few[0 : part // 2, LANES:WIDE]
    norm_ref[...] = few[part // 2 : part // 2 + 8, :]


class Links:
    def __init__(self, n_grp, n_ctx):
        self.n_grp, self.n_ctx, self.n_pair = n_grp, n_ctx, n_ctx // 2
        self.small = (n_grp, n_ctx) == (4, 8)
        self.ctx = lax.axis_index("ctx")
        self.grp = lax.axis_index("grp")
        self.core = self.ctx % 2
        self.chip = self.ctx // 2
        self.groups = [[2 * z + c for z in range(self.n_pair)] for c in range(2)]

    def swap(self, value):
        return lax.ppermute(value, "ctx", [(i, i ^ 1) for i in range(self.n_ctx)])

    def permute(self, value, target):
        pairs = []
        for g in range(self.n_grp):
            for i in range(self.n_ctx):
                y, x, z, c = target(g // 2, g % 2, i // 2, i % 2)
                pairs.append((g * self.n_ctx + i, (2 * y + x) * self.n_ctx + 2 * z + c))
        return lax.ppermute(value, ("grp", "ctx"), pairs)

    def cross(self, value, stage):
        return self.permute(
            value, lambda y, x, z, c: (y, 1 - x, z, c) if c == stage else (1 - y, x, z, c)
        )

    def bit(self, stage):
        y, x = self.grp // 2, self.grp % 2
        return jnp.where(self.core == stage, x, y)

    def flip(self, value, bit):
        return self.permute(value, lambda y, x, z, c: (y, x, z ^ bit, c))

    def reduce(self, parts):
        moved = lax.all_to_all(parts, "ctx", 0, 0, axis_index_groups=self.groups)
        return lax.psum(jnp.sum(moved.astype(F32), 0).astype(BF), "grp")


def add(*values):
    return sum(value.astype(F32) for value in values).astype(BF)


def low(value):
    return value.astype(BF)


def shards_small(
    layer_input, block_table, ln1_gain, ln1_bias, ln2_gain, ln2_bias,
    w_query, w_keyval, w_out, w_up, w_down, cotangent, *, n_grp, n_ctx,
):
    links = Links(n_grp, n_ctx)
    core, chip, n_pair = links.core, links.chip, links.n_pair
    rows, width = layer_input.shape
    lanes = w_keyval.shape[1]
    size = lanes // 2
    hidden = w_up.shape[1]
    group_len = block_table.shape[1] * BLK
    part, part_hidden = width // n_ctx, hidden // n_ctx
    half = width // 2
    per_chip = 2 * rows // BLK
    table = block_table[0]
    count = rows // BLK
    gains = jnp.concatenate(
        [v.astype(F32) for v in (ln1_gain, ln1_bias, ln2_gain, ln2_bias)]
    ).reshape(1, 4 * width)

    x_other, g_other = links.swap(layer_input), links.swap(cotangent)
    column = jnp.arange(2 * rows, dtype=jnp.int32)
    slot = chip * per_chip + lax.rem(column // BLK + core * count, per_chip)
    slots = jnp.arange(table.shape[0], dtype=jnp.int32)
    canon = jnp.sum(jnp.where(slots[:, None] == slot[None, :], table[:, None], 0), 0)
    canon = canon * BLK + column % BLK
    prompt_len = group_len // 2
    cont_span = min(CONT, prompt_len)
    position = jnp.where(
        canon < prompt_len, canon, prompt_len + (canon - prompt_len) % cont_span
    )
    cosine, sine = rope_tables(position)

    h_one, h_two, g_two, kv_low = call(
        prologue_kernel,
        "prologue",
        [shape((2 * rows, width), BF)] * 3 + [shape((2 * rows, lanes), BF)],
        [HBM, VM, HBM, VM, VM, HBM, VM, VM],
        [VM] * 4,
        [
            pltpu.VMEM((rows, width), BF),
            pltpu.VMEM((width, lanes), BF),
            pltpu.SemaphoreType.DMA((3,)),
        ],
        16,
    )(table, layer_input, x_other, cotangent, g_other, gains, w_keyval, cosine, sine)

    kv_got = links.flip(kv_low, 1)
    ffn = functools.partial(
        ffn_gradients, table, w_up=w_up, w_down=w_down, part=part_hidden, n_pair=n_pair
    )
    act_1, dup_1, b_send = ffn(h_two, g_two, n=1)
    b_send, kv_got = meet(b_send, kv_got)
    kv_near = jnp.concatenate([kv_low, kv_got], 0)
    kv_far = links.flip(kv_near, 2)
    b_got = links.cross(b_send, 0)
    act_2, dup_2, b_keep = ffn(tie(h_two, b_send, kv_near), g_two, n=2)
    act_0, dup_0, a_send, a_keep = ffn(tie(h_two, b_keep), g_two, n=0)
    a_send, kv_far = meet(a_send, kv_far)
    a_got = links.flip(a_send, 1)

    q_t, do_t = call(
        functools.partial(project_kernel, size=size),
        "project",
        [shape((half, 2 * rows), BF), shape((half, 2 * rows), F32)],
        [VM] * 4 + [HBM] * 2,
        [VM] * 2,
        [
            pltpu.VMEM((width, half), BF),
            pltpu.VMEM((half, width), BF),
            pltpu.SemaphoreType.DMA((2,)),
        ],
        16,
    )(table, tie(h_one, a_send), g_two, cosine, sine, w_query, w_out)
    q_t, b_got = meet(q_t, b_got)
    b_send = add(b_keep[1], b_got[1])
    b_got_2 = links.cross(b_send, 1)

    attend = functools.partial(
        attention, table, do_t=do_t, cosine=cosine, sine=sine, kvs=(kv_near, kv_far),
        count=count, per_chip=per_chip, split=True,
    )
    mix_0, dq_0, carried = attend(
        q_t=tie(q_t, b_send), carried=None, start=0, last_call=False
    )
    carried, a_got, b_got_2 = meet(carried, a_got, b_got_2)
    b_send = add(b_keep[0, 1], b_got[0, 1], b_got_2[1])
    b_got_3 = links.flip(b_send, 1)
    a_send = add(a_keep[1], tie(a_got, b_send)[1])
    a_got_2 = links.flip(a_send, 2)
    mix_1, dq_1, dkv_send, dkv_keep = attend(
        q_t=tie(q_t, a_send, b_send, carried), carried=carried, start=count, last_call=True
    )
    mix_0, mix_1, dkv_send, a_got_2, b_got_3 = meet(mix_0, mix_1, dkv_send, a_got_2, b_got_3)
    dkv_got = links.swap(dkv_send)
    mix_0_got, mix_1_got = links.swap(mix_0), links.swap(mix_1)
    dkv_got, mix_0_got, mix_1_got = meet(dkv_got, mix_0_got, mix_1_got)
    dkv_sends = [add(dkv_keep[at], dkv_got[at]) for at in ((1, 0), (0, 1), (1, 1))]
    dkv_gots = [links.flip(value, n + 1) for n, value in enumerate(dkv_sends)]
    a_sum = add(a_keep[0], a_got[0], tie(a_got_2, *dkv_sends))
    a_got = links.cross(a_sum, 1)
    late_send, late_keep, mix_own, dq_own = late_gradients(
        table, tie(h_one, a_sum, *dkv_sends), (dq_0, dq_1), (mix_0, mix_1), (mix_0_got, mix_1_got), g_two, n_pair
    )
    late_got = links.cross(late_send, 0)
    b_send = add(b_keep[0, 0, 1], b_got[0, 0, 1], b_got_2[0, 1], tie(b_got_3, late_send)[1])
    b_got_4 = links.flip(b_send, 2)

    w_specs = [HBM] * 2
    hat_own, hat_send, sums = call(
        functools.partial(hat_kernel, part=part_hidden, n_pair=n_pair),
        "norms",
        [shape((rows, width), F32), shape((rows, width), BF), shape((8, width), F32)],
        [VM] * 7 + w_specs,
        [VM] * 3,
        [
            pltpu.VMEM((3, width, n_pair * LANES), BF),
            pltpu.VMEM((width, half), BF),
            pltpu.SemaphoreType.DMA((2,)),
        ],
        24,
    )(
        table, dup_0, dup_1, tie(dup_2, b_send), dq_own, layer_input, x_other, gains,
        w_up, w_query,
    )
    hat_send, late_got, a_got, *dkv_gots = meet(hat_send, late_got, a_got, *dkv_gots)
    hat_got = links.swap(hat_send)
    late_send = add(late_keep[1], late_got[1])
    late_got_2 = links.cross(late_send, 1)
    a_sum = add(a_sum, tie(a_got, late_send))
    a_got = links.cross(a_sum, 0)
    dkv_own = add(dkv_keep[0, 0], dkv_got[0, 0])
    a_sum, hat_got = meet(a_sum, hat_got)

    few = part // 2 + 8
    in_grad, few_send, few_keep = call(
        functools.partial(last_kernel, n_pair=n_pair),
        "last",
        [shape((rows, width), F32)] + [shape((2, 2 * few, 2 * lanes), BF)] * 2,
        [VM] * 14,
        [VM] * 3,
        [],
        16,
    )(
        table, dkv_own, *dkv_gots, tie(cosine, a_sum), sine, w_keyval, h_one,
        layer_input, gains, hat_own, hat_got, sums, cotangent,
    )
    few_send, late_got_2, b_got_4 = meet(few_send, late_got_2, b_got_4)
    quarter = late_keep.shape[3]
    last_send = jnp.concatenate(
        [add(late_keep[0, 1], late_got[0, 1], late_got_2[1]), few_send], 1
    )
    last_got = links.flip(last_send, 1)
    b_sum = add(
        b_keep[0, 0, 0], b_got[0, 0, 0], b_got_2[0, 0], b_got_3[0], tie(b_got_4, last_send)
    )
    b_got = links.cross(b_sum, 1)

    out_own, out_send = call(
        functools.partial(out_kernel, part=part_hidden, n_pair=n_pair),
        "outputs",
        [shape((rows, width), F32), shape((rows, width), BF)],
        [VM] * 5 + w_specs,
        [VM] * 2,
        [
            pltpu.VMEM((3, n_pair * LANES, width), BF),
            pltpu.VMEM((half, width), BF),
            pltpu.SemaphoreType.DMA((2,)),
        ],
        24,
    )(
        table, act_0, act_1, tie(act_2, b_sum), mix_own, layer_input, w_down, w_out,
    )
    out_send, last_got, a_got, b_got = meet(out_send, last_got, a_got, b_got)
    out_got = links.swap(out_send)
    last_keep = jnp.concatenate(
        [add(late_keep[0, 0], late_got[0, 0], late_got_2[0]), few_keep], 1
    )
    last_send = add(last_keep[1], last_got[1])
    last_got_2 = links.flip(last_send, 2)
    b_sum = jnp.concatenate([b_sum, b_got], 0)
    b_got = links.cross(tie(b_sum, last_send), 0)
    out_got = tie(out_got, b_sum, last_send)
    layer_output = low(out_own + out_got.astype(F32))
    b_got, layer_output = meet(b_got, layer_output)
    up_send, up_own = call(
        functools.partial(pack_up_kernel, width=width, part=part),
        "pack_up", [shape((6 * part, WIDE), BF)] * 2, [VM] * 4, [VM] * 2, [], 8,
    )(table, a_sum, a_got, b_sum, b_got)
    up_got = links.swap(up_send)
    last_got_2 = tie(last_got_2, up_send)
    last = add(last_keep[0], last_got[0], last_got_2)
    last_got = links.cross(last, 1)
    total_down = call(
        functools.partial(down_kernel, width=width),
        "down", shape((part_hidden, width), F32), [VM] * 4, VM, [], 8,
    )(table, tie(a_sum, last), a_got, b_sum, b_got)
    total_down, last_got, up_got = meet(total_down, last_got, up_got)
    last = jnp.concatenate(
        [last[:quarter], last_got[:quarter], add(last[quarter:], last_got[quarter:])], 0
    )
    last_got = links.cross(last, 0)
    total_up = call(
        functools.partial(final_up_kernel, part=part, n_pair=n_pair),
        "final_up", shape((part, hidden), F32), [VM] * 2, VM, [], 8,
    )(table, tie(up_own, last), up_got)
    total_up, last_got = meet(total_up, last_got)
    other, own = call(
        functools.partial(pack_late_kernel, width=width, part=part, quarter=quarter),
        "pack_late", [shape((width // WIDE * part + few, WIDE), BF)] * 2, [VM] * 2, [VM] * 2, [], 8,
    )(table, last, last_got)
    got = links.swap(other)
    total_query, total_out, total_kv, norm = call(
        functools.partial(final_late_kernel, part=part),
        "final_late",
        [
            shape((part, width), F32),
            shape((part, width), F32),
            shape((part, lanes), F32),
            shape((8, WIDE), F32),
        ],
        [VM] * 2,
        [VM] * 4,
        [],
        8,
    )(table, own, got)
    norms = [norm[n, :part] for n in range(4)]
    return (layer_output, in_grad, *norms, total_query, total_kv, total_out, total_up, total_down)


def rotate_rows(values, cosine, sine):
    return turn(values.T, cosine, sine).T


def shards(
    layer_input, block_table, ln1_gain, ln1_bias, ln2_gain, ln2_bias,
    w_query, w_keyval, w_out, w_up, w_down, cotangent, *, n_grp, n_ctx,
):
    links = Links(n_grp, n_ctx)
    core, chip, n_pair = links.core, links.chip, links.n_pair
    rows, width = layer_input.shape
    size = w_keyval.shape[1] // 2
    hidden = w_up.shape[1]
    group_len = block_table.shape[1] * BLK
    part_rows, part_hidden = width // n_ctx, hidden // n_ctx
    half_width, half_hidden = width // 2, hidden // 2
    per_chip = 2 * rows // BLK
    table = block_table[0]

    def both(own, other):
        return jnp.concatenate(
            [jnp.where(core == 0, own, other), jnp.where(core == 0, other, own)], 0
        )

    def mine(value, own_core):
        return lax.dynamic_slice_in_dim(value, own_core * rows, rows, 0)

    x_two = both(layer_input, links.swap(layer_input))
    g_two = both(cotangent, links.swap(cotangent))
    canon = (
        lax.dynamic_slice_in_dim(table, chip * per_chip, per_chip)[:, None] * BLK
        + jnp.arange(BLK, dtype=jnp.int32)[None, :]
    ).reshape(2 * rows)
    prompt_len = group_len // 2
    cont_span = min(CONT, prompt_len)
    position = jnp.where(
        canon < prompt_len, canon, prompt_len + (canon - prompt_len) % cont_span
    )
    cosine, sine = rope_tables(position)
    gain_one, gain_two = ln1_gain.astype(F32), ln2_gain.astype(F32)
    hat, scale = normed(x_two.astype(F32))
    h_one = low(hat * gain_one + ln1_bias.astype(F32))
    h_two = low(hat * gain_two + ln2_bias.astype(F32))
    kv_raw = dot(h_one, w_keyval)
    kv_low = low(
        jnp.concatenate([rotate_rows(kv_raw[:, :size], cosine, sine), kv_raw[:, size:]], -1)
    )
    kv_all = lax.all_gather(kv_low, "ctx", axis=0, axis_index_groups=links.groups, tiled=True)

    up_half = lax.dynamic_index_in_dim(
        w_up.reshape(width, n_pair, 2, part_hidden), core, 2, False
    ).reshape(width, half_hidden)
    down_half = lax.dynamic_index_in_dim(
        w_down.reshape(n_pair, 2, part_hidden, width), core, 1, False
    ).reshape(half_hidden, width)
    act, slope = gelu_parts(dot(h_two, up_half))
    act = low(act)
    grad_down = low(dot(act, g_two, ((0,), (0,))))
    total_down = links.reduce(grad_down.reshape(n_pair, part_hidden, width))
    grad_up = low(dot(g_two, down_half, ((1,), (1,))) * slope)
    grad_up_w = low(dot(h_two, grad_up, ((0,), (0,))))
    total_up = links.reduce(grad_up_w.reshape(n_pair, 2 * part_rows, half_hidden))

    query_half = lax.dynamic_slice_in_dim(w_query, core * half_width, half_width, 1)
    out_half = lax.dynamic_slice_in_dim(w_out, core * half_width, half_width, 0)
    q_raw = dot(query_half, h_one, ((0,), (1,))) * (0.125 * LOG2E)
    q_t = low(
        jax.vmap(turn, (0, None, None))(q_raw.reshape(-1, size, 2 * rows), cosine, sine)
    ).reshape(half_width, 2 * rows)
    do_t = dot(out_half, g_two, ((1,), (1,)))
    mix_t, dq_t, dkv_part = attention(
        table, q_t, do_t, cosine, sine, (kv_all,), None, 0, per_chip, per_chip, True, False
    )

    dkv_part = dkv_part.reshape(n_pair, 2, rows, 2 * size)
    dkv_own = lax.dynamic_index_in_dim(dkv_part, core, 1, False)
    dkv_got = links.swap(lax.dynamic_index_in_dim(dkv_part, 1 - core, 1, False))
    moved = lax.all_to_all(
        add(dkv_own, dkv_got), "ctx", 0, 0, axis_index_groups=links.groups
    )
    dkv = jnp.sum(moved.astype(F32), 0)
    cos_own = lax.dynamic_slice_in_dim(cosine, core * rows, rows, 1)
    sin_own = lax.dynamic_slice_in_dim(sine, core * rows, rows, 1)
    dkv_low = low(
        jnp.concatenate([rotate_rows(dkv[:, :size], cos_own, -sin_own), dkv[:, size:]], -1)
    )

    mix_got = links.swap(mix_t)
    mix_all = jnp.concatenate(
        [jnp.where(core == 0, mix_t, mix_got), jnp.where(core == 0, mix_got, mix_t)], 0
    )
    g_half = lax.dynamic_slice_in_dim(g_two, core * half_width, half_width, 1)
    grad_q_w = low(dot(h_one, dq_t, ((0,), (1,))))
    grad_out_w = low(dot(mix_all, g_half))
    late = jnp.concatenate([grad_q_w, grad_out_w], 1).reshape(n_pair, 2 * part_rows, width)
    total_late = links.reduce(late)

    out_part = dot(act, down_half) + dot(mix_t, out_half, ((0,), (0,)))
    out_got = links.swap(low(mine(out_part, 1 - core)))
    layer_output = low(layer_input.astype(F32) + mine(out_part, core) + out_got.astype(F32))

    d_two = dot(grad_up, up_half, ((1,), (1,)))
    d_one = dot(dq_t, query_half, ((0,), (1,)))
    d_kv = dot(dkv_low, w_keyval, ((1,), (1,)))
    row_core = lax.broadcasted_iota(jnp.int32, (2 * rows, 1), 0) // rows
    d_one = d_one + jnp.where(row_core == core, jnp.concatenate([d_kv, d_kv], 0), 0.0)
    sums = jnp.stack([jnp.sum(v, 0) for v in (d_one * hat, d_one, d_two * hat, d_two)])
    d_hat = d_one * gain_one + d_two * gain_two
    hat_got = links.swap(low(mine(d_hat, 1 - core)))
    d_hat = mine(d_hat, core) + hat_got.astype(F32)
    hat_own = mine(hat, core)
    in_grad = cotangent.astype(F32) + mine(scale, core) * (
        d_hat
        - jnp.mean(d_hat, -1, keepdims=True)
        - hat_own * jnp.mean(d_hat * hat_own, -1, keepdims=True)
    )

    grad_kv_w = dot(mine(h_one, core), dkv_low, ((0,), (0,)))
    sum_rows = sums.reshape(4, n_pair, 2, part_rows).transpose(1, 2, 0, 3)
    sum_rows = jnp.pad(sum_rows, ((0, 0), (0, 0), (0, 0), (0, 2 * size - part_rows)))
    few = jnp.concatenate([grad_kv_w.reshape(n_pair, 2, part_rows, 2 * size), sum_rows], 2)
    few = links.reduce(low(few).reshape(n_pair, 2 * (part_rows + 4), 2 * size))
    few = few.reshape(2, part_rows + 4, 2 * size)
    few_got = links.swap(lax.dynamic_index_in_dim(few, 1 - core, 0, False))
    few = lax.dynamic_index_in_dim(few, core, 0, False).astype(F32) + few_got.astype(F32)

    halves = jnp.concatenate(
        [total_up.reshape(2, part_rows, half_hidden), total_late.reshape(2, part_rows, width)], -1
    )
    own = lax.dynamic_index_in_dim(halves, core, 0, False)
    got = links.swap(lax.dynamic_index_in_dim(halves, 1 - core, 0, False))
    sides = jnp.stack([jnp.where(core == 0, own, got), jnp.where(core == 0, got, own)]).astype(F32)
    ups = sides[:, :, :half_hidden].reshape(2, part_rows, n_pair, part_hidden)
    total_up = ups.transpose(1, 2, 0, 3).reshape(part_rows, hidden)
    lates = sides[:, :, half_hidden:]
    total_query = lates[:, :, :half_width].transpose(1, 0, 2).reshape(part_rows, width)
    total_out = lates[:, :, half_width:].transpose(1, 0, 2).reshape(part_rows, width)
    norms = [few[part_rows + n, :part_rows] for n in range(4)]
    total_kv = few[:part_rows]
    total_down = total_down.astype(F32)
    return (layer_output, in_grad, *norms, total_query, total_kv, total_out, total_up, total_down)


def solution(mesh):
    n_grp, n_ctx = mesh.shape["grp"], mesh.shape["ctx"]
    body = shards_small if (n_grp, n_ctx) == (4, 8) else shards
    return jax.shard_map(
        functools.partial(body, n_grp=n_grp, n_ctx=n_ctx),
        mesh=mesh,
        in_specs=(P(("grp", "ctx"), None), P("grp", None))
        + (P(),) * 9
        + (P(("grp", "ctx"), None),),
        out_specs=(P(("grp", "ctx"), None),) * 2 + (P("ctx"),) * 4 + (P("ctx", None),) * 5,
        check_vma=False,
    )
```
